32 devices in a mesh: narrow: 2 (over y), wide: 4 (over x, core), seq: 4 (over z).
Axes of the slice: x: 2, y: 2, z: 4, core: 2. Of those that a mesh axis runs over, the one named last changes fastest.
Arguments:
- tokens: bfloat16 [6144, 2048], P(('narrow', 'seq'), 'wide'), may hold values from -6 to 6
- gain_attn: float32 [2048], replicated, may hold values from 0.1 to 1.9
- w_query: bfloat16 [2048, 8, 256], P(('narrow', 'seq'), 'wide'), may hold values from -0.125 to 0.125
- w_key: bfloat16 [2048, 8, 64], P(('narrow', 'seq'), 'wide'), may hold values from -0.125 to 0.125
- w_value: bfloat16 [2048, 8, 64], P(('narrow', 'seq'), 'wide'), may hold values from -0.125 to 0.125
- w_out: bfloat16 [2048, 8, 256], P(('narrow', 'seq'), 'wide'), may hold values from -1 to 1
- gain_ffn: float32 [2048], replicated, may hold values from 0.1 to 1.9
- w_gate: bfloat16 [2048, 8192], P('narrow', 'wide'), may hold values from -0.125 to 0.125
- w_up: bfloat16 [2048, 8192], P('narrow', 'wide'), may hold values from -0.125 to 0.125
- w_down: bfloat16 [2048, 8192], P('narrow', 'wide'), may hold values from -0.0625 to 0.0625
- lengths: int32 [4], replicated, may hold values from 128 to 5376, as said below
- cotangent: bfloat16 [6144, 2048], P(('narrow', 'seq'), 'wide'), may hold values from -6 to 6
Outputs:
- output: bfloat16 [6144, 2048], P(('narrow', 'seq'), 'wide')
- grad_input: bfloat16 [6144, 2048], P(('narrow', 'seq'), 'wide')
- grad_gain_attn: float32 [2048], P(('narrow', 'seq'))
- grad_query: float32 [2048, 8, 256], P(('narrow', 'seq'), 'wide')
- grad_key: float32 [2048, 8, 64], P(('narrow', 'seq'), 'wide')
- grad_value: float32 [2048, 8, 64], P(('narrow', 'seq'), 'wide')
- grad_out: float32 [2048, 8, 256], P(('narrow', 'seq'), 'wide')
- grad_gain_ffn: float32 [2048], P(('narrow', 'seq'))
- grad_gate: float32 [2048, 8192], P(('narrow', 'seq'), 'wide')
- grad_up: float32 [2048, 8192], P(('narrow', 'seq'), 'wide')
- grad_down: float32 [2048, 8192], P(('narrow', 'seq'), 'wide')
The draws below stay inside these ranges and needn't reach their ends.
Inputs may be any that keep to these rules, and one draw needn't show every extreme that they name: The second sequence has 5376 tokens and the last 128; the first has fewer than 768; the lengths sum to 6144.
All inputs are finite; a program needn't handle non-finite values.
Results may differ from the reference program's by a relative error of at most 0.02.
Values may be sent and summed in bfloat16 or wider, within the bound.
A program may use at most 192 MiB of HBM per device.

```python
import math
import jax
import jax.numpy as jnp
from jax import lax

D = 2048
KVH = 8
HD = 64
FF = 8192
GROUP = 4
TOK_DEV = 768
MINLEN = 128
TOKENS = 6144


def draw_lengths(key, part):
    head_len = jax.random.randint(key, (1,), MINLEN, TOK_DEV - 2 * MINLEN + 1).astype(jnp.int32)
    longest = jnp.full((1,), TOKENS - TOK_DEV, jnp.int32)
    third_len = TOK_DEV - MINLEN - head_len
    last_len = jnp.full((1,), MINLEN, jnp.int32)
    return jnp.concatenate([head_len, longest, third_len, last_len]).astype(jnp.int32)


def block_scale(key, extent, cuts, least, high):
    loudness, own = 1.0, jax.random.fold_in(key, 6)
    for position, blocks in cuts:
        draws = jnp.exp(jax.random.uniform(jax.random.fold_in(own, position), (blocks,), jnp.float32, least / len(cuts), high / len(cuts)))
        loudness = loudness * jnp.repeat(draws, extent[position] // blocks).reshape([-1 if axis == position else 1 for axis in range(len(extent))])
    return loudness


def noise(own_key, extent, width, most, shards=(), kind=jnp.bfloat16):
    entries = jax.random.normal(own_key, extent, jnp.float32) * width
    if len(shards) > 0:
        entries = block_scale(own_key, extent, shards, -0.22, 0.18) * entries
    return jnp.clip(entries, min=-most, max=most).astype(kind)


def setup_inputs(seed: int = 0) -> dict:
    splits = jax.random.split(jax.random.key(seed), 13)
    return {
        "tokens": noise(splits[0], (TOKENS, D), 1.0, 6.0, ((0, 8), (1, 4))),
        "gain_attn": jnp.clip(1.0 + 0.18 * jax.random.normal(splits[1], (D,), jnp.float32), 0.1, 1.9),
        "w_query": noise(splits[2], (D, KVH, GROUP * HD), D ** -0.5, 0.125, ((0, 8), (1, 4))),
        "w_key": noise(splits[3], (D, KVH, HD), D ** -0.5, 0.125, ((0, 8), (1, 4))),
        "w_value": noise(splits[4], (D, KVH, HD), D ** -0.5, 0.125, ((0, 8), (1, 4))),
        "w_out": noise(splits[5], (D, KVH, GROUP * HD), 32 ** -0.5, 1.0, ((0, 8), (1, 4))),
        "gain_ffn": jnp.clip(1.0 + 0.18 * jax.random.normal(splits[6], (D,), jnp.float32), 0.1, 1.9),
        "w_gate": noise(splits[7], (D, FF), D ** -0.5, 0.125, ((0, 2), (1, 4))),
        "w_up": noise(splits[8], (D, FF), D ** -0.5, 0.125, ((0, 2), (1, 4))),
        "w_down": noise(splits[9], (D, FF), FF ** -0.5, 0.0625, ((0, 2), (1, 4))),
        "lengths": draw_lengths(jax.random.fold_in(splits[12], 71), 0),
        "cotangent": noise(splits[11], (TOKENS, D), 1.0, 6.0, ((0, 8), (1, 4))),
    }


ROPE_THETA = 500000.0
ROPE_FACTOR = 32.0
LOW_FACTOR = 1.0
HIGH_FACTOR = 4.0
OLD_CONTEXT = 8192.0
NORM_EPSILON = 1e-05
HIGHEST = lax.Precision.HIGHEST

@jax.custom_vjp
def low(v):
    return lax.optimization_barrier(v.astype(jnp.bfloat16)).astype(jnp.float32)

@jax.custom_vjp
def low_back(v):
    return v

def low_keep(v):
    return (low(v), None)

def low_pass(kept, grad):
    return (grad,)

def back_keep(v):
    return (v, None)

def back_low(kept, grad):
    return (low(grad),)
low.defvjp(low_keep, low_pass)
low_back.defvjp(back_keep, back_low)

def frequencies(head_dim):
    freq_index = jnp.arange(head_dim // 2, dtype=jnp.float32)
    base_freq = jnp.exp(freq_index * (-2.0 * math.log(ROPE_THETA) / head_dim))
    wavelen = 2.0 * math.pi / base_freq
    smooth = jnp.clip((OLD_CONTEXT / wavelen - LOW_FACTOR) / (HIGH_FACTOR - LOW_FACTOR), 0.0, 1.0)
    return (1.0 - smooth) * base_freq / ROPE_FACTOR + smooth * base_freq

def seq_starts(lengths, row_ids):
    seq_ends = jnp.cumsum(lengths)
    begins = seq_ends - lengths
    found_at = jnp.where(begins[None, :] <= row_ids[:, None], begins[None, :], 0)
    return lax.optimization_barrier(jnp.max(found_at, axis=1)).astype(jnp.int32)

def rotation(positions, head_dim):
    angles = positions.astype(jnp.float32)[:, None] * frequencies(head_dim)[None, :]
    return (jnp.cos(angles), jnp.sin(angles))

def rotate(values, cos_table, sin_table):
    half_dim = values.shape[-1] // 2
    bcast_shape = (cos_table.shape[0],) + (1,) * (values.ndim - 2) + (half_dim,)
    cos_part = cos_table.reshape(bcast_shape)
    sin_part = sin_table.reshape(bcast_shape)
    first_half = values[..., :half_dim]
    second = values[..., half_dim:]
    return jnp.concatenate([first_half * cos_part - second * sin_part, second * cos_part + first_half * sin_part], axis=-1)

def attend(query_all, key_all, value_all, seq_first):
    total_rows = query_all.shape[0]
    heads_kv = key_all.shape[1]
    head_dim = key_all.shape[2]
    group_size = query_all.shape[2]
    score_scale = 1.0 / math.sqrt(head_dim)
    block_count = total_rows // TOK_DEV
    key_rows = jnp.arange(total_rows, dtype=jnp.int32)
    query_blocks = query_all.reshape(block_count, TOK_DEV, heads_kv, group_size, head_dim)
    first_blocks = seq_first.reshape(block_count, TOK_DEV)
    row_blocks = key_rows.reshape(block_count, TOK_DEV)
    keys_by_head = jnp.transpose(key_all, (1, 0, 2))
    values_by_head = jnp.transpose(value_all, (1, 0, 2))

    @jax.checkpoint
    def one_block(block_args):
        query_blk, first_blk, row_blk = block_args
        causal_mask = (key_rows[None, :] >= first_blk[:, None]) & (key_rows[None, :] <= row_blk[:, None])

        def one_head(head_args):
            query_head, key_head, value_head = head_args
            raw_scores = low_back(jnp.einsum('qgd,kd->gqk', query_head, key_head, precision=HIGHEST) * score_scale)
            weights = jnp.where(causal_mask[None], jnp.exp(raw_scores), 0.0)
            row_total = lax.optimization_barrier(jnp.sum(weights, axis=2))
            summed = low_back(jnp.einsum('gqk,kd->qgd', low(weights), value_head, precision=HIGHEST))
            return summed / jnp.transpose(row_total)[:, :, None]
        per_head = lax.map(one_head, (jnp.transpose(query_blk, (1, 0, 2, 3)), keys_by_head, values_by_head))
        return jnp.transpose(per_head, (1, 0, 2, 3))
    result = lax.map(one_block, (query_blocks, first_blocks, row_blocks))
    return result.reshape(total_rows, heads_kv, group_size, head_dim)

def forward(inputs, gain_attn, w_query, w_key, w_value, w_out, gain_ffn, w_gate, w_up, w_down, seq_first, cos_table, sin_table):
    total_rows = inputs.shape[0]
    model_width = inputs.shape[1]
    heads_kv = w_key.shape[1]
    head_dim = w_key.shape[2]
    group_size = w_query.shape[2] // head_dim
    recip1 = lax.rsqrt(lax.optimization_barrier(jnp.mean(inputs * inputs, axis=1, keepdims=True)) + NORM_EPSILON)
    normed1 = low(inputs * recip1 * gain_attn)
    query_raw = low_back(jnp.dot(normed1, w_query.reshape(model_width, -1), precision=HIGHEST))
    key_raw = low_back(jnp.dot(normed1, w_key.reshape(model_width, -1), precision=HIGHEST))
    value_raw = low_back(jnp.dot(normed1, w_value.reshape(model_width, -1), precision=HIGHEST))
    query_rot = low(rotate(query_raw.reshape(total_rows, heads_kv, group_size, head_dim), cos_table, sin_table))
    key_rot = low(rotate(key_raw.reshape(total_rows, heads_kv, head_dim), cos_table, sin_table))
    value_low = low(value_raw.reshape(total_rows, heads_kv, head_dim))
    attn_out = attend(query_rot, key_rot, value_low, seq_first)
    attn_low = low(attn_out).reshape(total_rows, heads_kv, group_size * head_dim)
    branch = low_back(jnp.einsum('tkc,dkc->td', attn_low, w_out, precision=HIGHEST))
    residual = inputs + branch
    recip2 = lax.rsqrt(lax.optimization_barrier(jnp.mean(residual * residual, axis=1, keepdims=True)) + NORM_EPSILON)
    normed2 = low(residual * recip2 * gain_ffn)
    gate_val = low_back(jnp.dot(normed2, w_gate, precision=HIGHEST))
    up_val = low_back(jnp.dot(normed2, w_up, precision=HIGHEST))
    hidden = low(jax.nn.silu(gate_val) * up_val)
    down = low_back(jnp.dot(hidden, jnp.transpose(w_down), precision=HIGHEST))
    return residual + down

def reference(tokens, gain_attn, w_query, w_key, w_value, w_out, gain_ffn, w_gate, w_up, w_down, lengths, cotangent):
    row_ids = jnp.arange(TOKENS, dtype=jnp.int32)
    seq_first = seq_starts(lengths, row_ids)
    cos_table, sin_table = rotation(row_ids - seq_first, HD)

    def wrapped(inputs, gain_one, query_w, key_w, value_w, out_w, gain_two, gate_w, up_w, down_w):
        return forward(inputs, gain_one, query_w, key_w, value_w, out_w, gain_two, gate_w, up_w, down_w, seq_first, cos_table, sin_table)
    result, pullback = jax.vjp(wrapped, tokens.astype(jnp.float32), gain_attn.astype(jnp.float32), w_query.astype(jnp.float32), w_key.astype(jnp.float32), w_value.astype(jnp.float32), w_out.astype(jnp.float32), gain_ffn.astype(jnp.float32), w_gate.astype(jnp.float32), w_up.astype(jnp.float32), w_down.astype(jnp.float32))
    grad_vals = pullback(cotangent.astype(jnp.float32))
    return (result.astype(jnp.bfloat16), grad_vals[0].astype(jnp.bfloat16), grad_vals[1], grad_vals[2], grad_vals[3], grad_vals[4], grad_vals[5], grad_vals[6], grad_vals[7], grad_vals[8], grad_vals[9])
```

```python
import functools
import math

import jax
import jax.numpy as jnp
from jax import lax
from jax.experimental import pallas as pl
from jax.experimental.pallas import tpu as pltpu
from jax.sharding import PartitionSpec as P

f32 = jnp.float32
bf16 = jnp.bfloat16
MESH = pl.DeviceIdType.MESH
NT = (((1,), (1,)), ((), ()))
NN = (((1,), (0,)), ((), ()))
TN = (((0,), (0,)), ((), ()))

ROPE_THETA = 500000.0
ROPE_FACTOR = 32.0
LOW_FACTOR = 1.0
HIGH_FACTOR = 4.0
OLD_CONTEXT = 8192.0
NORM_EPSILON = 1e-05


def frequencies(head_dim):
    freq_index = jnp.arange(head_dim // 2, dtype=jnp.float32)
    base_freq = jnp.exp(freq_index * (-2.0 * math.log(ROPE_THETA) / head_dim))
    wavelen = 2.0 * math.pi / base_freq
    smooth = jnp.clip((OLD_CONTEXT / wavelen - LOW_FACTOR) / (HIGH_FACTOR - LOW_FACTOR), 0.0, 1.0)
    return (1.0 - smooth) * base_freq / ROPE_FACTOR + smooth * base_freq


def seq_starts(lengths, row_ids):
    seq_ends = jnp.cumsum(lengths)
    begins = seq_ends - lengths
    found_at = jnp.where(begins[None, :] <= row_ids[:, None], begins[None, :], 0)
    return jnp.max(found_at, axis=1)


def rotation(positions, head_dim):
    angles = positions.astype(jnp.float32)[:, None] * frequencies(head_dim)[None, :]
    return (jnp.cos(angles), jnp.sin(angles))


def table_shape(values, cos_table, sin_table):
    half_dim = values.shape[-1] // 2
    bcast_shape = (cos_table.shape[0],) + (1,) * (values.ndim - 2) + (half_dim,)
    return (half_dim, cos_table.reshape(bcast_shape), sin_table.reshape(bcast_shape))


def rotate(values, cos_table, sin_table):
    half_dim, cos_part, sin_part = table_shape(values, cos_table, sin_table)
    first_half = values[..., :half_dim]
    second = values[..., half_dim:]
    return jnp.concatenate(
        [first_half * cos_part - second * sin_part, second * cos_part + first_half * sin_part],
        axis=-1,
    )


def unrotate(grad_vals, cos_table, sin_table):
    half_dim, cos_part, sin_part = table_shape(grad_vals, cos_table, sin_table)
    first_half = grad_vals[..., :half_dim]
    second = grad_vals[..., half_dim:]
    return jnp.concatenate(
        [first_half * cos_part + second * sin_part, second * cos_part - first_half * sin_part],
        axis=-1,
    )


def over_blocks(block_fn, state_now, kv_piece, block_len, lowest, highest):
    piece_rows = kv_piece.shape[0]
    block_count = piece_rows // block_len

    def one_step(block_no, state_in):
        begin = block_no * block_len
        kv_part = lax.dynamic_slice_in_dim(kv_piece, block_no * block_len, block_len, 0)
        live = (begin <= highest) & (begin + block_len - 1 >= lowest)

        def compute(carried):
            return block_fn(carried, kv_part, begin)

        def skipped(carried):
            return carried

        return lax.cond(live, compute, skipped, state_in)

    return lax.fori_loop(0, block_count, one_step, state_now)


def dot(a, b, dims):
    return lax.dot_general(a, b, dims, preferred_element_type=f32)


class Place:
    def __init__(self):
        self.N, self.W, self.S = (lax.axis_size(a) for a in ("narrow", "wide", "seq"))
        self.n, self.w, self.s = (lax.axis_index(a) for a in ("narrow", "wide", "seq"))
        self.X = self.W // 2
        self.chips = self.N * self.X
        self.core = lax.rem(self.w, 2)
        self.chip = self.n * self.X + self.w // 2

    def chip_device(self, chip, core):
        return {"narrow": chip // self.X, "wide": lax.rem(chip, self.X) * 2 + core}

    def ahead(self, k):
        return lax.rem(self.chip + k, self.chips)

    def behind(self, k):
        return lax.rem(self.chip - k + self.chips, self.chips)

    def seq_device(self, k):
        return lax.rem(self.s + k, self.S)


def remote(src, dst, ss, rs, device):
    return pltpu.make_async_remote_copy(
        src_ref=src, dst_ref=dst, send_sem=ss, recv_sem=rs, device_id=device, device_id_type=MESH
    )


class PlaneGather:
    def __init__(self, chips, view):
        self.view = view
        self.scratch = [pltpu.SemaphoreType.DMA((chips,))] * 4 + [pltpu.SemaphoreType.DMA]

    def peers(self, at):
        ids = [at.chip_device(at.ahead(k), at.core) for k in range(1, at.chips)]
        return ids + [at.chip_device(at.chip, 1 - at.core)]

    def mid(self):
        pass

    def start(self, at, src, dst, scratch):
        ss, rs, fs, fr, ls = scratch
        self.at, self.dst, self.sems_now = at, dst, scratch
        own = self.view(dst, at.chip, at.core)
        self.local = pltpu.make_async_copy(src, own, ls)
        self.local.start()
        self.far = []
        for k in range(1, at.chips):
            c = remote(src, own, ss.at[k], rs.at[k], at.chip_device(at.ahead(k), at.core))
            c.start()
            self.far.append(c)
        c = remote(src, own, fs.at[0], fr.at[0], at.chip_device(at.chip, 1 - at.core))
        c.start()
        self.near = [c]

    def finish(self):
        at, (ss, rs, fs, fr, ls) = self.at, self.sems_now
        for k in range(1, at.chips):
            block = self.view(self.dst, at.behind(k), at.core)
            self.far[k - 1].wait_recv()
            c = remote(block, block, fs.at[k], fr.at[k], at.chip_device(at.chip, 1 - at.core))
            c.start()
            self.near.append(c)
        self.local.wait()
        for c in self.far:
            c.wait_send()
        for c in self.near:
            c.wait()


class Exchange:
    def __init__(self, count, group, send):
        self.count, self.group, self.send = count, group, send
        self.scratch = [pltpu.SemaphoreType.DMA((count,))] * 2 + [pltpu.SemaphoreType.DMA]

    def device(self, at, k):
        if self.group == "seq":
            j = lax.rem(at.s + k, at.S)
            return j, {"seq": j}
        p = lax.rem(at.n * at.S + at.s + k, at.N * at.S)
        return p, {"narrow": p // at.S, "seq": lax.rem(p, at.S)}

    def peers(self, at):
        return [self.device(at, k)[1] for k in range(1, self.count)]

    def start(self, at, src, dst, scratch):
        ss, rs, ls = scratch
        me = self.device(at, 0)[0]
        self.copies = [pltpu.make_async_copy(self.send(src, me, at), dst.at[me], ls)]
        for k in range(1, self.count):
            j, d = self.device(at, k)
            self.copies.append(remote(self.send(src, j, at), dst.at[me], ss.at[k], rs.at[k], d))
        for c in self.copies:
            c.start()

    def mid(self):
        pass

    def finish(self):
        for c in self.copies:
            c.wait()


class PlaneScatter:
    def __init__(self, chips, block, view):
        self.chips, self.view, self.block = chips, view, block
        sem = pltpu.SemaphoreType.DMA((chips,))
        self.scratch = [pltpu.VMEM((chips,) + block, bf16)] * 3 + [sem] * 5

    def peers(self, at):
        ids = [at.chip_device(at.ahead(k), at.core) for k in range(1, at.chips)]
        return ids + [at.chip_device(at.chip, 1 - at.core)]

    def start(self, at, src, dst, scratch):
        self.at, self.dst = at, dst
        self.mine, self.sib, self.got, ls, ns, nr, self.ss, self.rs = scratch
        sibling = at.chip_device(at.chip, 1 - at.core)
        self.local, self.near = {}, {}
        for k in self.order():
            d = at.ahead(k)
            self.near[k] = remote(self.view(src, d, 1 - at.core), self.sib.at[k], ns.at[k], nr.at[k], sibling)
            self.near[k].start()
            self.local[k] = pltpu.make_async_copy(self.view(src, d, at.core), self.mine.at[k], ls.at[k])
            self.local[k].start()

    def order(self):
        return list(range(1, self.chips)) + [0]

    def mid(self):
        at = self.at
        self.far = {}
        for k in self.order():
            self.local[k].wait()
            self.near[k].wait()
            if k:
                self.mine[k] = (self.mine[k].astype(f32) + self.sib[k].astype(f32)).astype(bf16)
                d = at.chip_device(at.ahead(k), at.core)
                self.far[k] = remote(self.mine.at[k], self.got.at[k], self.ss.at[k], self.rs.at[k], d)
                self.far[k].start()

    def finish(self):
        total = self.mine[0].astype(f32) + self.sib[0].astype(f32)
        for k in self.order()[:-1]:
            self.far[k].wait()
            total = total + self.got[k].astype(f32)
        self.dst[...] = total.astype(self.dst.dtype)


def cost(us):
    return pl.CostEstimate(flops=int(us * 1.1e9), bytes_accessed=0, transcendentals=0)


def greet(ids):
    barrier = pltpu.get_barrier_semaphore()
    for d in ids:
        pl.semaphore_signal(barrier, inc=1, device_id=d, device_id_type=MESH)
    pl.semaphore_wait(barrier, len(ids))


HBM = pl.BlockSpec(memory_space=pl.ANY)
VMEM = pl.BlockSpec(memory_space=pltpu.VMEM)


def fused(cid, name, us, rides, compute=None, ins=(), outs=(), scratch=(), specs=None, vmem=16):
    count = len(rides)
    specs = specs or [VMEM] * len(ins)
    n_in, n_out = count + len(ins), count + len(outs)

    def kernel(*refs):
        left = list(refs[n_in + n_out :])
        at = Place()
        greet([d for part, _, _ in rides for d in part.peers(at)])
        for i, (part, _, _) in enumerate(rides):
            mine, left = left[: len(part.scratch)], left[len(part.scratch) :]
            part.start(at, refs[i], refs[n_in + i], mine)

        def mid():
            for part, _, _ in rides:
                part.mid()

        if compute is None:
            mid()
        else:
            compute(mid, *refs[count:n_in], *refs[n_in + count : n_in + n_out], *left)
        for part, _, _ in rides:
            part.finish()

    shapes = [s for _, _, s in rides] + list(outs)
    out_specs = [VMEM if isinstance(p, PlaneScatter) else HBM for p, _, _ in rides] + [VMEM] * len(outs)
    return pl.pallas_call(
        kernel,
        out_shape=tuple(jax.ShapeDtypeStruct(*s) for s in shapes),
        in_specs=[HBM] * count + list(specs),
        out_specs=tuple(out_specs),
        scratch_shapes=[s for p, _, _ in rides for s in p.scratch] + list(scratch),
        compiler_params=pltpu.CompilerParams(
            collective_id=cid, has_side_effects=True, vmem_limit_bytes=vmem << 20
        ),
        cost_estimate=cost(us),
        name=name,
    )(*[x for _, x, _ in rides], *ins)


FAR = 2.0**30
FQ = 1
FB = 1

def segment_lanes(rows, lanes, starts_ref, count):
    hit=jnp.zeros((rows.shape[0],lanes.shape[1]),f32)
    for j in range(count):
        inside=rows>=starts_ref[j]
        if j+1<count: inside=inside&(rows<starts_ref[j+1])
        hit=hit+jnp.where((lanes==64+j)&inside,1.0,0.0)
    return hit

def key_sides(S,RB,N,nseq,starts_ref,kv_ref,ka_ref,v1_ref):
    lanes=lax.broadcasted_iota(jnp.int32,(1,128),1)
    iota=lax.broadcasted_iota(jnp.int32,(RB,1),0)
    def fill(s,_):
        for n in range(N):
            kv=kv_ref[s,n*RB:(n+1)*RB,:]
            hot=segment_lanes((n*S+s)*RB+iota,lanes,starts_ref,nseq).astype(bf16)
            ka_ref[s,n*RB:(n+1)*RB,:]=jnp.where(lanes<64,kv,hot)
            v1_ref[s,n*RB:(n+1)*RB,:]=jnp.where(lanes<64,jnp.ones_like(kv),kv)
        return 0
    lax.fori_loop(0,S,fill,0)

def query_side(q,n,b,RB,nseq,starts_ref):
    lanes=lax.broadcasted_iota(jnp.int32,(1,128),1)
    iota=lax.broadcasted_iota(jnp.int32,(RB,1),0)
    if n==1: q=pltpu.roll(q.astype(f32),64,1).astype(bf16)
    far=jnp.where((lanes>=64)&(lanes<64+nseq),-FAR,0.0)*(1.0-segment_lanes(b*RB+iota,lanes,starts_ref,nseq))
    return jnp.where(lanes<64,q,jnp.zeros_like(q)),jnp.where(lanes<64,q,far.astype(bf16))

def attn_fwd_body(S,RB,N,nseq,mid,starts_ref,q_ref,kv_ref,ob_ref,res_ref,ka_ref,v1_ref,acc_ref):
    key_sides(S,RB,N,nseq,starts_ref,kv_ref,ka_ref,v1_ref)
    lanes=lax.broadcasted_iota(jnp.int32,(1,128),1)
    for n in range(N):
        def qblock(s,_):
            b=n*S+s
            _,qa=query_side(q_ref[s],n,b,RB,nseq,starts_ref)
            acc_ref[...]=jnp.zeros_like(acc_ref)
            def at(ref,j): return ref[lax.rem(j,S),pl.ds(pl.multiple_of((j//S)*RB,RB),RB),:]
            m=RB//FQ
            def kstep(j,_):
                k=at(ka_ref,j); v=at(v1_ref,j)
                sc=[dot(qa[i*m:(i+1)*m],k,NT) for i in range(FQ)]
                for i in range(FQ):
                    acc_ref[i*m:(i+1)*m]+=dot(jnp.exp2(sc[i]).astype(bf16),v,NN)
                return 0
            lax.fori_loop(0,b,kstep,0)
            sc=dot(qa,at(ka_ref,b),NT)
            half=RB//2
            tri=lax.broadcasted_iota(jnp.int32,(half,half),1)<=lax.broadcasted_iota(jnp.int32,(half,half),0)
            v=at(v1_ref,b)
            e=jnp.where(tri,jnp.exp2(sc[:half,:half]),0.0).astype(bf16)
            acc_ref[:half]+=dot(e,v[:half],NN)
            e1=jnp.exp2(sc[half:,:half]).astype(bf16)
            e2=jnp.where(tri,jnp.exp2(sc[half:,half:]),0.0).astype(bf16)
            acc_ref[half:]+=dot(e1,v[:half],NN)+dot(e2,v[half:],NN)
            acc=acc_ref[...]
            inv=1.0/acc
            o=acc*pltpu.roll(inv,64,1)
            res_ref[b]=jnp.where(lanes<64,inv,o)
            if n==0: ob_ref[s,:,0:64]=pltpu.roll(o,64,1)[:,0:64].astype(bf16)
            else: ob_ref[s,:,64:128]=o[:,64:128].astype(bf16)
            return 0
        lax.fori_loop(0,S,qblock,0)
        if n==0: mid()

def attn_bwd_body(S,RB,N,nseq,mid,starts_ref,q_ref,kv_ref,do_ref,res_ref,dq_ref,dkv_ref,ka_ref,v1_ref,acc_ref,dq_acc):
    key_sides(S,RB,N,nseq,starts_ref,kv_ref,ka_ref,v1_ref)
    acc_ref[...]=jnp.zeros_like(acc_ref)
    lanes=lax.broadcasted_iota(jnp.int32,(1,128),1)
    for n in range(N):
        def qblock(s,_):
            b=n*S+s
            do=do_ref[s].astype(f32)
            res=res_ref[b]
            q,qa=query_side(q_ref[s],n,b,RB,nseq,starts_ref)
            if n==0: do=pltpu.roll(do,64,1)
            du=jnp.where(lanes<64,0.0,do*pltpu.roll(res,64,1))
            delta=jnp.sum(du*res,axis=1,keepdims=True)
            hi=(-delta).astype(bf16).astype(f32)
            du0=du.astype(bf16)
            dua=jnp.where(lanes==0,hi,jnp.where(lanes==1,-delta-hi,du)).astype(bf16)
            dq_acc[...]=jnp.zeros_like(dq_acc)
            def where(j): return lax.rem(j,S),pl.ds(pl.multiple_of((j//S)*RB,RB),RB)
            def at(ref,j):
                a,c=where(j); return ref[a,c,:]
            m=RB//FB
            def kstep(j,_):
                a,c=where(j)
                for i in range(FB):
                    qs=slice(i*m,(i+1)*m)
                    k=at(ka_ref,j); v=at(v1_ref,j)
                    e=jnp.exp2(dot(k,qa[qs],NT))
                    ds=(e*dot(v,dua[qs],NT)).astype(bf16)
                    acc_ref[a,c,:]+=dot(e.astype(bf16),du0[qs],NN)+dot(ds,q[qs],NN)
                    dq_acc[qs]+=dot(ds,at(kv_ref,j),TN)
                return 0
            lax.fori_loop(0,b,kstep,0)
            sc=dot(at(ka_ref,b),qa,NT); dp=dot(at(v1_ref,b),dua,NT)
            half=RB//2
            tri=lax.broadcasted_iota(jnp.int32,(half,half),0)<=lax.broadcasted_iota(jnp.int32,(half,half),1)
            a=lax.rem(b,S); base=(b//S)*RB
            def piece(k0,q0,masked):
                e=jnp.exp2(sc[k0:k0+half,q0:q0+half])
                if masked: e=jnp.where(tri,e,0.0)
                ds=(e*dp[k0:k0+half,q0:q0+half]).astype(bf16)
                c=pl.ds(pl.multiple_of(base+k0,half),half)
                acc_ref[a,c,:]+=dot(e.astype(bf16),du0[q0:q0+half],NN)+dot(ds,q[q0:q0+half],NN)
                dq_acc[q0:q0+half]+=dot(ds,kv_ref[a,c,:],TN)
            piece(0,0,True); piece(0,half,False); piece(half,half,True)
            dq=dq_acc[...]*0.125
            if n==0: dq_ref[s,:,0:64]=dq[:,0:64].astype(bf16)
            else: dq_ref[s,:,64:128]=pltpu.roll(dq,64,1)[:,64:128].astype(bf16)
            return 0
        lax.fori_loop(0,S,qblock,0)
        if n==0: mid()
    ln2=0.6931471805599453
    def finish(s,_):
        acc=acc_ref[s]
        dkv_ref[s]=jnp.where(lanes<64,acc*ln2,acc).astype(bf16)
        return 0
    lax.fori_loop(0,S,finish,0)


def by_rows(
    tokens,
    gain_attn,
    w_query,
    w_key,
    w_value,
    w_out,
    gain_ffn,
    w_gate,
    w_up,
    w_down,
    lengths,
    cotangent,
):
    f32 = jnp.float32
    bf16 = jnp.bfloat16
    tok_rows = tokens.shape[0]
    col_count = tokens.shape[1]
    all_rows = tok_rows * lax.axis_size("narrow") * lax.axis_size("seq")
    block_id = lax.axis_index(("narrow", "seq"))
    row_ids = block_id * tok_rows + jnp.arange(tok_rows, dtype=jnp.int32)
    seq_first = seq_starts(lengths, row_ids)
    lowest_key = jnp.min(seq_first)
    highest_key = block_id * tok_rows + tok_rows - 1
    full_in = lax.all_gather(tokens, "wide", axis=1, tiled=True)
    inputs = full_in.astype(f32)
    recip1 = lax.rsqrt(jnp.mean(inputs * inputs, axis=1, keepdims=True) + NORM_EPSILON)
    normed1 = (inputs * recip1 * gain_attn).astype(bf16)
    query_w, key_w, value_w, out_w = (
        lax.all_gather(w_query, ("narrow", "seq"), axis=0, tiled=True),
        lax.all_gather(w_key, ("narrow", "seq"), axis=0, tiled=True),
        lax.all_gather(w_value, ("narrow", "seq"), axis=0, tiled=True),
        lax.all_gather(w_out, ("narrow", "seq"), axis=0, tiled=True),
    )
    gate_w, up_w, down_w = (
        lax.all_gather(w_gate, "narrow", axis=0, tiled=True),
        lax.all_gather(w_up, "narrow", axis=0, tiled=True),
        lax.all_gather(w_down, "narrow", axis=0, tiled=True),
    )
    heads_kv = key_w.shape[1]
    head_dim = key_w.shape[2]
    group_size = query_w.shape[2] // head_dim
    kv_width = heads_kv * head_dim
    score_scale = 1.0 / math.sqrt(head_dim)
    cos_table, sin_table = rotation(row_ids - seq_first, head_dim)
    query_raw = jnp.einsum("td,dkc->tkc", normed1, query_w, preferred_element_type=f32)
    key_raw = jnp.einsum("td,dkc->tkc", normed1, key_w, preferred_element_type=f32)
    value_raw = jnp.einsum("td,dkc->tkc", normed1, value_w, preferred_element_type=f32)
    query_b = rotate(
        query_raw.reshape(tok_rows, heads_kv, group_size, head_dim), cos_table, sin_table
    ).astype(bf16)
    key_b = rotate(key_raw, cos_table, sin_table).astype(bf16)
    value_b = value_raw.astype(bf16)
    kv_local = jnp.concatenate(
        [key_b.reshape(tok_rows, kv_width), value_b.reshape(tok_rows, kv_width)], axis=1
    )

    def block_scores(kv_part, key_start):
        part_rows = kv_part.shape[0]
        key_part = kv_part[:, :kv_width].reshape(part_rows, heads_kv, head_dim)
        value_part = kv_part[:, kv_width:].reshape(part_rows, heads_kv, head_dim)
        raw_scores = (
            jnp.einsum("qkgh,pkh->kgqp", query_b, key_part, preferred_element_type=f32)
            * score_scale
        )
        key_rows = key_start + jnp.arange(part_rows, dtype=jnp.int32)
        causal_mask = (key_rows[None, :] >= seq_first[:, None]) & (
            key_rows[None, :] <= row_ids[:, None]
        )
        weights = jnp.where(causal_mask[None, None], jnp.exp(raw_scores), 0.0)
        return (weights, key_part, value_part)

    def forward_block(state_in, kv_part, key_start):
        summed, row_total = state_in
        weights, key_part, value_part = block_scores(kv_part, key_start)
        row_total = row_total + jnp.sum(weights, axis=3)
        summed = summed + jnp.einsum(
            "kgqp,pkh->qkgh", weights.astype(bf16), value_part, preferred_element_type=f32
        )
        return (summed, row_total)

    start_state = (
        jnp.zeros((tok_rows, heads_kv, group_size, head_dim), f32),
        jnp.zeros((heads_kv, group_size, tok_rows), f32),
    )
    summed, row_total = over_blocks(
        forward_block,
        start_state,
        lax.all_gather(kv_local, ("narrow", "seq"), axis=0, tiled=True),
        tok_rows,
        lowest_key,
        highest_key,
    )
    inv_total = 1.0 / jnp.transpose(row_total, (2, 0, 1))
    attn_out = summed * inv_total[..., None]
    attn_b = attn_out.astype(bf16).reshape(tok_rows, heads_kv, group_size * head_dim)
    branch_part = jnp.einsum("tkc,dkc->td", attn_b, out_w, preferred_element_type=f32)
    branch = lax.psum(branch_part, "wide")
    residual = inputs + branch
    recip2 = lax.rsqrt(jnp.mean(residual * residual, axis=1, keepdims=True) + NORM_EPSILON)
    normed2 = (residual * recip2 * gain_ffn).astype(bf16)
    gate_val = jnp.dot(normed2, gate_w, preferred_element_type=f32)
    up_val = jnp.dot(normed2, up_w, preferred_element_type=f32)
    sigmoid_gate = jax.nn.sigmoid(gate_val)
    hidden = (gate_val * sigmoid_gate * up_val).astype(bf16)
    down_part = jnp.einsum("tf,df->td", hidden, down_w, preferred_element_type=f32)
    down = lax.psum_scatter(
        down_part.astype(jnp.bfloat16), "wide", scatter_dimension=1, tiled=True
    ).astype(jnp.float32)
    wide_id = lax.axis_index("wide")
    local_resid = lax.dynamic_slice_in_dim(residual, wide_id * col_count, col_count, 1)
    output = (local_resid + down).astype(bf16)
    grad_full = lax.all_gather(cotangent, "wide", axis=1, tiled=True)
    grad_hidden = jnp.einsum("td,df->tf", grad_full, down_w, preferred_element_type=f32)
    silu_slope = sigmoid_gate * (1.0 + gate_val * (1.0 - sigmoid_gate))
    grad_gate_val = (grad_hidden * up_val * silu_slope).astype(bf16)
    grad_up_val = (grad_hidden * gate_val * sigmoid_gate).astype(bf16)
    dw_down = jnp.einsum("td,tf->df", grad_full, hidden, preferred_element_type=f32)
    dw_gate = jnp.einsum("td,tf->df", normed2, grad_gate_val, preferred_element_type=f32)
    dw_up = jnp.einsum("td,tf->df", normed2, grad_up_val, preferred_element_type=f32)
    dn2_part = jnp.einsum(
        "tf,df->td", grad_gate_val, gate_w, preferred_element_type=f32
    ) + jnp.einsum("tf,df->td", grad_up_val, up_w, preferred_element_type=f32)
    dn2 = lax.psum(dn2_part, "wide")
    dgain_ffn = jnp.sum(dn2 * residual * recip2, axis=0)
    scaled2 = dn2 * gain_ffn
    dresid = (
        grad_full.astype(f32)
        + recip2 * scaled2
        - residual
        * (recip2 * recip2 * recip2)
        * jnp.mean(scaled2 * residual, axis=1, keepdims=True)
    )
    dbranch = dresid.astype(bf16)
    dw_out = jnp.einsum("td,tkc->dkc", dbranch, attn_b, preferred_element_type=f32)
    grad_attn = jnp.einsum("td,dkc->tkc", dbranch, out_w, preferred_element_type=f32).reshape(
        tok_rows, heads_kv, group_size, head_dim
    )
    grad_summed = (grad_attn * inv_total[..., None]).astype(bf16)
    delta_rows = jnp.transpose(jnp.sum(grad_attn * attn_out, axis=3) * inv_total, (1, 2, 0))

    def backward_block(state_in, kv_part, key_start):
        dquery, dkv_all = state_in
        weights, key_part, value_part = block_scores(kv_part, key_start)
        part_rows = kv_part.shape[0]
        dprob = jnp.einsum("qkgh,pkh->kgqp", grad_summed, value_part, preferred_element_type=f32)
        dscore = (weights * (dprob - delta_rows[..., None])).astype(bf16)
        dquery = dquery + jnp.einsum("kgqp,pkh->qkgh", dscore, key_part, preferred_element_type=f32)
        dkey = (
            jnp.einsum("kgqp,qkgh->pkh", dscore, query_b, preferred_element_type=f32) * score_scale
        )
        dvalue = jnp.einsum(
            "kgqp,qkgh->pkh", weights.astype(bf16), grad_summed, preferred_element_type=f32
        )
        block_grad = jnp.concatenate(
            [dkey.reshape(part_rows, kv_width), dvalue.reshape(part_rows, kv_width)], axis=1
        )
        current = lax.dynamic_slice_in_dim(dkv_all, key_start, part_rows, 0)
        dkv_all = lax.dynamic_update_slice_in_dim(dkv_all, current + block_grad, key_start, 0)
        return (dquery, dkv_all)

    back_state = (
        jnp.zeros((tok_rows, heads_kv, group_size, head_dim), f32),
        jnp.zeros((all_rows, 2 * kv_width), f32),
    )
    dquery, dkv_all = over_blocks(
        backward_block,
        back_state,
        lax.all_gather(kv_local, ("narrow", "seq"), axis=0, tiled=True),
        tok_rows,
        lowest_key,
        highest_key,
    )
    dkv_own = lax.psum_scatter(
        dkv_all.astype(jnp.bfloat16), ("narrow", "seq"), scatter_dimension=0, tiled=True
    ).astype(jnp.float32)
    dquery_b = (
        unrotate(dquery * score_scale, cos_table, sin_table)
        .astype(bf16)
        .reshape(tok_rows, heads_kv, group_size * head_dim)
    )
    dkey_b = unrotate(
        dkv_own[:, :kv_width].reshape(tok_rows, heads_kv, head_dim), cos_table, sin_table
    ).astype(bf16)
    dvalue_b = dkv_own[:, kv_width:].reshape(tok_rows, heads_kv, head_dim).astype(bf16)
    dw_query = jnp.einsum("td,tkc->dkc", normed1, dquery_b, preferred_element_type=f32)
    dw_key = jnp.einsum("td,tkc->dkc", normed1, dkey_b, preferred_element_type=f32)
    dw_value = jnp.einsum("td,tkc->dkc", normed1, dvalue_b, preferred_element_type=f32)
    dn1_part = jnp.einsum("tkc,dkc->td", dquery_b, query_w, preferred_element_type=f32)
    dn1_part = dn1_part + jnp.einsum("tkc,dkc->td", dkey_b, key_w, preferred_element_type=f32)
    dn1_part = dn1_part + jnp.einsum("tkc,dkc->td", dvalue_b, value_w, preferred_element_type=f32)
    dn1 = lax.psum(dn1_part.astype(jnp.bfloat16), "wide").astype(jnp.float32)
    dgain_attn = jnp.sum(dn1 * inputs * recip1, axis=0)
    scaled1 = dn1 * gain_attn
    dinputs = (
        dresid
        + recip1 * scaled1
        - inputs * (recip1 * recip1 * recip1) * jnp.mean(scaled1 * inputs, axis=1, keepdims=True)
    )
    grad_input = lax.dynamic_slice_in_dim(dinputs, wide_id * col_count, col_count, 1).astype(bf16)
    summed_grads = (
        lax.psum_scatter(
            dgain_attn.astype(jnp.bfloat16), ("narrow", "seq"), scatter_dimension=0, tiled=True
        ).astype(jnp.float32),
        lax.psum_scatter(
            dw_query.astype(jnp.bfloat16), ("narrow", "seq"), scatter_dimension=0, tiled=True
        ).astype(jnp.float32),
        lax.psum_scatter(
            dw_key.astype(jnp.bfloat16), ("narrow", "seq"), scatter_dimension=0, tiled=True
        ).astype(jnp.float32),
        lax.psum_scatter(
            dw_value.astype(jnp.bfloat16), ("narrow", "seq"), scatter_dimension=0, tiled=True
        ).astype(jnp.float32),
        lax.psum_scatter(
            dw_out.astype(jnp.bfloat16), ("narrow", "seq"), scatter_dimension=0, tiled=True
        ).astype(jnp.float32),
        lax.psum_scatter(
            dgain_ffn.astype(jnp.bfloat16), ("narrow", "seq"), scatter_dimension=0, tiled=True
        ).astype(jnp.float32),
        lax.psum_scatter(
            dw_gate.astype(jnp.bfloat16), ("narrow", "seq"), scatter_dimension=0, tiled=True
        ).astype(jnp.float32),
        lax.psum_scatter(
            dw_up.astype(jnp.bfloat16), ("narrow", "seq"), scatter_dimension=0, tiled=True
        ).astype(jnp.float32),
        lax.psum_scatter(
            dw_down.astype(jnp.bfloat16), ("narrow", "seq"), scatter_dimension=0, tiled=True
        ).astype(jnp.float32),
    )
    return (
        output,
        grad_input,
        summed_grads[0],
        summed_grads[1],
        summed_grads[2],
        summed_grads[3],
        summed_grads[4],
        summed_grads[5],
        summed_grads[6],
        summed_grads[7],
        summed_grads[8],
    )


def by_plane(
    tokens,
    gain_attn,
    w_query,
    w_key,
    w_value,
    w_out,
    gain_ffn,
    w_gate,
    w_up,
    w_down,
    lengths,
    cotangent,
):
    N, W, S = (lax.axis_size(a) for a in ("narrow", "wide", "seq"))
    n, w, s = (lax.axis_index(a) for a in ("narrow", "wide", "seq"))
    P8, chips = N * W, N * W // 2
    RB, cols = tokens.shape
    R, D = N * RB, W * cols
    hd = w_key.shape[2]
    group = w_query.shape[2] // hd
    qw = group * hd
    rows = RB // W
    starts = jnp.cumsum(lengths) - lengths

    def block_view(dst, chip, core):
        a, b = chip // (W // 2), lax.rem(chip, W // 2) * 2 + core
        return dst.at[pl.ds(a * RB, RB), pl.ds(b * cols, cols)]

    def row_view(dst, chip, core):
        return dst.at[chip * 2 + core]

    def plane_rows(x, cid, name, *rides):
        full, *rest = fused(cid, name, 40, [(PlaneGather(chips, row_view), x, ((P8,) + x.shape, x.dtype)), *rides])
        return full.reshape(R, D), *rest

    def plane_sum(x, cid, name, *rides):
        part = PlaneScatter(chips, (rows, D), row_view)
        return fused(cid, name, 40, [(part, x.reshape(P8, rows, D), ((rows, D), f32)), *rides], vmem=32)

    def seq_ride(x, spread=False):
        pick = (lambda src, j, at: src) if spread else (lambda src, j, at: src.at[j])
        shape = x.shape if spread else x.shape[1:]
        return Exchange(S, "seq", pick), x, ((S,) + shape, x.dtype)

    def head_ride(x):
        x = x.transpose(1, 0, 2)
        pick = lambda src, j, at: src.at[j // at.S]
        return Exchange(N * S, "rows", pick), x, ((N * S,) + x.shape[1:], x.dtype)

    def rows_ride(x, part=0, parts=1):
        x = x.reshape(N * S, D // (N * S), x.shape[1])
        m = x.shape[1] // parts
        pick = lambda src, j, at: src.at[j, pl.ds(part * m, m)]
        return Exchange(N * S, "rows", pick), x, ((N * S, m, x.shape[2]), x.dtype)

    def block_ride(x):
        return PlaneGather(chips, block_view), x, ((R, D), x.dtype)

    w_mine = jnp.concatenate([w_query, w_key, w_value], axis=2)
    full_in, w_qkv = fused(1, "gather_start", 45, [block_ride(tokens), head_ride(w_mine)])
    w_qkv = w_qkv.reshape(D, w_mine.shape[2])

    half_h = w_gate.shape[1] // N
    full_in, w_gate, w_up, w_down = lax.optimization_barrier((full_in, w_gate, w_up, w_down))

    def own_half(x, i):
        return lax.dynamic_slice_in_dim(x, i * half_h, half_h, 1)

    def swapped(x):
        mine, other = own_half(x, n), own_half(x, 1 - n)
        got = lax.ppermute(other, "narrow", [(0, 1), (1, 0)])
        return jnp.concatenate([jnp.where(n == 0, mine, got), jnp.where(n == 0, got, mine)], axis=0)

    gate_w, up_w, down_w = swapped(w_gate), swapped(w_up), swapped(w_down)

    row_ids = ((jnp.arange(N, dtype=jnp.int32) * S + s) * RB)[:, None] + jnp.arange(RB, dtype=jnp.int32)
    row_ids = row_ids.reshape(R)
    cos_table, sin_table = rotation(row_ids - seq_starts(lengths, row_ids), hd)

    inputs = full_in.astype(f32)
    recip1 = lax.rsqrt(jnp.mean(inputs * inputs, axis=1, keepdims=True) + NORM_EPSILON)
    normed1 = (inputs * recip1 * gain_attn).astype(bf16)
    qkv = jnp.dot(normed1, w_qkv, preferred_element_type=f32)
    fold = math.log2(math.e) / math.sqrt(hd)
    query = (rotate(qkv[:, :qw].reshape(R, group, hd), cos_table, sin_table) * fold).astype(bf16)
    key = rotate(qkv[:, qw : qw + hd].reshape(R, 1, hd), cos_table, sin_table).reshape(R, hd)
    kv = jnp.concatenate([key, qkv[:, qw + hd :]], axis=1).astype(bf16)

    def pack(x):
        return x.reshape(N, RB, group, hd).transpose(2, 1, 0, 3).reshape(group, RB, N * hd)

    def unpack(x):
        return x.reshape(group, RB, N, hd).transpose(2, 1, 0, 3).reshape(R, qw)

    heads_shape = ((S, RB, N * hd), bf16)
    q_all, kv_all = fused(2, "to_heads", 48, [seq_ride(pack(query)), seq_ride(kv, True)])
    nseq = lengths.shape[0]
    grad_full, w_o, attn_own, attn_res = fused(
        11,
        "attn_fwd",
        42,
        [block_ride(cotangent), head_ride(w_out)],
        functools.partial(attn_fwd_body, S, RB, N, nseq),
        (starts, q_all, kv_all),
        (heads_shape, ((N * S, RB, 2 * hd), f32)),
        [pltpu.VMEM(kv_all.shape, bf16), pltpu.VMEM(kv_all.shape, bf16), pltpu.VMEM((RB, 2 * hd), f32)],
        [pl.BlockSpec(memory_space=pltpu.SMEM), VMEM, VMEM],
        48,
    )
    w_o = w_o.reshape(D, qw)
    (attn_back,) = fused(3, "from_heads", 18, [seq_ride(attn_own)])
    attn_b = unpack(attn_back)
    (branch,) = plane_sum(dot(attn_b, w_o, NT).astype(bf16), 4, "branch_sum")
    own_row = n * RB + w * rows
    own_in = lax.dynamic_slice_in_dim(full_in, own_row, rows, 0).astype(f32)
    residual = own_in + branch
    recip2 = lax.rsqrt(jnp.mean(residual * residual, axis=1, keepdims=True) + NORM_EPSILON)
    (normed2,) = plane_rows((residual * recip2 * gain_ffn).astype(bf16), 5, "normed2")

    gate_val = jnp.dot(normed2, gate_w, preferred_element_type=f32)
    up_val = jnp.dot(normed2, up_w, preferred_element_type=f32)
    grad_hidden = jnp.dot(grad_full, down_w, preferred_element_type=f32)
    sigmoid_gate = jax.nn.sigmoid(gate_val)
    hidden = (gate_val * sigmoid_gate * up_val).astype(bf16)
    silu_slope = sigmoid_gate * (1.0 + gate_val * (1.0 - sigmoid_gate))
    grad_gate_val = (grad_hidden * up_val * silu_slope).astype(bf16)
    grad_up_val = (grad_hidden * gate_val * sigmoid_gate).astype(bf16)
    dn2_part = dot(grad_gate_val, gate_w, NT) + dot(grad_up_val, up_w, NT)
    dw_down = dot(grad_full, hidden, TN).astype(bf16)
    dw_gate = dot(normed2, grad_gate_val, TN).astype(bf16)
    dw_up = dot(normed2, grad_up_val, TN).astype(bf16)
    dn2, got_a = plane_sum(dn2_part.astype(bf16), 6, "dn2_sum", rows_ride(dw_down, 0, 2))

    down_part = dot(hidden, down_w, NT).astype(bf16)
    own_part = lax.dynamic_slice_in_dim(down_part, own_row, rows, 0).astype(f32) + residual
    down_part = lax.dynamic_update_slice_in_dim(down_part, own_part.astype(bf16), own_row, 0)

    dgain_ffn = jnp.sum(dn2 * residual * recip2, axis=0)
    scaled2 = dn2 * gain_ffn
    own_grad = lax.dynamic_slice_in_dim(grad_full, own_row, rows, 0).astype(f32)
    dresid = (
        own_grad
        + recip2 * scaled2
        - residual * (recip2 * recip2 * recip2) * jnp.mean(scaled2 * residual, axis=1, keepdims=True)
    )
    dbranch, got_b = plane_rows(dresid.astype(bf16), 7, "dbranch", rows_ride(dw_down, 1, 2))
    dw_o = dot(dbranch, attn_b, TN).astype(bf16)
    grad_attn = jnp.dot(dbranch, w_o, preferred_element_type=f32).astype(bf16)
    (do_all,) = fused(8, "grad_to_heads", 20, [seq_ride(pack(grad_attn.reshape(R, group, hd)))])
    got_gate, output, dq_own, dkv_own = fused(
        12,
        "attn_bwd",
        85,
        [
            rows_ride(dw_gate),
            (PlaneScatter(chips, (RB, cols), block_view), down_part, ((RB, cols), bf16)),
        ],
        functools.partial(attn_bwd_body, S, RB, N, nseq),
        (starts, q_all, kv_all, do_all, attn_res),
        (heads_shape, (kv_all.shape, bf16)),
        [
            pltpu.VMEM(kv_all.shape, bf16),
            pltpu.VMEM(kv_all.shape, bf16),
            pltpu.VMEM(kv_all.shape, f32),
            pltpu.VMEM((RB, 2 * hd), f32),
        ],
        [pl.BlockSpec(memory_space=pltpu.SMEM)] + [VMEM] * 4,
        60,
    )
    dq_all, dkv_all = fused(9, "grad_from_heads", 50, [seq_ride(dq_own), seq_ride(dkv_own)])
    dkv = jnp.sum(dkv_all.astype(f32), axis=0)
    dquery = unrotate(unpack(dq_all).astype(f32).reshape(R, group, hd), cos_table, sin_table)
    dkey = unrotate(dkv[:, :hd].reshape(R, 1, hd), cos_table, sin_table)
    dqkv = jnp.concatenate([dquery.reshape(R, qw), dkey.reshape(R, hd), dkv[:, hd:]], axis=1)
    dqkv = dqkv.astype(bf16)
    dw_attn = jnp.concatenate([dot(normed1, dqkv, TN).astype(bf16), dw_o], axis=1)
    dn1, got_up, got_attn = plane_sum(
        dot(dqkv, w_qkv, NT).astype(bf16), 10, "dn1_sum", rows_ride(dw_up), rows_ride(dw_attn)
    )

    def over_seq(got):
        return jnp.sum(got.reshape(N, S, *got.shape[1:]).astype(f32), axis=1)

    def ffn_grad(got):
        return jnp.concatenate(list(over_seq(got)), axis=1)

    attn_grads = over_seq(got_attn).transpose(1, 0, 2)

    recip1_own = lax.rsqrt(jnp.mean(own_in * own_in, axis=1, keepdims=True) + NORM_EPSILON)
    dgain_attn = jnp.sum(dn1 * own_in * recip1_own, axis=0)
    scaled1 = dn1 * gain_attn
    dinputs = (
        dresid
        + recip1_own * scaled1
        - own_in
        * (recip1_own * recip1_own * recip1_own)
        * jnp.mean(scaled1 * own_in, axis=1, keepdims=True)
    )
    grad_input = lax.all_to_all(dinputs.astype(bf16), "wide", split_axis=1, concat_axis=0, tiled=True)

    def gain_grad(part):
        total = lax.psum(part, ("narrow", "wide", "seq"))
        return lax.dynamic_slice_in_dim(total, (n * S + s) * (D // (N * S)), D // (N * S), 0)

    return (
        output,
        grad_input,
        gain_grad(dgain_attn),
        attn_grads[:, :, :qw],
        attn_grads[:, :, qw : qw + hd],
        attn_grads[:, :, qw + hd : qw + 2 * hd],
        attn_grads[:, :, qw + 2 * hd :],
        gain_grad(dgain_ffn),
        ffn_grad(got_gate),
        ffn_grad(got_up),
        jnp.concatenate([ffn_grad(got_a), ffn_grad(got_b)], axis=0),
    )


def local(tokens, gain_attn, w_query, w_key, *others):
    plane = lax.axis_size("narrow") * lax.axis_size("wide")
    heads_kv = w_key.shape[1] * lax.axis_size("wide")
    group = w_query.shape[2] // w_key.shape[2]
    fits = lax.axis_size("narrow") == 2 and heads_kv == plane and group == lax.axis_size("seq")
    body = by_plane if fits and w_key.shape[2] == 64 else by_rows
    return body(tokens, gain_attn, w_query, w_key, *others)


def solution(mesh):
    return jax.shard_map(
        local,
        mesh=mesh,
        in_specs=(
            P(("narrow", "seq"), "wide"),
            P(),
            P(("narrow", "seq"), "wide", None),
            P(("narrow", "seq"), "wide", None),
            P(("narrow", "seq"), "wide", None),
            P(("narrow", "seq"), "wide", None),
            P(),
            P("narrow", "wide"),
            P("narrow", "wide"),
            P("narrow", "wide"),
            P(),
            P(("narrow", "seq"), "wide"),
        ),
        out_specs=(
            P(("narrow", "seq"), "wide"),
            P(("narrow", "seq"), "wide"),
            P(("narrow", "seq")),
            P(("narrow", "seq"), "wide", None),
            P(("narrow", "seq"), "wide", None),
            P(("narrow", "seq"), "wide", None),
            P(("narrow", "seq"), "wide", None),
            P(("narrow", "seq")),
            P(("narrow", "seq"), "wide"),
            P(("narrow", "seq"), "wide"),
            P(("narrow", "seq"), "wide"),
        ),
        check_vma=False,
    )
```

```python
import functools
import math

import jax
import jax.numpy as jnp
from jax import lax
from jax.experimental import pallas as pl
from jax.experimental.pallas import tpu as pltpu
from jax.sharding import PartitionSpec as P

f32 = jnp.float32
bf16 = jnp.bfloat16
MESH = pl.DeviceIdType.MESH
NT = (((1,), (1,)), ((), ()))
NN = (((1,), (0,)), ((), ()))
TN = (((0,), (0,)), ((), ()))

ROPE_THETA = 500000.0
ROPE_FACTOR = 32.0
LOW_FACTOR = 1.0
HIGH_FACTOR = 4.0
OLD_CONTEXT = 8192.0
NORM_EPSILON = 1e-05


def frequencies(head_dim):
    freq_index = jnp.arange(head_dim // 2, dtype=jnp.float32)
    base_freq = jnp.exp(freq_index * (-2.0 * math.log(ROPE_THETA) / head_dim))
    wavelen = 2.0 * math.pi / base_freq
    smooth = jnp.clip((OLD_CONTEXT / wavelen - LOW_FACTOR) / (HIGH_FACTOR - LOW_FACTOR), 0.0, 1.0)
    return (1.0 - smooth) * base_freq / ROPE_FACTOR + smooth * base_freq


def seq_starts(lengths, row_ids):
    seq_ends = jnp.cumsum(lengths)
    begins = seq_ends - lengths
    found_at = jnp.where(begins[None, :] <= row_ids[:, None], begins[None, :], 0)
    return jnp.max(found_at, axis=1)


def rotation(positions, head_dim):
    angles = positions.astype(jnp.float32)[:, None] * frequencies(head_dim)[None, :]
    return (jnp.cos(angles), jnp.sin(angles))


def table_shape(values, cos_table, sin_table):
    half_dim = values.shape[-1] // 2
    bcast_shape = (cos_table.shape[0],) + (1,) * (values.ndim - 2) + (half_dim,)
    return (half_dim, cos_table.reshape(bcast_shape), sin_table.reshape(bcast_shape))


def rotate(values, cos_table, sin_table):
    half_dim, cos_part, sin_part = table_shape(values, cos_table, sin_table)
    first_half = values[..., :half_dim]
    second = values[..., half_dim:]
    return jnp.concatenate(
        [first_half * cos_part - second * sin_part, second * cos_part + first_half * sin_part],
        axis=-1,
    )


def unrotate(grad_vals, cos_table, sin_table):
    half_dim, cos_part, sin_part = table_shape(grad_vals, cos_table, sin_table)
    first_half = grad_vals[..., :half_dim]
    second = grad_vals[..., half_dim:]
    return jnp.concatenate(
        [first_half * cos_part + second * sin_part, second * cos_part - first_half * sin_part],
        axis=-1,
    )


def over_blocks(block_fn, state_now, kv_piece, block_len, lowest, highest):
    piece_rows = kv_piece.shape[0]
    block_count = piece_rows // block_len

    def one_step(block_no, state_in):
        begin = block_no * block_len
        kv_part = lax.dynamic_slice_in_dim(kv_piece, block_no * block_len, block_len, 0)
        live = (begin <= highest) & (begin + block_len - 1 >= lowest)

        def compute(carried):
            return block_fn(carried, kv_part, begin)

        def skipped(carried):
            return carried

        return lax.cond(live, compute, skipped, state_in)

    return lax.fori_loop(0, block_count, one_step, state_now)


def dot(a, b, dims):
    return lax.dot_general(a, b, dims, preferred_element_type=f32)


class Place:
    def __init__(self):
        self.N, self.W, self.S = (lax.axis_size(a) for a in ("narrow", "wide", "seq"))
        self.n, self.w, self.s = (lax.axis_index(a) for a in ("narrow", "wide", "seq"))
        self.X = self.W // 2
        self.chips = self.N * self.X
        self.core = lax.rem(self.w, 2)
        self.chip = self.n * self.X + self.w // 2
        self.sibling = self.chip_device(self.chip, 1 - self.core)

    def chip_device(self, chip, core):
        return {"narrow": chip // self.X, "wide": lax.rem(chip, self.X) * 2 + core}

    def ahead(self, k):
        return lax.rem(self.chip + k, self.chips)

    def behind(self, k):
        return lax.rem(self.chip - k + self.chips, self.chips)


def remote(src, dst, ss, rs, device):
    return pltpu.make_async_remote_copy(
        src_ref=src, dst_ref=dst, send_sem=ss, recv_sem=rs, device_id=device, device_id_type=MESH
    )


class Move:
    scratch = [pltpu.SemaphoreType.DMA]

    def peers(self, at):
        return []

    def start(self, at, src, dst):
        self.copy = pltpu.make_async_copy(src, dst, self.bufs[0])
        self.copy.start()

    def finish(self):
        self.copy.wait()


class PlaneGather:
    def __init__(self, chips, view):
        self.view = view
        self.scratch = [pltpu.SemaphoreType.DMA((chips,))] * 4 + [pltpu.SemaphoreType.DMA]

    def peers(self, at):
        return [at.chip_device(at.ahead(k), at.core) for k in range(1, at.chips)] + [at.sibling]

    def start(self, at, src, dst):
        ss, rs, fs, fr, ls = self.bufs
        self.at, self.dst = at, dst
        own = self.view(dst, at.chip, at.core)
        self.far = []
        for k in range(1, at.chips):
            c = remote(src, own, ss.at[k], rs.at[k], at.chip_device(at.ahead(k), at.core))
            c.start()
            self.far.append(c)
        self.near = [remote(src, own, fs.at[0], fr.at[0], at.sibling)]
        self.near[0].start()
        self.local = pltpu.make_async_copy(src, own, ls)
        self.local.start()

    def finish(self):
        at, (ss, rs, fs, fr, ls) = self.at, self.bufs
        for k in range(1, at.chips):
            block = self.view(self.dst, at.behind(k), at.core)
            self.far[k - 1].wait_recv()
            c = remote(block, block, fs.at[k], fr.at[k], at.sibling)
            c.start()
            self.near.append(c)
        self.local.wait()
        for c in self.far:
            c.wait_send()
        for c in self.near:
            c.wait()


class Exchange:
    def __init__(self, count, group, pick):
        self.count, self.group, self.pick = count, group, pick
        self.scratch = [pltpu.SemaphoreType.DMA((count,))] * 2 + [pltpu.SemaphoreType.DMA]

    def device(self, at, k):
        if self.group == "rows":
            p = lax.rem(at.n * at.S + at.s + k, at.N * at.S)
            return p, {"narrow": p // at.S, "seq": lax.rem(p, at.S)}
        if self.group == "all":
            j = lax.rem((at.n * at.S + at.s) * at.W + at.w + k, at.N * at.S * at.W)
            p = j // at.W
            return j, {"narrow": p // at.S, "seq": lax.rem(p, at.S), "wide": lax.rem(j, at.W)}
        me = {"seq": at.s, "narrow": at.n, "wide": at.w}[self.group]
        j = lax.rem(me + k, self.count)
        return j, {self.group: j}

    def peers(self, at):
        return [self.device(at, k)[1] for k in range(1, self.count)]

    def begin(self, at, src, dst):
        ss, rs, ls = self.bufs
        me = self.device(at, 0)[0]
        self.copies = [pltpu.make_async_copy(self.pick(src, me), dst.at[me], ls)]
        for k in range(1, self.count):
            j, d = self.device(at, k)
            self.copies.append(remote(self.pick(src, j), dst.at[me], ss.at[k], rs.at[k], d))

    def start(self, at, src, dst):
        self.begin(at, src, dst)
        for c in self.copies[1:] + self.copies[:1]:
            c.start()

    def finish(self):
        for c in self.copies:
            c.wait()


class PlaneScatter:
    def __init__(self, chips, block, view):
        self.chips, self.view = chips, view
        sem = pltpu.SemaphoreType.DMA((chips,))
        self.scratch = [pltpu.VMEM((chips,) + block, bf16)] * 3 + [sem] * 5

    def peers(self, at):
        return [at.chip_device(at.ahead(k), at.core) for k in range(1, at.chips)] + [at.sibling]

    def start(self, at, src):
        self.at = at
        mine, sib, got, ls, ns, nr, ss, rs = self.bufs
        self.local, self.near = {}, {}
        for k in self.order():
            d = at.ahead(k)
            self.near[k] = remote(self.view(src, d, 1 - at.core), sib.at[k], ns.at[k], nr.at[k], at.sibling)
            self.near[k].start()
            self.local[k] = pltpu.make_async_copy(self.view(src, d, at.core), mine.at[k], ls.at[k])
            self.local[k].start()

    def order(self):
        return list(range(1, self.chips)) + [0]

    def mid(self):
        at = self.at
        mine, sib, got, ls, ns, nr, ss, rs = self.bufs
        self.far = {}
        for k in self.order():
            self.local[k].wait()
            self.near[k].wait()
            if k:
                mine[k] = (mine[k].astype(f32) + sib[k].astype(f32)).astype(bf16)
                d = at.chip_device(at.ahead(k), at.core)
                self.far[k] = remote(mine.at[k], got.at[k], ss.at[k], rs.at[k], d)
                self.far[k].start()

    def finish(self):
        mine, sib, got = self.bufs[:3]
        total = mine[0].astype(f32) + sib[0].astype(f32)
        for k in self.order()[:-1]:
            self.far[k].wait()
            total = total + got[k].astype(f32)
        return total


def greet(ids):
    barrier = pltpu.get_barrier_semaphore()
    for d in ids:
        pl.semaphore_signal(barrier, inc=1, device_id=d, device_id_type=MESH)
    pl.semaphore_wait(barrier, len(ids))


HBM = pl.BlockSpec(memory_space=pl.ANY)
VMEM = pl.BlockSpec(memory_space=pltpu.VMEM)
SMEM = pl.BlockSpec(memory_space=pltpu.SMEM)


def fused(cid, name, us, parts, body, ins, outs, scratch=(), vmem=16):
    def kernel(*refs):
        a, refs = refs[: len(ins)], refs[len(ins) :]
        b, refs = refs[: len(outs)], refs[len(outs) :]
        c, refs = refs[: len(scratch)], refs[len(scratch) :]
        for p in parts:
            p.bufs, refs = refs[: len(p.scratch)], refs[len(p.scratch) :]
        at = Place()
        greet([d for p in parts for d in p.peers(at)])
        body(at, a, b, c)

    return pl.pallas_call(
        kernel,
        out_shape=tuple(jax.ShapeDtypeStruct(s, t) for s, t, _ in outs),
        in_specs=[spec for _, spec in ins],
        out_specs=tuple(spec for _, _, spec in outs),
        scratch_shapes=list(scratch) + [s for p in parts for s in p.scratch],
        compiler_params=pltpu.CompilerParams(
            collective_id=cid, has_side_effects=True, vmem_limit_bytes=vmem << 20
        ),
        cost_estimate=pl.CostEstimate(flops=int(us * 1.1e9), bytes_accessed=0, transcendentals=0),
        name=name,
    )(*[x for x, _ in ins])


def lane_roll(x, shift):
    return pltpu.roll(x.astype(f32), shift, 1)


def half_swap(x):
    lanes = lax.broadcasted_iota(jnp.int32, (1, x.shape[1]), 1)
    return jnp.where(lax.rem(lanes, 64) < 32, pltpu.roll(x, 96, 1), pltpu.roll(x, 32, 1))


def pair_up(a, b, n):
    lanes = lax.broadcasted_iota(jnp.int32, (1, 128), 1)
    if n == 0:
        return jnp.where(lanes < 64, a.astype(f32), lane_roll(b, 64))
    return jnp.where(lanes < 64, lane_roll(a, 64), b.astype(f32))


def put_pair(ref, g, rows, n, x):
    y = pltpu.roll(x, 64, 1)
    lo = slice(0, 64) if n == 0 else slice(64, 128)
    a, b = (x, y) if n == 0 else (y, x)
    ref[g, rows, lo] = a[:, lo].astype(bf16)
    ref[g + 1, rows, lo] = b[:, lo].astype(bf16)


FAR = 2.0**30
FQ = 1
FB = 1

def segment_lanes(rows, lanes, starts_ref, count):
    hit=jnp.zeros((rows.shape[0],lanes.shape[1]),f32)
    for j in range(count):
        inside=rows>=starts_ref[j]
        if j+1<count: inside=inside&(rows<starts_ref[j+1])
        hit=hit+jnp.where((lanes==64+j)&inside,1.0,0.0)
    return hit

def key_sides(S,RB,N,nseq,starts_ref,kv_ref,ka_ref,v1_ref):
    lanes=lax.broadcasted_iota(jnp.int32,(1,128),1)
    iota=lax.broadcasted_iota(jnp.int32,(RB,1),0)
    def fill(s,_):
        for n in range(N):
            kv=kv_ref[s,n*RB:(n+1)*RB,:]
            hot=segment_lanes((n*S+s)*RB+iota,lanes,starts_ref,nseq).astype(bf16)
            ka_ref[s,n*RB:(n+1)*RB,:]=jnp.where(lanes<64,kv,hot)
            v1_ref[s,n*RB:(n+1)*RB,:]=jnp.where(lanes<64,jnp.ones_like(kv),kv)
        return 0
    lax.fori_loop(0,S,fill,0)

def query_side(q,n,b,RB,nseq,starts_ref):
    lanes=lax.broadcasted_iota(jnp.int32,(1,128),1)
    iota=lax.broadcasted_iota(jnp.int32,(RB,1),0)
    if n==1: q=pltpu.roll(q.astype(f32),64,1).astype(bf16)
    far=jnp.where((lanes>=64)&(lanes<64+nseq),-FAR,0.0)*(1.0-segment_lanes(b*RB+iota,lanes,starts_ref,nseq))
    return jnp.where(lanes<64,q,jnp.zeros_like(q)),jnp.where(lanes<64,q,far.astype(bf16))

def attn_fwd_body(S,RB,N,nseq,mid,starts_ref,q_ref,kv_ref,ob_ref,res_ref,ka_ref,v1_ref,acc_ref):
    key_sides(S,RB,N,nseq,starts_ref,kv_ref,ka_ref,v1_ref)
    lanes=lax.broadcasted_iota(jnp.int32,(1,128),1)
    for n in range(N):
        def qblock(s,_):
            b=n*S+s
            _,qa=query_side(q_ref[s],n,b,RB,nseq,starts_ref)
            acc_ref[...]=jnp.zeros_like(acc_ref)
            def at(ref,j): return ref[lax.rem(j,S),pl.ds(pl.multiple_of((j//S)*RB,RB),RB),:]
            m=RB//FQ
            def kstep(j,_):
                k=at(ka_ref,j); v=at(v1_ref,j)
                sc=[dot(qa[i*m:(i+1)*m],k,NT) for i in range(FQ)]
                for i in range(FQ):
                    acc_ref[i*m:(i+1)*m]+=dot(jnp.exp2(sc[i]).astype(bf16),v,NN)
                return 0
            lax.fori_loop(0,b,kstep,0)
            sc=dot(qa,at(ka_ref,b),NT)
            half=RB//2
            tri=lax.broadcasted_iota(jnp.int32,(half,half),1)<=lax.broadcasted_iota(jnp.int32,(half,half),0)
            v=at(v1_ref,b)
            e=jnp.where(tri,jnp.exp2(sc[:half,:half]),0.0).astype(bf16)
            acc_ref[:half]+=dot(e,v[:half],NN)
            e1=jnp.exp2(sc[half:,:half]).astype(bf16)
            e2=jnp.where(tri,jnp.exp2(sc[half:,half:]),0.0).astype(bf16)
            acc_ref[half:]+=dot(e1,v[:half],NN)+dot(e2,v[half:],NN)
            acc=acc_ref[...]
            inv=1.0/acc
            o=acc*pltpu.roll(inv,64,1)
            res_ref[b]=jnp.where(lanes<64,inv,o)
            if n==0: ob_ref[s,:,0:64]=pltpu.roll(o,64,1)[:,0:64].astype(bf16)
            else: ob_ref[s,:,64:128]=o[:,64:128].astype(bf16)
            return 0
        lax.fori_loop(0,S,qblock,0)
        if n==0: mid()

def attn_bwd_body(S,RB,N,nseq,mid,starts_ref,q_ref,kv_ref,do_ref,res_ref,dq_ref,dkv_ref,ka_ref,v1_ref,acc_ref,dq_acc):
    key_sides(S,RB,N,nseq,starts_ref,kv_ref,ka_ref,v1_ref)
    acc_ref[...]=jnp.zeros_like(acc_ref)
    lanes=lax.broadcasted_iota(jnp.int32,(1,128),1)
    for n in range(N):
        def qblock(s,_):
            b=n*S+s
            do=do_ref[s].astype(f32)
            res=res_ref[b]
            q,qa=query_side(q_ref[s],n,b,RB,nseq,starts_ref)
            if n==0: do=pltpu.roll(do,64,1)
            du=jnp.where(lanes<64,0.0,do*pltpu.roll(res,64,1))
            delta=jnp.sum(du*res,axis=1,keepdims=True)
            hi=(-delta).astype(bf16).astype(f32)
            du0=du.astype(bf16)
            dua=jnp.where(lanes==0,hi,jnp.where(lanes==1,-delta-hi,du)).astype(bf16)
            dq_acc[...]=jnp.zeros_like(dq_acc)
            def where(j): return lax.rem(j,S),pl.ds(pl.multiple_of((j//S)*RB,RB),RB)
            def at(ref,j):
                a,c=where(j); return ref[a,c,:]
            m=RB//FB
            def kstep(j,_):
                a,c=where(j)
                for i in range(FB):
                    qs=slice(i*m,(i+1)*m)
                    k=at(ka_ref,j); v=at(v1_ref,j)
                    e=jnp.exp2(dot(k,qa[qs],NT))
                    ds=(e*dot(v,dua[qs],NT)).astype(bf16)
                    acc_ref[a,c,:]+=dot(e.astype(bf16),du0[qs],NN)+dot(ds,q[qs],NN)
                    dq_acc[qs]+=dot(ds,at(kv_ref,j),TN)
                return 0
            lax.fori_loop(0,b,kstep,0)
            sc=dot(at(ka_ref,b),qa,NT); dp=dot(at(v1_ref,b),dua,NT)
            half=RB//2
            tri=lax.broadcasted_iota(jnp.int32,(half,half),0)<=lax.broadcasted_iota(jnp.int32,(half,half),1)
            a=lax.rem(b,S); base=(b//S)*RB
            def piece(k0,q0,masked):
                e=jnp.exp2(sc[k0:k0+half,q0:q0+half])
                if masked: e=jnp.where(tri,e,0.0)
                ds=(e*dp[k0:k0+half,q0:q0+half]).astype(bf16)
                c=pl.ds(pl.multiple_of(base+k0,half),half)
                acc_ref[a,c,:]+=dot(e.astype(bf16),du0[q0:q0+half],NN)+dot(ds,q[q0:q0+half],NN)
                dq_acc[q0:q0+half]+=dot(ds,kv_ref[a,c,:],TN)
            piece(0,0,True); piece(0,half,False); piece(half,half,True)
            dq=dq_acc[...]*0.125
            if n==0: dq_ref[s,:,0:64]=dq[:,0:64].astype(bf16)
            else: dq_ref[s,:,64:128]=pltpu.roll(dq,64,1)[:,64:128].astype(bf16)
            return 0
        lax.fori_loop(0,S,qblock,0)
        if n==0: mid()
    ln2=0.6931471805599453
    def finish(s,_):
        acc=acc_ref[s]
        dkv_ref[s]=jnp.where(lanes<64,acc*ln2,acc).astype(bf16)
        return 0
    lax.fori_loop(0,S,finish,0)


def hidden_kernel(chunks, n_ref, x_ref, dy_ref, g0, g1, u0, u1, d0, d1, m_ref, dg_ref, dp_ref):
    half = g0.shape[0]
    a = pl.ds(pl.multiple_of(n_ref[0] * half, half), half)
    b = pl.ds(pl.multiple_of((1 - n_ref[0]) * half, half), half)
    rows = x_ref.shape[0] // chunks
    for c in range(chunks):
        r = slice(c * rows, (c + 1) * rows)
        xa, xb = x_ref[r, a], x_ref[r, b]
        gate = dot(xa, g0[...], NN) + dot(xb, g1[...], NN)
        up = dot(xa, u0[...], NN) + dot(xb, u1[...], NN)
        dh = dot(dy_ref[r, a], d0[...], NN) + dot(dy_ref[r, b], d1[...], NN)
        sig = 1.0 / (1.0 + jnp.exp(-gate))
        act = gate * sig
        m_ref[r] = (act * up).astype(bf16)
        dp_ref[r] = (dh * act).astype(bf16)
        dg_ref[r] = (dh * up * (sig + act * (1.0 - sig))).astype(bf16)


def hidden_units(n_idx, x, dy, mine, got, tile=256, chunks=3):
    R, D = x.shape
    half, H = got[0].shape
    steps = H // tile
    own = pl.BlockSpec((half, tile), lambda i, n: (0, n[0] * steps + i))
    oth = pl.BlockSpec((half, tile), lambda i, n: (0, i))
    full = pl.BlockSpec((R, D), lambda i, n: (0, 0), pipeline_mode=pl.Buffered(1))
    out = pl.BlockSpec((R, tile), lambda i, n: (0, i))
    return pl.pallas_call(
        functools.partial(hidden_kernel, chunks),
        grid_spec=pltpu.PrefetchScalarGridSpec(
            num_scalar_prefetch=1,
            grid=(steps,),
            in_specs=[full, full, own, oth, own, oth, own, oth],
            out_specs=[out] * 3,
        ),
        out_shape=[jax.ShapeDtypeStruct((R, H), bf16)] * 3,
        compiler_params=pltpu.CompilerParams(vmem_limit_bytes=56 << 20),
        cost_estimate=pl.CostEstimate(flops=6 * R * D * H, bytes_accessed=0, transcendentals=0),
        name="hidden",
    )(n_idx, x, dy, mine[0], got[0], mine[1], got[1], mine[2], got[2])


def back_kernel(chunks, per, n_ref, dg, dp, g0, g1, u0, u1, o_ref):
    here = pl.program_id(0) // per == n_ref[0]
    rows = dg.shape[0] // chunks

    def go(g, u):
        for c in range(chunks):
            r = slice(c * rows, (c + 1) * rows)
            o_ref[r] = (dot(dg[r], g[...], NT) + dot(dp[r], u[...], NT)).astype(bf16)

    @pl.when(here)
    def _():
        go(g0, u0)

    @pl.when(jnp.logical_not(here))
    def _():
        go(g1, u1)


def hidden_back(n_idx, dg, dp, mine, got, tile=256, chunks=3):
    R, H = dg.shape
    half = got[0].shape[0]
    per = half // tile

    def kept(i, n, turn):
        return jnp.where((i // per == n[0]) == turn, i % per, jnp.where((n[0] == 0) == turn, per - 1, 0))

    own = pl.BlockSpec((tile, H), lambda i, n: (kept(i, n, True), n[0]))
    oth = pl.BlockSpec((tile, H), lambda i, n: (kept(i, n, False), 0))
    full = pl.BlockSpec((R, H), lambda i, n: (0, 0), pipeline_mode=pl.Buffered(1))
    return pl.pallas_call(
        functools.partial(back_kernel, chunks, per),
        grid_spec=pltpu.PrefetchScalarGridSpec(
            num_scalar_prefetch=1,
            grid=(2 * per,),
            in_specs=[full, full, own, oth, own, oth],
            out_specs=pl.BlockSpec((R, tile), lambda i, n: (0, i)),
        ),
        out_shape=jax.ShapeDtypeStruct((R, 2 * half), bf16),
        compiler_params=pltpu.CompilerParams(vmem_limit_bytes=56 << 20),
        cost_estimate=pl.CostEstimate(flops=8 * R * H * half, bytes_accessed=0, transcendentals=0),
        name="hidden_back",
    )(n_idx, dg, dp, mine[0], got[0], mine[1], got[1])


def by_rows(
    tokens,
    gain_attn,
    w_query,
    w_key,
    w_value,
    w_out,
    gain_ffn,
    w_gate,
    w_up,
    w_down,
    lengths,
    cotangent,
):
    f32 = jnp.float32
    bf16 = jnp.bfloat16
    tok_rows = tokens.shape[0]
    col_count = tokens.shape[1]
    all_rows = tok_rows * lax.axis_size("narrow") * lax.axis_size("seq")
    block_id = lax.axis_index(("narrow", "seq"))
    row_ids = block_id * tok_rows + jnp.arange(tok_rows, dtype=jnp.int32)
    seq_first = seq_starts(lengths, row_ids)
    lowest_key = jnp.min(seq_first)
    highest_key = block_id * tok_rows + tok_rows - 1
    full_in = lax.all_gather(tokens, "wide", axis=1, tiled=True)
    inputs = full_in.astype(f32)
    recip1 = lax.rsqrt(jnp.mean(inputs * inputs, axis=1, keepdims=True) + NORM_EPSILON)
    normed1 = (inputs * recip1 * gain_attn).astype(bf16)
    query_w, key_w, value_w, out_w = (
        lax.all_gather(w_query, ("narrow", "seq"), axis=0, tiled=True),
        lax.all_gather(w_key, ("narrow", "seq"), axis=0, tiled=True),
        lax.all_gather(w_value, ("narrow", "seq"), axis=0, tiled=True),
        lax.all_gather(w_out, ("narrow", "seq"), axis=0, tiled=True),
    )
    gate_w, up_w, down_w = (
        lax.all_gather(w_gate, "narrow", axis=0, tiled=True),
        lax.all_gather(w_up, "narrow", axis=0, tiled=True),
        lax.all_gather(w_down, "narrow", axis=0, tiled=True),
    )
    heads_kv = key_w.shape[1]
    head_dim = key_w.shape[2]
    group_size = query_w.shape[2] // head_dim
    kv_width = heads_kv * head_dim
    score_scale = 1.0 / math.sqrt(head_dim)
    cos_table, sin_table = rotation(row_ids - seq_first, head_dim)
    query_raw = jnp.einsum("td,dkc->tkc", normed1, query_w, preferred_element_type=f32)
    key_raw = jnp.einsum("td,dkc->tkc", normed1, key_w, preferred_element_type=f32)
    value_raw = jnp.einsum("td,dkc->tkc", normed1, value_w, preferred_element_type=f32)
    query_b = rotate(
        query_raw.reshape(tok_rows, heads_kv, group_size, head_dim), cos_table, sin_table
    ).astype(bf16)
    key_b = rotate(key_raw, cos_table, sin_table).astype(bf16)
    value_b = value_raw.astype(bf16)
    kv_local = jnp.concatenate(
        [key_b.reshape(tok_rows, kv_width), value_b.reshape(tok_rows, kv_width)], axis=1
    )

    def block_scores(kv_part, key_start):
        part_rows = kv_part.shape[0]
        key_part = kv_part[:, :kv_width].reshape(part_rows, heads_kv, head_dim)
        value_part = kv_part[:, kv_width:].reshape(part_rows, heads_kv, head_dim)
        raw_scores = (
            jnp.einsum("qkgh,pkh->kgqp", query_b, key_part, preferred_element_type=f32)
            * score_scale
        )
        key_rows = key_start + jnp.arange(part_rows, dtype=jnp.int32)
        causal_mask = (key_rows[None, :] >= seq_first[:, None]) & (
            key_rows[None, :] <= row_ids[:, None]
        )
        weights = jnp.where(causal_mask[None, None], jnp.exp(raw_scores), 0.0)
        return (weights, key_part, value_part)

    def forward_block(state_in, kv_part, key_start):
        summed, row_total = state_in
        weights, key_part, value_part = block_scores(kv_part, key_start)
        row_total = row_total + jnp.sum(weights, axis=3)
        summed = summed + jnp.einsum(
            "kgqp,pkh->qkgh", weights.astype(bf16), value_part, preferred_element_type=f32
        )
        return (summed, row_total)

    start_state = (
        jnp.zeros((tok_rows, heads_kv, group_size, head_dim), f32),
        jnp.zeros((heads_kv, group_size, tok_rows), f32),
    )
    summed, row_total = over_blocks(
        forward_block,
        start_state,
        lax.all_gather(kv_local, ("narrow", "seq"), axis=0, tiled=True),
        tok_rows,
        lowest_key,
        highest_key,
    )
    inv_total = 1.0 / jnp.transpose(row_total, (2, 0, 1))
    attn_out = summed * inv_total[..., None]
    attn_b = attn_out.astype(bf16).reshape(tok_rows, heads_kv, group_size * head_dim)
    branch_part = jnp.einsum("tkc,dkc->td", attn_b, out_w, preferred_element_type=f32)
    branch = lax.psum(branch_part, "wide")
    residual = inputs + branch
    recip2 = lax.rsqrt(jnp.mean(residual * residual, axis=1, keepdims=True) + NORM_EPSILON)
    normed2 = (residual * recip2 * gain_ffn).astype(bf16)
    gate_val = jnp.dot(normed2, gate_w, preferred_element_type=f32)
    up_val = jnp.dot(normed2, up_w, preferred_element_type=f32)
    sigmoid_gate = jax.nn.sigmoid(gate_val)
    hidden = (gate_val * sigmoid_gate * up_val).astype(bf16)
    down_part = jnp.einsum("tf,df->td", hidden, down_w, preferred_element_type=f32)
    down = lax.psum_scatter(
        down_part.astype(jnp.bfloat16), "wide", scatter_dimension=1, tiled=True
    ).astype(jnp.float32)
    wide_id = lax.axis_index("wide")
    local_resid = lax.dynamic_slice_in_dim(residual, wide_id * col_count, col_count, 1)
    output = (local_resid + down).astype(bf16)
    grad_full = lax.all_gather(cotangent, "wide", axis=1, tiled=True)
    grad_hidden = jnp.einsum("td,df->tf", grad_full, down_w, preferred_element_type=f32)
    silu_slope = sigmoid_gate * (1.0 + gate_val * (1.0 - sigmoid_gate))
    grad_gate_val = (grad_hidden * up_val * silu_slope).astype(bf16)
    grad_up_val = (grad_hidden * gate_val * sigmoid_gate).astype(bf16)
    dw_down = jnp.einsum("td,tf->df", grad_full, hidden, preferred_element_type=f32)
    dw_gate = jnp.einsum("td,tf->df", normed2, grad_gate_val, preferred_element_type=f32)
    dw_up = jnp.einsum("td,tf->df", normed2, grad_up_val, preferred_element_type=f32)
    dn2_part = jnp.einsum(
        "tf,df->td", grad_gate_val, gate_w, preferred_element_type=f32
    ) + jnp.einsum("tf,df->td", grad_up_val, up_w, preferred_element_type=f32)
    dn2 = lax.psum(dn2_part, "wide")
    dgain_ffn = jnp.sum(dn2 * residual * recip2, axis=0)
    scaled2 = dn2 * gain_ffn
    dresid = (
        grad_full.astype(f32)
        + recip2 * scaled2
        - residual
        * (recip2 * recip2 * recip2)
        * jnp.mean(scaled2 * residual, axis=1, keepdims=True)
    )
    dbranch = dresid.astype(bf16)
    dw_out = jnp.einsum("td,tkc->dkc", dbranch, attn_b, preferred_element_type=f32)
    grad_attn = jnp.einsum("td,dkc->tkc", dbranch, out_w, preferred_element_type=f32).reshape(
        tok_rows, heads_kv, group_size, head_dim
    )
    grad_summed = (grad_attn * inv_total[..., None]).astype(bf16)
    delta_rows = jnp.transpose(jnp.sum(grad_attn * attn_out, axis=3) * inv_total, (1, 2, 0))

    def backward_block(state_in, kv_part, key_start):
        dquery, dkv_all = state_in
        weights, key_part, value_part = block_scores(kv_part, key_start)
        part_rows = kv_part.shape[0]
        dprob = jnp.einsum("qkgh,pkh->kgqp", grad_summed, value_part, preferred_element_type=f32)
        dscore = (weights * (dprob - delta_rows[..., None])).astype(bf16)
        dquery = dquery + jnp.einsum("kgqp,pkh->qkgh", dscore, key_part, preferred_element_type=f32)
        dkey = (
            jnp.einsum("kgqp,qkgh->pkh", dscore, query_b, preferred_element_type=f32) * score_scale
        )
        dvalue = jnp.einsum(
            "kgqp,qkgh->pkh", weights.astype(bf16), grad_summed, preferred_element_type=f32
        )
        block_grad = jnp.concatenate(
            [dkey.reshape(part_rows, kv_width), dvalue.reshape(part_rows, kv_width)], axis=1
        )
        current = lax.dynamic_slice_in_dim(dkv_all, key_start, part_rows, 0)
        dkv_all = lax.dynamic_update_slice_in_dim(dkv_all, current + block_grad, key_start, 0)
        return (dquery, dkv_all)

    back_state = (
        jnp.zeros((tok_rows, heads_kv, group_size, head_dim), f32),
        jnp.zeros((all_rows, 2 * kv_width), f32),
    )
    dquery, dkv_all = over_blocks(
        backward_block,
        back_state,
        lax.all_gather(kv_local, ("narrow", "seq"), axis=0, tiled=True),
        tok_rows,
        lowest_key,
        highest_key,
    )
    dkv_own = lax.psum_scatter(
        dkv_all.astype(jnp.bfloat16), ("narrow", "seq"), scatter_dimension=0, tiled=True
    ).astype(jnp.float32)
    dquery_b = (
        unrotate(dquery * score_scale, cos_table, sin_table)
        .astype(bf16)
        .reshape(tok_rows, heads_kv, group_size * head_dim)
    )
    dkey_b = unrotate(
        dkv_own[:, :kv_width].reshape(tok_rows, heads_kv, head_dim), cos_table, sin_table
    ).astype(bf16)
    dvalue_b = dkv_own[:, kv_width:].reshape(tok_rows, heads_kv, head_dim).astype(bf16)
    dw_query = jnp.einsum("td,tkc->dkc", normed1, dquery_b, preferred_element_type=f32)
    dw_key = jnp.einsum("td,tkc->dkc", normed1, dkey_b, preferred_element_type=f32)
    dw_value = jnp.einsum("td,tkc->dkc", normed1, dvalue_b, preferred_element_type=f32)
    dn1_part = jnp.einsum("tkc,dkc->td", dquery_b, query_w, preferred_element_type=f32)
    dn1_part = dn1_part + jnp.einsum("tkc,dkc->td", dkey_b, key_w, preferred_element_type=f32)
    dn1_part = dn1_part + jnp.einsum("tkc,dkc->td", dvalue_b, value_w, preferred_element_type=f32)
    dn1 = lax.psum(dn1_part.astype(jnp.bfloat16), "wide").astype(jnp.float32)
    dgain_attn = jnp.sum(dn1 * inputs * recip1, axis=0)
    scaled1 = dn1 * gain_attn
    dinputs = (
        dresid
        + recip1 * scaled1
        - inputs * (recip1 * recip1 * recip1) * jnp.mean(scaled1 * inputs, axis=1, keepdims=True)
    )
    grad_input = lax.dynamic_slice_in_dim(dinputs, wide_id * col_count, col_count, 1).astype(bf16)
    summed_grads = (
        lax.psum_scatter(
            dgain_attn.astype(jnp.bfloat16), ("narrow", "seq"), scatter_dimension=0, tiled=True
        ).astype(jnp.float32),
        lax.psum_scatter(
            dw_query.astype(jnp.bfloat16), ("narrow", "seq"), scatter_dimension=0, tiled=True
        ).astype(jnp.float32),
        lax.psum_scatter(
            dw_key.astype(jnp.bfloat16), ("narrow", "seq"), scatter_dimension=0, tiled=True
        ).astype(jnp.float32),
        lax.psum_scatter(
            dw_value.astype(jnp.bfloat16), ("narrow", "seq"), scatter_dimension=0, tiled=True
        ).astype(jnp.float32),
        lax.psum_scatter(
            dw_out.astype(jnp.bfloat16), ("narrow", "seq"), scatter_dimension=0, tiled=True
        ).astype(jnp.float32),
        lax.psum_scatter(
            dgain_ffn.astype(jnp.bfloat16), ("narrow", "seq"), scatter_dimension=0, tiled=True
        ).astype(jnp.float32),
        lax.psum_scatter(
            dw_gate.astype(jnp.bfloat16), ("narrow", "seq"), scatter_dimension=0, tiled=True
        ).astype(jnp.float32),
        lax.psum_scatter(
            dw_up.astype(jnp.bfloat16), ("narrow", "seq"), scatter_dimension=0, tiled=True
        ).astype(jnp.float32),
        lax.psum_scatter(
            dw_down.astype(jnp.bfloat16), ("narrow", "seq"), scatter_dimension=0, tiled=True
        ).astype(jnp.float32),
    )
    return (
        output,
        grad_input,
        summed_grads[0],
        summed_grads[1],
        summed_grads[2],
        summed_grads[3],
        summed_grads[4],
        summed_grads[5],
        summed_grads[6],
        summed_grads[7],
        summed_grads[8],
    )


def by_plane(
    tokens,
    gain_attn,
    w_query,
    w_key,
    w_value,
    w_out,
    gain_ffn,
    w_gate,
    w_up,
    w_down,
    lengths,
    cotangent,
):
    N, W, S = (lax.axis_size(a) for a in ("narrow", "wide", "seq"))
    n, s = lax.axis_index("narrow"), lax.axis_index("seq")
    P8, chips = N * W, N * W // 2
    RB, cols = tokens.shape
    R, D = N * RB, W * cols
    hd = w_key.shape[2]
    group = w_query.shape[2] // hd
    qw = group * hd
    rows, block = RB // W, D // (N * S)
    half_d, half_h = w_gate.shape[0], w_gate.shape[1] // N
    nseq = lengths.shape[0]
    chunk = RB // 2
    chunks = R // chunk
    fold = math.log2(math.e) / math.sqrt(hd)
    starts = jnp.cumsum(lengths) - lengths
    heads_shape, kv_shape, full_shape = (S, RB, N * hd), (S, R, 2 * hd), (R, D)
    slab_shape, own_shape = (N, S, block, half_h), (rows, D)

    def block_view(ref, chip, core):
        a, b = chip // (W // 2), lax.rem(chip, W // 2) * 2 + core
        return ref.at[pl.ds(a * RB, RB), pl.ds(b * cols, cols)]

    def row_view(ref, chip, core):
        return ref.at[chip * 2 + core]

    def to_seq():
        return Exchange(S, "seq", lambda src, j: src.at[j])

    def to_rows():
        return Exchange(N * S, "rows", lambda src, j: src.at[j])

    def to_slabs():
        return Exchange(S, "seq", lambda src, j: src.at[:, j])

    def to_head():
        return Exchange(N * S, "rows", lambda src, j: src.at[j // S])

    def to_narrow():
        return Exchange(N, "narrow", lambda src, j: src.at[j])

    def own_rows(at):
        return pl.ds(pl.multiple_of(at.n * RB + at.w * rows, rows), rows)

    def chunk_rows(c):
        k = c * chunk // RB
        return slice(c * chunk, (c + 1) * chunk), slice(c * chunk - k * RB, (c + 1) * chunk - k * RB), k

    def scale_of(x):
        return lax.rsqrt(jnp.mean(x * x, axis=1, keepdims=True) + NORM_EPSILON)

    w_mine = jnp.concatenate([w_query, w_key, w_value], axis=2).transpose(1, 0, 2)
    width = w_mine.shape[2]
    g_tok, g_w = PlaneGather(chips, block_view), to_head()

    def start_body(at, ins, outs, scratch):
        g_tok.start(at, ins[0], outs[0])
        g_w.start(at, ins[1], outs[1])
        g_tok.finish()
        g_w.finish()

    full_in, w_qkv = fused(
        1,
        "gather_start",
        55,
        [g_tok, g_w],
        start_body,
        [(tokens, HBM), (w_mine, HBM)],
        [(full_shape, bf16, HBM), ((N * S,) + w_mine.shape[1:], bf16, HBM)],
    )
    w_qkv = w_qkv.reshape(D, width)

    full_in, w_gate, w_up, w_down = lax.optimization_barrier((full_in, w_gate, w_up, w_down))

    def swapped(x):
        other = lax.dynamic_slice_in_dim(x, (1 - n) * half_h, half_h, 1)
        return lax.ppermute(other, "narrow", [(0, 1), (1, 0)])

    got_w = [swapped(x) for x in (w_gate, w_up, w_down)]
    mine_w = [w_gate, w_up, w_down]
    n_idx = jnp.full((1,), n, jnp.int32)

    row_ids = ((jnp.arange(N, dtype=jnp.int32) * S + s) * RB)[:, None] + jnp.arange(RB, dtype=jnp.int32)
    row_ids = row_ids.reshape(R)
    cos_table, sin_table = rotation(row_ids - seq_starts(lengths, row_ids), hd)
    cos_lanes = jnp.tile(cos_table, (1, 4))
    sin_lanes = jnp.tile(jnp.concatenate([-sin_table, sin_table], axis=1), (1, 2))

    e_q, e_kv, mv = to_seq(), Exchange(S, "seq", lambda src, j: src), Move()

    def qkv_body(at, ins, outs, scratch):
        x_ref, w_ref, gain_ref, cos_ref, sin_ref = ins
        q_out, kv_out, n1_out = outs
        n1, qs, kvs = scratch
        lanes = lax.broadcasted_iota(jnp.int32, (1, 128), 1)
        for c in range(chunks):
            r, rb, k = chunk_rows(c)
            x = x_ref[r].astype(f32)
            normed = (x * scale_of(x) * gain_ref[...]).astype(bf16)
            n1[r] = normed
            qkv = dot(normed, w_ref[...], NN)
            cos, sin = cos_ref[r], sin_ref[r]
            for g in range(0, group, 2):
                y = qkv[:, g * hd : (g + 2) * hd]
                put_pair(qs, g, rb, k, (y * cos + half_swap(y) * sin) * fold)
            y = qkv[:, qw:]
            kvs[r] = jnp.where(lanes < hd, y * cos + half_swap(y) * sin, y).astype(bf16)
        e_kv.start(at, kvs, kv_out)
        e_q.start(at, qs, q_out)
        mv.start(at, n1, n1_out)
        e_kv.finish()
        e_q.finish()
        mv.finish()

    q_all, kv_all, normed1 = fused(
        2,
        "qkv_to_heads",
        60,
        [e_q, e_kv, mv],
        qkv_body,
        [(full_in, VMEM), (w_qkv, VMEM), (gain_attn[None], VMEM), (cos_lanes, VMEM), (sin_lanes, VMEM)],
        [(heads_shape, bf16, HBM), (kv_shape, bf16, HBM), (full_shape, bf16, HBM)],
        [pltpu.VMEM(full_shape, bf16), pltpu.VMEM((group, RB, N * hd), bf16), pltpu.VMEM((R, 2 * hd), bf16)],
        40,
    )

    def forward_body(at, ins, outs, scratch):
        attn_fwd_body(S, RB, N, nseq, lambda: None, *ins, *outs, *scratch)

    kv_scratch = pltpu.VMEM(kv_shape, bf16)
    attn_own, attn_res = pl.pallas_call(
        lambda *refs: forward_body(None, refs[:3], refs[3:5], refs[5:]),
        out_shape=(
            jax.ShapeDtypeStruct(heads_shape, bf16),
            jax.ShapeDtypeStruct((N * S, RB, 2 * hd), f32),
        ),
        in_specs=[SMEM, VMEM, VMEM],
        out_specs=(VMEM, VMEM),
        scratch_shapes=[kv_scratch, kv_scratch, pltpu.VMEM((RB, 2 * hd), f32)],
        compiler_params=pltpu.CompilerParams(vmem_limit_bytes=48 << 20),
        cost_estimate=pl.CostEstimate(flops=int(42 * 1.1e9), bytes_accessed=0, transcendentals=0),
        name="attn_fwd",
    )(starts, q_all, kv_all)

    e_o, e_wo, g_cot = to_seq(), to_head(), PlaneGather(chips, block_view)
    sc_a, g_n2, mv_x, mv_w = PlaneScatter(chips, own_shape, row_view), PlaneGather(chips, row_view), Move(), Move()

    def mid_body(at, ins, outs, scratch):
        o_in, wo_in, cot_in, x_in, gain_ref = ins
        attn_b, grad_full, wo_out, resid, n2_out = outs
        heads, wo, part, xr, n2 = scratch
        e_o.start(at, o_in, heads)
        e_wo.start(at, wo_in, wo)
        mv_x.start(at, x_in.at[own_rows(at)], xr)
        g_cot.start(at, cot_in, grad_full)
        e_o.finish()
        for k in range(N):
            for g in range(0, group, 2):
                pair = pair_up(heads[g], heads[g + 1], k).astype(bf16)
                attn_b[k * RB : (k + 1) * RB, g * hd : (g + 2) * hd] = pair
        e_wo.finish()
        mv_w.start(at, wo, wo_out)
        w_all = wo[...].reshape(D, qw)
        for c in range(chunks):
            r = slice(c * chunk, (c + 1) * chunk)
            b = c * chunk // rows
            out = dot(attn_b[r], w_all, NT).astype(bf16)
            part[b : b + chunk // rows] = out.reshape(chunk // rows, rows, D)
        sc_a.start(at, part)
        sc_a.mid()
        g_cot.finish()
        mv_x.finish()
        h = xr[...].astype(f32) + sc_a.finish()
        resid[...] = h
        n2[...] = (h * scale_of(h) * gain_ref[...]).astype(bf16)
        g_n2.start(at, n2, n2_out)
        g_n2.finish()
        mv_w.finish()

    attn_b, grad_full, w_o, residual, normed2 = fused(
        3,
        "attn_to_ffn",
        120,
        [e_o, e_wo, g_cot, sc_a, g_n2, mv_x, mv_w],
        mid_body,
        [
            (attn_own, HBM),
            (w_out.transpose(1, 0, 2), HBM),
            (cotangent, HBM),
            (full_in, HBM),
            (gain_ffn[None], VMEM),
        ],
        [
            ((R, qw), bf16, VMEM),
            (full_shape, bf16, HBM),
            ((N * S, block, qw), bf16, HBM),
            (own_shape, f32, VMEM),
            ((P8,) + own_shape, bf16, HBM),
        ],
        [
            pltpu.VMEM(heads_shape, bf16),
            pltpu.VMEM((N * S, block, qw), bf16),
            pltpu.VMEM((P8,) + own_shape, bf16),
            pltpu.VMEM(own_shape, bf16),
            pltpu.VMEM(own_shape, bf16),
        ],
        48,
    )
    normed2 = normed2.reshape(full_shape)

    hidden, grad_gate_val, grad_up_val = hidden_units(n_idx, normed2, grad_full, mine_w, got_w)
    dn2_part = hidden_back(n_idx, grad_gate_val, grad_up_val, mine_w[:2], got_w[:2])

    sc_n, g_db, e_down = PlaneScatter(chips, own_shape, row_view), PlaneGather(chips, row_view), to_slabs()
    mvs = [Move() for _ in range(7)]

    def tile_cols(a, j):
        return pl.ds(pl.multiple_of((a * S + j) * block, block), block)

    def ffn_body(at, ins, outs, scratch):
        part_in, dy_in, m_in, n2_in, dg_in, dp_in, resid, gain_ref = ins
        db_out, dresid, dgain, got_down, gate_out, up_out = outs
        dy, m, n2, dg, dp, down, gate, up, db = scratch
        for mv_, src, dst in zip(mvs, (m_in, dy_in, n2_in, dg_in, dp_in), (m, dy, n2, dg, dp)):
            mv_.start(at, src, dst)
        sc_n.start(at, part_in)
        e_down.begin(at, down, got_down)
        mvs[0].finish()
        mvs[1].finish()

        def down_block(k):
            j = lax.rem(at.s + k, S)
            for a in range(N):
                down[a, j] = dot(dy[:, tile_cols(a, j)], m[...], TN).astype(bf16)
            e_down.copies[k].start()

        down_block(1)
        down_block(2)
        sc_n.mid()
        down_block(3)
        down_block(0)
        for mv_ in mvs[2:5]:
            mv_.finish()

        def other_tiles(j, _):
            for a in range(N):
                c = tile_cols(a, j)
                gate[a, j] = dot(n2[:, c], dg[...], TN).astype(bf16)
                up[a, j] = dot(n2[:, c], dp[...], TN).astype(bf16)
            return 0

        lax.fori_loop(0, S, other_tiles, 0)
        mvs[5].start(at, gate, gate_out)
        mvs[6].start(at, up, up_out)
        dn2 = sc_n.finish()
        h = resid[...]
        r2 = scale_of(h)
        dgain[...] = jnp.sum(dn2 * h * r2, axis=0, keepdims=True)
        scaled = dn2 * gain_ref[...]
        own = dy[own_rows(at)].astype(f32)
        grad = own + r2 * scaled - h * (r2 * r2 * r2) * jnp.mean(scaled * h, axis=1, keepdims=True)
        dresid[...] = grad
        db[...] = grad.astype(bf16)
        g_db.start(at, db, db_out)
        g_db.finish()
        e_down.finish()
        mvs[5].finish()
        mvs[6].finish()

    dbranch, dresid, dgain_ffn, got_down, dw_gate, dw_up = fused(
        4,
        "ffn_grads",
        110,
        [sc_n, g_db, e_down] + mvs,
        ffn_body,
        [
            (dn2_part.reshape((P8,) + own_shape), HBM),
            (grad_full, HBM),
            (hidden, HBM),
            (normed2, HBM),
            (grad_gate_val, HBM),
            (grad_up_val, HBM),
            (residual, VMEM),
            (gain_ffn[None], VMEM),
        ],
        [
            ((P8,) + own_shape, bf16, HBM),
            (own_shape, f32, VMEM),
            ((1, D), f32, VMEM),
            ((S, N, block, half_h), bf16, HBM),
            (slab_shape, bf16, HBM),
            (slab_shape, bf16, HBM),
        ],
        [
            pltpu.VMEM(full_shape, bf16),
            pltpu.VMEM((R, half_h), bf16),
            pltpu.VMEM(full_shape, bf16),
            pltpu.VMEM((R, half_h), bf16),
            pltpu.VMEM((R, half_h), bf16),
            pltpu.VMEM(slab_shape, bf16),
            pltpu.VMEM(slab_shape, bf16),
            pltpu.VMEM(slab_shape, bf16),
            pltpu.VMEM(own_shape, bf16),
        ],
        60,
    )

    e_do, t_down = to_seq(), to_narrow()
    mvt = [Move() for _ in range(7)]
    tile = half_d // 4

    def grad_heads_body(at, ins, outs, scratch):
        db_in, w_ref, ab, gd_in, m_in, wd_in, wdo_in, resid = ins
        do_out, dwo_out, y_out, down_out = outs
        db, dos, gd, gsum, m, wd, y, dwo = scratch
        mine = wd_in.at[:, pl.ds(pl.multiple_of(at.n * half_h, half_h), half_h)]
        moves = [(db_in, db), (gd_in, gd), (m_in, m), (mine, wd.at[at.n]), (wdo_in, wd.at[1 - at.n])]
        for mv_, (src, dst) in zip(mvt, moves):
            mv_.start(at, src, dst)
        mvt[0].finish()
        for c in range(chunks):
            r, rb, k = chunk_rows(c)
            out = dot(db[r], w_ref[...], NN)
            for g in range(0, group, 2):
                put_pair(dos, g, rb, k, out[:, g * hd : (g + 2) * hd])
        e_do.start(at, dos, do_out)
        mvt[1].finish()
        gsum[...] = sum(gd[i].astype(f32) for i in range(S)).astype(bf16)
        t_down.start(at, gsum, down_out)

        def wo_tile(p, _):
            c = pl.ds(pl.multiple_of(p * block, block), block)
            dwo[p] = dot(db[:, c], ab[...], TN).astype(bf16)
            return 0

        lax.fori_loop(0, N * S, wo_tile, 0)
        mvt[5].start(at, dwo, dwo_out)
        for mv_ in mvt[2:5]:
            mv_.finish()
        for a in range(N):

            def y_tile(i, _):
                c = pl.ds(pl.multiple_of(a * half_d + i * tile, tile), tile)
                w_tile = wd[a, pl.ds(pl.multiple_of(i * tile, tile), tile), :]
                y[:, c] = dot(m[...], w_tile, NT).astype(bf16)
                return 0

            lax.fori_loop(0, half_d // tile, y_tile, 0)
        o = own_rows(at)
        y[o] = (y[o].astype(f32) + resid[...]).astype(bf16)
        mvt[6].start(at, y, y_out)
        e_do.finish()
        t_down.finish()
        mvt[5].finish()
        mvt[6].finish()

    do_all, dw_o, down_part, down_grad = fused(
        5,
        "grad_to_heads",
        25,
        [e_do, t_down] + mvt,
        grad_heads_body,
        [
            (dbranch.reshape(full_shape), HBM),
            (w_o.reshape(D, qw), VMEM),
            (attn_b, VMEM),
            (got_down, HBM),
            (hidden, HBM),
            (w_down, HBM),
            (got_w[2], HBM),
            (residual, VMEM),
        ],
        [
            (heads_shape, bf16, HBM),
            ((N * S, block, qw), bf16, HBM),
            (full_shape, bf16, HBM),
            ((N, block, half_h), bf16, HBM),
        ],
        [
            pltpu.VMEM(full_shape, bf16),
            pltpu.VMEM((group, RB, N * hd), bf16),
            pltpu.VMEM((S, N, block, half_h), bf16),
            pltpu.VMEM((N, block, half_h), bf16),
            pltpu.VMEM((R, half_h), bf16),
            pltpu.VMEM((N, half_d, half_h), bf16),
            pltpu.VMEM(full_shape, bf16),
            pltpu.VMEM((N * S, block, qw), bf16),
        ],
        56,
    )

    e_gate, e_wog, sc_y = to_slabs(), to_rows(), PlaneScatter(chips, (RB, cols), block_view)

    def backward_body(at, ins, outs, scratch):
        gate_in, dwo_in, y_in, *attn_ins = ins
        got_gate, got_wo, out_ref, dq_ref, dkv_ref = outs
        sc_y.start(at, y_in)
        e_gate.start(at, gate_in, got_gate)
        e_wog.start(at, dwo_in, got_wo)
        attn_bwd_body(S, RB, N, nseq, sc_y.mid, *attn_ins, dq_ref, dkv_ref, *scratch)
        out_ref[...] = sc_y.finish().astype(bf16)
        e_gate.finish()
        e_wog.finish()

    got_gate, got_wo, output, dq_own, dkv_own = fused(
        6,
        "attn_bwd",
        90,
        [e_gate, e_wog, sc_y],
        backward_body,
        [
            (dw_gate, HBM),
            (dw_o, HBM),
            (down_part, HBM),
            (starts, SMEM),
            (q_all, VMEM),
            (kv_all, VMEM),
            (do_all, VMEM),
            (attn_res, VMEM),
        ],
        [
            ((S, N, block, half_h), bf16, HBM),
            ((N * S, block, qw), bf16, HBM),
            ((RB, cols), bf16, VMEM),
            (heads_shape, bf16, VMEM),
            (kv_shape, bf16, VMEM),
        ],
        [kv_scratch, kv_scratch, pltpu.VMEM(kv_shape, f32), pltpu.VMEM((RB, 2 * hd), f32)],
        60,
    )

    e_dq, e_dkv, t_gate, e_up, e_wq = to_seq(), to_seq(), to_narrow(), to_rows(), to_rows()
    sc_1 = PlaneScatter(chips, own_shape, row_view)
    e_in = Exchange(W, "wide", lambda src, j: src.at[:, pl.ds(pl.multiple_of(j * cols, cols), cols)])
    e_gain = Exchange(N * S * W, "all", lambda src, j: src.at[j // W])
    mvu = [Move() for _ in range(3)]

    def last_body(at, ins, outs, scratch):
        dq_in, dkv_in, gg_in, n1_in, up_in, x_in, w_ref, cos_ref, sin_ref, dresid_ref, gain_ref, dgain_ref = ins
        gi_out, gains_out, got_up, got_wq, gate_out = outs
        dq, dkv, n1, gg, gsum, dqkv, part, dwq, xr, gi, gains = scratch
        e_dq.start(at, dq_in, dq)
        e_dkv.start(at, dkv_in, dkv)
        mvu[0].start(at, gg_in, gg)
        mvu[1].start(at, n1_in, n1)
        mvu[2].start(at, x_in.at[own_rows(at)], xr)
        mvu[0].finish()
        gsum[...] = sum(gg[i].astype(f32) for i in range(S)).astype(bf16)
        t_gate.start(at, gsum, gate_out)
        lanes = lax.broadcasted_iota(jnp.int32, (1, 128), 1)
        e_dq.finish()
        e_dkv.finish()
        e_up.start(at, up_in, got_up)
        for c in range(chunks):
            r, rb, k = chunk_rows(c)
            cos, sin = cos_ref[r], sin_ref[r]
            for g in range(0, group, 2):
                y = pair_up(dq[g, rb], dq[g + 1, rb], k)
                dqkv[r, g * hd : (g + 2) * hd] = (y * cos - half_swap(y) * sin).astype(bf16)
            y = sum(dkv[i, r].astype(f32) for i in range(S))
            dqkv[r, qw:] = jnp.where(lanes < hd, y * cos - half_swap(y) * sin, y).astype(bf16)
            out = dot(dqkv[r], w_ref[...], NT).astype(bf16)
            b = c * chunk // rows
            part[b : b + chunk // rows] = out.reshape(chunk // rows, rows, D)
        sc_1.start(at, part)
        mvu[1].finish()

        def wq_tile(p, _):
            c = pl.ds(pl.multiple_of(p * block, block), block)
            dwq[p] = dot(n1[:, c], dqkv[...], TN).astype(bf16)
            return 0

        lax.fori_loop(0, N * S, wq_tile, 0)
        sc_1.mid()
        e_wq.start(at, dwq, got_wq)
        mvu[2].finish()
        x = xr[...].astype(f32)
        r1 = scale_of(x)
        dn1 = sc_1.finish()
        dgain = jnp.sum(dn1 * x * r1, axis=0, keepdims=True)
        dgain2 = dgain_ref[...]
        for p in range(N * S):
            for i in range(block // 128):
                c = slice(p * block + i * 128, p * block + (i + 1) * 128)
                gains[p, i : i + 1, :] = dgain[:, c]
                gains[p, block // 128 + i : block // 128 + i + 1, :] = dgain2[:, c]
        e_gain.start(at, gains, gains_out)
        scaled = dn1 * gain_ref[...]
        grad = dresid_ref[...] + r1 * scaled - x * (r1 * r1 * r1) * jnp.mean(scaled * x, axis=1, keepdims=True)
        gi[...] = grad.astype(bf16)
        e_in.start(at, gi, gi_out)
        for p in (e_in, e_gain, t_gate, e_wq, e_up):
            p.finish()

    gains_shape = (N * S, 2 * block // 128, 128)
    grad_input, gains, got_up, got_wq, gate_grad = fused(
        7,
        "last",
        160,
        [e_dq, e_dkv, t_gate, e_up, e_wq, sc_1, e_in, e_gain] + mvu,
        last_body,
        [
            (dq_own, HBM),
            (dkv_own, HBM),
            (got_gate, HBM),
            (normed1, HBM),
            (dw_up.reshape(N * S, block, half_h), HBM),
            (full_in, HBM),
            (w_qkv, VMEM),
            (cos_lanes, VMEM),
            (sin_lanes, VMEM),
            (dresid, VMEM),
            (gain_attn[None], VMEM),
            (dgain_ffn, VMEM),
        ],
        [
            ((W, rows, cols), bf16, HBM),
            ((N * S * W,) + gains_shape[1:], f32, HBM),
            ((N * S, block, half_h), bf16, HBM),
            ((N * S, block, width), bf16, HBM),
            ((N, block, half_h), bf16, HBM),
        ],
        [
            pltpu.VMEM(heads_shape, bf16),
            pltpu.VMEM(kv_shape, bf16),
            pltpu.VMEM(full_shape, bf16),
            pltpu.VMEM((S, N, block, half_h), bf16),
            pltpu.VMEM((N, block, half_h), bf16),
            pltpu.VMEM((R, width), bf16),
            pltpu.VMEM((P8,) + own_shape, bf16),
            pltpu.VMEM((N * S, block, width), bf16),
            pltpu.VMEM(own_shape, bf16),
            pltpu.VMEM(own_shape, bf16),
            pltpu.VMEM(gains_shape, f32),
        ],
        60,
    )

    def over_seq(got):
        return jnp.sum(got.reshape(N, S, *got.shape[1:]).astype(f32), axis=1)

    def side_by_side(halves):
        return jnp.concatenate(list(halves), axis=1).astype(f32)

    gains = jnp.sum(gains, axis=0).reshape(2, block)
    qkv_grads = over_seq(got_wq).transpose(1, 0, 2)
    return (
        output,
        grad_input.reshape(RB, cols),
        gains[0],
        qkv_grads[:, :, :qw],
        qkv_grads[:, :, qw : qw + hd],
        qkv_grads[:, :, qw + hd :],
        over_seq(got_wo).transpose(1, 0, 2),
        gains[1],
        side_by_side(gate_grad),
        side_by_side(over_seq(got_up)),
        side_by_side(down_grad),
    )


def local(tokens, gain_attn, w_query, w_key, *others):
    plane = lax.axis_size("narrow") * lax.axis_size("wide")
    heads_kv = w_key.shape[1] * lax.axis_size("wide")
    group = w_query.shape[2] // w_key.shape[2]
    fits = lax.axis_size("narrow") == 2 and heads_kv == plane and group == lax.axis_size("seq")
    body = by_plane if fits and w_key.shape[2] == 64 else by_rows
    return body(tokens, gain_attn, w_query, w_key, *others)


def solution(mesh):
    return jax.shard_map(
        local,
        mesh=mesh,
        in_specs=(
            P(("narrow", "seq"), "wide"),
            P(),
            P(("narrow", "seq"), "wide", None),
            P(("narrow", "seq"), "wide", None),
            P(("narrow", "seq"), "wide", None),
            P(("narrow", "seq"), "wide", None),
            P(),
            P("narrow", "wide"),
            P("narrow", "wide"),
            P("narrow", "wide"),
            P(),
            P(("narrow", "seq"), "wide"),
        ),
        out_specs=(
            P(("narrow", "seq"), "wide"),
            P(("narrow", "seq"), "wide"),
            P(("narrow", "seq")),
            P(("narrow", "seq"), "wide", None),
            P(("narrow", "seq"), "wide", None),
            P(("narrow", "seq"), "wide", None),
            P(("narrow", "seq"), "wide", None),
            P(("narrow", "seq")),
            P(("narrow", "seq"), "wide"),
            P(("narrow", "seq"), "wide"),
            P(("narrow", "seq"), "wide"),
        ),
        check_vma=False,
    )
```

```python
import functools
import math

import jax
import jax.numpy as jnp
from jax import lax
from jax.experimental import pallas as pl
from jax.experimental.pallas import tpu as pltpu
from jax.sharding import PartitionSpec as P

f32 = jnp.float32
bf16 = jnp.bfloat16
MESH = pl.DeviceIdType.MESH
NT = (((1,), (1,)), ((), ()))
NN = (((1,), (0,)), ((), ()))
TN = (((0,), (0,)), ((), ()))

ROPE_THETA = 500000.0
ROPE_FACTOR = 32.0
LOW_FACTOR = 1.0
HIGH_FACTOR = 4.0
OLD_CONTEXT = 8192.0
NORM_EPSILON = 1e-05


def frequencies(head_dim):
    freq_index = jnp.arange(head_dim // 2, dtype=jnp.float32)
    base_freq = jnp.exp(freq_index * (-2.0 * math.log(ROPE_THETA) / head_dim))
    wavelen = 2.0 * math.pi / base_freq
    smooth = jnp.clip((OLD_CONTEXT / wavelen - LOW_FACTOR) / (HIGH_FACTOR - LOW_FACTOR), 0.0, 1.0)
    return (1.0 - smooth) * base_freq / ROPE_FACTOR + smooth * base_freq


def seq_starts(lengths, row_ids):
    seq_ends = jnp.cumsum(lengths)
    begins = seq_ends - lengths
    found_at = jnp.where(begins[None, :] <= row_ids[:, None], begins[None, :], 0)
    return jnp.max(found_at, axis=1)


def rotation(positions, head_dim):
    angles = positions.astype(jnp.float32)[:, None] * frequencies(head_dim)[None, :]
    return (jnp.cos(angles), jnp.sin(angles))


def table_shape(values, cos_table, sin_table):
    half_dim = values.shape[-1] // 2
    bcast_shape = (cos_table.shape[0],) + (1,) * (values.ndim - 2) + (half_dim,)
    return (half_dim, cos_table.reshape(bcast_shape), sin_table.reshape(bcast_shape))


def rotate(values, cos_table, sin_table):
    half_dim, cos_part, sin_part = table_shape(values, cos_table, sin_table)
    first_half = values[..., :half_dim]
    second = values[..., half_dim:]
    return jnp.concatenate(
        [first_half * cos_part - second * sin_part, second * cos_part + first_half * sin_part],
        axis=-1,
    )


def unrotate(grad_vals, cos_table, sin_table):
    half_dim, cos_part, sin_part = table_shape(grad_vals, cos_table, sin_table)
    first_half = grad_vals[..., :half_dim]
    second = grad_vals[..., half_dim:]
    return jnp.concatenate(
        [first_half * cos_part + second * sin_part, second * cos_part - first_half * sin_part],
        axis=-1,
    )


def over_blocks(block_fn, state_now, kv_piece, block_len, lowest, highest):
    piece_rows = kv_piece.shape[0]
    block_count = piece_rows // block_len

    def one_step(block_no, state_in):
        begin = block_no * block_len
        kv_part = lax.dynamic_slice_in_dim(kv_piece, block_no * block_len, block_len, 0)
        live = (begin <= highest) & (begin + block_len - 1 >= lowest)

        def compute(carried):
            return block_fn(carried, kv_part, begin)

        def skipped(carried):
            return carried

        return lax.cond(live, compute, skipped, state_in)

    return lax.fori_loop(0, block_count, one_step, state_now)


def dot(a, b, dims):
    return lax.dot_general(a, b, dims, preferred_element_type=f32)


class Place:
    def __init__(self):
        self.N, self.W, self.S = (lax.axis_size(a) for a in ("narrow", "wide", "seq"))
        self.n, self.w, self.s = (lax.axis_index(a) for a in ("narrow", "wide", "seq"))
        self.X = self.W // 2
        self.chips = self.N * self.X
        self.core = lax.rem(self.w, 2)
        self.chip = self.n * self.X + self.w // 2
        self.sibling = self.chip_device(self.chip, 1 - self.core)

    def chip_device(self, chip, core):
        return {"narrow": chip // self.X, "wide": lax.rem(chip, self.X) * 2 + core}

    def ahead(self, k):
        return lax.rem(self.chip + k, self.chips)

    def behind(self, k):
        return lax.rem(self.chip - k + self.chips, self.chips)


def remote(src, dst, ss, rs, device):
    return pltpu.make_async_remote_copy(
        src_ref=src, dst_ref=dst, send_sem=ss, recv_sem=rs, device_id=device, device_id_type=MESH
    )


class Move:
    scratch = [pltpu.SemaphoreType.DMA]

    def peers(self, at):
        return []

    def start(self, at, src, dst):
        self.copy = pltpu.make_async_copy(src, dst, self.bufs[0])
        self.copy.start()

    def finish(self):
        self.copy.wait()


class PlaneGather:
    def __init__(self, chips, view):
        self.view = view
        self.scratch = [pltpu.SemaphoreType.DMA((chips,))] * 4 + [pltpu.SemaphoreType.DMA]

    def peers(self, at):
        return [at.chip_device(at.ahead(k), at.core) for k in range(1, at.chips)] + [at.sibling]

    def start(self, at, src, dst):
        ss, rs, fs, fr, ls = self.bufs
        own = self.view(dst, at.chip, at.core)
        self.local = pltpu.make_async_copy(src, own, ls)
        self.far, self.near = [], [remote(src, own, fs.at[0], fr.at[0], at.sibling)]
        for k in range(1, at.chips):
            self.far.append(remote(src, own, ss.at[k], rs.at[k], at.chip_device(at.ahead(k), at.core)))
            block = self.view(dst, at.behind(k), at.core)
            self.near.append(remote(block, block, fs.at[k], fr.at[k], at.sibling))
        for c in self.far + self.near[:1] + [self.local]:
            c.start()

    def relay(self):
        for c, d in zip(self.far, self.near[1:]):
            c.wait_recv()
            d.start()

    def finish(self, relayed=False):
        if not relayed:
            self.relay()
        self.local.wait()
        for c in self.far:
            c.wait_send()
        for c in self.near:
            c.wait()


class Exchange:
    def __init__(self, count, group, pick):
        self.count, self.group, self.pick = count, group, pick
        self.scratch = [pltpu.SemaphoreType.DMA((count,))] * 2 + [pltpu.SemaphoreType.DMA]

    def device(self, at, k):
        if self.group == "rows":
            p = lax.rem(at.n * at.S + at.s + k, at.N * at.S)
            return p, {"narrow": p // at.S, "seq": lax.rem(p, at.S)}
        if self.group == "all":
            j = lax.rem((at.n * at.S + at.s) * at.W + at.w + k, at.N * at.S * at.W)
            p = j // at.W
            return j, {"narrow": p // at.S, "seq": lax.rem(p, at.S), "wide": lax.rem(j, at.W)}
        me = {"seq": at.s, "narrow": at.n, "wide": at.w}[self.group]
        j = lax.rem(me + k, self.count)
        return j, {self.group: j}

    def peers(self, at):
        return [self.device(at, k)[1] for k in range(1, self.count)]

    def begin(self, at, src, dst):
        ss, rs, ls = self.bufs
        me = self.device(at, 0)[0]
        self.copies = [pltpu.make_async_copy(self.pick(src, me), dst.at[me], ls)]
        for k in range(1, self.count):
            j, d = self.device(at, k)
            self.copies.append(remote(self.pick(src, j), dst.at[me], ss.at[k], rs.at[k], d))

    def start(self, at, src, dst):
        self.begin(at, src, dst)
        for c in self.copies[1:] + self.copies[:1]:
            c.start()

    def finish(self):
        for c in self.copies:
            c.wait()


class Stream:
    def __init__(self, S):
        self.scratch = [pltpu.SemaphoreType.DMA((S,))] * 2 + [pltpu.SemaphoreType.DMA]

    def peers(self, at):
        return [{"seq": lax.rem(at.s + k, at.S)} for k in range(1, at.S)]

    def away(self, at, src, dst, j):
        ss, rs, _ = self.bufs
        k = lax.rem(j - at.s + at.S, at.S)
        return remote(src, dst, ss.at[k], rs.at[k], {"seq": j})

    def send(self, at, src, dst, j):
        @pl.when(j == at.s)
        def _():
            pltpu.make_async_copy(src, dst, self.bufs[2]).start()

        @pl.when(j != at.s)
        def _():
            self.away(at, src, dst, j).start()

    def finish(self, at, src, dst):
        pltpu.make_async_copy(src, dst, self.bufs[2]).wait()
        for k in range(1, at.S):
            self.away(at, src, dst, lax.rem(at.s + k, at.S)).wait()


class SeqSum:
    def __init__(self, block, pick):
        self.pick = pick
        self.scratch = [pltpu.VMEM((8,) + block, bf16)] + [pltpu.SemaphoreType.DMA((6,))] * 2
        self.scratch += [pltpu.SemaphoreType.DMA((3,))]

    def peers(self, at):
        return [{"seq": at.s + 1 - 2 * lax.rem(at.s, 2)}, {"seq": 3 - at.s}]

    def order(self, at):
        low = at.s < 2
        return jnp.where(low, 3, 0), jnp.where(low, 2, 1), at.s + 1 - 2 * lax.rem(at.s, 2), at.s

    def copy(self, at, i):
        buf, ss, rs, _ = self.bufs
        far_outer, far_inner, pair, _ = self.order(at)
        src, slot, sem, to = {
            0: (self.pick(self.src, far_outer), 0, 0, pair),
            1: (self.pick(self.src, far_inner), 1, 1, pair),
            2: (self.pick(self.src, pair), 2, 2, pair),
            3: (buf.at[5], 4, 3, 3 - at.s),
            4: (buf.at[6], 3, 4, 3 - at.s),
            5: (buf.at[4], 3, 4, pair),
        }[i]
        return remote(src, buf.at[slot], ss.at[i], rs.at[sem], {"seq": to})

    def inner(self, at):
        return (at.s == 1) | (at.s == 2)

    def load(self, at, i):
        far_outer, far_inner, _, own = self.order(at)
        j = (far_outer, far_inner, own)[i]
        return pltpu.make_async_copy(self.pick(self.src, j), self.bufs[0].at[5 + i], self.bufs[3].at[i])

    def begin(self, at, src):
        self.src = src

    def ready(self, at, i):
        inner = self.inner(at)
        if i == 0:

            @pl.when(jnp.logical_not(inner))
            def _():
                self.copy(at, 0).start()

        if i == 2:

            @pl.when(inner)
            def _():
                self.copy(at, 2).start()

        if i < 2:

            @pl.when(inner)
            def _():
                self.load(at, i).start()

        if i == 3:
            self.load(at, 2).start()

    def start(self, at, src):
        self.begin(at, src)
        for i in range(4):
            self.ready(at, i)

    def cross(self, at, i):
        buf = self.bufs[0]
        self.copy(at, i).wait_recv()
        self.load(at, i).wait()
        buf[5 + i] = (buf[5 + i].astype(f32) + buf[i].astype(f32)).astype(bf16)
        self.copy(at, 3 + i).start()

    def step(self, at, i):
        @pl.when(self.inner(at))
        def _():
            self.cross(at, i)

        @pl.when(jnp.logical_not(self.inner(at)))
        def _():
            self.copy(at, i).wait_send()
            self.copy(at, i + 1).start()

    def step3(self, at):
        @pl.when(self.inner(at))
        def _():
            self.copy(at, 3).wait_recv()
            self.copy(at, 5).start()

    def total(self, at):
        inner = self.inner(at)
        buf = self.bufs[0]
        self.load(at, 2).wait()
        self.copy(at, 2).wait()
        self.copy(at, 4).wait_recv()

        @pl.when(inner)
        def _():
            for i in (3, 4, 5):
                self.copy(at, i).wait_send()

        return buf[7].astype(f32) + buf[2].astype(f32) + buf[3].astype(f32)


class Swap:
    scratch = [pltpu.SemaphoreType.DMA] * 2

    def __init__(self, axis):
        self.axis = axis

    def partner(self, at):
        return {"narrow": 1 - at.n} if self.axis == "narrow" else {"seq": at.s + 1 - 2 * lax.rem(at.s, 2)}

    def peers(self, at):
        return [self.partner(at)]

    def start(self, at, src, dst):
        self.copy = remote(src, dst, *self.bufs, self.partner(at))
        self.copy.start()

    def finish(self):
        self.copy.wait()


class HeadGather:
    def __init__(self, S):
        self.scratch = [pltpu.SemaphoreType.DMA((S,))] * 4 + [pltpu.SemaphoreType.DMA]

    def peers(self, at):
        return [{"seq": lax.rem(at.s + k, at.S)} for k in range(1, at.S)] + [{"narrow": 1 - at.n}]

    def start(self, at, src, dst):
        ss, rs, fs, fr, ls = self.bufs
        own, other = dst.at[at.n * at.S + at.s], dst.at[(1 - at.n) * at.S + at.s]
        self.cross = remote(src.at[1 - at.n], own, ss.at[0], rs.at[0], {"narrow": 1 - at.n})
        self.cross.start()
        self.direct, self.relayed = [], []
        for k in range(1, at.S):
            to = {"seq": lax.rem(at.s + k, at.S)}
            self.direct.append(remote(src.at[at.n], own, ss.at[k], rs.at[k], to))
            self.direct[-1].start()
            self.relayed.append(remote(other, other, fs.at[k], fr.at[k], to))
        self.local = pltpu.make_async_copy(src.at[at.n], own, ls)
        self.local.start()

    def relay(self):
        self.cross.wait_recv()
        for c in self.relayed:
            c.start()

    def finish(self):
        self.cross.wait_send()
        for c in self.direct + self.relayed + [self.local]:
            c.wait()


class PlaneScatter:
    def __init__(self, chips, block, view):
        self.chips, self.view = chips, view
        sem = pltpu.SemaphoreType.DMA((chips,))
        self.scratch = [pltpu.VMEM((chips,) + block, bf16)] * 3 + [sem] * 5

    def peers(self, at):
        return [at.chip_device(at.ahead(k), at.core) for k in range(1, at.chips)] + [at.sibling]

    def start(self, at, src):
        mine, sib, got, ls, ns, nr, ss, rs = self.bufs
        self.local, self.near, self.far = {}, {}, {}
        for k in self.order():
            d = at.ahead(k)
            if k:
                self.far[k] = remote(mine.at[k], got.at[k], ss.at[k], rs.at[k], at.chip_device(d, at.core))
            self.near[k] = remote(self.view(src, d, 1 - at.core), sib.at[k], ns.at[k], nr.at[k], at.sibling)
            self.near[k].start()
            self.local[k] = pltpu.make_async_copy(self.view(src, d, at.core), mine.at[k], ls.at[k])
            self.local[k].start()

    def order(self):
        return list(range(1, self.chips)) + [0]

    def mid(self):
        mine, sib = self.bufs[:2]
        for k in self.order():
            self.local[k].wait()
            self.near[k].wait()
            if k:
                mine[k] = (mine[k].astype(f32) + sib[k].astype(f32)).astype(bf16)
                self.far[k].start()

    def finish(self):
        mine, sib, got = self.bufs[:3]
        total = mine[0].astype(f32) + sib[0].astype(f32)
        for k in self.order()[:-1]:
            self.far[k].wait()
            total = total + got[k].astype(f32)
        return total


def greet(ids):
    barrier = pltpu.get_barrier_semaphore()
    for d in ids:
        pl.semaphore_signal(barrier, inc=1, device_id=d, device_id_type=MESH)
    pl.semaphore_wait(barrier, len(ids))


HBM = pl.BlockSpec(memory_space=pl.ANY)
VMEM = pl.BlockSpec(memory_space=pltpu.VMEM)
SMEM = pl.BlockSpec(memory_space=pltpu.SMEM)


def fused(cid, name, us, parts, body, ins, outs, scratch=(), vmem=16):
    def kernel(*refs):
        a, refs = refs[: len(ins)], refs[len(ins) :]
        b, refs = refs[: len(outs)], refs[len(outs) :]
        c, refs = refs[: len(scratch)], refs[len(scratch) :]
        for p in parts:
            p.bufs, refs = refs[: len(p.scratch)], refs[len(p.scratch) :]
        at = Place()
        greet([d for p in parts for d in p.peers(at)])
        body(at, a, b, c)

    return pl.pallas_call(
        kernel,
        out_shape=tuple(jax.ShapeDtypeStruct(s, t) for s, t, _ in outs),
        in_specs=[spec for _, spec in ins],
        out_specs=tuple(spec for _, _, spec in outs),
        scratch_shapes=list(scratch) + [s for p in parts for s in p.scratch],
        compiler_params=pltpu.CompilerParams(
            collective_id=cid, has_side_effects=True, vmem_limit_bytes=vmem << 20
        ),
        cost_estimate=pl.CostEstimate(flops=int(us * 1.1e9), bytes_accessed=0, transcendentals=0),
        name=name,
    )(*[x for x, _ in ins])


def lane_roll(x, shift):
    return pltpu.roll(x.astype(f32), shift, 1)


def half_swap(x):
    lanes = lax.broadcasted_iota(jnp.int32, (1, x.shape[1]), 1)
    return jnp.where(lax.rem(lanes, 64) < 32, pltpu.roll(x, 96, 1), pltpu.roll(x, 32, 1))


def pair_up(a, b, n):
    lanes = lax.broadcasted_iota(jnp.int32, (1, 128), 1)
    if n == 0:
        return jnp.where(lanes < 64, a.astype(f32), lane_roll(b, 64))
    return jnp.where(lanes < 64, lane_roll(a, 64), b.astype(f32))


def put_pair(ref, g, rows, n, x):
    y = pltpu.roll(x, 64, 1)
    lo = slice(0, 64) if n == 0 else slice(64, 128)
    a, b = (x, y) if n == 0 else (y, x)
    ref[g, rows, lo] = a[:, lo].astype(bf16)
    ref[g + 1, rows, lo] = b[:, lo].astype(bf16)


FAR = 2.0**30


def segment_lanes(rows, lanes, starts_ref, count):
    hit = jnp.zeros((rows.shape[0], lanes.shape[1]), f32)
    for j in range(count):
        inside = rows >= starts_ref[j]
        if j + 1 < count:
            inside = inside & (rows < starts_ref[j + 1])
        hit = hit + jnp.where((lanes == 64 + j) & inside, 1.0, 0.0)
    return hit


def key_sides(S, RB, N, nseq, starts_ref, kv_ref, ka_ref, v1_ref):
    lanes = lax.broadcasted_iota(jnp.int32, (1, 128), 1)
    iota = lax.broadcasted_iota(jnp.int32, (RB, 1), 0)

    def fill(s, _):
        for n in range(N):
            kv = kv_ref[s, n * RB : (n + 1) * RB, :]
            hot = segment_lanes((n * S + s) * RB + iota, lanes, starts_ref, nseq).astype(bf16)
            ka_ref[s, n * RB : (n + 1) * RB, :] = jnp.where(lanes < 64, kv, hot)
            v1_ref[s, n * RB : (n + 1) * RB, :] = jnp.where(lanes < 64, jnp.ones_like(kv), kv)
        return 0

    lax.fori_loop(0, S, fill, 0)


def query_side(q, n, b, RB, nseq, starts_ref):
    lanes = lax.broadcasted_iota(jnp.int32, (1, 128), 1)
    iota = lax.broadcasted_iota(jnp.int32, (RB, 1), 0)
    if n == 1:
        q = pltpu.roll(q.astype(f32), 64, 1).astype(bf16)
    others = 1.0 - segment_lanes(b * RB + iota, lanes, starts_ref, nseq)
    far = jnp.where((lanes >= 64) & (lanes < 64 + nseq), -FAR, 0.0) * others
    return jnp.where(lanes < 64, q, far.astype(bf16))


def key_block(j, S, RB):
    return lax.rem(j, S), pl.ds(pl.multiple_of((j // S) * RB, RB), RB)


def attn_fwd_body(S, RB, N, nseq, done, starts_ref, q_ref, kv_ref, ob_ref, res_ref, ka_ref, v1_ref, acc_ref):
    key_sides(S, RB, N, nseq, starts_ref, kv_ref, ka_ref, v1_ref)
    lanes = lax.broadcasted_iota(jnp.int32, (1, 128), 1)
    for n in range(N):

        def qblock(s, _):
            b = n * S + s
            qa = query_side(q_ref[s], n, b, RB, nseq, starts_ref)
            acc_ref[...] = jnp.zeros_like(acc_ref)

            def at(ref, j):
                a, c = key_block(j, S, RB)
                return ref[a, c, :]

            def kstep(j, _):
                e = jnp.exp2(dot(qa, at(ka_ref, j), NT))
                acc_ref[...] += dot(e.astype(bf16), at(v1_ref, j), NN)
                return 0

            lax.fori_loop(0, b, kstep, 0)
            sc = dot(qa, at(ka_ref, b), NT)
            half = RB // 2
            tri = lax.broadcasted_iota(jnp.int32, (half, half), 1) <= lax.broadcasted_iota(jnp.int32, (half, half), 0)
            v = at(v1_ref, b)
            e = jnp.where(tri, jnp.exp2(sc[:half, :half]), 0.0).astype(bf16)
            acc_ref[:half] += dot(e, v[:half], NN)
            e1 = jnp.exp2(sc[half:, :half]).astype(bf16)
            e2 = jnp.where(tri, jnp.exp2(sc[half:, half:]), 0.0).astype(bf16)
            acc_ref[half:] += dot(e1, v[:half], NN) + dot(e2, v[half:], NN)
            acc = acc_ref[...]
            inv = 1.0 / acc
            o = acc * pltpu.roll(inv, 64, 1)
            res_ref[b] = jnp.where(lanes < 64, inv, o)
            if n == 0:
                ob_ref[s, :, 0:64] = pltpu.roll(o, 64, 1)[:, 0:64].astype(bf16)
            else:
                ob_ref[s, :, 64:128] = o[:, 64:128].astype(bf16)
            done(n, s)
            return 0

        lax.fori_loop(0, S, qblock, 0)


def attn_bwd_body(
    S, RB, N, nseq, done,
    starts_ref, q_ref, kv_ref, do_ref, res_ref, dq_ref, dkv_ref,
    ka_ref, v1_ref, qa_ref, du_ref, dq_acc, k_acc, v_acc,
):
    key_sides(S, RB, N, nseq, starts_ref, kv_ref, ka_ref, v1_ref)
    lanes = lax.broadcasted_iota(jnp.int32, (1, 128), 1)
    for n in range(N):

        def prepare(s, _):
            b = n * S + s
            do = do_ref[s].astype(f32)
            res = res_ref[b]
            if n == 0:
                do = pltpu.roll(do, 64, 1)
            du = jnp.where(lanes < 64, 0.0, do * pltpu.roll(res, 64, 1))
            delta = jnp.sum(du * res, axis=1, keepdims=True)
            hi = (-delta).astype(bf16).astype(f32)
            du_ref[b] = jnp.where(lanes == 0, hi, jnp.where(lanes == 1, -delta - hi, du)).astype(bf16)
            qa_ref[b] = query_side(q_ref[s], n, b, RB, nseq, starts_ref)
            dq_acc[b] = jnp.zeros((RB, 128), f32)
            return 0

        lax.fori_loop(0, S, prepare, 0)
    half = RB // 2
    tri = lax.broadcasted_iota(jnp.int32, (half, half), 0) <= lax.broadcasted_iota(jnp.int32, (half, half), 1)
    for n in range(N):

        def kblock(s, _):
            j = n * S + s
            key = ka_ref[s, n * RB : (n + 1) * RB, :]
            value = v1_ref[s, n * RB : (n + 1) * RB, :]
            kv = kv_ref[s, n * RB : (n + 1) * RB, :]

            def weights(k0, q0):
                qs = slice(q0, q0 + half)
                sc = dot(key[k0 : k0 + half], qa_ref[j, qs], NT)
                dp = dot(value[k0 : k0 + half], du_ref[j, qs], NT)
                e = jnp.exp2(sc)
                if k0 == q0:
                    e = jnp.where(tri, e, 0.0)
                return e.astype(bf16), (e * dp).astype(bf16)

            lo, hi = slice(0, half), slice(half, RB)
            e00, s00 = weights(0, 0)
            e01, s01 = weights(0, half)
            e11, s11 = weights(half, half)
            v_acc[lo] = dot(e00, du_ref[j, lo], NN) + dot(e01, du_ref[j, hi], NN)
            v_acc[hi] = dot(e11, du_ref[j, hi], NN)
            k_acc[lo] = dot(s00, qa_ref[j, lo], NN) + dot(s01, qa_ref[j, hi], NN)
            k_acc[hi] = dot(s11, qa_ref[j, hi], NN)
            dq_acc[j, lo] += dot(s00, kv[:half], TN)
            dq_acc[j, hi] += dot(s01, kv[:half], TN) + dot(s11, kv[half:], TN)

            def qstep(b, _):
                e = jnp.exp2(dot(key, qa_ref[b], NT))
                ds = (e * dot(value, du_ref[b], NT)).astype(bf16)
                v_acc[...] += dot(e.astype(bf16), du_ref[b], NN)
                k_acc[...] += dot(ds, qa_ref[b], NN)
                dq_acc[b] += dot(ds, kv, TN)
                return 0

            lax.fori_loop(j + 1, N * S, qstep, 0)
            whole = jnp.where(lanes < 64, k_acc[...] * math.log(2.0), v_acc[...])
            dkv_ref[s, n * RB : (n + 1) * RB, :] = whole.astype(bf16)
            dq = dq_acc[j] * 0.125
            if n == 0:
                dq_ref[s, :, 0:64] = dq[:, 0:64].astype(bf16)
            else:
                dq_ref[s, :, 64:128] = pltpu.roll(dq, 64, 1)[:, 64:128].astype(bf16)
            done(n, s)
            return 0

        lax.fori_loop(0, S, kblock, 0)


def hidden_kernel(chunks, n_ref, x_ref, dy_ref, g0, g1, g2, u0, u1, u2, d0, d1, d2, m_ref, dg_ref, dp_ref):
    half = g0.shape[0]
    a = pl.ds(pl.multiple_of(n_ref[0] * half, half), half)
    part = half // 2
    b = pl.ds(pl.multiple_of((1 - n_ref[0]) * half + n_ref[1] * part, part), part)
    d = pl.ds(pl.multiple_of((1 - n_ref[0]) * half + (1 - n_ref[1]) * part, part), part)
    rows = x_ref.shape[0] // chunks
    for c in range(chunks):
        r = slice(c * rows, (c + 1) * rows)

        def product(y, w0, w1, w2):
            return dot(y[r, a], w0[...], NN) + dot(y[r, b], w1[...], NN) + dot(y[r, d], w2[...], NN)

        gate, up, dh = product(x_ref, g0, g1, g2), product(x_ref, u0, u1, u2), product(dy_ref, d0, d1, d2)
        sig = 1.0 / (1.0 + jnp.exp(-gate))
        act = gate * sig
        m_ref[r] = (act * up).astype(bf16)
        dp_ref[r] = (dh * act).astype(bf16)
        dg_ref[r] = (dh * up * (sig + act * (1.0 - sig))).astype(bf16)


def hidden_units(n_idx, x, dy, mine, got, tile=256, chunks=3):
    R, D = x.shape
    half, H = 2 * got[0][0].shape[0], got[0][0].shape[1]
    steps = H // tile
    own = pl.BlockSpec((half, tile), lambda i, n: (0, n[0] * steps + i))
    oth = pl.BlockSpec((half // 2, tile), lambda i, n: (0, i))
    full = pl.BlockSpec((R, D), lambda i, n: (0, 0), pipeline_mode=pl.Buffered(1))
    out = pl.BlockSpec((R, tile), lambda i, n: (0, i))
    return pl.pallas_call(
        functools.partial(hidden_kernel, chunks),
        grid_spec=pltpu.PrefetchScalarGridSpec(
            num_scalar_prefetch=1,
            grid=(steps,),
            in_specs=[full, full] + [own, oth, oth] * 3,
            out_specs=[out] * 3,
        ),
        out_shape=[jax.ShapeDtypeStruct((R, H), bf16)] * 3,
        compiler_params=pltpu.CompilerParams(vmem_limit_bytes=56 << 20),
        cost_estimate=pl.CostEstimate(flops=6 * R * D * H, bytes_accessed=0, transcendentals=0),
        name="hidden",
    )(n_idx, x, dy, mine[0], *got[0], mine[1], *got[1], mine[2], *got[2])


def back_kernel(chunks, per, n_ref, dg, dp, g0, g1, g2, u0, u1, u2, o_ref):
    i = pl.program_id(0)
    rows = dg.shape[0] // chunks

    def go(g, u):
        for c in range(chunks):
            r = slice(c * rows, (c + 1) * rows)
            o_ref[r] = (dot(dg[r], g[...], NT) + dot(dp[r], u[...], NT)).astype(bf16)

    for which, (g, u) in enumerate(((g0, u0), (g1, u1), (g2, u2))):

        @pl.when(source_of(i, per, n_ref) == which)
        def _(g=g, u=u):
            go(g, u)


def source_of(i, per, n_ref):
    part = i % per // (per // 2)
    return jnp.where(i // per == n_ref[0], 0, jnp.where(part == n_ref[1], 1, 2))


def hidden_back(n_idx, dg, dp, mine, got, tile=256, chunks=3):
    R, H = dg.shape
    half = 2 * got[0][0].shape[0]
    per = half // tile

    def spec(which, count, column):
        def index(i, n):
            return jnp.where(source_of(i, per, n) == which, i % count, 0), column(n)

        return pl.BlockSpec((tile, H), index)

    specs = [spec(0, per, lambda n: n[0]), spec(1, per // 2, lambda n: 0), spec(2, per // 2, lambda n: 0)]
    full = pl.BlockSpec((R, H), lambda i, n: (0, 0), pipeline_mode=pl.Buffered(1))
    return pl.pallas_call(
        functools.partial(back_kernel, chunks, per),
        grid_spec=pltpu.PrefetchScalarGridSpec(
            num_scalar_prefetch=1,
            grid=(2 * per,),
            in_specs=[full, full] + specs * 2,
            out_specs=pl.BlockSpec((R, tile), lambda i, n: (0, i)),
        ),
        out_shape=jax.ShapeDtypeStruct((R, 2 * half), bf16),
        compiler_params=pltpu.CompilerParams(vmem_limit_bytes=56 << 20),
        cost_estimate=pl.CostEstimate(flops=8 * R * H * half, bytes_accessed=0, transcendentals=0),
        name="hidden_back",
    )(n_idx, dg, dp, mine[0], *got[0], mine[1], *got[1])


def by_rows(
    tokens,
    gain_attn,
    w_query,
    w_key,
    w_value,
    w_out,
    gain_ffn,
    w_gate,
    w_up,
    w_down,
    lengths,
    cotangent,
):
    f32 = jnp.float32
    bf16 = jnp.bfloat16
    tok_rows = tokens.shape[0]
    col_count = tokens.shape[1]
    all_rows = tok_rows * lax.axis_size("narrow") * lax.axis_size("seq")
    block_id = lax.axis_index(("narrow", "seq"))
    row_ids = block_id * tok_rows + jnp.arange(tok_rows, dtype=jnp.int32)
    seq_first = seq_starts(lengths, row_ids)
    lowest_key = jnp.min(seq_first)
    highest_key = block_id * tok_rows + tok_rows - 1
    full_in = lax.all_gather(tokens, "wide", axis=1, tiled=True)
    inputs = full_in.astype(f32)
    recip1 = lax.rsqrt(jnp.mean(inputs * inputs, axis=1, keepdims=True) + NORM_EPSILON)
    normed1 = (inputs * recip1 * gain_attn).astype(bf16)
    query_w, key_w, value_w, out_w = (
        lax.all_gather(w_query, ("narrow", "seq"), axis=0, tiled=True),
        lax.all_gather(w_key, ("narrow", "seq"), axis=0, tiled=True),
        lax.all_gather(w_value, ("narrow", "seq"), axis=0, tiled=True),
        lax.all_gather(w_out, ("narrow", "seq"), axis=0, tiled=True),
    )
    gate_w, up_w, down_w = (
        lax.all_gather(w_gate, "narrow", axis=0, tiled=True),
        lax.all_gather(w_up, "narrow", axis=0, tiled=True),
        lax.all_gather(w_down, "narrow", axis=0, tiled=True),
    )
    heads_kv = key_w.shape[1]
    head_dim = key_w.shape[2]
    group_size = query_w.shape[2] // head_dim
    kv_width = heads_kv * head_dim
    score_scale = 1.0 / math.sqrt(head_dim)
    cos_table, sin_table = rotation(row_ids - seq_first, head_dim)
    query_raw = jnp.einsum("td,dkc->tkc", normed1, query_w, preferred_element_type=f32)
    key_raw = jnp.einsum("td,dkc->tkc", normed1, key_w, preferred_element_type=f32)
    value_raw = jnp.einsum("td,dkc->tkc", normed1, value_w, preferred_element_type=f32)
    query_b = rotate(
        query_raw.reshape(tok_rows, heads_kv, group_size, head_dim), cos_table, sin_table
    ).astype(bf16)
    key_b = rotate(key_raw, cos_table, sin_table).astype(bf16)
    value_b = value_raw.astype(bf16)
    kv_local = jnp.concatenate(
        [key_b.reshape(tok_rows, kv_width), value_b.reshape(tok_rows, kv_width)], axis=1
    )

    def block_scores(kv_part, key_start):
        part_rows = kv_part.shape[0]
        key_part = kv_part[:, :kv_width].reshape(part_rows, heads_kv, head_dim)
        value_part = kv_part[:, kv_width:].reshape(part_rows, heads_kv, head_dim)
        raw_scores = (
            jnp.einsum("qkgh,pkh->kgqp", query_b, key_part, preferred_element_type=f32)
            * score_scale
        )
        key_rows = key_start + jnp.arange(part_rows, dtype=jnp.int32)
        causal_mask = (key_rows[None, :] >= seq_first[:, None]) & (
            key_rows[None, :] <= row_ids[:, None]
        )
        weights = jnp.where(causal_mask[None, None], jnp.exp(raw_scores), 0.0)
        return (weights, key_part, value_part)

    def forward_block(state_in, kv_part, key_start):
        summed, row_total = state_in
        weights, key_part, value_part = block_scores(kv_part, key_start)
        row_total = row_total + jnp.sum(weights, axis=3)
        summed = summed + jnp.einsum(
            "kgqp,pkh->qkgh", weights.astype(bf16), value_part, preferred_element_type=f32
        )
        return (summed, row_total)

    start_state = (
        jnp.zeros((tok_rows, heads_kv, group_size, head_dim), f32),
        jnp.zeros((heads_kv, group_size, tok_rows), f32),
    )
    summed, row_total = over_blocks(
        forward_block,
        start_state,
        lax.all_gather(kv_local, ("narrow", "seq"), axis=0, tiled=True),
        tok_rows,
        lowest_key,
        highest_key,
    )
    inv_total = 1.0 / jnp.transpose(row_total, (2, 0, 1))
    attn_out = summed * inv_total[..., None]
    attn_b = attn_out.astype(bf16).reshape(tok_rows, heads_kv, group_size * head_dim)
    branch_part = jnp.einsum("tkc,dkc->td", attn_b, out_w, preferred_element_type=f32)
    branch = lax.psum(branch_part, "wide")
    residual = inputs + branch
    recip2 = lax.rsqrt(jnp.mean(residual * residual, axis=1, keepdims=True) + NORM_EPSILON)
    normed2 = (residual * recip2 * gain_ffn).astype(bf16)
    gate_val = jnp.dot(normed2, gate_w, preferred_element_type=f32)
    up_val = jnp.dot(normed2, up_w, preferred_element_type=f32)
    sigmoid_gate = jax.nn.sigmoid(gate_val)
    hidden = (gate_val * sigmoid_gate * up_val).astype(bf16)
    down_part = jnp.einsum("tf,df->td", hidden, down_w, preferred_element_type=f32)
    down = lax.psum_scatter(
        down_part.astype(jnp.bfloat16), "wide", scatter_dimension=1, tiled=True
    ).astype(jnp.float32)
    wide_id = lax.axis_index("wide")
    local_resid = lax.dynamic_slice_in_dim(residual, wide_id * col_count, col_count, 1)
    output = (local_resid + down).astype(bf16)
    grad_full = lax.all_gather(cotangent, "wide", axis=1, tiled=True)
    grad_hidden = jnp.einsum("td,df->tf", grad_full, down_w, preferred_element_type=f32)
    silu_slope = sigmoid_gate * (1.0 + gate_val * (1.0 - sigmoid_gate))
    grad_gate_val = (grad_hidden * up_val * silu_slope).astype(bf16)
    grad_up_val = (grad_hidden * gate_val * sigmoid_gate).astype(bf16)
    dw_down = jnp.einsum("td,tf->df", grad_full, hidden, preferred_element_type=f32)
    dw_gate = jnp.einsum("td,tf->df", normed2, grad_gate_val, preferred_element_type=f32)
    dw_up = jnp.einsum("td,tf->df", normed2, grad_up_val, preferred_element_type=f32)
    dn2_part = jnp.einsum(
        "tf,df->td", grad_gate_val, gate_w, preferred_element_type=f32
    ) + jnp.einsum("tf,df->td", grad_up_val, up_w, preferred_element_type=f32)
    dn2 = lax.psum(dn2_part, "wide")
    dgain_ffn = jnp.sum(dn2 * residual * recip2, axis=0)
    scaled2 = dn2 * gain_ffn
    dresid = (
        grad_full.astype(f32)
        + recip2 * scaled2
        - residual
        * (recip2 * recip2 * recip2)
        * jnp.mean(scaled2 * residual, axis=1, keepdims=True)
    )
    dbranch = dresid.astype(bf16)
    dw_out = jnp.einsum("td,tkc->dkc", dbranch, attn_b, preferred_element_type=f32)
    grad_attn = jnp.einsum("td,dkc->tkc", dbranch, out_w, preferred_element_type=f32).reshape(
        tok_rows, heads_kv, group_size, head_dim
    )
    grad_summed = (grad_attn * inv_total[..., None]).astype(bf16)
    delta_rows = jnp.transpose(jnp.sum(grad_attn * attn_out, axis=3) * inv_total, (1, 2, 0))

    def backward_block(state_in, kv_part, key_start):
        dquery, dkv_all = state_in
        weights, key_part, value_part = block_scores(kv_part, key_start)
        part_rows = kv_part.shape[0]
        dprob = jnp.einsum("qkgh,pkh->kgqp", grad_summed, value_part, preferred_element_type=f32)
        dscore = (weights * (dprob - delta_rows[..., None])).astype(bf16)
        dquery = dquery + jnp.einsum("kgqp,pkh->qkgh", dscore, key_part, preferred_element_type=f32)
        dkey = (
            jnp.einsum("kgqp,qkgh->pkh", dscore, query_b, preferred_element_type=f32) * score_scale
        )
        dvalue = jnp.einsum(
            "kgqp,qkgh->pkh", weights.astype(bf16), grad_summed, preferred_element_type=f32
        )
        block_grad = jnp.concatenate(
            [dkey.reshape(part_rows, kv_width), dvalue.reshape(part_rows, kv_width)], axis=1
        )
        current = lax.dynamic_slice_in_dim(dkv_all, key_start, part_rows, 0)
        dkv_all = lax.dynamic_update_slice_in_dim(dkv_all, current + block_grad, key_start, 0)
        return (dquery, dkv_all)

    back_state = (
        jnp.zeros((tok_rows, heads_kv, group_size, head_dim), f32),
        jnp.zeros((all_rows, 2 * kv_width), f32),
    )
    dquery, dkv_all = over_blocks(
        backward_block,
        back_state,
        lax.all_gather(kv_local, ("narrow", "seq"), axis=0, tiled=True),
        tok_rows,
        lowest_key,
        highest_key,
    )
    dkv_own = lax.psum_scatter(
        dkv_all.astype(jnp.bfloat16), ("narrow", "seq"), scatter_dimension=0, tiled=True
    ).astype(jnp.float32)
    dquery_b = (
        unrotate(dquery * score_scale, cos_table, sin_table)
        .astype(bf16)
        .reshape(tok_rows, heads_kv, group_size * head_dim)
    )
    dkey_b = unrotate(
        dkv_own[:, :kv_width].reshape(tok_rows, heads_kv, head_dim), cos_table, sin_table
    ).astype(bf16)
    dvalue_b = dkv_own[:, kv_width:].reshape(tok_rows, heads_kv, head_dim).astype(bf16)
    dw_query = jnp.einsum("td,tkc->dkc", normed1, dquery_b, preferred_element_type=f32)
    dw_key = jnp.einsum("td,tkc->dkc", normed1, dkey_b, preferred_element_type=f32)
    dw_value = jnp.einsum("td,tkc->dkc", normed1, dvalue_b, preferred_element_type=f32)
    dn1_part = jnp.einsum("tkc,dkc->td", dquery_b, query_w, preferred_element_type=f32)
    dn1_part = dn1_part + jnp.einsum("tkc,dkc->td", dkey_b, key_w, preferred_element_type=f32)
    dn1_part = dn1_part + jnp.einsum("tkc,dkc->td", dvalue_b, value_w, preferred_element_type=f32)
    dn1 = lax.psum(dn1_part.astype(jnp.bfloat16), "wide").astype(jnp.float32)
    dgain_attn = jnp.sum(dn1 * inputs * recip1, axis=0)
    scaled1 = dn1 * gain_attn
    dinputs = (
        dresid
        + recip1 * scaled1
        - inputs * (recip1 * recip1 * recip1) * jnp.mean(scaled1 * inputs, axis=1, keepdims=True)
    )
    grad_input = lax.dynamic_slice_in_dim(dinputs, wide_id * col_count, col_count, 1).astype(bf16)
    summed_grads = (
        lax.psum_scatter(
            dgain_attn.astype(jnp.bfloat16), ("narrow", "seq"), scatter_dimension=0, tiled=True
        ).astype(jnp.float32),
        lax.psum_scatter(
            dw_query.astype(jnp.bfloat16), ("narrow", "seq"), scatter_dimension=0, tiled=True
        ).astype(jnp.float32),
        lax.psum_scatter(
            dw_key.astype(jnp.bfloat16), ("narrow", "seq"), scatter_dimension=0, tiled=True
        ).astype(jnp.float32),
        lax.psum_scatter(
            dw_value.astype(jnp.bfloat16), ("narrow", "seq"), scatter_dimension=0, tiled=True
        ).astype(jnp.float32),
        lax.psum_scatter(
            dw_out.astype(jnp.bfloat16), ("narrow", "seq"), scatter_dimension=0, tiled=True
        ).astype(jnp.float32),
        lax.psum_scatter(
            dgain_ffn.astype(jnp.bfloat16), ("narrow", "seq"), scatter_dimension=0, tiled=True
        ).astype(jnp.float32),
        lax.psum_scatter(
            dw_gate.astype(jnp.bfloat16), ("narrow", "seq"), scatter_dimension=0, tiled=True
        ).astype(jnp.float32),
        lax.psum_scatter(
            dw_up.astype(jnp.bfloat16), ("narrow", "seq"), scatter_dimension=0, tiled=True
        ).astype(jnp.float32),
        lax.psum_scatter(
            dw_down.astype(jnp.bfloat16), ("narrow", "seq"), scatter_dimension=0, tiled=True
        ).astype(jnp.float32),
    )
    return (
        output,
        grad_input,
        summed_grads[0],
        summed_grads[1],
        summed_grads[2],
        summed_grads[3],
        summed_grads[4],
        summed_grads[5],
        summed_grads[6],
        summed_grads[7],
        summed_grads[8],
    )


def by_plane(
    tokens,
    gain_attn,
    w_query,
    w_key,
    w_value,
    w_out,
    gain_ffn,
    w_gate,
    w_up,
    w_down,
    lengths,
    cotangent,
):
    N, W, S = (lax.axis_size(a) for a in ("narrow", "wide", "seq"))
    n, s = lax.axis_index("narrow"), lax.axis_index("seq")
    P8, chips = N * W, N * W // 2
    RB, cols = tokens.shape
    R, D = N * RB, W * cols
    hd = w_key.shape[2]
    group = w_query.shape[2] // hd
    qw = group * hd
    rows, block = RB // W, D // (N * S)
    half_d, half_h = w_gate.shape[0], w_gate.shape[1] // N
    nseq = lengths.shape[0]
    chunk = RB // 2
    chunks = R // chunk
    fold = math.log2(math.e) / math.sqrt(hd)
    starts = jnp.cumsum(lengths) - lengths
    heads_shape, kv_shape, full_shape = (S, RB, N * hd), (S, R, 2 * hd), (R, D)
    slab_shape, own_shape = (N, S, block, half_h), (rows, D)

    def block_view(ref, chip, core):
        a, b = chip // (W // 2), lax.rem(chip, W // 2) * 2 + core
        return ref.at[pl.ds(a * RB, RB), pl.ds(b * cols, cols)]

    def row_view(ref, chip, core):
        return ref.at[chip * 2 + core]

    def to_seq():
        return Exchange(S, "seq", lambda src, j: src.at[j])

    def to_rows():
        return Exchange(N * S, "rows", lambda src, j: src.at[j])

    def to_narrow():
        return Exchange(N, "narrow", lambda src, j: src.at[j])

    def own_rows(at):
        return pl.ds(pl.multiple_of(at.n * RB + at.w * rows, rows), rows)

    def chunk_rows(c):
        k = c * chunk // RB
        return slice(c * chunk, (c + 1) * chunk), slice(c * chunk - k * RB, (c + 1) * chunk - k * RB), k

    def scale_of(x):
        return lax.rsqrt(jnp.mean(x * x, axis=1, keepdims=True) + NORM_EPSILON)

    w_mine = jnp.concatenate([w_query, w_key, w_value], axis=2).transpose(1, 0, 2)
    width = w_mine.shape[2]
    g_tok, g_w, g_wo = PlaneGather(chips, block_view), HeadGather(S), HeadGather(S)

    def start_body(at, ins, outs, scratch):
        g_w.start(at, ins[1], outs[1])
        g_wo.start(at, ins[2], outs[2])
        g_tok.start(at, ins[0], outs[0])
        g_w.relay()
        g_wo.relay()
        g_tok.finish()
        g_w.finish()
        g_wo.finish()

    full_in, w_qkv, w_o = fused(
        1,
        "gather_start",
        55,
        [g_tok, g_w, g_wo],
        start_body,
        [(tokens, HBM), (w_mine, HBM), (w_out.transpose(1, 0, 2), HBM)],
        [
            (full_shape, bf16, HBM),
            ((N * S,) + w_mine.shape[1:], bf16, HBM),
            ((N * S, block, qw), bf16, HBM),
        ],
    )
    w_qkv, w_o = w_qkv.reshape(D, width), w_o.reshape(D, qw)

    part_d = half_d // 2
    part_shape = (part_d, half_h)
    mine_w = [w_gate, w_up, w_down]
    n_idx = jnp.stack([n, lax.rem(s, 2)]).astype(jnp.int32)
    swaps = [Swap("narrow") for _ in mine_w]
    passes = [Swap("seq") for _ in mine_w]

    def for_partner(at, ref):
        rows_ = pl.ds(pl.multiple_of(lax.rem(at.s, 2) * part_d, part_d), part_d)
        return ref.at[rows_, pl.ds(pl.multiple_of((1 - at.n) * half_h, half_h), half_h)]

    row_ids = ((jnp.arange(N, dtype=jnp.int32) * S + s) * RB)[:, None] + jnp.arange(RB, dtype=jnp.int32)
    row_ids = row_ids.reshape(R)
    cos_table, sin_table = rotation(row_ids - seq_starts(lengths, row_ids), hd)
    cos_lanes = jnp.tile(cos_table, (1, 4))
    sin_lanes = jnp.tile(jnp.concatenate([-sin_table, sin_table], axis=1), (1, 2))

    e_q, e_kv, mv = to_seq(), Exchange(S, "seq", lambda src, j: src), Move()

    def qkv_body(at, ins, outs, scratch):
        x_ref, w_ref, gain_ref, cos_ref, sin_ref, *w_ins = ins
        q_out, kv_out, n1_out, *w_outs = outs
        n1, qs, kvs = scratch
        for sw, src, dst in zip(swaps, w_ins, w_outs):
            sw.start(at, for_partner(at, src), dst)
        lanes = lax.broadcasted_iota(jnp.int32, (1, 128), 1)
        for c in range(chunks):
            r, rb, k = chunk_rows(c)
            x = x_ref[r].astype(f32)
            normed = (x * scale_of(x) * gain_ref[...]).astype(bf16)
            n1[r] = normed
            qkv = dot(normed, w_ref[...], NN)
            cos, sin = cos_ref[r], sin_ref[r]
            for g in range(0, group, 2):
                y = qkv[:, g * hd : (g + 2) * hd]
                put_pair(qs, g, rb, k, (y * cos + half_swap(y) * sin) * fold)
            y = qkv[:, qw:]
            kvs[r] = jnp.where(lanes < hd, y * cos + half_swap(y) * sin, y).astype(bf16)
        e_kv.start(at, kvs, kv_out)
        e_q.start(at, qs, q_out)
        mv.start(at, n1, n1_out)
        e_kv.finish()
        e_q.finish()
        mv.finish()
        for sw in swaps[:2]:
            sw.finish()

    q_all, kv_all, normed1, near_gate, near_up = fused(
        2,
        "qkv_to_heads",
        60,
        [e_q, e_kv, mv] + swaps[:2],
        qkv_body,
        [
            (full_in, VMEM),
            (w_qkv, VMEM),
            (gain_attn[None], VMEM),
            (cos_lanes, VMEM),
            (sin_lanes, VMEM),
            (w_gate, HBM),
            (w_up, HBM),
        ],
        [(heads_shape, bf16, HBM), (kv_shape, bf16, HBM), (full_shape, bf16, HBM)] + [(part_shape, bf16, HBM)] * 2,
        [pltpu.VMEM(full_shape, bf16), pltpu.VMEM((group, RB, N * hd), bf16), pltpu.VMEM((R, 2 * hd), bf16)],
        40,
    )

    g_cot, st_o = PlaneGather(chips, block_view), Stream(S)

    def forward_body(at, ins, outs, scratch):
        cot_in, w_in, *attn_ins = ins
        grad_full, back, near, res = outs
        heads, *work = scratch
        g_cot.start(at, cot_in, grad_full)
        swaps[2].start(at, for_partner(at, w_in), near)

        def done(k, j):
            if k == N - 1:
                st_o.send(at, heads.at[j], back.at[at.s], j)

                @pl.when(j == S - 2)
                def _():
                    g_cot.relay()

        attn_fwd_body(S, RB, N, nseq, done, *attn_ins, heads, res, *work)
        st_o.finish(at, heads.at[0], back.at[at.s])
        g_cot.finish(True)
        swaps[2].finish()

    kv_scratch = pltpu.VMEM(kv_shape, bf16)
    grad_full, attn_back, near_down, attn_res = fused(
        8,
        "attn_fwd",
        48,
        [g_cot, st_o, swaps[2]],
        forward_body,
        [(cotangent, HBM), (w_down, HBM), (starts, SMEM), (q_all, VMEM), (kv_all, VMEM)],
        [
            (full_shape, bf16, HBM),
            (heads_shape, bf16, HBM),
            (part_shape, bf16, HBM),
            ((N * S, RB, 2 * hd), f32, VMEM),
        ],
        [pltpu.VMEM(heads_shape, bf16), kv_scratch, kv_scratch, pltpu.VMEM((RB, 2 * hd), f32)],
        48,
    )

    sc_a, g_n2, mv_x = PlaneScatter(chips, own_shape, row_view), PlaneGather(chips, row_view), Move()

    def mid_body(at, ins, outs, scratch):
        heads, wo, x_in, gain_ref, *w_ins = ins
        attn_b, resid, n2_out, *w_outs = outs
        part, xr, n2 = scratch
        for ps, src, dst in zip(passes, w_ins, w_outs):
            ps.start(at, src, dst)
        mv_x.start(at, x_in.at[own_rows(at)], xr)
        for k in range(N):
            for g in range(0, group, 2):
                pair = pair_up(heads[g], heads[g + 1], k).astype(bf16)
                attn_b[k * RB : (k + 1) * RB, g * hd : (g + 2) * hd] = pair
        for c in range(chunks):
            r = slice(c * chunk, (c + 1) * chunk)
            b = c * chunk // rows
            out = dot(attn_b[r], wo[...], NT).astype(bf16)
            part[b : b + chunk // rows] = out.reshape(chunk // rows, rows, D)
        sc_a.start(at, part)
        sc_a.mid()
        mv_x.finish()
        h = xr[...].astype(f32) + sc_a.finish()
        resid[...] = h
        n2[...] = (h * scale_of(h) * gain_ref[...]).astype(bf16)
        g_n2.start(at, n2, n2_out)
        g_n2.finish()
        for ps in passes:
            ps.finish()

    attn_b, residual, normed2, *far_w = fused(
        3,
        "attn_to_ffn",
        88,
        [sc_a, g_n2, mv_x] + passes,
        mid_body,
        [
            (attn_back, VMEM),
            (w_o, VMEM),
            (full_in, HBM),
            (gain_ffn[None], VMEM),
            (near_gate, HBM),
            (near_up, HBM),
            (near_down, HBM),
        ],
        [
            ((R, qw), bf16, VMEM),
            (own_shape, f32, VMEM),
            ((P8,) + own_shape, bf16, HBM),
        ]
        + [(part_shape, bf16, HBM)] * 3,
        [
            pltpu.VMEM((P8,) + own_shape, bf16),
            pltpu.VMEM(own_shape, bf16),
            pltpu.VMEM(own_shape, bf16),
        ],
        48,
    )
    normed2 = normed2.reshape(full_shape)
    got_w = list(zip((near_gate, near_up, near_down), far_w))

    hidden, grad_gate_val, grad_up_val = hidden_units(n_idx, normed2, grad_full, mine_w, got_w)
    dn2_part = hidden_back(n_idx, grad_gate_val, grad_up_val, mine_w[:2], got_w[:2])

    slab_block = (N, block, half_h)

    def seq_sum():
        return SeqSum(slab_block, lambda src, j: src.at[:, j])

    sc_n, g_db, q_down = PlaneScatter(chips, own_shape, row_view), PlaneGather(chips, row_view), seq_sum()
    mvs = [Move() for _ in range(7)]

    def tile_cols(a, j):
        return pl.ds(pl.multiple_of((a * S + j) * block, block), block)

    def ffn_body(at, ins, outs, scratch):
        part_in, dy_in, m_in, n2_in, dg_in, dp_in, resid, gain_ref = ins
        db_out, dresid, dgain, down_out, gate_out, up_out = outs
        dy, m, n2, dg, dp, down, gate, up, db = scratch
        for mv_, src, dst in zip(mvs, (m_in, dy_in, n2_in, dg_in, dp_in), (m, dy, n2, dg, dp)):
            mv_.start(at, src, dst)
        sc_n.start(at, part_in)
        q_down.begin(at, down)
        mvs[0].finish()
        mvs[1].finish()

        def down_block(i):
            j = q_down.order(at)[i]
            for a in range(N):
                down[a, j] = dot(dy[:, tile_cols(a, j)], m[...], TN).astype(bf16)
            q_down.ready(at, i)

        down_block(0)
        down_block(1)
        sc_n.mid()
        down_block(2)
        down_block(3)
        for mv_ in mvs[2:5]:
            mv_.finish()

        def other_tiles(j, _):
            for a in range(N):
                c = tile_cols(a, j)
                gate[a, j] = dot(n2[:, c], dg[...], TN).astype(bf16)
                up[a, j] = dot(n2[:, c], dp[...], TN).astype(bf16)
            return 0

        lax.fori_loop(0, 2, other_tiles, 0)
        q_down.step(at, 0)
        lax.fori_loop(2, S, other_tiles, 0)
        mvs[5].start(at, gate, gate_out)
        mvs[6].start(at, up, up_out)
        dn2 = sc_n.finish()
        h = resid[...]
        r2 = scale_of(h)
        dgain[...] = jnp.sum(dn2 * h * r2, axis=0, keepdims=True)
        scaled = dn2 * gain_ref[...]
        own = dy[own_rows(at)].astype(f32)
        grad = own + r2 * scaled - h * (r2 * r2 * r2) * jnp.mean(scaled * h, axis=1, keepdims=True)
        dresid[...] = grad
        db[...] = grad.astype(bf16)
        g_db.start(at, db, db_out)
        q_down.step(at, 1)
        q_down.step3(at)
        g_db.relay()
        g_db.finish(True)
        down_out[...] = q_down.total(at).astype(bf16)
        mvs[5].finish()
        mvs[6].finish()

    dbranch, dresid, dgain_ffn, down_own, dw_gate, dw_up = fused(
        4,
        "ffn_grads",
        110,
        [sc_n, g_db, q_down] + mvs,
        ffn_body,
        [
            (dn2_part.reshape((P8,) + own_shape), HBM),
            (grad_full, HBM),
            (hidden, HBM),
            (normed2, HBM),
            (grad_gate_val, HBM),
            (grad_up_val, HBM),
            (residual, VMEM),
            (gain_ffn[None], VMEM),
        ],
        [
            ((P8,) + own_shape, bf16, HBM),
            (own_shape, f32, VMEM),
            ((1, D), f32, VMEM),
            (slab_block, bf16, VMEM),
            (slab_shape, bf16, HBM),
            (slab_shape, bf16, HBM),
        ],
        [
            pltpu.VMEM(full_shape, bf16),
            pltpu.VMEM((R, half_h), bf16),
            pltpu.VMEM(full_shape, bf16),
            pltpu.VMEM((R, half_h), bf16),
            pltpu.VMEM((R, half_h), bf16),
            pltpu.VMEM(slab_shape, bf16),
            pltpu.VMEM(slab_shape, bf16),
            pltpu.VMEM(slab_shape, bf16),
            pltpu.VMEM(own_shape, bf16),
        ],
        60,
    )

    e_do, t_down = to_seq(), to_narrow()
    mvt = [Move() for _ in range(7)]
    tile = half_d // 4

    def grad_heads_body(at, ins, outs, scratch):
        db_in, w_ref, ab, down_in, m_in, wd_in, wd1_in, wd2_in, resid = ins
        do_out, dwo_out, y_out, down_out = outs
        db, dos, m, wd, y, dwo = scratch
        mine = wd_in.at[:, pl.ds(pl.multiple_of(at.n * half_h, half_h), half_h)]
        at_odd = lax.rem(at.s, 2)
        first = wd.at[1 - at.n, pl.ds(pl.multiple_of(at_odd * part_d, part_d), part_d)]
        second = wd.at[1 - at.n, pl.ds(pl.multiple_of((1 - at_odd) * part_d, part_d), part_d)]
        moves = [(db_in, db), (m_in, m), (mine, wd.at[at.n]), (wd1_in, first), (wd2_in, second)]
        for mv_, (src, dst) in zip(mvt, moves):
            mv_.start(at, src, dst)
        mvt[0].finish()
        for c in range(chunks):
            r, rb, k = chunk_rows(c)
            out = dot(db[r], w_ref[...], NN)
            for g in range(0, group, 2):
                put_pair(dos, g, rb, k, out[:, g * hd : (g + 2) * hd])
        e_do.start(at, dos, do_out)
        t_down.start(at, down_in, down_out)

        def wo_tile(p, _):
            c = pl.ds(pl.multiple_of(p * block, block), block)
            dwo[p] = dot(db[:, c], ab[...], TN).astype(bf16)
            return 0

        lax.fori_loop(0, N * S, wo_tile, 0)
        mvt[5].start(at, dwo, dwo_out)
        for mv_ in mvt[1:5]:
            mv_.finish()
        for a in range(N):

            def y_tile(i, _):
                c = pl.ds(pl.multiple_of(a * half_d + i * tile, tile), tile)
                w_tile = wd[a, pl.ds(pl.multiple_of(i * tile, tile), tile), :]
                y[:, c] = dot(m[...], w_tile, NT).astype(bf16)
                return 0

            lax.fori_loop(0, half_d // tile, y_tile, 0)
        o = own_rows(at)
        y[o] = (y[o].astype(f32) + resid[...]).astype(bf16)
        mvt[6].start(at, y, y_out)
        e_do.finish()
        t_down.finish()
        mvt[5].finish()
        mvt[6].finish()

    do_all, dw_o, down_part, down_grad = fused(
        5,
        "grad_to_heads",
        25,
        [e_do, t_down] + mvt,
        grad_heads_body,
        [
            (dbranch.reshape(full_shape), HBM),
            (w_o, VMEM),
            (attn_b, VMEM),
            (down_own, HBM),
            (hidden, HBM),
            (w_down, HBM),
            (got_w[2][0], HBM),
            (got_w[2][1], HBM),
            (residual, VMEM),
        ],
        [
            (heads_shape, bf16, HBM),
            ((N * S, block, qw), bf16, HBM),
            (full_shape, bf16, HBM),
            ((N, block, half_h), bf16, HBM),
        ],
        [
            pltpu.VMEM(full_shape, bf16),
            pltpu.VMEM((group, RB, N * hd), bf16),
            pltpu.VMEM((R, half_h), bf16),
            pltpu.VMEM((N, half_d, half_h), bf16),
            pltpu.VMEM(full_shape, bf16),
            pltpu.VMEM((N * S, block, qw), bf16),
        ],
        56,
    )

    q_gate, sc_y, st_q = seq_sum(), PlaneScatter(chips, (RB, cols), block_view), Stream(S)
    st_kv = [Stream(S) for _ in range(N)]

    def backward_body(at, ins, outs, scratch):
        gate_in, y_in, *attn_ins = ins
        gate_out, out_ref, dq_all, dkv_all = outs
        dq, dkv, *work = scratch
        sc_y.start(at, y_in)
        q_gate.start(at, gate_in)

        def pieces(k):
            r = pl.ds(k * RB, RB)
            return (lambda j: dkv.at[j, r]), dkv_all.at[at.s, r]

        def done(k, j):
            src, dst = pieces(k)
            st_kv[k].send(at, src(j), dst, j)
            if k == N - 1:
                st_q.send(at, dq.at[j], dq_all.at[at.s], j)
            hooks = {0: sc_y.mid, 1: lambda: q_gate.step(at, 0), 3: lambda: q_gate.step(at, 1)}
            if k == N - 1:
                hooks = {0: lambda: q_gate.step3(at)}
            for i, hook in hooks.items():
                pl.when(j == i)(hook)

        attn_bwd_body(S, RB, N, nseq, done, *attn_ins, dq, dkv, *work)
        out_ref[...] = sc_y.finish().astype(bf16)
        gate_out[...] = q_gate.total(at).astype(bf16)
        for k in range(N):
            src, dst = pieces(k)
            st_kv[k].finish(at, src(0), dst)
        st_q.finish(at, dq.at[0], dq_all.at[at.s])

    q_scratch, acc_scratch = pltpu.VMEM((N * S, RB, 2 * hd), bf16), pltpu.VMEM((RB, 2 * hd), f32)
    gate_own, output, dq_all, dkv_all = fused(
        6,
        "attn_bwd",
        110,
        [q_gate, sc_y, st_q] + st_kv,
        backward_body,
        [
            (dw_gate, HBM),
            (down_part, HBM),
            (starts, SMEM),
            (q_all, VMEM),
            (kv_all, VMEM),
            (do_all, VMEM),
            (attn_res, VMEM),
        ],
        [
            (slab_block, bf16, VMEM),
            ((RB, cols), bf16, VMEM),
            (heads_shape, bf16, HBM),
            (kv_shape, bf16, HBM),
        ],
        [
            pltpu.VMEM(heads_shape, bf16),
            kv_scratch,
            kv_scratch,
            kv_scratch,
            q_scratch,
            q_scratch,
            pltpu.VMEM((N * S, RB, 2 * hd), f32),
            acc_scratch,
            acc_scratch,
        ],
        60,
    )

    q_up, t_gate, t_up, e_wog, e_wq = seq_sum(), to_narrow(), to_narrow(), to_rows(), to_rows()
    sc_1 = PlaneScatter(chips, own_shape, row_view)
    e_in = Exchange(W, "wide", lambda src, j: src.at[:, pl.ds(pl.multiple_of(j * cols, cols), cols)])
    e_gain = Exchange(N * S * W, "all", lambda src, j: src.at[j // W])
    mvu = [Move() for _ in range(2)]

    def last_body(at, ins, outs, scratch):
        dq, dkv, gate_in, dwo_in, n1_in, up_in, x_in, w_ref, cos_ref, sin_ref, dresid_ref, gain_ref, dgain_ref = ins
        gi_out, gains_out, up_out, got_wq, got_wo, gate_out = outs
        n1, dqkv, part, dwq, xr, gi, gains, up_own = scratch
        q_up.start(at, up_in)
        mvu[0].start(at, n1_in, n1)
        mvu[1].start(at, x_in.at[own_rows(at)], xr)
        t_gate.start(at, gate_in, gate_out)
        lanes = lax.broadcasted_iota(jnp.int32, (1, 128), 1)
        for c in range(chunks):
            r, rb, k = chunk_rows(c)
            cos, sin = cos_ref[r], sin_ref[r]
            for g in range(0, group, 2):
                y = pair_up(dq[g, rb], dq[g + 1, rb], k)
                dqkv[r, g * hd : (g + 2) * hd] = (y * cos - half_swap(y) * sin).astype(bf16)
            y = sum(dkv[i, r].astype(f32) for i in range(S))
            dqkv[r, qw:] = jnp.where(lanes < hd, y * cos - half_swap(y) * sin, y).astype(bf16)
            out = dot(dqkv[r], w_ref[...], NT).astype(bf16)
            b = c * chunk // rows
            part[b : b + chunk // rows] = out.reshape(chunk // rows, rows, D)
        sc_1.start(at, part)
        mvu[0].finish()

        def wq_tile(p, _):
            c = pl.ds(pl.multiple_of(p * block, block), block)
            dwq[p] = dot(n1[:, c], dqkv[...], TN).astype(bf16)
            return 0

        lax.fori_loop(0, N * S, wq_tile, 0)
        sc_1.mid()
        q_up.step(at, 0)
        e_wq.start(at, dwq, got_wq)
        e_wog.start(at, dwo_in, got_wo)
        mvu[1].finish()
        x = xr[...].astype(f32)
        r1 = scale_of(x)
        dn1 = sc_1.finish()
        dgain = jnp.sum(dn1 * x * r1, axis=0, keepdims=True)
        dgain2 = dgain_ref[...]
        for p in range(N * S):
            for i in range(block // 128):
                c = slice(p * block + i * 128, p * block + (i + 1) * 128)
                gains[p, i : i + 1, :] = dgain[:, c]
                gains[p, block // 128 + i : block // 128 + i + 1, :] = dgain2[:, c]
        e_gain.start(at, gains, gains_out)
        scaled = dn1 * gain_ref[...]
        grad = dresid_ref[...] + r1 * scaled - x * (r1 * r1 * r1) * jnp.mean(scaled * x, axis=1, keepdims=True)
        gi[...] = grad.astype(bf16)
        e_in.start(at, gi, gi_out)
        q_up.step(at, 1)
        q_up.step3(at)
        for p in (e_in, e_gain, t_gate):
            p.finish()
        up_own[...] = q_up.total(at).astype(bf16)
        t_up.start(at, up_own, up_out)
        for p in (t_up, e_wq, e_wog):
            p.finish()

    gains_shape = (N * S, 2 * block // 128, 128)
    grad_input, gains, up_grad, got_wq, got_wo, gate_grad = fused(
        7,
        "last",
        160,
        [q_up, t_gate, t_up, e_wog, e_wq, sc_1, e_in, e_gain] + mvu,
        last_body,
        [
            (dq_all, VMEM),
            (dkv_all, VMEM),
            (gate_own, HBM),
            (dw_o, HBM),
            (normed1, HBM),
            (dw_up, HBM),
            (full_in, HBM),
            (w_qkv, VMEM),
            (cos_lanes, VMEM),
            (sin_lanes, VMEM),
            (dresid, VMEM),
            (gain_attn[None], VMEM),
            (dgain_ffn, VMEM),
        ],
        [
            ((W, rows, cols), bf16, HBM),
            ((N * S * W,) + gains_shape[1:], f32, HBM),
            (slab_block, bf16, HBM),
            ((N * S, block, width), bf16, HBM),
            ((N * S, block, qw), bf16, HBM),
            (slab_block, bf16, HBM),
        ],
        [
            pltpu.VMEM(full_shape, bf16),
            pltpu.VMEM((R, width), bf16),
            pltpu.VMEM((P8,) + own_shape, bf16),
            pltpu.VMEM((N * S, block, width), bf16),
            pltpu.VMEM(own_shape, bf16),
            pltpu.VMEM(own_shape, bf16),
            pltpu.VMEM(gains_shape, f32),
            pltpu.VMEM(slab_block, bf16),
        ],
        60,
    )

    def over_seq(got):
        return jnp.sum(got.reshape(N, S, *got.shape[1:]).astype(f32), axis=1)

    def side_by_side(halves):
        return jnp.concatenate(list(halves), axis=1).astype(f32)

    gains = jnp.sum(gains, axis=0).reshape(2, block)
    qkv_grads = over_seq(got_wq).transpose(1, 0, 2)
    return (
        output,
        grad_input.reshape(RB, cols),
        gains[0],
        qkv_grads[:, :, :qw],
        qkv_grads[:, :, qw : qw + hd],
        qkv_grads[:, :, qw + hd :],
        over_seq(got_wo).transpose(1, 0, 2),
        gains[1],
        side_by_side(gate_grad),
        side_by_side(up_grad),
        side_by_side(down_grad),
    )


def local(tokens, gain_attn, w_query, w_key, *others):
    plane = lax.axis_size("narrow") * lax.axis_size("wide")
    heads_kv = w_key.shape[1] * lax.axis_size("wide")
    group = w_query.shape[2] // w_key.shape[2]
    fits = lax.axis_size("narrow") == 2 and heads_kv == plane and group == lax.axis_size("seq")
    body = by_plane if fits and w_key.shape[2] == 64 else by_rows
    return body(tokens, gain_attn, w_query, w_key, *others)


def solution(mesh):
    return jax.shard_map(
        local,
        mesh=mesh,
        in_specs=(
            P(("narrow", "seq"), "wide"),
            P(),
            P(("narrow", "seq"), "wide", None),
            P(("narrow", "seq"), "wide", None),
            P(("narrow", "seq"), "wide", None),
            P(("narrow", "seq"), "wide", None),
            P(),
            P("narrow", "wide"),
            P("narrow", "wide"),
            P("narrow", "wide"),
            P(),
            P(("narrow", "seq"), "wide"),
        ),
        out_specs=(
            P(("narrow", "seq"), "wide"),
            P(("narrow", "seq"), "wide"),
            P(("narrow", "seq")),
            P(("narrow", "seq"), "wide", None),
            P(("narrow", "seq"), "wide", None),
            P(("narrow", "seq"), "wide", None),
            P(("narrow", "seq"), "wide", None),
            P(("narrow", "seq")),
            P(("narrow", "seq"), "wide"),
            P(("narrow", "seq"), "wide"),
            P(("narrow", "seq"), "wide"),
        ),
        check_vma=False,
    )
```

```python
import functools
import math

import jax
import jax.numpy as jnp
from jax import lax
from jax.experimental import pallas as pl
from jax.experimental.pallas import tpu as pltpu
from jax.sharding import PartitionSpec as P

f32 = jnp.float32
bf16 = jnp.bfloat16
MESH = pl.DeviceIdType.MESH
NT = (((1,), (1,)), ((), ()))
NN = (((1,), (0,)), ((), ()))
TN = (((0,), (0,)), ((), ()))

ROPE_THETA = 500000.0
ROPE_FACTOR = 32.0
LOW_FACTOR = 1.0
HIGH_FACTOR = 4.0
OLD_CONTEXT = 8192.0
NORM_EPSILON = 1e-05


def frequencies(head_dim):
    freq_index = jnp.arange(head_dim // 2, dtype=jnp.float32)
    base_freq = jnp.exp(freq_index * (-2.0 * math.log(ROPE_THETA) / head_dim))
    wavelen = 2.0 * math.pi / base_freq
    smooth = jnp.clip((OLD_CONTEXT / wavelen - LOW_FACTOR) / (HIGH_FACTOR - LOW_FACTOR), 0.0, 1.0)
    return (1.0 - smooth) * base_freq / ROPE_FACTOR + smooth * base_freq


def seq_starts(lengths, row_ids):
    seq_ends = jnp.cumsum(lengths)
    begins = seq_ends - lengths
    found_at = jnp.where(begins[None, :] <= row_ids[:, None], begins[None, :], 0)
    return jnp.max(found_at, axis=1)


def rotation(positions, head_dim):
    angles = positions.astype(jnp.float32)[:, None] * frequencies(head_dim)[None, :]
    return (jnp.cos(angles), jnp.sin(angles))


def table_shape(values, cos_table, sin_table):
    half_dim = values.shape[-1] // 2
    bcast_shape = (cos_table.shape[0],) + (1,) * (values.ndim - 2) + (half_dim,)
    return (half_dim, cos_table.reshape(bcast_shape), sin_table.reshape(bcast_shape))


def rotate(values, cos_table, sin_table):
    half_dim, cos_part, sin_part = table_shape(values, cos_table, sin_table)
    first_half = values[..., :half_dim]
    second = values[..., half_dim:]
    return jnp.concatenate(
        [first_half * cos_part - second * sin_part, second * cos_part + first_half * sin_part],
        axis=-1,
    )


def unrotate(grad_vals, cos_table, sin_table):
    half_dim, cos_part, sin_part = table_shape(grad_vals, cos_table, sin_table)
    first_half = grad_vals[..., :half_dim]
    second = grad_vals[..., half_dim:]
    return jnp.concatenate(
        [first_half * cos_part + second * sin_part, second * cos_part - first_half * sin_part],
        axis=-1,
    )


def over_blocks(block_fn, state_now, kv_piece, block_len, lowest, highest):
    piece_rows = kv_piece.shape[0]
    block_count = piece_rows // block_len

    def one_step(block_no, state_in):
        begin = block_no * block_len
        kv_part = lax.dynamic_slice_in_dim(kv_piece, block_no * block_len, block_len, 0)
        live = (begin <= highest) & (begin + block_len - 1 >= lowest)

        def compute(carried):
            return block_fn(carried, kv_part, begin)

        def skipped(carried):
            return carried

        return lax.cond(live, compute, skipped, state_in)

    return lax.fori_loop(0, block_count, one_step, state_now)


def dot(a, b, dims):
    return lax.dot_general(a, b, dims, preferred_element_type=f32)


class Place:
    def __init__(self):
        self.N, self.W, self.S = (lax.axis_size(a) for a in ("narrow", "wide", "seq"))
        self.n, self.w, self.s = (lax.axis_index(a) for a in ("narrow", "wide", "seq"))
        self.X = self.W // 2
        self.core = lax.rem(self.w, 2)
        x = self.w // 2
        self.chip, self.chip_x = self.n * self.X + x, self.n * self.X + 1 - x
        self.chip_y, self.chip_xy = (1 - self.n) * self.X + x, (1 - self.n) * self.X + 1 - x
        self.sibling = {"wide": 2 * x + 1 - self.core}
        self.near_x, self.near_y = {"wide": 2 * (1 - x) + self.core}, {"narrow": 1 - self.n}


def remote(src, dst, ss, rs, device):
    return pltpu.make_async_remote_copy(
        src_ref=src, dst_ref=dst, send_sem=ss, recv_sem=rs, device_id=device, device_id_type=MESH
    )


class Move:
    scratch = [pltpu.SemaphoreType.DMA]

    def peers(self, at):
        return []

    def start(self, at, src, dst):
        self.copy = pltpu.make_async_copy(src, dst, self.bufs[0])
        self.copy.start()

    def finish(self):
        self.copy.wait()


class PlaneGather:
    def __init__(self, view):
        self.view = view
        self.scratch = [pltpu.SemaphoreType.DMA((4,))] * 2 + [pltpu.SemaphoreType.DMA((5,))] * 2
        self.scratch += [pltpu.SemaphoreType.DMA]
        self.stage = 0

    def peers(self, at):
        return [at.near_x, at.near_y, at.sibling]

    def half(self, block, h):
        m = block.shape[0] // 2
        return block.at[pl.ds(h * m, m)]

    def start(self, at, src, dst):
        ss, rs, fs, fr, ls = self.bufs
        own = self.view(dst, at.chip, at.core)
        from_x, from_y, across = (self.view(dst, i, at.core) for i in (at.chip_x, at.chip_y, at.chip_xy))
        self.local = pltpu.make_async_copy(src, own, ls)
        sent = [(src, own, at.near_x), (src, own, at.near_y)]
        sent += [(self.half(from_x, 0), self.half(from_x, 0), at.near_y)]
        sent += [(self.half(from_y, 1), self.half(from_y, 1), at.near_x)]
        self.far = [remote(x, y, ss.at[i], rs.at[i], d) for i, (x, y, d) in enumerate(sent)]
        shared = [src, from_x, from_y, self.half(across, 0), self.half(across, 1)]
        kept = [own] + shared[1:]
        self.near = [remote(x, y, fs.at[i], fr.at[i], at.sibling) for i, (x, y) in enumerate(zip(shared, kept))]
        for copy in (*self.far[:2], self.near[0], self.local):
            copy.start()

    def relay(self):
        for i in range(2):
            self.far[i].wait_recv()
            self.far[2 + i].start()
            self.near[1 + i].start()

    def relay2(self):
        for i in range(2, 4):
            self.far[i].wait_recv()
            self.near[1 + i].start()

    def finish(self):
        self.local.wait()
        for c in self.far:
            c.wait_send()
        for c in self.near:
            c.wait()


class Exchange:
    def __init__(self, count, group, pick):
        self.count, self.group, self.pick = count, group, pick
        self.scratch = [pltpu.SemaphoreType.DMA((count,))] * 2 + [pltpu.SemaphoreType.DMA]

    def device(self, at, k):
        if self.group == "rows":
            p = lax.rem(at.n * at.S + at.s + k, at.N * at.S)
            return p, {"narrow": p // at.S, "seq": lax.rem(p, at.S)}
        if self.group == "all":
            j = lax.rem((at.n * at.S + at.s) * at.W + at.w + k, at.N * at.S * at.W)
            p = j // at.W
            return j, {"narrow": p // at.S, "seq": lax.rem(p, at.S), "wide": lax.rem(j, at.W)}
        me = {"seq": at.s, "narrow": at.n, "wide": at.w}[self.group]
        j = lax.rem(me + k, self.count)
        return j, {self.group: j}

    def peers(self, at):
        return [self.device(at, k)[1] for k in range(1, self.count)]

    def begin(self, at, src, dst):
        ss, rs, ls = self.bufs
        me = self.device(at, 0)[0]
        self.copies = [pltpu.make_async_copy(self.pick(src, me), dst.at[me], ls)]
        for k in range(1, self.count):
            j, d = self.device(at, k)
            self.copies.append(remote(self.pick(src, j), dst.at[me], ss.at[k], rs.at[k], d))

    def start(self, at, src, dst):
        self.begin(at, src, dst)
        for c in self.copies[1:] + self.copies[:1]:
            c.start()

    def finish(self):
        for c in self.copies:
            c.wait()


class Stream:
    def __init__(self, S):
        self.scratch = [pltpu.SemaphoreType.DMA((S,))] * 2 + [pltpu.SemaphoreType.DMA]

    def peers(self, at):
        return [{"seq": lax.rem(at.s + k, at.S)} for k in range(1, at.S)]

    def away(self, at, src, dst, j):
        ss, rs, _ = self.bufs
        k = lax.rem(j - at.s + at.S, at.S)
        return remote(src, dst, ss.at[k], rs.at[k], {"seq": j})

    def send(self, at, src, dst, j):
        @pl.when(j == at.s)
        def _():
            pltpu.make_async_copy(src, dst, self.bufs[2]).start()

        @pl.when(j != at.s)
        def _():
            self.away(at, src, dst, j).start()

    def finish(self, at, src, dst):
        pltpu.make_async_copy(src, dst, self.bufs[2]).wait()
        for k in range(1, at.S):
            self.away(at, src, dst, lax.rem(at.s + k, at.S)).wait()


class SeqSum:
    def __init__(self, block, pick):
        self.pick = pick
        self.scratch = [pltpu.VMEM((8,) + block, bf16)] + [pltpu.SemaphoreType.DMA((6,))] * 2
        self.scratch += [pltpu.SemaphoreType.DMA((3,))]

    def peers(self, at):
        return [{"seq": at.s + 1 - 2 * lax.rem(at.s, 2)}, {"seq": 3 - at.s}]

    def order(self, at):
        low = at.s < 2
        return jnp.where(low, 3, 0), jnp.where(low, 2, 1), at.s + 1 - 2 * lax.rem(at.s, 2), at.s

    def copy(self, at, i):
        buf, ss, rs, _ = self.bufs
        far_outer, far_inner, pair, _ = self.order(at)
        src, slot, sem, to = {
            0: (self.pick(self.src, far_outer), 0, 0, pair),
            1: (self.pick(self.src, far_inner), 1, 1, pair),
            2: (self.pick(self.src, pair), 2, 2, pair),
            3: (buf.at[5], 4, 3, 3 - at.s),
            4: (buf.at[6], 3, 4, 3 - at.s),
            5: (buf.at[4], 3, 4, pair),
        }[i]
        return remote(src, buf.at[slot], ss.at[i], rs.at[sem], {"seq": to})

    def inner(self, at):
        return (at.s == 1) | (at.s == 2)

    def load(self, at, i):
        far_outer, far_inner, _, own = self.order(at)
        j = (far_outer, far_inner, own)[i]
        return pltpu.make_async_copy(self.pick(self.src, j), self.bufs[0].at[5 + i], self.bufs[3].at[i])

    def begin(self, at, src):
        self.src = src

    def ready(self, at, i):
        inner = self.inner(at)
        if i == 0:

            @pl.when(jnp.logical_not(inner))
            def _():
                self.copy(at, 0).start()

        if i == 2:

            @pl.when(inner)
            def _():
                self.copy(at, 2).start()

        if i < 2:

            @pl.when(inner)
            def _():
                self.load(at, i).start()

        if i == 3:
            self.load(at, 2).start()

    def start(self, at, src):
        self.begin(at, src)
        for i in range(4):
            self.ready(at, i)

    def cross(self, at, i):
        buf = self.bufs[0]
        self.copy(at, i).wait_recv()
        self.load(at, i).wait()
        buf[5 + i] = (buf[5 + i].astype(f32) + buf[i].astype(f32)).astype(bf16)
        self.copy(at, 3 + i).start()

    def step(self, at, i):
        @pl.when(self.inner(at))
        def _():
            self.cross(at, i)

        @pl.when(jnp.logical_not(self.inner(at)))
        def _():
            self.copy(at, i).wait_send()
            self.copy(at, i + 1).start()

    def step3(self, at):
        @pl.when(self.inner(at))
        def _():
            self.copy(at, 3).wait_recv()
            self.copy(at, 5).start()

    def total(self, at):
        inner = self.inner(at)
        buf = self.bufs[0]
        self.load(at, 2).wait()
        self.copy(at, 2).wait()
        self.copy(at, 4).wait_recv()

        @pl.when(inner)
        def _():
            for i in (3, 4, 5):
                self.copy(at, i).wait_send()

        return buf[7].astype(f32) + buf[2].astype(f32) + buf[3].astype(f32)


class Swap:
    scratch = [pltpu.SemaphoreType.DMA] * 2

    def __init__(self, axis):
        self.axis = axis

    def partner(self, at):
        return {"narrow": 1 - at.n} if self.axis == "narrow" else {"seq": at.s + 1 - 2 * lax.rem(at.s, 2)}

    def peers(self, at):
        return [self.partner(at)]

    def start(self, at, src, dst):
        self.copy = remote(src, dst, *self.bufs, self.partner(at))
        self.copy.start()

    def finish(self):
        self.copy.wait()


class HeadGather:
    def __init__(self, S):
        self.scratch = [pltpu.SemaphoreType.DMA((S,))] * 4 + [pltpu.SemaphoreType.DMA]

    def peers(self, at):
        return [{"seq": lax.rem(at.s + k, at.S)} for k in range(1, at.S)] + [{"narrow": 1 - at.n}]

    def start(self, at, src, dst):
        ss, rs, fs, fr, ls = self.bufs
        own, other = dst.at[at.n * at.S + at.s], dst.at[(1 - at.n) * at.S + at.s]
        self.cross = remote(src.at[1 - at.n], own, ss.at[0], rs.at[0], {"narrow": 1 - at.n})
        self.cross.start()
        self.direct, self.relayed = [], []
        for k in range(1, at.S):
            to = {"seq": lax.rem(at.s + k, at.S)}
            self.direct.append(remote(src.at[at.n], own, ss.at[k], rs.at[k], to))
            self.direct[-1].start()
            self.relayed.append(remote(other, other, fs.at[k], fr.at[k], to))
        self.local = pltpu.make_async_copy(src.at[at.n], own, ls)
        self.local.start()

    def relay(self):
        self.cross.wait_recv()
        for c in self.relayed:
            c.start()

    def finish(self):
        self.cross.wait_send()
        for c in self.direct + self.relayed + [self.local]:
            c.wait()


class PlaneScatter:
    def __init__(self, block, view):
        self.view = view
        half = (block[0] // 2,) + block[1:]
        self.scratch = [pltpu.VMEM((4,) + block, bf16)] * 2 + [pltpu.VMEM((6,) + half, bf16)]
        self.scratch += [pltpu.SemaphoreType.DMA((4,))] * 3 + [pltpu.SemaphoreType.DMA((6,))] * 2

    def peers(self, at):
        return [at.near_x, at.near_y, at.sibling]

    def start(self, at, src):
        mine, sib, got, ls, ns, nr, ss, rs = self.bufs
        m = mine.shape[1] // 2
        self.local, self.near = [], []
        for i, chip in enumerate((at.chip_xy, at.chip_x, at.chip_y, at.chip)):
            self.near.append(remote(self.view(src, chip, 1 - at.core), sib.at[i], ns.at[i], nr.at[i], at.sibling))
            self.near[i].start()
            self.local.append(pltpu.make_async_copy(self.view(src, chip, at.core), mine.at[i], ls.at[i]))
            self.local[i].start()
        sent = [(0, 0, at.near_x), (0, 1, at.near_y), (1, 0, at.near_x), (2, 1, at.near_y)]
        sent += [(1, 1, at.near_x), (2, 0, at.near_y)]
        self.far = [
            remote(mine.at[i, pl.ds(h * m, m)], got.at[j], ss.at[j], rs.at[j], d) for j, (i, h, d) in enumerate(sent)
        ]

    def add(self, i):
        mine, sib = self.bufs[:2]
        self.local[i].wait()
        self.near[i].wait()
        mine[i] = (mine[i].astype(f32) + sib[i].astype(f32)).astype(bf16)

    def mid(self):
        self.add(0)
        self.far[0].start()
        self.far[1].start()
        self.add(1)
        self.far[2].start()
        self.add(2)
        self.far[3].start()

    def mid2(self):
        mine, _, got = self.bufs[:3]
        m = mine.shape[1] // 2
        self.far[1].wait_recv()
        mine[1, m:] = (mine[1, m:].astype(f32) + got[1].astype(f32)).astype(bf16)
        self.far[4].start()
        self.far[0].wait_recv()
        mine[2, :m] = (mine[2, :m].astype(f32) + got[0].astype(f32)).astype(bf16)
        self.far[5].start()

    def finish(self):
        mine, sib, got = self.bufs[:3]
        self.local[3].wait()
        self.near[3].wait()
        total = mine[3].astype(f32) + sib[3].astype(f32)
        for i in range(2, 6):
            self.far[i].wait_recv()
        for c in self.far:
            c.wait_send()
        low = got[2].astype(f32) + got[5].astype(f32)
        high = got[3].astype(f32) + got[4].astype(f32)
        return total + jnp.concatenate([low, high], axis=0)


def greet(ids):
    barrier = pltpu.get_barrier_semaphore()
    for d in ids:
        pl.semaphore_signal(barrier, inc=1, device_id=d, device_id_type=MESH)
    pl.semaphore_wait(barrier, len(ids))


HBM = pl.BlockSpec(memory_space=pl.ANY)
VMEM = pl.BlockSpec(memory_space=pltpu.VMEM)
SMEM = pl.BlockSpec(memory_space=pltpu.SMEM)


def fused(cid, name, us, parts, body, ins, outs, scratch=(), vmem=16):
    def kernel(*refs):
        a, refs = refs[: len(ins)], refs[len(ins) :]
        b, refs = refs[: len(outs)], refs[len(outs) :]
        c, refs = refs[: len(scratch)], refs[len(scratch) :]
        for p in parts:
            p.bufs, refs = refs[: len(p.scratch)], refs[len(p.scratch) :]
        at = Place()
        greet([d for p in parts for d in p.peers(at)])
        body(at, a, b, c)

    return pl.pallas_call(
        kernel,
        out_shape=tuple(jax.ShapeDtypeStruct(s, t) for s, t, _ in outs),
        in_specs=[spec for _, spec in ins],
        out_specs=tuple(spec for _, _, spec in outs),
        scratch_shapes=list(scratch) + [s for p in parts for s in p.scratch],
        compiler_params=pltpu.CompilerParams(
            collective_id=cid, has_side_effects=True, vmem_limit_bytes=vmem << 20
        ),
        cost_estimate=pl.CostEstimate(flops=int(us * 1.1e9), bytes_accessed=0, transcendentals=0),
        name=name,
    )(*[x for x, _ in ins])


def lane_roll(x, shift):
    return pltpu.roll(x.astype(f32), shift, 1)


def half_swap(x):
    lanes = lax.broadcasted_iota(jnp.int32, (1, x.shape[1]), 1)
    return jnp.where(lax.rem(lanes, 64) < 32, pltpu.roll(x, 96, 1), pltpu.roll(x, 32, 1))


def pair_up(a, b, n):
    lanes = lax.broadcasted_iota(jnp.int32, (1, 128), 1)
    if n == 0:
        return jnp.where(lanes < 64, a.astype(f32), lane_roll(b, 64))
    return jnp.where(lanes < 64, lane_roll(a, 64), b.astype(f32))


def put_pair(ref, g, rows, n, x):
    y = pltpu.roll(x, 64, 1)
    lo = slice(0, 64) if n == 0 else slice(64, 128)
    a, b = (x, y) if n == 0 else (y, x)
    ref[g, rows, lo] = a[:, lo].astype(bf16)
    ref[g + 1, rows, lo] = b[:, lo].astype(bf16)


FAR = 2.0**30


def segment_lanes(rows, lanes, starts_ref, count):
    hit = jnp.zeros((rows.shape[0], lanes.shape[1]), f32)
    for j in range(count):
        inside = rows >= starts_ref[j]
        if j + 1 < count:
            inside = inside & (rows < starts_ref[j + 1])
        hit = hit + jnp.where((lanes == 64 + j) & inside, 1.0, 0.0)
    return hit


def key_sides(S, RB, N, nseq, starts_ref, kv_ref, ka_ref, v1_ref):
    lanes = lax.broadcasted_iota(jnp.int32, (1, 128), 1)
    iota = lax.broadcasted_iota(jnp.int32, (RB, 1), 0)

    def fill(s, _):
        for n in range(N):
            kv = kv_ref[s, n * RB : (n + 1) * RB, :]
            hot = segment_lanes((n * S + s) * RB + iota, lanes, starts_ref, nseq).astype(bf16)
            ka_ref[s, n * RB : (n + 1) * RB, :] = jnp.where(lanes < 64, kv, hot)
            v1_ref[s, n * RB : (n + 1) * RB, :] = jnp.where(lanes < 64, jnp.ones_like(kv), kv)
        return 0

    lax.fori_loop(0, S, fill, 0)


def query_side(q, n, b, RB, nseq, starts_ref):
    lanes = lax.broadcasted_iota(jnp.int32, (1, 128), 1)
    iota = lax.broadcasted_iota(jnp.int32, (RB, 1), 0)
    if n == 1:
        q = pltpu.roll(q.astype(f32), 64, 1).astype(bf16)
    others = 1.0 - segment_lanes(b * RB + iota, lanes, starts_ref, nseq)
    far = jnp.where((lanes >= 64) & (lanes < 64 + nseq), -FAR, 0.0) * others
    return jnp.where(lanes < 64, q, far.astype(bf16))


def key_block(j, S, RB):
    return lax.rem(j, S), pl.ds(pl.multiple_of((j // S) * RB, RB), RB)


def attn_fwd_body(S, RB, N, nseq, first, done, starts_ref, q_ref, kv_ref, ob_ref, res_ref, ka_ref, v1_ref, acc_ref):
    key_sides(S, RB, N, nseq, starts_ref, kv_ref, ka_ref, v1_ref)
    lanes = lax.broadcasted_iota(jnp.int32, (1, 128), 1)
    for n in range(N):

        def qblock(i, _):
            s = lax.rem(first + i, S)
            b = n * S + s
            qa = query_side(q_ref[s], n, b, RB, nseq, starts_ref)
            acc_ref[...] = jnp.zeros_like(acc_ref)

            def at(ref, j):
                a, c = key_block(j, S, RB)
                return ref[a, c, :]

            def kstep(j, _):
                e = jnp.exp2(dot(qa, at(ka_ref, j), NT))
                acc_ref[...] += dot(e.astype(bf16), at(v1_ref, j), NN)
                return 0

            lax.fori_loop(0, b, kstep, 0)
            sc = dot(qa, at(ka_ref, b), NT)
            half = RB // 2
            tri = lax.broadcasted_iota(jnp.int32, (half, half), 1) <= lax.broadcasted_iota(jnp.int32, (half, half), 0)
            v = at(v1_ref, b)
            e = jnp.where(tri, jnp.exp2(sc[:half, :half]), 0.0).astype(bf16)
            acc_ref[:half] += dot(e, v[:half], NN)
            e1 = jnp.exp2(sc[half:, :half]).astype(bf16)
            e2 = jnp.where(tri, jnp.exp2(sc[half:, half:]), 0.0).astype(bf16)
            acc_ref[half:] += dot(e1, v[:half], NN) + dot(e2, v[half:], NN)
            acc = acc_ref[...]
            inv = 1.0 / acc
            o = acc * pltpu.roll(inv, 64, 1)
            res_ref[b] = jnp.where(lanes < 64, inv, o)
            if n == 0:
                ob_ref[s, :, 0:64] = pltpu.roll(o, 64, 1)[:, 0:64].astype(bf16)
            else:
                ob_ref[s, :, 64:128] = o[:, 64:128].astype(bf16)
            done(n, s)
            return 0

        lax.fori_loop(0, S, qblock, 0)


def attn_bwd_body(
    S, RB, N, nseq, first, done, phase,
    starts_ref, q_ref, kv_ref, do_ref, res_ref, dq_ref, dkv_ref,
    ka_ref, v1_ref, qa_ref, du_ref, dq_acc, k_acc, v_acc,
):
    key_sides(S, RB, N, nseq, starts_ref, kv_ref, ka_ref, v1_ref)
    lanes = lax.broadcasted_iota(jnp.int32, (1, 128), 1)
    for n in range(N):

        def prepare(s, _):
            b = n * S + s
            do = do_ref[s].astype(f32)
            res = res_ref[b]
            if n == 0:
                do = pltpu.roll(do, 64, 1)
            du = jnp.where(lanes < 64, 0.0, do * pltpu.roll(res, 64, 1))
            delta = jnp.sum(du * res, axis=1, keepdims=True)
            hi = (-delta).astype(bf16).astype(f32)
            du_ref[b] = jnp.where(lanes == 0, hi, jnp.where(lanes == 1, -delta - hi, du)).astype(bf16)
            qa_ref[b] = query_side(q_ref[s], n, b, RB, nseq, starts_ref)
            dq_acc[b] = jnp.zeros((RB, 128), f32)
            return 0

        lax.fori_loop(0, S, prepare, 0)
    half = RB // 2
    tri = lax.broadcasted_iota(jnp.int32, (half, half), 0) <= lax.broadcasted_iota(jnp.int32, (half, half), 1)
    for n in range(N):

        def kblock(i, _):
            s = lax.rem(first + i, S)
            j = n * S + s
            key = ka_ref[s, n * RB : (n + 1) * RB, :]
            value = v1_ref[s, n * RB : (n + 1) * RB, :]
            kv = kv_ref[s, n * RB : (n + 1) * RB, :]

            def weights(k0, q0):
                qs = slice(q0, q0 + half)
                sc = dot(key[k0 : k0 + half], qa_ref[j, qs], NT)
                dp = dot(value[k0 : k0 + half], du_ref[j, qs], NT)
                e = jnp.exp2(sc)
                if k0 == q0:
                    e = jnp.where(tri, e, 0.0)
                return e.astype(bf16), (e * dp).astype(bf16)

            lo, hi = slice(0, half), slice(half, RB)
            e00, s00 = weights(0, 0)
            e01, s01 = weights(0, half)
            e11, s11 = weights(half, half)
            v_acc[lo] = dot(e00, du_ref[j, lo], NN) + dot(e01, du_ref[j, hi], NN)
            v_acc[hi] = dot(e11, du_ref[j, hi], NN)
            k_acc[lo] = dot(s00, qa_ref[j, lo], NN) + dot(s01, qa_ref[j, hi], NN)
            k_acc[hi] = dot(s11, qa_ref[j, hi], NN)
            dq_acc[j, lo] += dot(s00, kv[:half], TN)
            dq_acc[j, hi] += dot(s01, kv[:half], TN) + dot(s11, kv[half:], TN)

            def qstep(b, _):
                e = jnp.exp2(dot(key, qa_ref[b], NT))
                ds = (e * dot(value, du_ref[b], NT)).astype(bf16)
                v_acc[...] += dot(e.astype(bf16), du_ref[b], NN)
                k_acc[...] += dot(ds, qa_ref[b], NN)
                dq_acc[b] += dot(ds, kv, TN)
                return 0

            lax.fori_loop(j + 1, N * S, qstep, 0)
            whole = jnp.where(lanes < 64, k_acc[...] * math.log(2.0), v_acc[...])
            dkv_ref[s, n * RB : (n + 1) * RB, :] = whole.astype(bf16)
            done(n, s, i)
            return 0

        lax.fori_loop(0, S, kblock, 0)

        def pack(s, _):
            dq = dq_acc[n * S + s] * 0.125
            dq_ref[n, s] = jnp.where(lanes < 64, dq[:half], pltpu.roll(dq[half:], 64, 1)).astype(bf16)
            return 0

        lax.fori_loop(0, S, pack, 0)
        phase(n)


def hidden_kernel(chunks, n_ref, x_ref, dm_ref, g0, g1, g2, u0, u1, u2, m_ref, dg_ref, dp_ref):
    half = g0.shape[0]
    a = pl.ds(pl.multiple_of(n_ref[0] * half, half), half)
    part = half // 2
    b = pl.ds(pl.multiple_of((1 - n_ref[0]) * half + n_ref[1] * part, part), part)
    d = pl.ds(pl.multiple_of((1 - n_ref[0]) * half + (1 - n_ref[1]) * part, part), part)
    rows = x_ref.shape[0] // chunks
    for c in range(chunks):
        r = slice(c * rows, (c + 1) * rows)

        def product(y, w0, w1, w2):
            return dot(y[r, a], w0[...], NN) + dot(y[r, b], w1[...], NN) + dot(y[r, d], w2[...], NN)

        gate, up, dh = product(x_ref, g0, g1, g2), product(x_ref, u0, u1, u2), dm_ref[r].astype(f32)
        sig = 1.0 / (1.0 + jnp.exp(-gate))
        act = gate * sig
        m_ref[r] = (act * up).astype(bf16)
        dp_ref[r] = (dh * act).astype(bf16)
        dg_ref[r] = (dh * up * (sig + act * (1.0 - sig))).astype(bf16)


def hidden_units(n_idx, x, dm, mine, got, tile=256, chunks=3):
    R, D = x.shape
    half, H = 2 * got[0][0].shape[0], got[0][0].shape[1]
    steps = H // tile
    own = pl.BlockSpec((half, tile), lambda i, n: (0, n[0] * steps + i))
    oth = pl.BlockSpec((half // 2, tile), lambda i, n: (0, i))
    full = pl.BlockSpec((R, D), lambda i, n: (0, 0), pipeline_mode=pl.Buffered(1))
    out = pl.BlockSpec((R, tile), lambda i, n: (0, i))
    return pl.pallas_call(
        functools.partial(hidden_kernel, chunks),
        grid_spec=pltpu.PrefetchScalarGridSpec(
            num_scalar_prefetch=1,
            grid=(steps,),
            in_specs=[full, out] + [own, oth, oth] * 2,
            out_specs=[out] * 3,
        ),
        out_shape=[jax.ShapeDtypeStruct((R, H), bf16)] * 3,
        compiler_params=pltpu.CompilerParams(vmem_limit_bytes=56 << 20),
        cost_estimate=pl.CostEstimate(flops=4 * R * D * H, bytes_accessed=0, transcendentals=0),
        name="hidden",
    )(n_idx, x, dm, mine[0], *got[0], mine[1], *got[1])


def back_kernel(chunks, per, n_ref, dg, dp, g0, g1, g2, u0, u1, u2, o_ref):
    i = pl.program_id(0)
    rows = dg.shape[0] // chunks

    def go(g, u):
        for c in range(chunks):
            r = slice(c * rows, (c + 1) * rows)
            o_ref[r] = (dot(dg[r], g[...], NT) + dot(dp[r], u[...], NT)).astype(bf16)

    for which, (g, u) in enumerate(((g0, u0), (g1, u1), (g2, u2))):

        @pl.when(source_of(i, per, n_ref) == which)
        def _(g=g, u=u):
            go(g, u)


def source_of(i, per, n_ref):
    part = i % per // (per // 2)
    return jnp.where(i // per == n_ref[0], 0, jnp.where(part == n_ref[1], 1, 2))


def hidden_back(n_idx, dg, dp, mine, got, tile=256, chunks=3):
    R, H = dg.shape
    half = 2 * got[0][0].shape[0]
    per = half // tile

    def spec(which, count, column):
        def index(i, n):
            return jnp.where(source_of(i, per, n) == which, i % count, 0), column(n)

        return pl.BlockSpec((tile, H), index)

    specs = [spec(0, per, lambda n: n[0]), spec(1, per // 2, lambda n: 0), spec(2, per // 2, lambda n: 0)]
    full = pl.BlockSpec((R, H), lambda i, n: (0, 0), pipeline_mode=pl.Buffered(1))
    return pl.pallas_call(
        functools.partial(back_kernel, chunks, per),
        grid_spec=pltpu.PrefetchScalarGridSpec(
            num_scalar_prefetch=1,
            grid=(2 * per,),
            in_specs=[full, full] + specs * 2,
            out_specs=pl.BlockSpec((R, tile), lambda i, n: (0, i)),
        ),
        out_shape=jax.ShapeDtypeStruct((R, 2 * half), bf16),
        compiler_params=pltpu.CompilerParams(vmem_limit_bytes=56 << 20),
        cost_estimate=pl.CostEstimate(flops=8 * R * H * half, bytes_accessed=0, transcendentals=0),
        name="hidden_back",
    )(n_idx, dg, dp, mine[0], *got[0], mine[1], *got[1])


def by_rows(
    tokens,
    gain_attn,
    w_query,
    w_key,
    w_value,
    w_out,
    gain_ffn,
    w_gate,
    w_up,
    w_down,
    lengths,
    cotangent,
):
    f32 = jnp.float32
    bf16 = jnp.bfloat16
    tok_rows = tokens.shape[0]
    col_count = tokens.shape[1]
    all_rows = tok_rows * lax.axis_size("narrow") * lax.axis_size("seq")
    block_id = lax.axis_index(("narrow", "seq"))
    row_ids = block_id * tok_rows + jnp.arange(tok_rows, dtype=jnp.int32)
    seq_first = seq_starts(lengths, row_ids)
    lowest_key = jnp.min(seq_first)
    highest_key = block_id * tok_rows + tok_rows - 1
    full_in = lax.all_gather(tokens, "wide", axis=1, tiled=True)
    inputs = full_in.astype(f32)
    recip1 = lax.rsqrt(jnp.mean(inputs * inputs, axis=1, keepdims=True) + NORM_EPSILON)
    normed1 = (inputs * recip1 * gain_attn).astype(bf16)
    query_w, key_w, value_w, out_w = (
        lax.all_gather(w_query, ("narrow", "seq"), axis=0, tiled=True),
        lax.all_gather(w_key, ("narrow", "seq"), axis=0, tiled=True),
        lax.all_gather(w_value, ("narrow", "seq"), axis=0, tiled=True),
        lax.all_gather(w_out, ("narrow", "seq"), axis=0, tiled=True),
    )
    gate_w, up_w, down_w = (
        lax.all_gather(w_gate, "narrow", axis=0, tiled=True),
        lax.all_gather(w_up, "narrow", axis=0, tiled=True),
        lax.all_gather(w_down, "narrow", axis=0, tiled=True),
    )
    heads_kv = key_w.shape[1]
    head_dim = key_w.shape[2]
    group_size = query_w.shape[2] // head_dim
    kv_width = heads_kv * head_dim
    score_scale = 1.0 / math.sqrt(head_dim)
    cos_table, sin_table = rotation(row_ids - seq_first, head_dim)
    query_raw = jnp.einsum("td,dkc->tkc", normed1, query_w, preferred_element_type=f32)
    key_raw = jnp.einsum("td,dkc->tkc", normed1, key_w, preferred_element_type=f32)
    value_raw = jnp.einsum("td,dkc->tkc", normed1, value_w, preferred_element_type=f32)
    query_b = rotate(
        query_raw.reshape(tok_rows, heads_kv, group_size, head_dim), cos_table, sin_table
    ).astype(bf16)
    key_b = rotate(key_raw, cos_table, sin_table).astype(bf16)
    value_b = value_raw.astype(bf16)
    kv_local = jnp.concatenate(
        [key_b.reshape(tok_rows, kv_width), value_b.reshape(tok_rows, kv_width)], axis=1
    )

    def block_scores(kv_part, key_start):
        part_rows = kv_part.shape[0]
        key_part = kv_part[:, :kv_width].reshape(part_rows, heads_kv, head_dim)
        value_part = kv_part[:, kv_width:].reshape(part_rows, heads_kv, head_dim)
        raw_scores = (
            jnp.einsum("qkgh,pkh->kgqp", query_b, key_part, preferred_element_type=f32)
            * score_scale
        )
        key_rows = key_start + jnp.arange(part_rows, dtype=jnp.int32)
        causal_mask = (key_rows[None, :] >= seq_first[:, None]) & (
            key_rows[None, :] <= row_ids[:, None]
        )
        weights = jnp.where(causal_mask[None, None], jnp.exp(raw_scores), 0.0)
        return (weights, key_part, value_part)

    def forward_block(state_in, kv_part, key_start):
        summed, row_total = state_in
        weights, key_part, value_part = block_scores(kv_part, key_start)
        row_total = row_total + jnp.sum(weights, axis=3)
        summed = summed + jnp.einsum(
            "kgqp,pkh->qkgh", weights.astype(bf16), value_part, preferred_element_type=f32
        )
        return (summed, row_total)

    start_state = (
        jnp.zeros((tok_rows, heads_kv, group_size, head_dim), f32),
        jnp.zeros((heads_kv, group_size, tok_rows), f32),
    )
    summed, row_total = over_blocks(
        forward_block,
        start_state,
        lax.all_gather(kv_local, ("narrow", "seq"), axis=0, tiled=True),
        tok_rows,
        lowest_key,
        highest_key,
    )
    inv_total = 1.0 / jnp.transpose(row_total, (2, 0, 1))
    attn_out = summed * inv_total[..., None]
    attn_b = attn_out.astype(bf16).reshape(tok_rows, heads_kv, group_size * head_dim)
    branch_part = jnp.einsum("tkc,dkc->td", attn_b, out_w, preferred_element_type=f32)
    branch = lax.psum(branch_part, "wide")
    residual = inputs + branch
    recip2 = lax.rsqrt(jnp.mean(residual * residual, axis=1, keepdims=True) + NORM_EPSILON)
    normed2 = (residual * recip2 * gain_ffn).astype(bf16)
    gate_val = jnp.dot(normed2, gate_w, preferred_element_type=f32)
    up_val = jnp.dot(normed2, up_w, preferred_element_type=f32)
    sigmoid_gate = jax.nn.sigmoid(gate_val)
    hidden = (gate_val * sigmoid_gate * up_val).astype(bf16)
    down_part = jnp.einsum("tf,df->td", hidden, down_w, preferred_element_type=f32)
    down = lax.psum_scatter(
        down_part.astype(jnp.bfloat16), "wide", scatter_dimension=1, tiled=True
    ).astype(jnp.float32)
    wide_id = lax.axis_index("wide")
    local_resid = lax.dynamic_slice_in_dim(residual, wide_id * col_count, col_count, 1)
    output = (local_resid + down).astype(bf16)
    grad_full = lax.all_gather(cotangent, "wide", axis=1, tiled=True)
    grad_hidden = jnp.einsum("td,df->tf", grad_full, down_w, preferred_element_type=f32)
    silu_slope = sigmoid_gate * (1.0 + gate_val * (1.0 - sigmoid_gate))
    grad_gate_val = (grad_hidden * up_val * silu_slope).astype(bf16)
    grad_up_val = (grad_hidden * gate_val * sigmoid_gate).astype(bf16)
    dw_down = jnp.einsum("td,tf->df", grad_full, hidden, preferred_element_type=f32)
    dw_gate = jnp.einsum("td,tf->df", normed2, grad_gate_val, preferred_element_type=f32)
    dw_up = jnp.einsum("td,tf->df", normed2, grad_up_val, preferred_element_type=f32)
    dn2_part = jnp.einsum(
        "tf,df->td", grad_gate_val, gate_w, preferred_element_type=f32
    ) + jnp.einsum("tf,df->td", grad_up_val, up_w, preferred_element_type=f32)
    dn2 = lax.psum(dn2_part, "wide")
    dgain_ffn = jnp.sum(dn2 * residual * recip2, axis=0)
    scaled2 = dn2 * gain_ffn
    dresid = (
        grad_full.astype(f32)
        + recip2 * scaled2
        - residual
        * (recip2 * recip2 * recip2)
        * jnp.mean(scaled2 * residual, axis=1, keepdims=True)
    )
    dbranch = dresid.astype(bf16)
    dw_out = jnp.einsum("td,tkc->dkc", dbranch, attn_b, preferred_element_type=f32)
    grad_attn = jnp.einsum("td,dkc->tkc", dbranch, out_w, preferred_element_type=f32).reshape(
        tok_rows, heads_kv, group_size, head_dim
    )
    grad_summed = (grad_attn * inv_total[..., None]).astype(bf16)
    delta_rows = jnp.transpose(jnp.sum(grad_attn * attn_out, axis=3) * inv_total, (1, 2, 0))

    def backward_block(state_in, kv_part, key_start):
        dquery, dkv_all = state_in
        weights, key_part, value_part = block_scores(kv_part, key_start)
        part_rows = kv_part.shape[0]
        dprob = jnp.einsum("qkgh,pkh->kgqp", grad_summed, value_part, preferred_element_type=f32)
        dscore = (weights * (dprob - delta_rows[..., None])).astype(bf16)
        dquery = dquery + jnp.einsum("kgqp,pkh->qkgh", dscore, key_part, preferred_element_type=f32)
        dkey = (
            jnp.einsum("kgqp,qkgh->pkh", dscore, query_b, preferred_element_type=f32) * score_scale
        )
        dvalue = jnp.einsum(
            "kgqp,qkgh->pkh", weights.astype(bf16), grad_summed, preferred_element_type=f32
        )
        block_grad = jnp.concatenate(
            [dkey.reshape(part_rows, kv_width), dvalue.reshape(part_rows, kv_width)], axis=1
        )
        current = lax.dynamic_slice_in_dim(dkv_all, key_start, part_rows, 0)
        dkv_all = lax.dynamic_update_slice_in_dim(dkv_all, current + block_grad, key_start, 0)
        return (dquery, dkv_all)

    back_state = (
        jnp.zeros((tok_rows, heads_kv, group_size, head_dim), f32),
        jnp.zeros((all_rows, 2 * kv_width), f32),
    )
    dquery, dkv_all = over_blocks(
        backward_block,
        back_state,
        lax.all_gather(kv_local, ("narrow", "seq"), axis=0, tiled=True),
        tok_rows,
        lowest_key,
        highest_key,
    )
    dkv_own = lax.psum_scatter(
        dkv_all.astype(jnp.bfloat16), ("narrow", "seq"), scatter_dimension=0, tiled=True
    ).astype(jnp.float32)
    dquery_b = (
        unrotate(dquery * score_scale, cos_table, sin_table)
        .astype(bf16)
        .reshape(tok_rows, heads_kv, group_size * head_dim)
    )
    dkey_b = unrotate(
        dkv_own[:, :kv_width].reshape(tok_rows, heads_kv, head_dim), cos_table, sin_table
    ).astype(bf16)
    dvalue_b = dkv_own[:, kv_width:].reshape(tok_rows, heads_kv, head_dim).astype(bf16)
    dw_query = jnp.einsum("td,tkc->dkc", normed1, dquery_b, preferred_element_type=f32)
    dw_key = jnp.einsum("td,tkc->dkc", normed1, dkey_b, preferred_element_type=f32)
    dw_value = jnp.einsum("td,tkc->dkc", normed1, dvalue_b, preferred_element_type=f32)
    dn1_part = jnp.einsum("tkc,dkc->td", dquery_b, query_w, preferred_element_type=f32)
    dn1_part = dn1_part + jnp.einsum("tkc,dkc->td", dkey_b, key_w, preferred_element_type=f32)
    dn1_part = dn1_part + jnp.einsum("tkc,dkc->td", dvalue_b, value_w, preferred_element_type=f32)
    dn1 = lax.psum(dn1_part.astype(jnp.bfloat16), "wide").astype(jnp.float32)
    dgain_attn = jnp.sum(dn1 * inputs * recip1, axis=0)
    scaled1 = dn1 * gain_attn
    dinputs = (
        dresid
        + recip1 * scaled1
        - inputs * (recip1 * recip1 * recip1) * jnp.mean(scaled1 * inputs, axis=1, keepdims=True)
    )
    grad_input = lax.dynamic_slice_in_dim(dinputs, wide_id * col_count, col_count, 1).astype(bf16)
    summed_grads = (
        lax.psum_scatter(
            dgain_attn.astype(jnp.bfloat16), ("narrow", "seq"), scatter_dimension=0, tiled=True
        ).astype(jnp.float32),
        lax.psum_scatter(
            dw_query.astype(jnp.bfloat16), ("narrow", "seq"), scatter_dimension=0, tiled=True
        ).astype(jnp.float32),
        lax.psum_scatter(
            dw_key.astype(jnp.bfloat16), ("narrow", "seq"), scatter_dimension=0, tiled=True
        ).astype(jnp.float32),
        lax.psum_scatter(
            dw_value.astype(jnp.bfloat16), ("narrow", "seq"), scatter_dimension=0, tiled=True
        ).astype(jnp.float32),
        lax.psum_scatter(
            dw_out.astype(jnp.bfloat16), ("narrow", "seq"), scatter_dimension=0, tiled=True
        ).astype(jnp.float32),
        lax.psum_scatter(
            dgain_ffn.astype(jnp.bfloat16), ("narrow", "seq"), scatter_dimension=0, tiled=True
        ).astype(jnp.float32),
        lax.psum_scatter(
            dw_gate.astype(jnp.bfloat16), ("narrow", "seq"), scatter_dimension=0, tiled=True
        ).astype(jnp.float32),
        lax.psum_scatter(
            dw_up.astype(jnp.bfloat16), ("narrow", "seq"), scatter_dimension=0, tiled=True
        ).astype(jnp.float32),
        lax.psum_scatter(
            dw_down.astype(jnp.bfloat16), ("narrow", "seq"), scatter_dimension=0, tiled=True
        ).astype(jnp.float32),
    )
    return (
        output,
        grad_input,
        summed_grads[0],
        summed_grads[1],
        summed_grads[2],
        summed_grads[3],
        summed_grads[4],
        summed_grads[5],
        summed_grads[6],
        summed_grads[7],
        summed_grads[8],
    )


def by_plane(
    tokens,
    gain_attn,
    w_query,
    w_key,
    w_value,
    w_out,
    gain_ffn,
    w_gate,
    w_up,
    w_down,
    lengths,
    cotangent,
):
    N, W, S = (lax.axis_size(a) for a in ("narrow", "wide", "seq"))
    n, s = lax.axis_index("narrow"), lax.axis_index("seq")
    P8 = N * W
    RB, cols = tokens.shape
    R, D = N * RB, W * cols
    hd = w_key.shape[2]
    group = w_query.shape[2] // hd
    qw = group * hd
    rows, block = RB // W, D // (N * S)
    half_d, half_h = w_gate.shape[0], w_gate.shape[1] // N
    nseq = lengths.shape[0]
    chunk = RB // 2
    chunks = R // chunk
    fold = math.log2(math.e) / math.sqrt(hd)
    starts = jnp.cumsum(lengths) - lengths
    heads_shape, kv_shape, full_shape = (S, RB, N * hd), (S, R, 2 * hd), (R, D)
    slab_shape, own_shape = (N, S, block, half_h), (rows, D)

    def block_view(ref, chip, core):
        a, b = chip // (W // 2), lax.rem(chip, W // 2) * 2 + core
        return ref.at[pl.ds(a * RB, RB), pl.ds(b * cols, cols)]

    def row_view(ref, chip, core):
        return ref.at[chip * 2 + core]

    def to_seq():
        return Exchange(S, "seq", lambda src, j: src.at[j])

    def to_rows():
        return Exchange(N * S, "rows", lambda src, j: src.at[j])

    def to_narrow():
        return Exchange(N, "narrow", lambda src, j: src.at[j])

    def own_rows(at):
        return pl.ds(pl.multiple_of(at.n * RB + at.w * rows, rows), rows)

    def chunk_rows(c):
        k = c * chunk // RB
        return slice(c * chunk, (c + 1) * chunk), slice(c * chunk - k * RB, (c + 1) * chunk - k * RB), k

    def scale_of(x):
        return lax.rsqrt(jnp.mean(x * x, axis=1, keepdims=True) + NORM_EPSILON)

    w_mine = jnp.concatenate([w_query, w_key, w_value], axis=2).transpose(1, 0, 2)
    width = w_mine.shape[2]
    g_tok, g_w, g_wo = PlaneGather(block_view), HeadGather(S), HeadGather(S)

    def start_body(at, ins, outs, scratch):
        g_w.start(at, ins[1], outs[1])
        g_tok.start(at, ins[0], outs[0])
        g_w.relay()
        g_tok.relay()
        g_tok.relay2()
        g_tok.finish()
        g_w.finish()

    full_in, w_qkv = fused(
        1,
        "gather_start",
        55,
        [g_tok, g_w],
        start_body,
        [(tokens, HBM), (w_mine, HBM)],
        [(full_shape, bf16, HBM), ((N * S,) + w_mine.shape[1:], bf16, HBM)],
    )
    w_qkv = w_qkv.reshape(D, width)

    part_d = half_d // 2
    part_shape = (part_d, half_h)
    mine_w = [w_gate, w_up, w_down]
    n_idx = jnp.stack([n, lax.rem(s, 2)]).astype(jnp.int32)
    swaps = [Swap("narrow") for _ in range(4)]
    passes = [Swap("seq") for _ in range(4)]

    def for_partner(at, ref, start=0, size=part_d):
        rows_ = pl.ds(pl.multiple_of(lax.rem(at.s, 2) * part_d + start, size), size)
        return ref.at[rows_, pl.ds(pl.multiple_of((1 - at.n) * half_h, half_h), half_h)]

    row_ids = ((jnp.arange(N, dtype=jnp.int32) * S + s) * RB)[:, None] + jnp.arange(RB, dtype=jnp.int32)
    row_ids = row_ids.reshape(R)
    cos_table, sin_table = rotation(row_ids - seq_starts(lengths, row_ids), hd)
    cos_lanes = jnp.tile(cos_table, (1, 4))
    sin_lanes = jnp.tile(jnp.concatenate([-sin_table, sin_table], axis=1), (1, 2))

    e_q, e_kv, mv = to_seq(), Exchange(S, "seq", lambda src, j: src), Move()

    def qkv_body(at, ins, outs, scratch):
        x_ref, w_ref, gain_ref, cos_ref, sin_ref, *w_ins = ins
        q_out, kv_out, n1_out, *w_outs = outs
        n1, qs, kvs = scratch
        for sw, src, dst in zip(swaps[:2], w_ins, w_outs):
            sw.start(at, for_partner(at, src), dst)
        swaps[2].start(at, for_partner(at, w_ins[2], 0, part_d // 2), w_outs[2])
        lanes = lax.broadcasted_iota(jnp.int32, (1, 128), 1)
        for c in range(chunks):
            r, rb, k = chunk_rows(c)
            x = x_ref[r].astype(f32)
            normed = (x * scale_of(x) * gain_ref[...]).astype(bf16)
            n1[r] = normed
            qkv = dot(normed, w_ref[...], NN)
            cos, sin = cos_ref[r], sin_ref[r]
            for g in range(0, group, 2):
                y = qkv[:, g * hd : (g + 2) * hd]
                put_pair(qs, g, rb, k, (y * cos + half_swap(y) * sin) * fold)
            y = qkv[:, qw:]
            kvs[r] = jnp.where(lanes < hd, y * cos + half_swap(y) * sin, y).astype(bf16)
        e_kv.start(at, kvs, kv_out)
        e_q.start(at, qs, q_out)
        mv.start(at, n1, n1_out)
        e_kv.finish()
        e_q.finish()
        mv.finish()
        for sw in swaps[:3]:
            sw.finish()

    q_all, kv_all, normed1, *near_w = fused(
        2,
        "qkv_to_heads",
        60,
        [e_q, e_kv, mv] + swaps[:3],
        qkv_body,
        [
            (full_in, VMEM),
            (w_qkv, VMEM),
            (gain_attn[None], VMEM),
            (cos_lanes, VMEM),
            (sin_lanes, VMEM),
            (w_gate, HBM),
            (w_up, HBM),
            (w_down, HBM),
        ],
        [
            (heads_shape, bf16, HBM),
            (kv_shape, bf16, HBM),
            (full_shape, bf16, HBM),
            (part_shape, bf16, HBM),
            (part_shape, bf16, HBM),
            ((part_d // 2, half_h), bf16, HBM),
        ],
        [pltpu.VMEM(full_shape, bf16), pltpu.VMEM((group, RB, N * hd), bf16), pltpu.VMEM((R, 2 * hd), bf16)],
        40,
    )

    g_cot, st_o = PlaneGather(block_view), Stream(S)

    def forward_body(at, ins, outs, scratch):
        cot_in, w_in, wd_in, *attn_ins = ins
        grad_full, back, wo_out, near_out, res = outs
        heads, *work = scratch
        g_wo.start(at, w_in, wo_out)
        swaps[3].start(at, for_partner(at, wd_in, part_d // 2, part_d // 2), near_out)
        g_cot.start(at, cot_in, grad_full)

        def done(k, j):
            turn = lax.rem(j - at.s - 1 + 2 * S, S)
            if k == N - 1:
                st_o.send(at, heads.at[j], back.at[at.s], j)
                pl.when(turn == 1)(g_cot.relay)
                pl.when(turn == 2)(g_cot.relay2)
            else:
                pl.when(turn == 2)(g_wo.relay)

        attn_fwd_body(S, RB, N, nseq, at.s + 1, done, *attn_ins, heads, res, *work)
        st_o.finish(at, heads.at[0], back.at[at.s])
        g_cot.finish()
        g_wo.finish()
        swaps[3].finish()

    kv_scratch = pltpu.VMEM(kv_shape, bf16)
    grad_full, attn_back, w_o, near_last, attn_res = fused(
        8,
        "attn_fwd",
        48,
        [g_cot, st_o, g_wo, swaps[3]],
        forward_body,
        [
            (cotangent, HBM),
            (w_out.transpose(1, 0, 2), HBM),
            (w_down, HBM),
            (starts, SMEM),
            (q_all, VMEM),
            (kv_all, VMEM),
        ],
        [
            (full_shape, bf16, HBM),
            (heads_shape, bf16, HBM),
            ((N * S, block, qw), bf16, HBM),
            ((part_d // 2, half_h), bf16, HBM),
            ((N * S, RB, 2 * hd), f32, VMEM),
        ],
        [pltpu.VMEM(heads_shape, bf16), kv_scratch, kv_scratch, pltpu.VMEM((RB, 2 * hd), f32)],
        48,
    )

    w_o = w_o.reshape(D, qw)

    sc_a, g_n2, mv_x = PlaneScatter(own_shape, row_view), PlaneGather(row_view), Move()
    mvd = [Move() for _ in range(6)]

    def down_parts(at, wd, own_in, near0, near1, far_in):
        odd, m = lax.rem(at.s, 2), part_d // 2
        mine = own_in.at[:, pl.ds(pl.multiple_of(at.n * half_h, half_h), half_h)]

        def place(start, size):
            return wd.at[1 - at.n, pl.ds(pl.multiple_of(start, m), size)]

        parts = [(mine, wd.at[at.n]), (near0, place(odd * part_d, m)), (near1, place(odd * part_d + m, m))]
        return parts + [(far_in, place((1 - odd) * part_d, part_d))]

    def mid_body(at, ins, outs, scratch):
        heads, wo, x_in, gain_ref, dy_in, wd_in, *w_ins = ins
        attn_b, resid, n2_out, dm_out, *w_outs = outs
        part, xr, n2, dy, wd, dm = scratch
        m = part_d // 2
        passes[2].start(at, w_ins[2], w_outs[2].at[pl.ds(0, m)])
        passes[3].start(at, w_ins[3], w_outs[2].at[pl.ds(m, m)])
        for i in range(2):
            passes[i].start(at, w_ins[i], w_outs[i])
        parts = down_parts(at, wd, wd_in, w_ins[2], w_ins[3], w_outs[2])
        mvd[0].start(at, dy_in, dy)
        for i in range(3):
            mvd[1 + i].start(at, *parts[i])
        mv_x.start(at, x_in.at[own_rows(at)], xr)
        for k in range(N):
            for g in range(0, group, 2):
                pair = pair_up(heads[g], heads[g + 1], k).astype(bf16)
                attn_b[k * RB : (k + 1) * RB, g * hd : (g + 2) * hd] = pair
        for c in range(chunks):
            r = slice(c * chunk, (c + 1) * chunk)
            b = c * chunk // rows
            out = dot(attn_b[r], wo[...], NT).astype(bf16)
            part[b : b + chunk // rows] = out.reshape(chunk // rows, rows, D)
        sc_a.start(at, part)
        sc_a.mid()
        sc_a.mid2()
        passes[2].finish()
        passes[3].finish()
        mvd[4].start(at, *parts[3])
        mv_x.finish()
        h = xr[...].astype(f32) + sc_a.finish()
        resid[...] = h
        n2[...] = (h * scale_of(h) * gain_ref[...]).astype(bf16)
        g_n2.start(at, n2, n2_out)
        for mv_ in mvd[:5]:
            mv_.finish()
        quarter = half_h // 4

        def dm_tile(i, _):
            c = pl.ds(pl.multiple_of(i * quarter, quarter), quarter)
            dm[:, c] = dot(dy[...], wd.at[:, :, c][...].reshape(D, quarter), NN).astype(bf16)
            return 0

        lax.fori_loop(0, 4, dm_tile, 0)
        mvd[5].start(at, dm, dm_out)
        g_n2.relay()
        g_n2.relay2()
        g_n2.finish()
        mvd[5].finish()
        for ps in passes[:2]:
            ps.finish()

    attn_b, residual, normed2, grad_hidden, *far_w = fused(
        3,
        "attn_to_ffn",
        88,
        [sc_a, g_n2, mv_x] + passes + mvd,
        mid_body,
        [
            (attn_back, VMEM),
            (w_o, VMEM),
            (full_in, HBM),
            (gain_ffn[None], VMEM),
            (grad_full, HBM),
            (w_down, HBM),
        ]
        + [(x, HBM) for x in (*near_w, near_last)],
        [
            ((R, qw), bf16, VMEM),
            (own_shape, f32, VMEM),
            ((P8,) + own_shape, bf16, HBM),
            ((R, half_h), bf16, HBM),
        ]
        + [(part_shape, bf16, HBM)] * 3,
        [
            pltpu.VMEM((P8,) + own_shape, bf16),
            pltpu.VMEM(own_shape, bf16),
            pltpu.VMEM(own_shape, bf16),
            pltpu.VMEM(full_shape, bf16),
            pltpu.VMEM((N, half_d, half_h), bf16),
            pltpu.VMEM((R, half_h), bf16),
        ],
        60,
    )
    normed2 = normed2.reshape(full_shape)
    got_w = list(zip(near_w[:2], far_w[:2]))

    hidden, grad_gate_val, grad_up_val = hidden_units(n_idx, normed2, grad_hidden, mine_w, got_w)
    dn2_part = hidden_back(n_idx, grad_gate_val, grad_up_val, mine_w[:2], got_w[:2])

    slab_block = (N, block, half_h)

    half_block = (1,) + slab_block[1:]

    def seq_sum():
        return SeqSum(slab_block, lambda src, j: src.at[:, j])

    def seq_sum_half(a):
        return SeqSum(half_block, lambda src, j: src.at[pl.ds(a, 1), j])

    sc_n, g_db = PlaneScatter(own_shape, row_view), PlaneGather(row_view)
    q_down, q_gate0 = seq_sum(), seq_sum_half(0)
    mvs, mvk = [Move() for _ in range(6)], [Move() for _ in range(N * S)]

    def tile_cols(a, j):
        return pl.ds(pl.multiple_of((a * S + j) * block, block), block)

    def ffn_body(at, ins, outs, scratch):
        part_in, dy_in, m_in, n2_in, dg_in, dp_in, resid, gain_ref = ins
        db_out, dresid, dgain, down_out, gate0_out, gate_out, up_out = outs
        dy, m, n2, dg, dp, down, gate, db = scratch
        for mv_, src, dst in zip(mvs, (m_in, dy_in, n2_in, dg_in, dp_in), (m, dy, n2, dg, dp)):
            mv_.start(at, src, dst)
        sc_n.start(at, part_in)
        q_down.begin(at, down)
        q_gate0.begin(at, gate)
        mvs[0].finish()
        mvs[1].finish()

        def down_block(i):
            j = q_down.order(at)[i]
            for a in range(N):
                down[a, j] = dot(dy[:, tile_cols(a, j)], m[...], TN).astype(bf16)
            q_down.ready(at, i)

        down_block(0)
        down_block(1)
        sc_n.mid()
        down_block(2)
        sc_n.mid2()
        for mv_ in mvs[2:5]:
            mv_.finish()
        for i in range(4):
            j = q_gate0.order(at)[i]
            gate[0, j] = dot(n2[:, tile_cols(0, j)], dg[...], TN).astype(bf16)
            q_gate0.ready(at, i)
        down_block(3)
        db[...] = dy[own_rows(at)]

        def up_tile(a, j):
            t = a * S + j
            return pl.ds(pl.multiple_of((t // 2) * block, block), block), pl.ds(
                pl.multiple_of(lax.rem(t, 2) * half_h, half_h), half_h
            )

        def other_tiles(j, _):
            for a in range(N):
                c = tile_cols(a, j)
                if a:
                    gate[a, j] = dot(n2[:, c], dg[...], TN).astype(bf16)
                r, k = up_tile(a, j)
                dy[r, k] = dot(n2[:, c], dp[...], TN).astype(bf16)
            return 0

        lax.fori_loop(0, 2, other_tiles, 0)
        q_down.step(at, 0)
        q_gate0.step(at, 0)
        lax.fori_loop(2, S, other_tiles, 0)
        mvs[5].start(at, gate, gate_out)
        for t, mv_ in enumerate(mvk):
            r, k = up_tile(t // S, t % S)
            mv_.start(at, dy.at[r, k], up_out.at[t // S, t % S])
        dn2 = sc_n.finish()
        h = resid[...]
        r2 = scale_of(h)
        dgain[...] = jnp.sum(dn2 * h * r2, axis=0, keepdims=True)
        scaled = dn2 * gain_ref[...]
        own = db[...].astype(f32)
        grad = own + r2 * scaled - h * (r2 * r2 * r2) * jnp.mean(scaled * h, axis=1, keepdims=True)
        dresid[...] = grad
        db[...] = grad.astype(bf16)
        g_db.start(at, db, db_out)
        q_down.step(at, 1)
        q_down.step3(at)
        q_gate0.step(at, 1)
        q_gate0.step3(at)
        g_db.relay()
        g_db.relay2()
        g_db.finish()
        down_out[...] = q_down.total(at).astype(bf16)
        gate0_out[...] = q_gate0.total(at).astype(bf16)
        for mv_ in mvs[5:] + mvk:
            mv_.finish()

    dbranch, dresid, dgain_ffn, down_own, gate_own0, dw_gate, dw_up = fused(
        4,
        "ffn_grads",
        110,
        [sc_n, g_db, q_down, q_gate0] + mvs + mvk,
        ffn_body,
        [
            (dn2_part.reshape((P8,) + own_shape), HBM),
            (grad_full, HBM),
            (hidden, HBM),
            (normed2, HBM),
            (grad_gate_val, HBM),
            (grad_up_val, HBM),
            (residual, VMEM),
            (gain_ffn[None], VMEM),
        ],
        [
            ((P8,) + own_shape, bf16, HBM),
            (own_shape, f32, VMEM),
            ((1, D), f32, VMEM),
            (slab_block, bf16, VMEM),
            (half_block, bf16, VMEM),
            (slab_shape, bf16, HBM),
            (slab_shape, bf16, HBM),
        ],
        [
            pltpu.VMEM(full_shape, bf16),
            pltpu.VMEM((R, half_h), bf16),
            pltpu.VMEM(full_shape, bf16),
            pltpu.VMEM((R, half_h), bf16),
            pltpu.VMEM((R, half_h), bf16),
            pltpu.VMEM(slab_shape, bf16),
            pltpu.VMEM(slab_shape, bf16),
            pltpu.VMEM(own_shape, bf16),
        ],
        60,
    )

    e_do, t_down = to_seq(), to_narrow()
    mvt = [Move() for _ in range(8)]
    tile = half_d // 4

    def grad_heads_body(at, ins, outs, scratch):
        db_in, w_ref, ab, down_in, m_in, wd_in, wd0_in, wd1_in, wd2_in, resid = ins
        do_out, dwo_out, y_out, down_out = outs
        db, dos, m, wd, y, dwo = scratch
        moves = [(db_in, db), (m_in, m)] + down_parts(at, wd, wd_in, wd0_in, wd1_in, wd2_in)
        for mv_, (src, dst) in zip(mvt, moves):
            mv_.start(at, src, dst)
        mvt[0].finish()
        for c in range(chunks):
            r, rb, k = chunk_rows(c)
            out = dot(db[r], w_ref[...], NN)
            for g in range(0, group, 2):
                put_pair(dos, g, rb, k, out[:, g * hd : (g + 2) * hd])
        e_do.start(at, dos, do_out)
        t_down.start(at, down_in, down_out)

        def wo_tile(p, _):
            c = pl.ds(pl.multiple_of(p * block, block), block)
            dwo[p] = dot(db[:, c], ab[...], TN).astype(bf16)
            return 0

        lax.fori_loop(0, N * S, wo_tile, 0)
        mvt[6].start(at, dwo, dwo_out)
        for mv_ in mvt[1:6]:
            mv_.finish()
        for a in range(N):

            def y_tile(i, _):
                c = pl.ds(pl.multiple_of(a * half_d + i * tile, tile), tile)
                w_tile = wd[a, pl.ds(pl.multiple_of(i * tile, tile), tile), :]
                y[:, c] = dot(m[...], w_tile, NT).astype(bf16)
                return 0

            lax.fori_loop(0, half_d // tile, y_tile, 0)
        o = own_rows(at)
        y[o] = (y[o].astype(f32) + resid[...]).astype(bf16)
        mvt[7].start(at, y, y_out)
        e_do.finish()
        t_down.finish()
        mvt[6].finish()
        mvt[7].finish()

    do_all, dw_o, down_part, traded_down = fused(
        5,
        "grad_to_heads",
        25,
        [e_do, t_down] + mvt,
        grad_heads_body,
        [
            (dbranch.reshape(full_shape), HBM),
            (w_o, VMEM),
            (attn_b, VMEM),
            (down_own, HBM),
            (hidden, HBM),
            (w_down, HBM),
            (near_w[2], HBM),
            (near_last, HBM),
            (far_w[2], HBM),
            (residual, VMEM),
        ],
        [
            (heads_shape, bf16, HBM),
            ((N * S, block, qw), bf16, HBM),
            (full_shape, bf16, HBM),
            ((N, block, half_h), bf16, HBM),
        ],
        [
            pltpu.VMEM(full_shape, bf16),
            pltpu.VMEM((group, RB, N * hd), bf16),
            pltpu.VMEM((R, half_h), bf16),
            pltpu.VMEM((N, half_d, half_h), bf16),
            pltpu.VMEM(full_shape, bf16),
            pltpu.VMEM((N * S, block, qw), bf16),
        ],
        56,
    )

    q_gate, t_up, sc_y = seq_sum_half(1), to_narrow(), PlaneScatter((RB, cols), block_view)
    st_kv, st_q = [Stream(S) for _ in range(N)], [Stream(S) for _ in range(N)]

    def backward_body(at, ins, outs, scratch):
        gate_in, up_in, y_in, *attn_ins = ins
        gate_out, up_out, out_ref, dq_all, dkv_all = outs
        dq, dkv, *work = scratch
        sc_y.start(at, y_in)
        t_up.start(at, up_in, up_out)
        q_gate.start(at, gate_in)

        def pieces(k):
            r = pl.ds(k * RB, RB)
            return (lambda j: dkv.at[j, r]), dkv_all.at[at.s, r]

        def done(k, j, turn):
            src, dst = pieces(k)
            st_kv[k].send(at, src(j), dst, j)
            if k == 0:

                @pl.when(turn == 0)
                def _():
                    sc_y.mid()
                    q_gate.step(at, 0)

                @pl.when(turn == 1)
                def _():
                    q_gate.step(at, 1)
                    q_gate.step3(at)

                pl.when(turn == 2)(sc_y.mid2)

        def phase(k):
            for j in range(S):
                st_q[k].send(at, dq.at[k, j], dq_all.at[at.s, k], j)

        attn_bwd_body(S, RB, N, nseq, at.s + 1, done, phase, *attn_ins, dq, dkv, *work)
        out_ref[...] = sc_y.finish().astype(bf16)
        gate_out[...] = q_gate.total(at).astype(bf16)
        for k in range(N):
            src, dst = pieces(k)
            st_kv[k].finish(at, src(0), dst)
            st_q[k].finish(at, dq.at[k, 0], dq_all.at[at.s, k])
        t_up.finish()

    q_scratch, acc_scratch = pltpu.VMEM((N * S, RB, 2 * hd), bf16), pltpu.VMEM((RB, 2 * hd), f32)
    gate_own1, traded_up, output, dq_all, dkv_all = fused(
        6,
        "attn_bwd",
        110,
        [q_gate, t_up, sc_y] + st_q + st_kv,
        backward_body,
        [
            (dw_gate, HBM),
            (dw_up, HBM),
            (down_part, HBM),
            (starts, SMEM),
            (q_all, VMEM),
            (kv_all, VMEM),
            (do_all, VMEM),
            (attn_res, VMEM),
        ],
        [
            (half_block, bf16, VMEM),
            (slab_shape, bf16, HBM),
            ((RB, cols), bf16, VMEM),
            ((S, N, chunk, 2 * hd), bf16, HBM),
            (kv_shape, bf16, HBM),
        ],
        [
            pltpu.VMEM((N, S, chunk, 2 * hd), bf16),
            kv_scratch,
            kv_scratch,
            kv_scratch,
            q_scratch,
            q_scratch,
            pltpu.VMEM((N * S, RB, 2 * hd), f32),
            acc_scratch,
            acc_scratch,
        ],
        60,
    )

    q_up, t_gate, e_wog, e_wq = seq_sum(), to_narrow(), to_rows(), to_rows()
    sc_1 = PlaneScatter(own_shape, row_view)
    e_in = Exchange(W, "wide", lambda src, j: src.at[:, pl.ds(pl.multiple_of(j * cols, cols), cols)])
    e_gain = Exchange(N * S * W, "all", lambda src, j: src.at[j // W])
    mvu = [Move() for _ in range(2)]

    def last_body(at, ins, outs, scratch):
        dq, dkv, gate_in0, gate_in1, down_in, dwo_in, n1_in, up_in, x_in, w_ref, cos_ref, sin_ref, dresid_ref, gain_ref, dgain_ref = ins
        gi_out, gains_out, got_wq, got_wo, gate_out, up_out, down_out = outs
        n1, dqkv, part, dwq, xr, gi, gains, gate_s, gate_r = scratch

        def widen(out, halves):
            for a in range(N):
                out[:, a * half_h : (a + 1) * half_h] = halves[a].astype(f32)

        q_up.start(at, up_in)
        mvu[0].start(at, n1_in, n1)
        mvu[1].start(at, x_in.at[own_rows(at)], xr)
        gate_s[0] = gate_in0[0]
        gate_s[1] = gate_in1[0]
        t_gate.start(at, gate_s, gate_r)
        lanes = lax.broadcasted_iota(jnp.int32, (1, 128), 1)
        for c in range(chunks):
            r, rb, k = chunk_rows(c)
            cos, sin = cos_ref[r], sin_ref[r]
            for g in range(0, group, 2):
                y = pair_up(dq[g, k], dq[g + 1, k], c % 2)
                dqkv[r, g * hd : (g + 2) * hd] = (y * cos - half_swap(y) * sin).astype(bf16)
            y = sum(dkv[i, r].astype(f32) for i in range(S))
            dqkv[r, qw:] = jnp.where(lanes < hd, y * cos - half_swap(y) * sin, y).astype(bf16)
            out = dot(dqkv[r], w_ref[...], NT).astype(bf16)
            b = c * chunk // rows
            part[b : b + chunk // rows] = out.reshape(chunk // rows, rows, D)
        sc_1.start(at, part)
        mvu[0].finish()

        def wq_tile(p, _):
            c = pl.ds(pl.multiple_of(p * block, block), block)
            dwq[p] = dot(n1[:, c], dqkv[...], TN).astype(bf16)
            return 0

        lax.fori_loop(0, N * S, wq_tile, 0)
        sc_1.mid()
        q_up.step(at, 0)
        sc_1.mid2()
        e_wq.start(at, dwq, got_wq)
        e_wog.start(at, dwo_in, got_wo)
        mvu[1].finish()
        x = xr[...].astype(f32)
        r1 = scale_of(x)
        dn1 = sc_1.finish()
        dgain = jnp.sum(dn1 * x * r1, axis=0, keepdims=True)
        dgain2 = dgain_ref[...]
        for p in range(N * S):
            for i in range(block // 128):
                c = slice(p * block + i * 128, p * block + (i + 1) * 128)
                gains[p, i : i + 1, :] = dgain[:, c]
                gains[p, block // 128 + i : block // 128 + i + 1, :] = dgain2[:, c]
        e_gain.start(at, gains, gains_out)
        scaled = dn1 * gain_ref[...]
        grad = dresid_ref[...] + r1 * scaled - x * (r1 * r1 * r1) * jnp.mean(scaled * x, axis=1, keepdims=True)
        gi[...] = grad.astype(bf16)
        e_in.start(at, gi, gi_out)
        q_up.step(at, 1)
        q_up.step3(at)
        widen(down_out, down_in)
        t_gate.finish()
        widen(gate_out, gate_r)
        widen(up_out, q_up.total(at))
        for p in (e_in, e_gain, e_wq, e_wog):
            p.finish()

    gains_shape = (N * S, 2 * block // 128, 128)
    grad_input, gains, got_wq, got_wo, gate_grad, up_grad, down_grad = fused(
        7,
        "last",
        160,
        [q_up, t_gate, e_wog, e_wq, sc_1, e_in, e_gain] + mvu,
        last_body,
        [
            (dq_all, VMEM),
            (dkv_all, VMEM),
            (gate_own0, VMEM),
            (gate_own1, VMEM),
            (traded_down, VMEM),
            (dw_o, HBM),
            (normed1, HBM),
            (traded_up, HBM),
            (full_in, HBM),
            (w_qkv, VMEM),
            (cos_lanes, VMEM),
            (sin_lanes, VMEM),
            (dresid, VMEM),
            (gain_attn[None], VMEM),
            (dgain_ffn, VMEM),
        ],
        [
            ((W, rows, cols), bf16, HBM),
            ((N * S * W,) + gains_shape[1:], f32, HBM),
            ((N * S, block, width), bf16, HBM),
            ((N * S, block, qw), bf16, HBM),
            ((block, N * half_h), f32, VMEM),
            ((block, N * half_h), f32, VMEM),
            ((block, N * half_h), f32, VMEM),
        ],
        [
            pltpu.VMEM(full_shape, bf16),
            pltpu.VMEM((R, width), bf16),
            pltpu.VMEM((P8,) + own_shape, bf16),
            pltpu.VMEM((N * S, block, width), bf16),
            pltpu.VMEM(own_shape, bf16),
            pltpu.VMEM(own_shape, bf16),
            pltpu.VMEM(gains_shape, f32),
            pltpu.VMEM(slab_block, bf16),
            pltpu.VMEM(slab_block, bf16),
        ],
        60,
    )

    def over_seq(got):
        return jnp.sum(got.reshape(N, S, *got.shape[1:]).astype(f32), axis=1)

    gains = jnp.sum(gains, axis=0).reshape(2, block)
    qkv_grads = over_seq(got_wq).transpose(1, 0, 2)
    return (
        output,
        grad_input.reshape(RB, cols),
        gains[0],
        qkv_grads[:, :, :qw],
        qkv_grads[:, :, qw : qw + hd],
        qkv_grads[:, :, qw + hd :],
        over_seq(got_wo).transpose(1, 0, 2),
        gains[1],
        gate_grad,
        up_grad,
        down_grad,
    )


def local(tokens, gain_attn, w_query, w_key, *others):
    plane = lax.axis_size("narrow") * lax.axis_size("wide")
    heads_kv = w_key.shape[1] * lax.axis_size("wide")
    group = w_query.shape[2] // w_key.shape[2]
    fits = lax.axis_size("narrow") == 2 and heads_kv == plane and group == lax.axis_size("seq")
    body = by_plane if fits and w_key.shape[2] == 64 else by_rows
    return body(tokens, gain_attn, w_query, w_key, *others)


def solution(mesh):
    return jax.shard_map(
        local,
        mesh=mesh,
        in_specs=(
            P(("narrow", "seq"), "wide"),
            P(),
            P(("narrow", "seq"), "wide", None),
            P(("narrow", "seq"), "wide", None),
            P(("narrow", "seq"), "wide", None),
            P(("narrow", "seq"), "wide", None),
            P(),
            P("narrow", "wide"),
            P("narrow", "wide"),
            P("narrow", "wide"),
            P(),
            P(("narrow", "seq"), "wide"),
        ),
        out_specs=(
            P(("narrow", "seq"), "wide"),
            P(("narrow", "seq"), "wide"),
            P(("narrow", "seq")),
            P(("narrow", "seq"), "wide", None),
            P(("narrow", "seq"), "wide", None),
            P(("narrow", "seq"), "wide", None),
            P(("narrow", "seq"), "wide", None),
            P(("narrow", "seq")),
            P(("narrow", "seq"), "wide"),
            P(("narrow", "seq"), "wide"),
            P(("narrow", "seq"), "wide"),
        ),
        check_vma=False,
    )
```

```python
import functools
import math

import jax
import jax.numpy as jnp
from jax import lax
from jax.experimental import pallas as pl
from jax.experimental.pallas import tpu as pltpu
from jax.sharding import PartitionSpec as P

f32 = jnp.float32
bf16 = jnp.bfloat16
MESH = pl.DeviceIdType.MESH
NT = (((1,), (1,)), ((), ()))
NN = (((1,), (0,)), ((), ()))
TN = (((0,), (0,)), ((), ()))

ROPE_THETA = 500000.0
ROPE_FACTOR = 32.0
LOW_FACTOR = 1.0
HIGH_FACTOR = 4.0
OLD_CONTEXT = 8192.0
NORM_EPSILON = 1e-05


def frequencies(head_dim):
    freq_index = jnp.arange(head_dim // 2, dtype=jnp.float32)
    base_freq = jnp.exp(freq_index * (-2.0 * math.log(ROPE_THETA) / head_dim))
    wavelen = 2.0 * math.pi / base_freq
    smooth = jnp.clip((OLD_CONTEXT / wavelen - LOW_FACTOR) / (HIGH_FACTOR - LOW_FACTOR), 0.0, 1.0)
    return (1.0 - smooth) * base_freq / ROPE_FACTOR + smooth * base_freq


def seq_starts(lengths, row_ids):
    seq_ends = jnp.cumsum(lengths)
    begins = seq_ends - lengths
    found_at = jnp.where(begins[None, :] <= row_ids[:, None], begins[None, :], 0)
    return jnp.max(found_at, axis=1)


def rotation(positions, head_dim):
    angles = positions.astype(jnp.float32)[:, None] * frequencies(head_dim)[None, :]
    return (jnp.cos(angles), jnp.sin(angles))


def table_shape(values, cos_table, sin_table):
    half_dim = values.shape[-1] // 2
    bcast_shape = (cos_table.shape[0],) + (1,) * (values.ndim - 2) + (half_dim,)
    return (half_dim, cos_table.reshape(bcast_shape), sin_table.reshape(bcast_shape))


def rotate(values, cos_table, sin_table):
    half_dim, cos_part, sin_part = table_shape(values, cos_table, sin_table)
    first_half = values[..., :half_dim]
    second = values[..., half_dim:]
    return jnp.concatenate(
        [first_half * cos_part - second * sin_part, second * cos_part + first_half * sin_part],
        axis=-1,
    )


def unrotate(grad_vals, cos_table, sin_table):
    half_dim, cos_part, sin_part = table_shape(grad_vals, cos_table, sin_table)
    first_half = grad_vals[..., :half_dim]
    second = grad_vals[..., half_dim:]
    return jnp.concatenate(
        [first_half * cos_part + second * sin_part, second * cos_part - first_half * sin_part],
        axis=-1,
    )


def over_blocks(block_fn, state_now, kv_piece, block_len, lowest, highest):
    piece_rows = kv_piece.shape[0]
    block_count = piece_rows // block_len

    def one_step(block_no, state_in):
        begin = block_no * block_len
        kv_part = lax.dynamic_slice_in_dim(kv_piece, block_no * block_len, block_len, 0)
        live = (begin <= highest) & (begin + block_len - 1 >= lowest)

        def compute(carried):
            return block_fn(carried, kv_part, begin)

        def skipped(carried):
            return carried

        return lax.cond(live, compute, skipped, state_in)

    return lax.fori_loop(0, block_count, one_step, state_now)


def dot(a, b, dims):
    return lax.dot_general(a, b, dims, preferred_element_type=f32)


class Place:
    def __init__(self):
        self.N, self.W, self.S = (lax.axis_size(a) for a in ("narrow", "wide", "seq"))
        self.n, self.w, self.s = (lax.axis_index(a) for a in ("narrow", "wide", "seq"))
        self.X = self.W // 2
        self.core = lax.rem(self.w, 2)
        x = self.w // 2
        self.chip, self.chip_x = self.n * self.X + x, self.n * self.X + 1 - x
        self.chip_y, self.chip_xy = (1 - self.n) * self.X + x, (1 - self.n) * self.X + 1 - x
        self.sibling = {"wide": 2 * x + 1 - self.core}
        self.near_x, self.near_y = {"wide": 2 * (1 - x) + self.core}, {"narrow": 1 - self.n}


def remote(src, dst, ss, rs, device):
    return pltpu.make_async_remote_copy(
        src_ref=src, dst_ref=dst, send_sem=ss, recv_sem=rs, device_id=device, device_id_type=MESH
    )


class Move:
    scratch = [pltpu.SemaphoreType.DMA]

    def peers(self, at):
        return []

    def start(self, at, src, dst):
        self.copy = pltpu.make_async_copy(src, dst, self.bufs[0])
        self.copy.start()

    def finish(self):
        self.copy.wait()


class PlaneGather:
    def __init__(self, view):
        self.view = view
        self.scratch = [pltpu.SemaphoreType.DMA((4,))] * 2 + [pltpu.SemaphoreType.DMA((5,))] * 2
        self.scratch += [pltpu.SemaphoreType.DMA]
        self.stage = 0

    def peers(self, at):
        return [at.near_x, at.near_y, at.sibling]

    def half(self, block, h):
        m = block.shape[0] // 2
        return block.at[pl.ds(h * m, m)]

    def start(self, at, src, dst):
        ss, rs, fs, fr, ls = self.bufs
        own = self.view(dst, at.chip, at.core)
        from_x, from_y, across = (self.view(dst, i, at.core) for i in (at.chip_x, at.chip_y, at.chip_xy))
        self.local = pltpu.make_async_copy(src, own, ls)
        sent = [(src, own, at.near_x), (src, own, at.near_y)]
        sent += [(self.half(from_x, 0), self.half(from_x, 0), at.near_y)]
        sent += [(self.half(from_y, 1), self.half(from_y, 1), at.near_x)]
        self.far = [remote(x, y, ss.at[i], rs.at[i], d) for i, (x, y, d) in enumerate(sent)]
        shared = [src, from_x, from_y, self.half(across, 0), self.half(across, 1)]
        kept = [own] + shared[1:]
        self.near = [remote(x, y, fs.at[i], fr.at[i], at.sibling) for i, (x, y) in enumerate(zip(shared, kept))]
        for copy in (*self.far[:2], self.near[0], self.local):
            copy.start()

    def relay(self):
        for i in range(2):
            self.far[i].wait_recv()
            self.far[2 + i].start()
            self.near[1 + i].start()

    def relay2(self):
        for i in range(2, 4):
            self.far[i].wait_recv()
            self.near[1 + i].start()

    def finish(self):
        self.local.wait()
        for c in self.far:
            c.wait_send()
        for c in self.near:
            c.wait()


class Exchange:
    def __init__(self, count, group, pick):
        self.count, self.group, self.pick = count, group, pick
        self.scratch = [pltpu.SemaphoreType.DMA((count,))] * 2 + [pltpu.SemaphoreType.DMA]

    def device(self, at, k):
        if self.group == "rows":
            p = lax.rem(at.n * at.S + at.s + k, at.N * at.S)
            return p, {"narrow": p // at.S, "seq": lax.rem(p, at.S)}
        if self.group == "all":
            j = lax.rem((at.n * at.S + at.s) * at.W + at.w + k, at.N * at.S * at.W)
            p = j // at.W
            return j, {"narrow": p // at.S, "seq": lax.rem(p, at.S), "wide": lax.rem(j, at.W)}
        me = {"seq": at.s, "narrow": at.n, "wide": at.w}[self.group]
        j = lax.rem(me + k, self.count)
        return j, {self.group: j}

    def peers(self, at):
        return [self.device(at, k)[1] for k in range(1, self.count)]

    def begin(self, at, src, dst):
        ss, rs, ls = self.bufs
        me = self.device(at, 0)[0]
        self.copies = [pltpu.make_async_copy(self.pick(src, me), dst.at[me], ls)]
        for k in range(1, self.count):
            j, d = self.device(at, k)
            self.copies.append(remote(self.pick(src, j), dst.at[me], ss.at[k], rs.at[k], d))

    def start(self, at, src, dst):
        self.begin(at, src, dst)
        for c in self.copies[1:] + self.copies[:1]:
            c.start()

    def finish(self):
        for c in self.copies:
            c.wait()


class Stream:
    def __init__(self, S):
        self.scratch = [pltpu.SemaphoreType.DMA((S,))] * 2 + [pltpu.SemaphoreType.DMA]

    def peers(self, at):
        return [{"seq": lax.rem(at.s + k, at.S)} for k in range(1, at.S)]

    def away(self, at, src, dst, j):
        ss, rs, _ = self.bufs
        k = lax.rem(j - at.s + at.S, at.S)
        return remote(src, dst, ss.at[k], rs.at[k], {"seq": j})

    def send(self, at, src, dst, j):
        @pl.when(j == at.s)
        def _():
            pltpu.make_async_copy(src, dst, self.bufs[2]).start()

        @pl.when(j != at.s)
        def _():
            self.away(at, src, dst, j).start()

    def finish(self, at, src, dst):
        pltpu.make_async_copy(src, dst, self.bufs[2]).wait()
        for k in range(1, at.S):
            self.away(at, src, dst, lax.rem(at.s + k, at.S)).wait()


class SeqSum:
    def __init__(self, block, pick):
        self.pick = pick
        self.scratch = [pltpu.VMEM((8,) + block, bf16)] + [pltpu.SemaphoreType.DMA((6,))] * 2
        self.scratch += [pltpu.SemaphoreType.DMA((3,))]

    def peers(self, at):
        return [{"seq": at.s + 1 - 2 * lax.rem(at.s, 2)}, {"seq": 3 - at.s}]

    def order(self, at):
        low = at.s < 2
        return jnp.where(low, 3, 0), jnp.where(low, 2, 1), at.s + 1 - 2 * lax.rem(at.s, 2), at.s

    def copy(self, at, i):
        buf, ss, rs, _ = self.bufs
        far_outer, far_inner, pair, _ = self.order(at)
        src, slot, sem, to = {
            0: (self.pick(self.src, far_outer), 0, 0, pair),
            1: (self.pick(self.src, far_inner), 1, 1, pair),
            2: (self.pick(self.src, pair), 2, 2, pair),
            3: (buf.at[5], 4, 3, 3 - at.s),
            4: (buf.at[6], 3, 4, 3 - at.s),
            5: (buf.at[4], 3, 4, pair),
        }[i]
        return remote(src, buf.at[slot], ss.at[i], rs.at[sem], {"seq": to})

    def inner(self, at):
        return (at.s == 1) | (at.s == 2)

    def load(self, at, i):
        far_outer, far_inner, _, own = self.order(at)
        j = (far_outer, far_inner, own)[i]
        return pltpu.make_async_copy(self.pick(self.src, j), self.bufs[0].at[5 + i], self.bufs[3].at[i])

    def begin(self, at, src):
        self.src = src

    def ready(self, at, i):
        inner = self.inner(at)
        if i == 0:

            @pl.when(jnp.logical_not(inner))
            def _():
                self.copy(at, 0).start()

        if i == 2:

            @pl.when(inner)
            def _():
                self.copy(at, 2).start()

        if i < 2:

            @pl.when(inner)
            def _():
                self.load(at, i).start()

        if i == 3:
            self.load(at, 2).start()

    def start(self, at, src):
        self.begin(at, src)
        for i in range(4):
            self.ready(at, i)

    def cross(self, at, i):
        buf = self.bufs[0]
        self.copy(at, i).wait_recv()
        self.load(at, i).wait()
        buf[5 + i] = (buf[5 + i].astype(f32) + buf[i].astype(f32)).astype(bf16)
        self.copy(at, 3 + i).start()

    def step(self, at, i):
        @pl.when(self.inner(at))
        def _():
            self.cross(at, i)

        @pl.when(jnp.logical_not(self.inner(at)))
        def _():
            self.copy(at, i).wait_send()
            self.copy(at, i + 1).start()

    def step3(self, at):
        @pl.when(self.inner(at))
        def _():
            self.copy(at, 3).wait_recv()
            self.copy(at, 5).start()

    def total(self, at):
        inner = self.inner(at)
        buf = self.bufs[0]
        self.load(at, 2).wait()
        self.copy(at, 2).wait()
        self.copy(at, 4).wait_recv()

        @pl.when(inner)
        def _():
            for i in (3, 4, 5):
                self.copy(at, i).wait_send()

        return buf[7].astype(f32) + buf[2].astype(f32) + buf[3].astype(f32)


class Swap:
    scratch = [pltpu.SemaphoreType.DMA] * 2

    def __init__(self, axis):
        self.axis = axis

    def partner(self, at):
        return {"narrow": 1 - at.n} if self.axis == "narrow" else {"seq": at.s + 1 - 2 * lax.rem(at.s, 2)}

    def peers(self, at):
        return [self.partner(at)]

    def start(self, at, src, dst):
        self.copy = remote(src, dst, *self.bufs, self.partner(at))
        self.copy.start()

    def finish(self):
        self.copy.wait()


class HeadGather:
    def __init__(self, S):
        self.scratch = [pltpu.SemaphoreType.DMA((S,))] * 4 + [pltpu.SemaphoreType.DMA]

    def peers(self, at):
        return [{"seq": lax.rem(at.s + k, at.S)} for k in range(1, at.S)] + [{"narrow": 1 - at.n}]

    def start(self, at, src, dst):
        ss, rs, fs, fr, ls = self.bufs
        own, other = dst.at[at.n * at.S + at.s], dst.at[(1 - at.n) * at.S + at.s]
        self.cross = remote(src.at[1 - at.n], own, ss.at[0], rs.at[0], {"narrow": 1 - at.n})
        self.cross.start()
        self.direct, self.relayed = [], []
        for k in range(1, at.S):
            to = {"seq": lax.rem(at.s + k, at.S)}
            self.direct.append(remote(src.at[at.n], own, ss.at[k], rs.at[k], to))
            self.direct[-1].start()
            self.relayed.append(remote(other, other, fs.at[k], fr.at[k], to))
        self.local = pltpu.make_async_copy(src.at[at.n], own, ls)
        self.local.start()

    def relay(self):
        self.cross.wait_recv()
        for c in self.relayed:
            c.start()

    def finish(self):
        self.cross.wait_send()
        for c in self.direct + self.relayed + [self.local]:
            c.wait()


class PlaneScatter:
    def __init__(self, block, view):
        self.view = view
        half = (block[0] // 2,) + block[1:]
        self.scratch = [pltpu.VMEM((4,) + block, bf16)] * 2 + [pltpu.VMEM((6,) + half, bf16)]
        self.scratch += [pltpu.SemaphoreType.DMA((4,))] * 3 + [pltpu.SemaphoreType.DMA((6,))] * 2

    def peers(self, at):
        return [at.near_x, at.near_y, at.sibling]

    def chips(self, at):
        return at.chip_xy, at.chip_x, at.chip_y, at.chip

    def start(self, at, src):
        self.begin(at)
        mine, ls = self.bufs[0], self.bufs[3]
        for i, chip in enumerate(self.chips(at)):
            self.hand(at, i, self.view(src, chip, 1 - at.core))
            self.local.append(pltpu.make_async_copy(self.view(src, chip, at.core), mine.at[i], ls.at[i]))
            self.local[i].start()

    def hand(self, at, i, block):
        sib, ns, nr = self.bufs[1], self.bufs[4], self.bufs[5]
        self.near.append(remote(block, sib.at[i], ns.at[i], nr.at[i], at.sibling))
        self.near[i].start()

    def begin(self, at):
        mine, sib, got, ls, ns, nr, ss, rs = self.bufs
        m = mine.shape[1] // 2
        self.local, self.near = [], []
        sent = [(0, 0, at.near_x), (0, 1, at.near_y), (1, 0, at.near_x), (2, 1, at.near_y)]
        sent += [(1, 1, at.near_x), (2, 0, at.near_y)]
        self.far = [
            remote(mine.at[i, pl.ds(h * m, m)], got.at[j], ss.at[j], rs.at[j], d) for j, (i, h, d) in enumerate(sent)
        ]

    def add(self, i):
        mine, sib = self.bufs[:2]
        self.settle(i)
        mine[i] = (mine[i].astype(f32) + sib[i].astype(f32)).astype(bf16)

    def settle(self, i):
        if self.local:
            self.local[i].wait()
            self.near[i].wait_send()
        self.near[i].wait_recv()

    def mid(self):
        self.add(0)
        self.far[0].start()
        self.far[1].start()
        self.add(1)
        self.far[2].start()
        self.add(2)
        self.far[3].start()

    def mid2(self):
        mine, _, got = self.bufs[:3]
        m = mine.shape[1] // 2
        self.far[1].wait_recv()
        mine[1, m:] = (mine[1, m:].astype(f32) + got[1].astype(f32)).astype(bf16)
        self.far[4].start()
        self.far[0].wait_recv()
        mine[2, :m] = (mine[2, :m].astype(f32) + got[0].astype(f32)).astype(bf16)
        self.far[5].start()

    def finish(self):
        mine, sib, got = self.bufs[:3]
        self.settle(3)
        total = mine[3].astype(f32) + sib[3].astype(f32)
        for i in range(2, 6):
            self.far[i].wait_recv()
        for c in self.far:
            c.wait_send()
        low = got[2].astype(f32) + got[5].astype(f32)
        high = got[3].astype(f32) + got[4].astype(f32)
        return total + jnp.concatenate([low, high], axis=0)


def greet(ids):
    barrier = pltpu.get_barrier_semaphore()
    for d in ids:
        pl.semaphore_signal(barrier, inc=1, device_id=d, device_id_type=MESH)
    pl.semaphore_wait(barrier, len(ids))


HBM = pl.BlockSpec(memory_space=pl.ANY)
VMEM = pl.BlockSpec(memory_space=pltpu.VMEM)
SMEM = pl.BlockSpec(memory_space=pltpu.SMEM)


def fused(cid, name, us, parts, body, ins, outs, scratch=(), vmem=16):
    def kernel(*refs):
        a, refs = refs[: len(ins)], refs[len(ins) :]
        b, refs = refs[: len(outs)], refs[len(outs) :]
        c, refs = refs[: len(scratch)], refs[len(scratch) :]
        for p in parts:
            p.bufs, refs = refs[: len(p.scratch)], refs[len(p.scratch) :]
        at = Place()
        greet([d for p in parts for d in p.peers(at)])
        body(at, a, b, c)

    return pl.pallas_call(
        kernel,
        out_shape=tuple(jax.ShapeDtypeStruct(s, t) for s, t, _ in outs),
        in_specs=[spec for _, spec in ins],
        out_specs=tuple(spec for _, _, spec in outs),
        scratch_shapes=list(scratch) + [s for p in parts for s in p.scratch],
        compiler_params=pltpu.CompilerParams(
            collective_id=cid, has_side_effects=True, vmem_limit_bytes=vmem << 20
        ),
        cost_estimate=pl.CostEstimate(flops=int(us * 1.1e9), bytes_accessed=0, transcendentals=0),
        name=name,
    )(*[x for x, _ in ins])


def lane_roll(x, shift):
    return pltpu.roll(x.astype(f32), shift, 1)


def half_swap(x):
    lanes = lax.broadcasted_iota(jnp.int32, (1, x.shape[1]), 1)
    return jnp.where(lax.rem(lanes, 64) < 32, pltpu.roll(x, 96, 1), pltpu.roll(x, 32, 1))


def pair_up(a, b, n):
    lanes = lax.broadcasted_iota(jnp.int32, (1, 128), 1)
    if n == 0:
        return jnp.where(lanes < 64, a.astype(f32), lane_roll(b, 64))
    return jnp.where(lanes < 64, lane_roll(a, 64), b.astype(f32))


def put_pair(ref, g, rows, n, x):
    y = pltpu.roll(x, 64, 1)
    lo = slice(0, 64) if n == 0 else slice(64, 128)
    a, b = (x, y) if n == 0 else (y, x)
    ref[g, rows, lo] = a[:, lo].astype(bf16)
    ref[g + 1, rows, lo] = b[:, lo].astype(bf16)


FAR = 2.0**30


def segment_lanes(rows, lanes, starts_ref, count):
    hit = jnp.zeros((rows.shape[0], lanes.shape[1]), f32)
    for j in range(count):
        inside = rows >= starts_ref[j]
        if j + 1 < count:
            inside = inside & (rows < starts_ref[j + 1])
        hit = hit + jnp.where((lanes == 64 + j) & inside, 1.0, 0.0)
    return hit


def key_sides(S, RB, N, nseq, starts_ref, kv_ref, ka_ref, v1_ref):
    lanes = lax.broadcasted_iota(jnp.int32, (1, 128), 1)
    iota = lax.broadcasted_iota(jnp.int32, (RB, 1), 0)

    def fill(s, _):
        for n in range(N):
            kv = kv_ref[s, n * RB : (n + 1) * RB, :]
            hot = segment_lanes((n * S + s) * RB + iota, lanes, starts_ref, nseq).astype(bf16)
            ka_ref[s, n * RB : (n + 1) * RB, :] = jnp.where(lanes < 64, kv, hot)
            v1_ref[s, n * RB : (n + 1) * RB, :] = jnp.where(lanes < 64, jnp.ones_like(kv), kv)
        return 0

    lax.fori_loop(0, S, fill, 0)


def query_side(q, n, b, RB, nseq, starts_ref):
    lanes = lax.broadcasted_iota(jnp.int32, (1, 128), 1)
    iota = lax.broadcasted_iota(jnp.int32, (RB, 1), 0)
    if n == 1:
        q = pltpu.roll(q.astype(f32), 64, 1).astype(bf16)
    others = 1.0 - segment_lanes(b * RB + iota, lanes, starts_ref, nseq)
    far = jnp.where((lanes >= 64) & (lanes < 64 + nseq), -FAR, 0.0) * others
    return jnp.where(lanes < 64, q, far.astype(bf16))


def key_block(j, S, RB):
    return lax.rem(j, S), pl.ds(pl.multiple_of((j // S) * RB, RB), RB)


def attn_fwd_body(S, RB, N, nseq, first, done, starts_ref, q_ref, kv_ref, ob_ref, res_ref, ka_ref, v1_ref, acc_ref):
    key_sides(S, RB, N, nseq, starts_ref, kv_ref, ka_ref, v1_ref)
    lanes = lax.broadcasted_iota(jnp.int32, (1, 128), 1)
    for n in range(N):

        def qblock(i, _):
            s = lax.rem(first + i, S)
            b = n * S + s
            qa = query_side(q_ref[s], n, b, RB, nseq, starts_ref)
            acc_ref[...] = jnp.zeros_like(acc_ref)

            def at(ref, j):
                a, c = key_block(j, S, RB)
                return ref[a, c, :]

            def kstep(j, _):
                e = jnp.exp2(dot(qa, at(ka_ref, j), NT))
                acc_ref[...] += dot(e.astype(bf16), at(v1_ref, j), NN)
                return 0

            lax.fori_loop(0, b, kstep, 0)
            sc = dot(qa, at(ka_ref, b), NT)
            half = RB // 2
            tri = lax.broadcasted_iota(jnp.int32, (half, half), 1) <= lax.broadcasted_iota(jnp.int32, (half, half), 0)
            v = at(v1_ref, b)
            e = jnp.where(tri, jnp.exp2(sc[:half, :half]), 0.0).astype(bf16)
            acc_ref[:half] += dot(e, v[:half], NN)
            e1 = jnp.exp2(sc[half:, :half]).astype(bf16)
            e2 = jnp.where(tri, jnp.exp2(sc[half:, half:]), 0.0).astype(bf16)
            acc_ref[half:] += dot(e1, v[:half], NN) + dot(e2, v[half:], NN)
            acc = acc_ref[...]
            inv = 1.0 / acc
            o = acc * pltpu.roll(inv, 64, 1)
            res_ref[b] = jnp.where(lanes < 64, inv, o)
            if n == 0:
                ob_ref[s, :, 0:64] = pltpu.roll(o, 64, 1)[:, 0:64].astype(bf16)
            else:
                ob_ref[s, :, 64:128] = o[:, 64:128].astype(bf16)
            done(n, s)
            return 0

        lax.fori_loop(0, S, qblock, 0)


def attn_bwd_body(
    S, RB, N, nseq, first, done, phase,
    starts_ref, q_ref, kv_ref, do_ref, res_ref, dq_ref, dkv_ref,
    ka_ref, v1_ref, qa_ref, du_ref, dq_acc, k_acc, v_acc,
):
    key_sides(S, RB, N, nseq, starts_ref, kv_ref, ka_ref, v1_ref)
    lanes = lax.broadcasted_iota(jnp.int32, (1, 128), 1)
    for n in range(N):

        def prepare(s, _):
            b = n * S + s
            do = do_ref[s].astype(f32)
            res = res_ref[b]
            if n == 0:
                do = pltpu.roll(do, 64, 1)
            du = jnp.where(lanes < 64, 0.0, do * pltpu.roll(res, 64, 1))
            delta = jnp.sum(du * res, axis=1, keepdims=True)
            hi = (-delta).astype(bf16).astype(f32)
            du_ref[b] = jnp.where(lanes == 0, hi, jnp.where(lanes == 1, -delta - hi, du)).astype(bf16)
            qa_ref[b] = query_side(q_ref[s], n, b, RB, nseq, starts_ref)
            dq_acc[b] = jnp.zeros((RB, 128), f32)
            return 0

        lax.fori_loop(0, S, prepare, 0)
    half = RB // 2
    tri = lax.broadcasted_iota(jnp.int32, (half, half), 0) <= lax.broadcasted_iota(jnp.int32, (half, half), 1)
    for n in range(N):

        def kblock(i, _):
            s = lax.rem(first + i, S)
            j = n * S + s
            key = ka_ref[s, n * RB : (n + 1) * RB, :]
            value = v1_ref[s, n * RB : (n + 1) * RB, :]
            kv = kv_ref[s, n * RB : (n + 1) * RB, :]

            def weights(k0, q0):
                qs = slice(q0, q0 + half)
                sc = dot(key[k0 : k0 + half], qa_ref[j, qs], NT)
                dp = dot(value[k0 : k0 + half], du_ref[j, qs], NT)
                e = jnp.exp2(sc)
                if k0 == q0:
                    e = jnp.where(tri, e, 0.0)
                return e.astype(bf16), (e * dp).astype(bf16)

            lo, hi = slice(0, half), slice(half, RB)
            e00, s00 = weights(0, 0)
            e01, s01 = weights(0, half)
            e11, s11 = weights(half, half)
            v_acc[lo] = dot(e00, du_ref[j, lo], NN) + dot(e01, du_ref[j, hi], NN)
            v_acc[hi] = dot(e11, du_ref[j, hi], NN)
            k_acc[lo] = dot(s00, qa_ref[j, lo], NN) + dot(s01, qa_ref[j, hi], NN)
            k_acc[hi] = dot(s11, qa_ref[j, hi], NN)
            dq_acc[j, lo] += dot(s00, kv[:half], TN)
            dq_acc[j, hi] += dot(s01, kv[:half], TN) + dot(s11, kv[half:], TN)

            def qstep(b, _):
                e = jnp.exp2(dot(key, qa_ref[b], NT))
                ds = (e * dot(value, du_ref[b], NT)).astype(bf16)
                v_acc[...] += dot(e.astype(bf16), du_ref[b], NN)
                k_acc[...] += dot(ds, qa_ref[b], NN)
                dq_acc[b] += dot(ds, kv, TN)
                return 0

            lax.fori_loop(j + 1, N * S, qstep, 0)
            whole = jnp.where(lanes < 64, k_acc[...] * math.log(2.0), v_acc[...])
            dkv_ref[s, n * RB : (n + 1) * RB, :] = whole.astype(bf16)
            done(n, s, i)
            return 0

        lax.fori_loop(0, S, kblock, 0)

        def pack(s, _):
            dq = dq_acc[n * S + s] * 0.125
            dq_ref[n, s] = jnp.where(lanes < 64, dq[:half], pltpu.roll(dq[half:], 64, 1)).astype(bf16)
            return 0

        lax.fori_loop(0, S, pack, 0)
        phase(n)


def hidden_kernel(chunks, n_ref, x_ref, dm_ref, g0, g1, g2, u0, u1, u2, m_ref, dg_ref, dp_ref):
    half = g0.shape[0]
    a = pl.ds(pl.multiple_of(n_ref[0] * half, half), half)
    part = half // 2
    b = pl.ds(pl.multiple_of((1 - n_ref[0]) * half + n_ref[1] * part, part), part)
    d = pl.ds(pl.multiple_of((1 - n_ref[0]) * half + (1 - n_ref[1]) * part, part), part)
    rows = x_ref.shape[0] // chunks
    for c in range(chunks):
        r = slice(c * rows, (c + 1) * rows)

        def product(y, w0, w1, w2):
            return dot(y[r, a], w0[...], NN) + dot(y[r, b], w1[...], NN) + dot(y[r, d], w2[...], NN)

        gate, up, dh = product(x_ref, g0, g1, g2), product(x_ref, u0, u1, u2), dm_ref[r].astype(f32)
        sig = 1.0 / (1.0 + jnp.exp(-gate))
        act = gate * sig
        m_ref[r] = (act * up).astype(bf16)
        dp_ref[r] = (dh * act).astype(bf16)
        dg_ref[r] = (dh * up * (sig + act * (1.0 - sig))).astype(bf16)


def hidden_units(n_idx, x, dm, mine, got, tile=256, chunks=3):
    R, D = x.shape
    half, H = 2 * got[0][0].shape[0], got[0][0].shape[1]
    steps = H // tile
    own = pl.BlockSpec((half, tile), lambda i, n: (0, n[0] * steps + i))
    oth = pl.BlockSpec((half // 2, tile), lambda i, n: (0, i))
    full = pl.BlockSpec((R, D), lambda i, n: (0, 0), pipeline_mode=pl.Buffered(1))
    out = pl.BlockSpec((R, tile), lambda i, n: (0, i))
    return pl.pallas_call(
        functools.partial(hidden_kernel, chunks),
        grid_spec=pltpu.PrefetchScalarGridSpec(
            num_scalar_prefetch=1,
            grid=(steps,),
            in_specs=[full, out] + [own, oth, oth] * 2,
            out_specs=[out] * 3,
        ),
        out_shape=[jax.ShapeDtypeStruct((R, H), bf16)] * 3,
        compiler_params=pltpu.CompilerParams(vmem_limit_bytes=56 << 20),
        cost_estimate=pl.CostEstimate(flops=4 * R * D * H, bytes_accessed=0, transcendentals=0),
        name="hidden",
    )(n_idx, x, dm, mine[0], *got[0], mine[1], *got[1])


def back_kernel(chunks, per, n_ref, dg, dp, g0, g1, g2, u0, u1, u2, o_ref):
    i = pl.program_id(0)
    rows = dg.shape[0] // chunks

    def go(g, u):
        for c in range(chunks):
            r = slice(c * rows, (c + 1) * rows)
            o_ref[r] = (dot(dg[r], g[...], NT) + dot(dp[r], u[...], NT)).astype(bf16)

    for which, (g, u) in enumerate(((g0, u0), (g1, u1), (g2, u2))):

        @pl.when(source_of(i, per, n_ref) == which)
        def _(g=g, u=u):
            go(g, u)


def source_of(i, per, n_ref):
    part = i % per // (per // 2)
    return jnp.where(i // per == n_ref[0], 0, jnp.where(part == n_ref[1], 1, 2))


def hidden_back(n_idx, dg, dp, mine, got, tile=256, chunks=3):
    R, H = dg.shape
    half = 2 * got[0][0].shape[0]
    per = half // tile

    def spec(which, count, column):
        def index(i, n):
            return jnp.where(source_of(i, per, n) == which, i % count, 0), column(n)

        return pl.BlockSpec((tile, H), index)

    specs = [spec(0, per, lambda n: n[0]), spec(1, per // 2, lambda n: 0), spec(2, per // 2, lambda n: 0)]
    full = pl.BlockSpec((R, H), lambda i, n: (0, 0), pipeline_mode=pl.Buffered(1))
    return pl.pallas_call(
        functools.partial(back_kernel, chunks, per),
        grid_spec=pltpu.PrefetchScalarGridSpec(
            num_scalar_prefetch=1,
            grid=(2 * per,),
            in_specs=[full, full] + specs * 2,
            out_specs=pl.BlockSpec((R, tile), lambda i, n: (0, i)),
        ),
        out_shape=jax.ShapeDtypeStruct((R, 2 * half), bf16),
        compiler_params=pltpu.CompilerParams(vmem_limit_bytes=56 << 20),
        cost_estimate=pl.CostEstimate(flops=8 * R * H * half, bytes_accessed=0, transcendentals=0),
        name="hidden_back",
    )(n_idx, dg, dp, mine[0], *got[0], mine[1], *got[1])


def by_rows(
    tokens,
    gain_attn,
    w_query,
    w_key,
    w_value,
    w_out,
    gain_ffn,
    w_gate,
    w_up,
    w_down,
    lengths,
    cotangent,
):
    f32 = jnp.float32
    bf16 = jnp.bfloat16
    tok_rows = tokens.shape[0]
    col_count = tokens.shape[1]
    all_rows = tok_rows * lax.axis_size("narrow") * lax.axis_size("seq")
    block_id = lax.axis_index(("narrow", "seq"))
    row_ids = block_id * tok_rows + jnp.arange(tok_rows, dtype=jnp.int32)
    seq_first = seq_starts(lengths, row_ids)
    lowest_key = jnp.min(seq_first)
    highest_key = block_id * tok_rows + tok_rows - 1
    full_in = lax.all_gather(tokens, "wide", axis=1, tiled=True)
    inputs = full_in.astype(f32)
    recip1 = lax.rsqrt(jnp.mean(inputs * inputs, axis=1, keepdims=True) + NORM_EPSILON)
    normed1 = (inputs * recip1 * gain_attn).astype(bf16)
    query_w, key_w, value_w, out_w = (
        lax.all_gather(w_query, ("narrow", "seq"), axis=0, tiled=True),
        lax.all_gather(w_key, ("narrow", "seq"), axis=0, tiled=True),
        lax.all_gather(w_value, ("narrow", "seq"), axis=0, tiled=True),
        lax.all_gather(w_out, ("narrow", "seq"), axis=0, tiled=True),
    )
    gate_w, up_w, down_w = (
        lax.all_gather(w_gate, "narrow", axis=0, tiled=True),
        lax.all_gather(w_up, "narrow", axis=0, tiled=True),
        lax.all_gather(w_down, "narrow", axis=0, tiled=True),
    )
    heads_kv = key_w.shape[1]
    head_dim = key_w.shape[2]
    group_size = query_w.shape[2] // head_dim
    kv_width = heads_kv * head_dim
    score_scale = 1.0 / math.sqrt(head_dim)
    cos_table, sin_table = rotation(row_ids - seq_first, head_dim)
    query_raw = jnp.einsum("td,dkc->tkc", normed1, query_w, preferred_element_type=f32)
    key_raw = jnp.einsum("td,dkc->tkc", normed1, key_w, preferred_element_type=f32)
    value_raw = jnp.einsum("td,dkc->tkc", normed1, value_w, preferred_element_type=f32)
    query_b = rotate(
        query_raw.reshape(tok_rows, heads_kv, group_size, head_dim), cos_table, sin_table
    ).astype(bf16)
    key_b = rotate(key_raw, cos_table, sin_table).astype(bf16)
    value_b = value_raw.astype(bf16)
    kv_local = jnp.concatenate(
        [key_b.reshape(tok_rows, kv_width), value_b.reshape(tok_rows, kv_width)], axis=1
    )

    def block_scores(kv_part, key_start):
        part_rows = kv_part.shape[0]
        key_part = kv_part[:, :kv_width].reshape(part_rows, heads_kv, head_dim)
        value_part = kv_part[:, kv_width:].reshape(part_rows, heads_kv, head_dim)
        raw_scores = (
            jnp.einsum("qkgh,pkh->kgqp", query_b, key_part, preferred_element_type=f32)
            * score_scale
        )
        key_rows = key_start + jnp.arange(part_rows, dtype=jnp.int32)
        causal_mask = (key_rows[None, :] >= seq_first[:, None]) & (
            key_rows[None, :] <= row_ids[:, None]
        )
        weights = jnp.where(causal_mask[None, None], jnp.exp(raw_scores), 0.0)
        return (weights, key_part, value_part)

    def forward_block(state_in, kv_part, key_start):
        summed, row_total = state_in
        weights, key_part, value_part = block_scores(kv_part, key_start)
        row_total = row_total + jnp.sum(weights, axis=3)
        summed = summed + jnp.einsum(
            "kgqp,pkh->qkgh", weights.astype(bf16), value_part, preferred_element_type=f32
        )
        return (summed, row_total)

    start_state = (
        jnp.zeros((tok_rows, heads_kv, group_size, head_dim), f32),
        jnp.zeros((heads_kv, group_size, tok_rows), f32),
    )
    summed, row_total = over_blocks(
        forward_block,
        start_state,
        lax.all_gather(kv_local, ("narrow", "seq"), axis=0, tiled=True),
        tok_rows,
        lowest_key,
        highest_key,
    )
    inv_total = 1.0 / jnp.transpose(row_total, (2, 0, 1))
    attn_out = summed * inv_total[..., None]
    attn_b = attn_out.astype(bf16).reshape(tok_rows, heads_kv, group_size * head_dim)
    branch_part = jnp.einsum("tkc,dkc->td", attn_b, out_w, preferred_element_type=f32)
    branch = lax.psum(branch_part, "wide")
    residual = inputs + branch
    recip2 = lax.rsqrt(jnp.mean(residual * residual, axis=1, keepdims=True) + NORM_EPSILON)
    normed2 = (residual * recip2 * gain_ffn).astype(bf16)
    gate_val = jnp.dot(normed2, gate_w, preferred_element_type=f32)
    up_val = jnp.dot(normed2, up_w, preferred_element_type=f32)
    sigmoid_gate = jax.nn.sigmoid(gate_val)
    hidden = (gate_val * sigmoid_gate * up_val).astype(bf16)
    down_part = jnp.einsum("tf,df->td", hidden, down_w, preferred_element_type=f32)
    down = lax.psum_scatter(
        down_part.astype(jnp.bfloat16), "wide", scatter_dimension=1, tiled=True
    ).astype(jnp.float32)
    wide_id = lax.axis_index("wide")
    local_resid = lax.dynamic_slice_in_dim(residual, wide_id * col_count, col_count, 1)
    output = (local_resid + down).astype(bf16)
    grad_full = lax.all_gather(cotangent, "wide", axis=1, tiled=True)
    grad_hidden = jnp.einsum("td,df->tf", grad_full, down_w, preferred_element_type=f32)
    silu_slope = sigmoid_gate * (1.0 + gate_val * (1.0 - sigmoid_gate))
    grad_gate_val = (grad_hidden * up_val * silu_slope).astype(bf16)
    grad_up_val = (grad_hidden * gate_val * sigmoid_gate).astype(bf16)
    dw_down = jnp.einsum("td,tf->df", grad_full, hidden, preferred_element_type=f32)
    dw_gate = jnp.einsum("td,tf->df", normed2, grad_gate_val, preferred_element_type=f32)
    dw_up = jnp.einsum("td,tf->df", normed2, grad_up_val, preferred_element_type=f32)
    dn2_part = jnp.einsum(
        "tf,df->td", grad_gate_val, gate_w, preferred_element_type=f32
    ) + jnp.einsum("tf,df->td", grad_up_val, up_w, preferred_element_type=f32)
    dn2 = lax.psum(dn2_part, "wide")
    dgain_ffn = jnp.sum(dn2 * residual * recip2, axis=0)
    scaled2 = dn2 * gain_ffn
    dresid = (
        grad_full.astype(f32)
        + recip2 * scaled2
        - residual
        * (recip2 * recip2 * recip2)
        * jnp.mean(scaled2 * residual, axis=1, keepdims=True)
    )
    dbranch = dresid.astype(bf16)
    dw_out = jnp.einsum("td,tkc->dkc", dbranch, attn_b, preferred_element_type=f32)
    grad_attn = jnp.einsum("td,dkc->tkc", dbranch, out_w, preferred_element_type=f32).reshape(
        tok_rows, heads_kv, group_size, head_dim
    )
    grad_summed = (grad_attn * inv_total[..., None]).astype(bf16)
    delta_rows = jnp.transpose(jnp.sum(grad_attn * attn_out, axis=3) * inv_total, (1, 2, 0))

    def backward_block(state_in, kv_part, key_start):
        dquery, dkv_all = state_in
        weights, key_part, value_part = block_scores(kv_part, key_start)
        part_rows = kv_part.shape[0]
        dprob = jnp.einsum("qkgh,pkh->kgqp", grad_summed, value_part, preferred_element_type=f32)
        dscore = (weights * (dprob - delta_rows[..., None])).astype(bf16)
        dquery = dquery + jnp.einsum("kgqp,pkh->qkgh", dscore, key_part, preferred_element_type=f32)
        dkey = (
            jnp.einsum("kgqp,qkgh->pkh", dscore, query_b, preferred_element_type=f32) * score_scale
        )
        dvalue = jnp.einsum(
            "kgqp,qkgh->pkh", weights.astype(bf16), grad_summed, preferred_element_type=f32
        )
        block_grad = jnp.concatenate(
            [dkey.reshape(part_rows, kv_width), dvalue.reshape(part_rows, kv_width)], axis=1
        )
        current = lax.dynamic_slice_in_dim(dkv_all, key_start, part_rows, 0)
        dkv_all = lax.dynamic_update_slice_in_dim(dkv_all, current + block_grad, key_start, 0)
        return (dquery, dkv_all)

    back_state = (
        jnp.zeros((tok_rows, heads_kv, group_size, head_dim), f32),
        jnp.zeros((all_rows, 2 * kv_width), f32),
    )
    dquery, dkv_all = over_blocks(
        backward_block,
        back_state,
        lax.all_gather(kv_local, ("narrow", "seq"), axis=0, tiled=True),
        tok_rows,
        lowest_key,
        highest_key,
    )
    dkv_own = lax.psum_scatter(
        dkv_all.astype(jnp.bfloat16), ("narrow", "seq"), scatter_dimension=0, tiled=True
    ).astype(jnp.float32)
    dquery_b = (
        unrotate(dquery * score_scale, cos_table, sin_table)
        .astype(bf16)
        .reshape(tok_rows, heads_kv, group_size * head_dim)
    )
    dkey_b = unrotate(
        dkv_own[:, :kv_width].reshape(tok_rows, heads_kv, head_dim), cos_table, sin_table
    ).astype(bf16)
    dvalue_b = dkv_own[:, kv_width:].reshape(tok_rows, heads_kv, head_dim).astype(bf16)
    dw_query = jnp.einsum("td,tkc->dkc", normed1, dquery_b, preferred_element_type=f32)
    dw_key = jnp.einsum("td,tkc->dkc", normed1, dkey_b, preferred_element_type=f32)
    dw_value = jnp.einsum("td,tkc->dkc", normed1, dvalue_b, preferred_element_type=f32)
    dn1_part = jnp.einsum("tkc,dkc->td", dquery_b, query_w, preferred_element_type=f32)
    dn1_part = dn1_part + jnp.einsum("tkc,dkc->td", dkey_b, key_w, preferred_element_type=f32)
    dn1_part = dn1_part + jnp.einsum("tkc,dkc->td", dvalue_b, value_w, preferred_element_type=f32)
    dn1 = lax.psum(dn1_part.astype(jnp.bfloat16), "wide").astype(jnp.float32)
    dgain_attn = jnp.sum(dn1 * inputs * recip1, axis=0)
    scaled1 = dn1 * gain_attn
    dinputs = (
        dresid
        + recip1 * scaled1
        - inputs * (recip1 * recip1 * recip1) * jnp.mean(scaled1 * inputs, axis=1, keepdims=True)
    )
    grad_input = lax.dynamic_slice_in_dim(dinputs, wide_id * col_count, col_count, 1).astype(bf16)
    summed_grads = (
        lax.psum_scatter(
            dgain_attn.astype(jnp.bfloat16), ("narrow", "seq"), scatter_dimension=0, tiled=True
        ).astype(jnp.float32),
        lax.psum_scatter(
            dw_query.astype(jnp.bfloat16), ("narrow", "seq"), scatter_dimension=0, tiled=True
        ).astype(jnp.float32),
        lax.psum_scatter(
            dw_key.astype(jnp.bfloat16), ("narrow", "seq"), scatter_dimension=0, tiled=True
        ).astype(jnp.float32),
        lax.psum_scatter(
            dw_value.astype(jnp.bfloat16), ("narrow", "seq"), scatter_dimension=0, tiled=True
        ).astype(jnp.float32),
        lax.psum_scatter(
            dw_out.astype(jnp.bfloat16), ("narrow", "seq"), scatter_dimension=0, tiled=True
        ).astype(jnp.float32),
        lax.psum_scatter(
            dgain_ffn.astype(jnp.bfloat16), ("narrow", "seq"), scatter_dimension=0, tiled=True
        ).astype(jnp.float32),
        lax.psum_scatter(
            dw_gate.astype(jnp.bfloat16), ("narrow", "seq"), scatter_dimension=0, tiled=True
        ).astype(jnp.float32),
        lax.psum_scatter(
            dw_up.astype(jnp.bfloat16), ("narrow", "seq"), scatter_dimension=0, tiled=True
        ).astype(jnp.float32),
        lax.psum_scatter(
            dw_down.astype(jnp.bfloat16), ("narrow", "seq"), scatter_dimension=0, tiled=True
        ).astype(jnp.float32),
    )
    return (
        output,
        grad_input,
        summed_grads[0],
        summed_grads[1],
        summed_grads[2],
        summed_grads[3],
        summed_grads[4],
        summed_grads[5],
        summed_grads[6],
        summed_grads[7],
        summed_grads[8],
    )


def by_plane(
    tokens,
    gain_attn,
    w_query,
    w_key,
    w_value,
    w_out,
    gain_ffn,
    w_gate,
    w_up,
    w_down,
    lengths,
    cotangent,
):
    N, W, S = (lax.axis_size(a) for a in ("narrow", "wide", "seq"))
    n, s = lax.axis_index("narrow"), lax.axis_index("seq")
    P8 = N * W
    RB, cols = tokens.shape
    R, D = N * RB, W * cols
    hd = w_key.shape[2]
    group = w_query.shape[2] // hd
    qw = group * hd
    rows, block = RB // W, D // (N * S)
    half_d, half_h = w_gate.shape[0], w_gate.shape[1] // N
    nseq = lengths.shape[0]
    chunk = RB // 2
    chunks = R // chunk
    fold = math.log2(math.e) / math.sqrt(hd)
    starts = jnp.cumsum(lengths) - lengths
    heads_shape, kv_shape, full_shape = (S, RB, N * hd), (S, R, 2 * hd), (R, D)
    slab_shape, own_shape = (N, S, block, half_h), (rows, D)

    def block_view(ref, chip, core):
        a, b = chip // (W // 2), lax.rem(chip, W // 2) * 2 + core
        return ref.at[pl.ds(a * RB, RB), pl.ds(b * cols, cols)]

    def row_view(ref, chip, core):
        return ref.at[chip * 2 + core]

    def to_seq():
        return Exchange(S, "seq", lambda src, j: src.at[j])

    def to_rows():
        return Exchange(N * S, "rows", lambda src, j: src.at[j])

    def to_narrow():
        return Exchange(N, "narrow", lambda src, j: src.at[j])

    def own_rows(at):
        return pl.ds(pl.multiple_of(at.n * RB + at.w * rows, rows), rows)

    def chunk_rows(c):
        k = c * chunk // RB
        return slice(c * chunk, (c + 1) * chunk), slice(c * chunk - k * RB, (c + 1) * chunk - k * RB), k

    def scale_of(x):
        return lax.rsqrt(jnp.mean(x * x, axis=1, keepdims=True) + NORM_EPSILON)

    w_mine = jnp.concatenate([w_query, w_key, w_value], axis=2).transpose(1, 0, 2)
    width = w_mine.shape[2]
    g_tok, g_w, g_wo = PlaneGather(block_view), HeadGather(S), HeadGather(S)

    def start_body(at, ins, outs, scratch):
        g_w.start(at, ins[1], outs[1])
        g_tok.start(at, ins[0], outs[0])
        g_w.relay()
        g_tok.relay()
        g_tok.relay2()
        g_tok.finish()
        g_w.finish()

    full_in, w_qkv = fused(
        1,
        "gather_start",
        55,
        [g_tok, g_w],
        start_body,
        [(tokens, HBM), (w_mine, HBM)],
        [(full_shape, bf16, HBM), ((N * S,) + w_mine.shape[1:], bf16, HBM)],
    )
    w_qkv = w_qkv.reshape(D, width)

    part_d = half_d // 2
    part_shape = (part_d, half_h)
    mine_w = [w_gate, w_up, w_down]
    n_idx = jnp.stack([n, lax.rem(s, 2)]).astype(jnp.int32)
    swaps = [Swap("narrow") for _ in range(4)]
    passes = [Swap("seq") for _ in range(4)]

    def for_partner(at, ref, start=0, size=part_d):
        rows_ = pl.ds(pl.multiple_of(lax.rem(at.s, 2) * part_d + start, size), size)
        return ref.at[rows_, pl.ds(pl.multiple_of((1 - at.n) * half_h, half_h), half_h)]

    row_ids = ((jnp.arange(N, dtype=jnp.int32) * S + s) * RB)[:, None] + jnp.arange(RB, dtype=jnp.int32)
    row_ids = row_ids.reshape(R)
    cos_table, sin_table = rotation(row_ids - seq_starts(lengths, row_ids), hd)
    cos_lanes = jnp.tile(cos_table, (1, 4))
    sin_lanes = jnp.tile(jnp.concatenate([-sin_table, sin_table], axis=1), (1, 2))

    e_q, e_kv, mv = to_seq(), Exchange(S, "seq", lambda src, j: src), Move()

    def qkv_body(at, ins, outs, scratch):
        x_ref, w_ref, gain_ref, cos_ref, sin_ref, *w_ins = ins
        q_out, kv_out, n1_out, *w_outs = outs
        n1, qs, kvs = scratch
        for sw, src, dst in zip(swaps[:2], w_ins, w_outs):
            sw.start(at, for_partner(at, src), dst)
        swaps[2].start(at, for_partner(at, w_ins[2], 0, part_d // 2), w_outs[2])
        lanes = lax.broadcasted_iota(jnp.int32, (1, 128), 1)
        for c in range(chunks):
            r, rb, k = chunk_rows(c)
            x = x_ref[r].astype(f32)
            normed = (x * scale_of(x) * gain_ref[...]).astype(bf16)
            n1[r] = normed
            qkv = dot(normed, w_ref[...], NN)
            cos, sin = cos_ref[r], sin_ref[r]
            for g in range(0, group, 2):
                y = qkv[:, g * hd : (g + 2) * hd]
                put_pair(qs, g, rb, k, (y * cos + half_swap(y) * sin) * fold)
            y = qkv[:, qw:]
            kvs[r] = jnp.where(lanes < hd, y * cos + half_swap(y) * sin, y).astype(bf16)
        e_kv.start(at, kvs, kv_out)
        e_q.start(at, qs, q_out)
        mv.start(at, n1, n1_out)
        e_kv.finish()
        e_q.finish()
        mv.finish()
        for sw in swaps[:3]:
            sw.finish()

    q_all, kv_all, normed1, *near_w = fused(
        2,
        "qkv_to_heads",
        60,
        [e_q, e_kv, mv] + swaps[:3],
        qkv_body,
        [
            (full_in, VMEM),
            (w_qkv, VMEM),
            (gain_attn[None], VMEM),
            (cos_lanes, VMEM),
            (sin_lanes, VMEM),
            (w_gate, HBM),
            (w_up, HBM),
            (w_down, HBM),
        ],
        [
            (heads_shape, bf16, HBM),
            (kv_shape, bf16, HBM),
            (full_shape, bf16, HBM),
            (part_shape, bf16, HBM),
            (part_shape, bf16, HBM),
            ((part_d // 2, half_h), bf16, HBM),
        ],
        [pltpu.VMEM(full_shape, bf16), pltpu.VMEM((group, RB, N * hd), bf16), pltpu.VMEM((R, 2 * hd), bf16)],
        40,
    )

    g_cot, st_o = PlaneGather(block_view), Stream(S)

    def forward_body(at, ins, outs, scratch):
        cot_in, w_in, wd_in, *attn_ins = ins
        grad_full, back, wo_out, near_out, res = outs
        heads, *work = scratch
        g_wo.start(at, w_in, wo_out)
        swaps[3].start(at, for_partner(at, wd_in, part_d // 2, part_d // 2), near_out)
        g_cot.start(at, cot_in, grad_full)

        def done(k, j):
            turn = lax.rem(j - at.s - 1 + 2 * S, S)
            if k == N - 1:
                st_o.send(at, heads.at[j], back.at[at.s], j)
                pl.when(turn == 1)(g_cot.relay)
                pl.when(turn == 2)(g_cot.relay2)
            else:
                pl.when(turn == 2)(g_wo.relay)

        attn_fwd_body(S, RB, N, nseq, at.s + 1, done, *attn_ins, heads, res, *work)
        st_o.finish(at, heads.at[0], back.at[at.s])
        g_cot.finish()
        g_wo.finish()
        swaps[3].finish()

    kv_scratch = pltpu.VMEM(kv_shape, bf16)
    grad_full, attn_back, w_o, near_last, attn_res = fused(
        8,
        "attn_fwd",
        48,
        [g_cot, st_o, g_wo, swaps[3]],
        forward_body,
        [
            (cotangent, HBM),
            (w_out.transpose(1, 0, 2), HBM),
            (w_down, HBM),
            (starts, SMEM),
            (q_all, VMEM),
            (kv_all, VMEM),
        ],
        [
            (full_shape, bf16, HBM),
            (heads_shape, bf16, HBM),
            ((N * S, block, qw), bf16, HBM),
            ((part_d // 2, half_h), bf16, HBM),
            ((N * S, RB, 2 * hd), f32, VMEM),
        ],
        [pltpu.VMEM(heads_shape, bf16), kv_scratch, kv_scratch, pltpu.VMEM((RB, 2 * hd), f32)],
        48,
    )

    w_o = w_o.reshape(D, qw)

    sc_a, g_n2, mv_x = PlaneScatter(own_shape, row_view), PlaneGather(row_view), Move()
    mvd = [Move() for _ in range(6)]

    def down_parts(at, wd, own_in, near0, near1, far_in):
        odd, m = lax.rem(at.s, 2), part_d // 2
        mine = own_in.at[:, pl.ds(pl.multiple_of(at.n * half_h, half_h), half_h)]

        def place(start, size):
            return wd.at[1 - at.n, pl.ds(pl.multiple_of(start, m), size)]

        parts = [(mine, wd.at[at.n]), (near0, place(odd * part_d, m)), (near1, place(odd * part_d + m, m))]
        return parts + [(far_in, place((1 - odd) * part_d, part_d))]

    def mid_body(at, ins, outs, scratch):
        heads, wo, x_in, gain_ref, dy_in, wd_in, *w_ins = ins
        attn_b, resid, n2_out, dm_out, *w_outs = outs
        part, xr, n2, dy, wd, dm = scratch
        m = part_d // 2
        passes[2].start(at, w_ins[2], w_outs[2].at[pl.ds(0, m)])
        passes[3].start(at, w_ins[3], w_outs[2].at[pl.ds(m, m)])
        for i in range(2):
            passes[i].start(at, w_ins[i], w_outs[i])
        parts = down_parts(at, wd, wd_in, w_ins[2], w_ins[3], w_outs[2])
        mvd[0].start(at, dy_in, dy)
        for i in range(3):
            mvd[1 + i].start(at, *parts[i])
        mv_x.start(at, x_in.at[own_rows(at)], xr)
        for k in range(N):
            for g in range(0, group, 2):
                pair = pair_up(heads[g], heads[g + 1], k).astype(bf16)
                attn_b[k * RB : (k + 1) * RB, g * hd : (g + 2) * hd] = pair
        for c in range(chunks):
            r = slice(c * chunk, (c + 1) * chunk)
            b = c * chunk // rows
            out = dot(attn_b[r], wo[...], NT).astype(bf16)
            part[b : b + chunk // rows] = out.reshape(chunk // rows, rows, D)
        sc_a.start(at, part)
        sc_a.mid()
        sc_a.mid2()
        passes[2].finish()
        passes[3].finish()
        mvd[4].start(at, *parts[3])
        mv_x.finish()
        h = xr[...].astype(f32) + sc_a.finish()
        resid[...] = h
        n2[...] = (h * scale_of(h) * gain_ref[...]).astype(bf16)
        g_n2.start(at, n2, n2_out)
        for mv_ in mvd[:5]:
            mv_.finish()
        quarter = half_h // 4

        def dm_tile(i, _):
            c = pl.ds(pl.multiple_of(i * quarter, quarter), quarter)
            dm[:, c] = dot(dy[...], wd.at[:, :, c][...].reshape(D, quarter), NN).astype(bf16)
            return 0

        lax.fori_loop(0, 4, dm_tile, 0)
        mvd[5].start(at, dm, dm_out)
        g_n2.relay()
        g_n2.relay2()
        g_n2.finish()
        mvd[5].finish()
        for ps in passes[:2]:
            ps.finish()

    attn_b, residual, normed2, grad_hidden, *far_w = fused(
        3,
        "attn_to_ffn",
        88,
        [sc_a, g_n2, mv_x] + passes + mvd,
        mid_body,
        [
            (attn_back, VMEM),
            (w_o, VMEM),
            (full_in, HBM),
            (gain_ffn[None], VMEM),
            (grad_full, HBM),
            (w_down, HBM),
        ]
        + [(x, HBM) for x in (*near_w, near_last)],
        [
            ((R, qw), bf16, VMEM),
            (own_shape, f32, VMEM),
            ((P8,) + own_shape, bf16, HBM),
            ((R, half_h), bf16, HBM),
        ]
        + [(part_shape, bf16, HBM)] * 3,
        [
            pltpu.VMEM((P8,) + own_shape, bf16),
            pltpu.VMEM(own_shape, bf16),
            pltpu.VMEM(own_shape, bf16),
            pltpu.VMEM(full_shape, bf16),
            pltpu.VMEM((N, half_d, half_h), bf16),
            pltpu.VMEM((R, half_h), bf16),
        ],
        60,
    )
    normed2 = normed2.reshape(full_shape)
    got_w = list(zip(near_w[:2], far_w[:2]))

    hidden, grad_gate_val, grad_up_val = hidden_units(n_idx, normed2, grad_hidden, mine_w, got_w)

    slab_block = (N, block, half_h)

    half_block = (1,) + slab_block[1:]

    def seq_sum():
        return SeqSum(slab_block, lambda src, j: src.at[:, j])

    def seq_sum_half(a):
        return SeqSum(half_block, lambda src, j: src.at[pl.ds(a, 1), j])

    sc_n, g_db = PlaneScatter(own_shape, row_view), PlaneGather(row_view)
    q_down, q_gate0 = seq_sum(), seq_sum_half(0)
    mvs, mvk, mvw = ([Move() for _ in range(i)] for i in (6, N * S, 2 * N * S))

    def tile_cols(a, j):
        return pl.ds(pl.multiple_of((a * S + j) * block, block), block)

    def ffn_body(at, ins, outs, scratch):
        dy_in, m_in, n2_in, dg_in, dp_in, resid, gain_ref, *w_ins = ins
        db_out, dresid, dgain, down_out, gate0_out, gate_out, up_out = outs
        dy, m, n2, dg, dp, down, gate, db = scratch
        for mv_, src, dst in zip(mvs, (m_in, dy_in, dg_in, dp_in), (m, dy, dg, dp)):
            mv_.start(at, src, dst)

        def side_tile(ref, t):
            r = pl.ds(pl.multiple_of((t // 2) * block, block), block)
            return ref.at[r, pl.ds(pl.multiple_of(lax.rem(t, 2) * half_h, half_h), half_h)]

        odd, per = lax.rem(at.s, 2), part_d // block
        for i, (own_w, near, far) in enumerate((w_ins[:3], w_ins[3:])):
            own_cols = pl.ds(pl.multiple_of(at.n * half_h, half_h), half_h)
            pieces = [(own_w.at[pl.ds(k * block, block), own_cols], at.n * S + k) for k in range(S)]
            for k in range(per):
                r = pl.ds(k * block, block)
                pieces.append((near.at[r], (1 - at.n) * S + odd * per + k))
                pieces.append((far.at[r], (1 - at.n) * S + (1 - odd) * per + k))
            for k, (src, t) in enumerate(pieces):
                dst = side_tile(n2, t) if i else gate.at[t // S, lax.rem(t, S)]
                mvw[i * N * S + k].start(at, src, dst)
        sc_n.begin(at)
        q_down.begin(at, down)
        q_gate0.begin(at, gate)
        mvs[0].finish()
        mvs[1].finish()

        def down_block(i):
            j = q_down.order(at)[i]
            for a in range(N):
                down[a, j] = dot(dy[:, tile_cols(a, j)], m[...], TN).astype(bf16)
            q_down.ready(at, i)

        down_block(0)
        down_block(1)
        for mv_ in mvs[2:4] + mvw:
            mv_.finish()
        mine = sc_n.bufs[0]

        def outgoing(i):
            return n2.at[pl.ds(half_d + (i % 2) * rows, rows)]

        def back_rows(i):
            r = pl.ds(pl.multiple_of(sc_n.chips(at)[i] * 2 * rows, 2 * rows), 2 * rows)

            def tile_(t, _):
                out = dot(dg[r], gate[t // S, lax.rem(t, S)], NT) + dot(dp[r], side_tile(n2, t)[...], NT)
                c = pl.ds(pl.multiple_of(t * block, block), block)
                low, high = out[:rows].astype(bf16), out[rows:].astype(bf16)
                first = at.core == 0
                mine[i, :, c] = jnp.where(first, low, high)
                outgoing(i)[:, c] = jnp.where(first, high, low)
                return 0

            lax.fori_loop(0, N * S, tile_, 0)
            sc_n.hand(at, i, outgoing(i))

        back_rows(0)
        back_rows(1)
        sc_n.near[0].wait_send()
        back_rows(2)
        sc_n.near[1].wait_send()
        back_rows(3)
        sc_n.mid()
        q_down.step(at, 0)
        sc_n.near[2].wait_send()
        sc_n.near[3].wait_send()
        mvs[4].start(at, n2_in, n2)
        down_block(2)
        sc_n.mid2()
        mvs[4].finish()
        for i in range(4):
            j = q_gate0.order(at)[i]
            gate[0, j] = dot(n2[:, tile_cols(0, j)], dg[...], TN).astype(bf16)
            q_gate0.ready(at, i)
        down_block(3)
        db[...] = dy[own_rows(at)]

        def other_tiles(j, _):
            for a in range(N):
                c = tile_cols(a, j)
                if a:
                    gate[a, j] = dot(n2[:, c], dg[...], TN).astype(bf16)
                side_tile(dy, a * S + j)[...] = dot(n2[:, c], dp[...], TN).astype(bf16)
            return 0

        lax.fori_loop(0, 2, other_tiles, 0)
        q_gate0.step(at, 0)
        lax.fori_loop(2, S, other_tiles, 0)
        mvs[5].start(at, gate, gate_out)
        for t, mv_ in enumerate(mvk):
            mv_.start(at, side_tile(dy, t), up_out.at[t // S, t % S])
        dn2 = sc_n.finish()
        h = resid[...]
        r2 = scale_of(h)
        dgain[...] = jnp.sum(dn2 * h * r2, axis=0, keepdims=True)
        scaled = dn2 * gain_ref[...]
        own = db[...].astype(f32)
        grad = own + r2 * scaled - h * (r2 * r2 * r2) * jnp.mean(scaled * h, axis=1, keepdims=True)
        dresid[...] = grad
        db[...] = grad.astype(bf16)
        g_db.start(at, db, db_out)
        q_down.step(at, 1)
        q_down.step3(at)
        q_gate0.step(at, 1)
        q_gate0.step3(at)
        g_db.relay()
        g_db.relay2()
        g_db.finish()
        down_out[...] = q_down.total(at).astype(bf16)
        gate0_out[...] = q_gate0.total(at).astype(bf16)
        for mv_ in mvs[5:] + mvk:
            mv_.finish()

    dbranch, dresid, dgain_ffn, down_own, gate_own0, dw_gate, dw_up = fused(
        4,
        "ffn_grads",
        110,
        [sc_n, g_db, q_down, q_gate0] + mvs + mvk + mvw,
        ffn_body,
        [
            (grad_full, HBM),
            (hidden, HBM),
            (normed2, HBM),
            (grad_gate_val, HBM),
            (grad_up_val, HBM),
            (residual, VMEM),
            (gain_ffn[None], VMEM),
            (w_gate, HBM),
            (got_w[0][0], HBM),
            (got_w[0][1], HBM),
            (w_up, HBM),
            (got_w[1][0], HBM),
            (got_w[1][1], HBM),
        ],
        [
            ((P8,) + own_shape, bf16, HBM),
            (own_shape, f32, VMEM),
            ((1, D), f32, VMEM),
            (slab_block, bf16, VMEM),
            (half_block, bf16, VMEM),
            (slab_shape, bf16, HBM),
            (slab_shape, bf16, HBM),
        ],
        [
            pltpu.VMEM(full_shape, bf16),
            pltpu.VMEM((R, half_h), bf16),
            pltpu.VMEM(full_shape, bf16),
            pltpu.VMEM((R, half_h), bf16),
            pltpu.VMEM((R, half_h), bf16),
            pltpu.VMEM(slab_shape, bf16),
            pltpu.VMEM(slab_shape, bf16),
            pltpu.VMEM(own_shape, bf16),
        ],
        60,
    )

    e_do, t_down = to_seq(), to_narrow()
    mvt = [Move() for _ in range(8)]
    tile = half_d // 4

    def grad_heads_body(at, ins, outs, scratch):
        db_in, w_ref, ab, down_in, m_in, wd_in, wd0_in, wd1_in, wd2_in, resid = ins
        do_out, dwo_out, y_out, down_out = outs
        db, dos, m, wd, y, dwo = scratch
        moves = [(db_in, db), (m_in, m)] + down_parts(at, wd, wd_in, wd0_in, wd1_in, wd2_in)
        for mv_, (src, dst) in zip(mvt, moves):
            mv_.start(at, src, dst)
        mvt[0].finish()
        for c in range(chunks):
            r, rb, k = chunk_rows(c)
            out = dot(db[r], w_ref[...], NN)
            for g in range(0, group, 2):
                put_pair(dos, g, rb, k, out[:, g * hd : (g + 2) * hd])
        e_do.start(at, dos, do_out)
        t_down.start(at, down_in, down_out)

        def wo_tile(p, _):
            c = pl.ds(pl.multiple_of(p * block, block), block)
            dwo[p] = dot(db[:, c], ab[...], TN).astype(bf16)
            return 0

        lax.fori_loop(0, N * S, wo_tile, 0)
        mvt[6].start(at, dwo, dwo_out)
        for mv_ in mvt[1:6]:
            mv_.finish()
        for a in range(N):

            def y_tile(i, _):
                c = pl.ds(pl.multiple_of(a * half_d + i * tile, tile), tile)
                w_tile = wd[a, pl.ds(pl.multiple_of(i * tile, tile), tile), :]
                y[:, c] = dot(m[...], w_tile, NT).astype(bf16)
                return 0

            lax.fori_loop(0, half_d // tile, y_tile, 0)
        o = own_rows(at)
        y[o] = (y[o].astype(f32) + resid[...]).astype(bf16)
        mvt[7].start(at, y, y_out)
        e_do.finish()
        t_down.finish()
        mvt[6].finish()
        mvt[7].finish()

    do_all, dw_o, down_part, traded_down = fused(
        5,
        "grad_to_heads",
        25,
        [e_do, t_down] + mvt,
        grad_heads_body,
        [
            (dbranch.reshape(full_shape), HBM),
            (w_o, VMEM),
            (attn_b, VMEM),
            (down_own, HBM),
            (hidden, HBM),
            (w_down, HBM),
            (near_w[2], HBM),
            (near_last, HBM),
            (far_w[2], HBM),
            (residual, VMEM),
        ],
        [
            (heads_shape, bf16, HBM),
            ((N * S, block, qw), bf16, HBM),
            (full_shape, bf16, HBM),
            ((N, block, half_h), bf16, HBM),
        ],
        [
            pltpu.VMEM(full_shape, bf16),
            pltpu.VMEM((group, RB, N * hd), bf16),
            pltpu.VMEM((R, half_h), bf16),
            pltpu.VMEM((N, half_d, half_h), bf16),
            pltpu.VMEM(full_shape, bf16),
            pltpu.VMEM((N * S, block, qw), bf16),
        ],
        56,
    )

    q_gate, t_up, sc_y = seq_sum_half(1), to_narrow(), PlaneScatter((RB, cols), block_view)
    st_kv, st_q = [Stream(S) for _ in range(N)], [Stream(S) for _ in range(N)]

    def backward_body(at, ins, outs, scratch):
        gate_in, up_in, y_in, *attn_ins = ins
        gate_out, up_out, out_ref, dq_all, dkv_all = outs
        dq, dkv, *work = scratch
        sc_y.start(at, y_in)
        t_up.start(at, up_in, up_out)
        q_gate.start(at, gate_in)

        def pieces(k):
            r = pl.ds(k * RB, RB)
            return (lambda j: dkv.at[j, r]), dkv_all.at[at.s, r]

        def done(k, j, turn):
            src, dst = pieces(k)
            st_kv[k].send(at, src(j), dst, j)
            if k == 0:

                @pl.when(turn == 0)
                def _():
                    sc_y.mid()
                    q_gate.step(at, 0)

                @pl.when(turn == 1)
                def _():
                    q_gate.step(at, 1)
                    q_gate.step3(at)

                pl.when(turn == 2)(sc_y.mid2)

        def phase(k):
            for j in range(S):
                st_q[k].send(at, dq.at[k, j], dq_all.at[at.s, k], j)

        attn_bwd_body(S, RB, N, nseq, at.s + 1, done, phase, *attn_ins, dq, dkv, *work)
        out_ref[...] = sc_y.finish().astype(bf16)
        gate_out[...] = q_gate.total(at).astype(bf16)
        for k in range(N):
            src, dst = pieces(k)
            st_kv[k].finish(at, src(0), dst)
            st_q[k].finish(at, dq.at[k, 0], dq_all.at[at.s, k])
        t_up.finish()

    q_scratch, acc_scratch = pltpu.VMEM((N * S, RB, 2 * hd), bf16), pltpu.VMEM((RB, 2 * hd), f32)
    gate_own1, traded_up, output, dq_all, dkv_all = fused(
        6,
        "attn_bwd",
        110,
        [q_gate, t_up, sc_y] + st_q + st_kv,
        backward_body,
        [
            (dw_gate, HBM),
            (dw_up, HBM),
            (down_part, HBM),
            (starts, SMEM),
            (q_all, VMEM),
            (kv_all, VMEM),
            (do_all, VMEM),
            (attn_res, VMEM),
        ],
        [
            (half_block, bf16, VMEM),
            (slab_shape, bf16, HBM),
            ((RB, cols), bf16, VMEM),
            ((S, N, chunk, 2 * hd), bf16, HBM),
            (kv_shape, bf16, HBM),
        ],
        [
            pltpu.VMEM((N, S, chunk, 2 * hd), bf16),
            kv_scratch,
            kv_scratch,
            kv_scratch,
            q_scratch,
            q_scratch,
            pltpu.VMEM((N * S, RB, 2 * hd), f32),
            acc_scratch,
            acc_scratch,
        ],
        60,
    )

    q_up, t_gate, e_wog, e_wq = seq_sum(), to_narrow(), to_rows(), to_rows()
    sc_1 = PlaneScatter(own_shape, row_view)
    e_in = Exchange(W, "wide", lambda src, j: src.at[:, pl.ds(pl.multiple_of(j * cols, cols), cols)])
    e_gain = Exchange(N * S * W, "all", lambda src, j: src.at[j // W])
    mvu = [Move() for _ in range(2)]

    def last_body(at, ins, outs, scratch):
        dq, dkv, gate_in0, gate_in1, down_in, dwo_in, n1_in, up_in, x_in, w_ref, cos_ref, sin_ref, dresid_ref, gain_ref, dgain_ref = ins
        gi_out, gains_out, got_wq, got_wo, gate_out, up_out, down_out = outs
        n1, dqkv, part, dwq, xr, gi, gains, gate_s, gate_r = scratch

        def widen(out, halves):
            for a in range(N):
                out[:, a * half_h : (a + 1) * half_h] = halves[a].astype(f32)

        q_up.start(at, up_in)
        mvu[0].start(at, n1_in, n1)
        mvu[1].start(at, x_in.at[own_rows(at)], xr)
        gate_s[0] = gate_in0[0]
        gate_s[1] = gate_in1[0]
        t_gate.start(at, gate_s, gate_r)
        lanes = lax.broadcasted_iota(jnp.int32, (1, 128), 1)
        for c in range(chunks):
            r, rb, k = chunk_rows(c)
            cos, sin = cos_ref[r], sin_ref[r]
            for g in range(0, group, 2):
                y = pair_up(dq[g, k], dq[g + 1, k], c % 2)
                dqkv[r, g * hd : (g + 2) * hd] = (y * cos - half_swap(y) * sin).astype(bf16)
            y = sum(dkv[i, r].astype(f32) for i in range(S))
            dqkv[r, qw:] = jnp.where(lanes < hd, y * cos - half_swap(y) * sin, y).astype(bf16)
            out = dot(dqkv[r], w_ref[...], NT).astype(bf16)
            b = c * chunk // rows
            part[b : b + chunk // rows] = out.reshape(chunk // rows, rows, D)
        sc_1.start(at, part)
        mvu[0].finish()

        def wq_tile(p, _):
            c = pl.ds(pl.multiple_of(p * block, block), block)
            dwq[p] = dot(n1[:, c], dqkv[...], TN).astype(bf16)
            return 0

        lax.fori_loop(0, N * S, wq_tile, 0)
        sc_1.mid()
        q_up.step(at, 0)
        sc_1.mid2()
        e_wq.start(at, dwq, got_wq)
        e_wog.start(at, dwo_in, got_wo)
        mvu[1].finish()
        x = xr[...].astype(f32)
        r1 = scale_of(x)
        dn1 = sc_1.finish()
        dgain = jnp.sum(dn1 * x * r1, axis=0, keepdims=True)
        dgain2 = dgain_ref[...]
        for p in range(N * S):
            for i in range(block // 128):
                c = slice(p * block + i * 128, p * block + (i + 1) * 128)
                gains[p, i : i + 1, :] = dgain[:, c]
                gains[p, block // 128 + i : block // 128 + i + 1, :] = dgain2[:, c]
        e_gain.start(at, gains, gains_out)
        scaled = dn1 * gain_ref[...]
        grad = dresid_ref[...] + r1 * scaled - x * (r1 * r1 * r1) * jnp.mean(scaled * x, axis=1, keepdims=True)
        gi[...] = grad.astype(bf16)
        e_in.start(at, gi, gi_out)
        q_up.step(at, 1)
        q_up.step3(at)
        widen(down_out, down_in)
        t_gate.finish()
        widen(gate_out, gate_r)
        widen(up_out, q_up.total(at))
        for p in (e_in, e_gain, e_wq, e_wog):
            p.finish()

    gains_shape = (N * S, 2 * block // 128, 128)
    grad_input, gains, got_wq, got_wo, gate_grad, up_grad, down_grad = fused(
        7,
        "last",
        160,
        [q_up, t_gate, e_wog, e_wq, sc_1, e_in, e_gain] + mvu,
        last_body,
        [
            (dq_all, VMEM),
            (dkv_all, VMEM),
            (gate_own0, VMEM),
            (gate_own1, VMEM),
            (traded_down, VMEM),
            (dw_o, HBM),
            (normed1, HBM),
            (traded_up, HBM),
            (full_in, HBM),
            (w_qkv, VMEM),
            (cos_lanes, VMEM),
            (sin_lanes, VMEM),
            (dresid, VMEM),
            (gain_attn[None], VMEM),
            (dgain_ffn, VMEM),
        ],
        [
            ((W, rows, cols), bf16, HBM),
            ((N * S * W,) + gains_shape[1:], f32, HBM),
            ((N * S, block, width), bf16, HBM),
            ((N * S, block, qw), bf16, HBM),
            ((block, N * half_h), f32, VMEM),
            ((block, N * half_h), f32, VMEM),
            ((block, N * half_h), f32, VMEM),
        ],
        [
            pltpu.VMEM(full_shape, bf16),
            pltpu.VMEM((R, width), bf16),
            pltpu.VMEM((P8,) + own_shape, bf16),
            pltpu.VMEM((N * S, block, width), bf16),
            pltpu.VMEM(own_shape, bf16),
            pltpu.VMEM(own_shape, bf16),
            pltpu.VMEM(gains_shape, f32),
            pltpu.VMEM(slab_block, bf16),
            pltpu.VMEM(slab_block, bf16),
        ],
        60,
    )

    def over_seq(got):
        return jnp.sum(got.reshape(N, S, *got.shape[1:]).astype(f32), axis=1)

    gains = jnp.sum(gains, axis=0).reshape(2, block)
    qkv_grads = over_seq(got_wq).transpose(1, 0, 2)
    return (
        output,
        grad_input.reshape(RB, cols),
        gains[0],
        qkv_grads[:, :, :qw],
        qkv_grads[:, :, qw : qw + hd],
        qkv_grads[:, :, qw + hd :],
        over_seq(got_wo).transpose(1, 0, 2),
        gains[1],
        gate_grad,
        up_grad,
        down_grad,
    )


def local(tokens, gain_attn, w_query, w_key, *others):
    plane = lax.axis_size("narrow") * lax.axis_size("wide")
    heads_kv = w_key.shape[1] * lax.axis_size("wide")
    group = w_query.shape[2] // w_key.shape[2]
    fits = lax.axis_size("narrow") == 2 and heads_kv == plane and group == lax.axis_size("seq")
    body = by_plane if fits and w_key.shape[2] == 64 else by_rows
    return body(tokens, gain_attn, w_query, w_key, *others)


def solution(mesh):
    return jax.shard_map(
        local,
        mesh=mesh,
        in_specs=(
            P(("narrow", "seq"), "wide"),
            P(),
            P(("narrow", "seq"), "wide", None),
            P(("narrow", "seq"), "wide", None),
            P(("narrow", "seq"), "wide", None),
            P(("narrow", "seq"), "wide", None),
            P(),
            P("narrow", "wide"),
            P("narrow", "wide"),
            P("narrow", "wide"),
            P(),
            P(("narrow", "seq"), "wide"),
        ),
        out_specs=(
            P(("narrow", "seq"), "wide"),
            P(("narrow", "seq"), "wide"),
            P(("narrow", "seq")),
            P(("narrow", "seq"), "wide", None),
            P(("narrow", "seq"), "wide", None),
            P(("narrow", "seq"), "wide", None),
            P(("narrow", "seq"), "wide", None),
            P(("narrow", "seq")),
            P(("narrow", "seq"), "wide"),
            P(("narrow", "seq"), "wide"),
            P(("narrow", "seq"), "wide"),
        ),
        check_vma=False,
    )
```

```python
import functools
import math

import jax
import jax.numpy as jnp
from jax import lax
from jax.experimental import pallas as pl
from jax.experimental.pallas import tpu as pltpu
from jax.sharding import PartitionSpec as P

f32 = jnp.float32
bf16 = jnp.bfloat16
MESH = pl.DeviceIdType.MESH
NT = (((1,), (1,)), ((), ()))
NN = (((1,), (0,)), ((), ()))
TN = (((0,), (0,)), ((), ()))

ROPE_THETA = 500000.0
ROPE_FACTOR = 32.0
LOW_FACTOR = 1.0
HIGH_FACTOR = 4.0
OLD_CONTEXT = 8192.0
NORM_EPSILON = 1e-05


def frequencies(head_dim):
    freq_index = jnp.arange(head_dim // 2, dtype=jnp.float32)
    base_freq = jnp.exp(freq_index * (-2.0 * math.log(ROPE_THETA) / head_dim))
    wavelen = 2.0 * math.pi / base_freq
    smooth = jnp.clip((OLD_CONTEXT / wavelen - LOW_FACTOR) / (HIGH_FACTOR - LOW_FACTOR), 0.0, 1.0)
    return (1.0 - smooth) * base_freq / ROPE_FACTOR + smooth * base_freq


def seq_starts(lengths, row_ids):
    seq_ends = jnp.cumsum(lengths)
    begins = seq_ends - lengths
    found_at = jnp.where(begins[None, :] <= row_ids[:, None], begins[None, :], 0)
    return jnp.max(found_at, axis=1)


def rotation(positions, head_dim):
    angles = positions.astype(jnp.float32)[:, None] * frequencies(head_dim)[None, :]
    return (jnp.cos(angles), jnp.sin(angles))


def table_shape(values, cos_table, sin_table):
    half_dim = values.shape[-1] // 2
    bcast_shape = (cos_table.shape[0],) + (1,) * (values.ndim - 2) + (half_dim,)
    return (half_dim, cos_table.reshape(bcast_shape), sin_table.reshape(bcast_shape))


def rotate(values, cos_table, sin_table):
    half_dim, cos_part, sin_part = table_shape(values, cos_table, sin_table)
    first_half = values[..., :half_dim]
    second = values[..., half_dim:]
    return jnp.concatenate(
        [first_half * cos_part - second * sin_part, second * cos_part + first_half * sin_part],
        axis=-1,
    )


def unrotate(grad_vals, cos_table, sin_table):
    half_dim, cos_part, sin_part = table_shape(grad_vals, cos_table, sin_table)
    first_half = grad_vals[..., :half_dim]
    second = grad_vals[..., half_dim:]
    return jnp.concatenate(
        [first_half * cos_part + second * sin_part, second * cos_part - first_half * sin_part],
        axis=-1,
    )


def over_blocks(block_fn, state_now, kv_piece, block_len, lowest, highest):
    piece_rows = kv_piece.shape[0]
    block_count = piece_rows // block_len

    def one_step(block_no, state_in):
        begin = block_no * block_len
        kv_part = lax.dynamic_slice_in_dim(kv_piece, block_no * block_len, block_len, 0)
        live = (begin <= highest) & (begin + block_len - 1 >= lowest)

        def compute(carried):
            return block_fn(carried, kv_part, begin)

        def skipped(carried):
            return carried

        return lax.cond(live, compute, skipped, state_in)

    return lax.fori_loop(0, block_count, one_step, state_now)


def dot(a, b, dims):
    return lax.dot_general(a, b, dims, preferred_element_type=f32)


class Place:
    def __init__(self):
        self.N, self.W, self.S = (lax.axis_size(a) for a in ("narrow", "wide", "seq"))
        self.n, self.w, self.s = (lax.axis_index(a) for a in ("narrow", "wide", "seq"))
        self.X = self.W // 2
        self.core = lax.rem(self.w, 2)
        x = self.w // 2
        self.chip, self.chip_x = self.n * self.X + x, self.n * self.X + 1 - x
        self.chip_y, self.chip_xy = (1 - self.n) * self.X + x, (1 - self.n) * self.X + 1 - x
        self.sibling = {"wide": 2 * x + 1 - self.core}
        self.near_x, self.near_y = {"wide": 2 * (1 - x) + self.core}, {"narrow": 1 - self.n}


def remote(src, dst, ss, rs, device):
    return pltpu.make_async_remote_copy(
        src_ref=src, dst_ref=dst, send_sem=ss, recv_sem=rs, device_id=device, device_id_type=MESH
    )


class Move:
    scratch = [pltpu.SemaphoreType.DMA]

    def peers(self, at):
        return []

    def start(self, at, src, dst):
        self.copy = pltpu.make_async_copy(src, dst, self.bufs[0])
        self.copy.start()

    def finish(self):
        self.copy.wait()


class PlaneGather:
    def __init__(self, view):
        self.view = view
        self.scratch = [pltpu.SemaphoreType.DMA((4,))] * 2 + [pltpu.SemaphoreType.DMA((5,))] * 2
        self.scratch += [pltpu.SemaphoreType.DMA]
        self.stage = 0

    def peers(self, at):
        return [at.near_x, at.near_y, at.sibling]

    def half(self, block, h):
        m = block.shape[0] // 2
        return block.at[pl.ds(h * m, m)]

    def start(self, at, src, dst):
        ss, rs, fs, fr, ls = self.bufs
        own = self.view(dst, at.chip, at.core)
        from_x, from_y, across = (self.view(dst, i, at.core) for i in (at.chip_x, at.chip_y, at.chip_xy))
        self.local = pltpu.make_async_copy(src, own, ls)
        sent = [(src, own, at.near_x), (src, own, at.near_y)]
        sent += [(self.half(from_x, 0), self.half(from_x, 0), at.near_y)]
        sent += [(self.half(from_y, 1), self.half(from_y, 1), at.near_x)]
        self.far = [remote(x, y, ss.at[i], rs.at[i], d) for i, (x, y, d) in enumerate(sent)]
        shared = [src, from_x, from_y, self.half(across, 0), self.half(across, 1)]
        kept = [own] + shared[1:]
        self.near = [remote(x, y, fs.at[i], fr.at[i], at.sibling) for i, (x, y) in enumerate(zip(shared, kept))]
        for copy in (*self.far[:2], self.near[0], self.local):
            copy.start()

    def relay(self):
        for i in range(2):
            self.far[i].wait_recv()
            self.far[2 + i].start()
            self.near[1 + i].start()

    def relay2(self):
        for i in range(2, 4):
            self.far[i].wait_recv()
            self.near[1 + i].start()

    def finish(self):
        self.local.wait()
        for c in self.far:
            c.wait_send()
        for c in self.near:
            c.wait()


class Exchange:
    def __init__(self, count, group, pick):
        self.count, self.group, self.pick = count, group, pick
        self.scratch = [pltpu.SemaphoreType.DMA((count,))] * 2 + [pltpu.SemaphoreType.DMA]

    def device(self, at, k):
        if self.group == "rows":
            p = lax.rem(at.n * at.S + at.s + k, at.N * at.S)
            return p, {"narrow": p // at.S, "seq": lax.rem(p, at.S)}
        if self.group == "all":
            j = lax.rem((at.n * at.S + at.s) * at.W + at.w + k, at.N * at.S * at.W)
            p = j // at.W
            return j, {"narrow": p // at.S, "seq": lax.rem(p, at.S), "wide": lax.rem(j, at.W)}
        me = {"seq": at.s, "narrow": at.n, "wide": at.w}[self.group]
        j = lax.rem(me + k, self.count)
        return j, {self.group: j}

    def peers(self, at):
        return [self.device(at, k)[1] for k in range(1, self.count)]

    def begin(self, at, src, dst):
        ss, rs, ls = self.bufs
        me = self.device(at, 0)[0]
        self.copies = [pltpu.make_async_copy(self.pick(src, me), dst.at[me], ls)]
        for k in range(1, self.count):
            j, d = self.device(at, k)
            self.copies.append(remote(self.pick(src, j), dst.at[me], ss.at[k], rs.at[k], d))

    def start(self, at, src, dst):
        self.begin(at, src, dst)
        for c in self.copies[1:] + self.copies[:1]:
            c.start()

    def finish(self):
        for c in self.copies:
            c.wait()


class Stream:
    def __init__(self, S):
        self.scratch = [pltpu.SemaphoreType.DMA((S,))] * 2 + [pltpu.SemaphoreType.DMA]

    def peers(self, at):
        return [{"seq": lax.rem(at.s + k, at.S)} for k in range(1, at.S)]

    def away(self, at, src, dst, j):
        ss, rs, _ = self.bufs
        k = lax.rem(j - at.s + at.S, at.S)
        return remote(src, dst, ss.at[k], rs.at[k], {"seq": j})

    def send(self, at, src, dst, j):
        @pl.when(j == at.s)
        def _():
            pltpu.make_async_copy(src, dst, self.bufs[2]).start()

        @pl.when(j != at.s)
        def _():
            self.away(at, src, dst, j).start()

    def finish(self, at, src, dst):
        pltpu.make_async_copy(src, dst, self.bufs[2]).wait()
        for k in range(1, at.S):
            self.away(at, src, dst, lax.rem(at.s + k, at.S)).wait()


class SeqSum:
    def __init__(self, block, pick):
        self.pick = pick
        self.scratch = [pltpu.VMEM((8,) + block, bf16)] + [pltpu.SemaphoreType.DMA((6,))] * 2
        self.scratch += [pltpu.SemaphoreType.DMA((3,))]

    def peers(self, at):
        return [{"seq": at.s + 1 - 2 * lax.rem(at.s, 2)}, {"seq": 3 - at.s}]

    def order(self, at):
        low = at.s < 2
        return jnp.where(low, 3, 0), jnp.where(low, 2, 1), at.s + 1 - 2 * lax.rem(at.s, 2), at.s

    def copy(self, at, i):
        buf, ss, rs, _ = self.bufs
        far_outer, far_inner, pair, _ = self.order(at)
        src, slot, sem, to = {
            0: (self.pick(self.src, far_outer), 0, 0, pair),
            1: (self.pick(self.src, far_inner), 1, 1, pair),
            2: (self.pick(self.src, pair), 2, 2, pair),
            3: (buf.at[5], 4, 3, 3 - at.s),
            4: (buf.at[6], 3, 4, 3 - at.s),
            5: (buf.at[4], 3, 4, pair),
        }[i]
        return remote(src, buf.at[slot], ss.at[i], rs.at[sem], {"seq": to})

    def inner(self, at):
        return (at.s == 1) | (at.s == 2)

    def load(self, at, i):
        far_outer, far_inner, _, own = self.order(at)
        j = (far_outer, far_inner, own)[i]
        return pltpu.make_async_copy(self.pick(self.src, j), self.bufs[0].at[5 + i], self.bufs[3].at[i])

    def begin(self, at, src):
        self.src = src

    def ready(self, at, i):
        inner = self.inner(at)
        if i == 0:

            @pl.when(jnp.logical_not(inner))
            def _():
                self.copy(at, 0).start()

        if i == 2:

            @pl.when(inner)
            def _():
                self.copy(at, 2).start()

        if i < 2:

            @pl.when(inner)
            def _():
                self.load(at, i).start()

        if i == 3:
            self.load(at, 2).start()

    def start(self, at, src):
        self.begin(at, src)
        for i in range(4):
            self.ready(at, i)

    def cross(self, at, i):
        buf = self.bufs[0]
        self.copy(at, i).wait_recv()
        self.load(at, i).wait()
        buf[5 + i] = (buf[5 + i].astype(f32) + buf[i].astype(f32)).astype(bf16)
        self.copy(at, 3 + i).start()

    def step(self, at, i):
        @pl.when(self.inner(at))
        def _():
            self.cross(at, i)

        @pl.when(jnp.logical_not(self.inner(at)))
        def _():
            self.copy(at, i).wait_send()
            self.copy(at, i + 1).start()

    def step3(self, at):
        @pl.when(self.inner(at))
        def _():
            self.copy(at, 3).wait_recv()
            self.copy(at, 5).start()

    def total(self, at):
        inner = self.inner(at)
        buf = self.bufs[0]
        self.load(at, 2).wait()
        self.copy(at, 2).wait()
        self.copy(at, 4).wait_recv()

        @pl.when(inner)
        def _():
            for i in (3, 4, 5):
                self.copy(at, i).wait_send()

        return buf[7].astype(f32) + buf[2].astype(f32) + buf[3].astype(f32)


class Swap:
    scratch = [pltpu.SemaphoreType.DMA] * 2

    def __init__(self, axis):
        self.axis = axis

    def partner(self, at):
        return {"narrow": 1 - at.n} if self.axis == "narrow" else {"seq": at.s + 1 - 2 * lax.rem(at.s, 2)}

    def peers(self, at):
        return [self.partner(at)]

    def start(self, at, src, dst):
        self.copy = remote(src, dst, *self.bufs, self.partner(at))
        self.copy.start()

    def finish(self):
        self.copy.wait()


class HeadGather:
    def __init__(self, S):
        self.scratch = [pltpu.SemaphoreType.DMA((S,))] * 4 + [pltpu.SemaphoreType.DMA]

    def peers(self, at):
        return [{"seq": lax.rem(at.s + k, at.S)} for k in range(1, at.S)] + [{"narrow": 1 - at.n}]

    def start(self, at, src, dst):
        ss, rs, fs, fr, ls = self.bufs
        own, other = dst.at[at.n * at.S + at.s], dst.at[(1 - at.n) * at.S + at.s]
        self.cross = remote(src.at[1 - at.n], own, ss.at[0], rs.at[0], {"narrow": 1 - at.n})
        self.cross.start()
        self.direct, self.relayed = [], []
        for k in range(1, at.S):
            to = {"seq": lax.rem(at.s + k, at.S)}
            self.direct.append(remote(src.at[at.n], own, ss.at[k], rs.at[k], to))
            self.direct[-1].start()
            self.relayed.append(remote(other, other, fs.at[k], fr.at[k], to))
        self.local = pltpu.make_async_copy(src.at[at.n], own, ls)
        self.local.start()

    def relay(self):
        self.cross.wait_recv()
        for c in self.relayed:
            c.start()

    def finish(self):
        self.cross.wait_send()
        for c in self.direct + self.relayed + [self.local]:
            c.wait()


class PlaneScatter:
    def __init__(self, block, view):
        self.view = view
        half = (block[0] // 2,) + block[1:]
        self.scratch = [pltpu.VMEM((4,) + block, bf16)] * 2 + [pltpu.VMEM((6,) + half, bf16)]
        self.scratch += [pltpu.SemaphoreType.DMA((4,))] * 3 + [pltpu.SemaphoreType.DMA((6,))] * 2

    def peers(self, at):
        return [at.near_x, at.near_y, at.sibling]

    def chips(self, at):
        return at.chip_xy, at.chip_x, at.chip_y, at.chip

    def start(self, at, src):
        self.begin(at)
        mine, ls = self.bufs[0], self.bufs[3]
        for i, chip in enumerate(self.chips(at)):
            self.hand(at, i, self.view(src, chip, 1 - at.core))
            self.local.append(pltpu.make_async_copy(self.view(src, chip, at.core), mine.at[i], ls.at[i]))
            self.local[i].start()

    def hand(self, at, i, block):
        sib, ns, nr = self.bufs[1], self.bufs[4], self.bufs[5]
        self.near.append(remote(block, sib.at[i], ns.at[i], nr.at[i], at.sibling))
        self.near[i].start()

    def begin(self, at):
        mine, sib, got, ls, ns, nr, ss, rs = self.bufs
        m = mine.shape[1] // 2
        self.local, self.near = [], []
        sent = [(0, 0, at.near_x), (0, 1, at.near_y), (1, 0, at.near_x), (2, 1, at.near_y)]
        sent += [(1, 1, at.near_x), (2, 0, at.near_y)]
        self.far = [
            remote(mine.at[i, pl.ds(h * m, m)], got.at[j], ss.at[j], rs.at[j], d) for j, (i, h, d) in enumerate(sent)
        ]

    def add(self, i):
        mine, sib = self.bufs[:2]
        self.settle(i)
        mine[i] = (mine[i].astype(f32) + sib[i].astype(f32)).astype(bf16)

    def settle(self, i):
        if self.local:
            self.local[i].wait()
            self.near[i].wait_send()
        self.near[i].wait_recv()

    def mid(self):
        self.add(0)
        self.far[0].start()
        self.far[1].start()
        self.add(1)
        self.far[2].start()
        self.add(2)
        self.far[3].start()

    def mid2(self):
        mine, _, got = self.bufs[:3]
        m = mine.shape[1] // 2
        self.far[1].wait_recv()
        mine[1, m:] = (mine[1, m:].astype(f32) + got[1].astype(f32)).astype(bf16)
        self.far[4].start()
        self.far[0].wait_recv()
        mine[2, :m] = (mine[2, :m].astype(f32) + got[0].astype(f32)).astype(bf16)
        self.far[5].start()

    def finish(self):
        mine, sib, got = self.bufs[:3]
        self.settle(3)
        total = mine[3].astype(f32) + sib[3].astype(f32)
        for i in range(2, 6):
            self.far[i].wait_recv()
        for c in self.far:
            c.wait_send()
        low = got[2].astype(f32) + got[5].astype(f32)
        high = got[3].astype(f32) + got[4].astype(f32)
        return total + jnp.concatenate([low, high], axis=0)


def greet(ids):
    barrier = pltpu.get_barrier_semaphore()
    for d in ids:
        pl.semaphore_signal(barrier, inc=1, device_id=d, device_id_type=MESH)
    pl.semaphore_wait(barrier, len(ids))


HBM = pl.BlockSpec(memory_space=pl.ANY)
VMEM = pl.BlockSpec(memory_space=pltpu.VMEM)
SMEM = pl.BlockSpec(memory_space=pltpu.SMEM)


def fused(cid, name, us, parts, body, ins, outs, scratch=(), vmem=16):
    def kernel(*refs):
        a, refs = refs[: len(ins)], refs[len(ins) :]
        b, refs = refs[: len(outs)], refs[len(outs) :]
        c, refs = refs[: len(scratch)], refs[len(scratch) :]
        for p in parts:
            p.bufs, refs = refs[: len(p.scratch)], refs[len(p.scratch) :]
        at = Place()
        greet([d for p in parts for d in p.peers(at)])
        body(at, a, b, c)

    return pl.pallas_call(
        kernel,
        out_shape=tuple(jax.ShapeDtypeStruct(s, t) for s, t, _ in outs),
        in_specs=[spec for _, spec in ins],
        out_specs=tuple(spec for _, _, spec in outs),
        scratch_shapes=list(scratch) + [s for p in parts for s in p.scratch],
        compiler_params=pltpu.CompilerParams(
            collective_id=cid, has_side_effects=True, vmem_limit_bytes=vmem << 20
        ),
        cost_estimate=pl.CostEstimate(flops=int(us * 1.1e9), bytes_accessed=0, transcendentals=0),
        name=name,
    )(*[x for x, _ in ins])


def lane_roll(x, shift):
    return pltpu.roll(x.astype(f32), shift, 1)


def half_swap(x):
    lanes = lax.broadcasted_iota(jnp.int32, (1, x.shape[1]), 1)
    return jnp.where(lax.rem(lanes, 64) < 32, pltpu.roll(x, 96, 1), pltpu.roll(x, 32, 1))


def pair_up(a, b, n):
    lanes = lax.broadcasted_iota(jnp.int32, (1, 128), 1)
    if n == 0:
        return jnp.where(lanes < 64, a.astype(f32), lane_roll(b, 64))
    return jnp.where(lanes < 64, lane_roll(a, 64), b.astype(f32))


def put_pair(ref, g, rows, n, x):
    y = pltpu.roll(x, 64, 1)
    lo = slice(0, 64) if n == 0 else slice(64, 128)
    a, b = (x, y) if n == 0 else (y, x)
    ref[g, rows, lo] = a[:, lo].astype(bf16)
    ref[g + 1, rows, lo] = b[:, lo].astype(bf16)


FAR = 2.0**30


def segment_lanes(rows, lanes, starts_ref, count):
    hit = jnp.zeros((rows.shape[0], lanes.shape[1]), f32)
    for j in range(count):
        inside = rows >= starts_ref[j]
        if j + 1 < count:
            inside = inside & (rows < starts_ref[j + 1])
        hit = hit + jnp.where((lanes == 64 + j) & inside, 1.0, 0.0)
    return hit


def key_sides(S, RB, N, nseq, starts_ref, kv_ref, ka_ref, v1_ref):
    lanes = lax.broadcasted_iota(jnp.int32, (1, 128), 1)
    iota = lax.broadcasted_iota(jnp.int32, (RB, 1), 0)

    def fill(s, _):
        for n in range(N):
            kv = kv_ref[s, n * RB : (n + 1) * RB, :]
            hot = segment_lanes((n * S + s) * RB + iota, lanes, starts_ref, nseq).astype(bf16)
            ka_ref[s, n * RB : (n + 1) * RB, :] = jnp.where(lanes < 64, kv, hot)
            v1_ref[s, n * RB : (n + 1) * RB, :] = jnp.where(lanes < 64, jnp.ones_like(kv), kv)
        return 0

    lax.fori_loop(0, S, fill, 0)


def query_side(q, n, b, RB, nseq, starts_ref):
    lanes = lax.broadcasted_iota(jnp.int32, (1, 128), 1)
    iota = lax.broadcasted_iota(jnp.int32, (RB, 1), 0)
    if n == 1:
        q = pltpu.roll(q.astype(f32), 64, 1).astype(bf16)
    others = 1.0 - segment_lanes(b * RB + iota, lanes, starts_ref, nseq)
    far = jnp.where((lanes >= 64) & (lanes < 64 + nseq), -FAR, 0.0) * others
    return jnp.where(lanes < 64, q, far.astype(bf16))


def key_block(j, S, RB):
    return lax.rem(j, S), pl.ds(pl.multiple_of((j // S) * RB, RB), RB)


def attn_fwd_body(S, RB, N, nseq, first, done, starts_ref, q_ref, kv_ref, ob_ref, res_ref, ka_ref, v1_ref, acc_ref):
    key_sides(S, RB, N, nseq, starts_ref, kv_ref, ka_ref, v1_ref)
    lanes = lax.broadcasted_iota(jnp.int32, (1, 128), 1)
    for n in range(N):

        def qblock(i, _):
            s = lax.rem(first + i, S)
            b = n * S + s
            qa = query_side(q_ref[s], n, b, RB, nseq, starts_ref)
            acc_ref[...] = jnp.zeros_like(acc_ref)

            def at(ref, j):
                a, c = key_block(j, S, RB)
                return ref[a, c, :]

            def kstep(j, _):
                e = jnp.exp2(dot(qa, at(ka_ref, j), NT))
                acc_ref[...] += dot(e.astype(bf16), at(v1_ref, j), NN)
                return 0

            lax.fori_loop(0, b, kstep, 0)
            sc = dot(qa, at(ka_ref, b), NT)
            half = RB // 2
            tri = lax.broadcasted_iota(jnp.int32, (half, half), 1) <= lax.broadcasted_iota(jnp.int32, (half, half), 0)
            v = at(v1_ref, b)
            e = jnp.where(tri, jnp.exp2(sc[:half, :half]), 0.0).astype(bf16)
            acc_ref[:half] += dot(e, v[:half], NN)
            e1 = jnp.exp2(sc[half:, :half]).astype(bf16)
            e2 = jnp.where(tri, jnp.exp2(sc[half:, half:]), 0.0).astype(bf16)
            acc_ref[half:] += dot(e1, v[:half], NN) + dot(e2, v[half:], NN)
            acc = acc_ref[...]
            inv = 1.0 / acc
            o = acc * pltpu.roll(inv, 64, 1)
            res_ref[b] = jnp.where(lanes < 64, inv, o)
            if n == 0:
                ob_ref[s, :, 0:64] = pltpu.roll(o, 64, 1)[:, 0:64].astype(bf16)
            else:
                ob_ref[s, :, 64:128] = o[:, 64:128].astype(bf16)
            done(n, s)
            return 0

        lax.fori_loop(0, S, qblock, 0)


def attn_bwd_body(
    S, RB, N, nseq, first, done, phase,
    starts_ref, q_ref, kv_ref, do_ref, res_ref, dq_ref, dkv_ref,
    ka_ref, v1_ref, qa_ref, du_ref, dq_acc, k_acc, v_acc,
):
    key_sides(S, RB, N, nseq, starts_ref, kv_ref, ka_ref, v1_ref)
    lanes = lax.broadcasted_iota(jnp.int32, (1, 128), 1)
    for n in range(N):

        def prepare(s, _):
            b = n * S + s
            do = do_ref[s].astype(f32)
            res = res_ref[b]
            if n == 0:
                do = pltpu.roll(do, 64, 1)
            du = jnp.where(lanes < 64, 0.0, do * pltpu.roll(res, 64, 1))
            delta = jnp.sum(du * res, axis=1, keepdims=True)
            hi = (-delta).astype(bf16).astype(f32)
            du_ref[b] = jnp.where(lanes == 0, hi, jnp.where(lanes == 1, -delta - hi, du)).astype(bf16)
            qa_ref[b] = query_side(q_ref[s], n, b, RB, nseq, starts_ref)
            dq_acc[b] = jnp.zeros((RB, 128), f32)
            return 0

        lax.fori_loop(0, S, prepare, 0)
    half = RB // 2
    tri = lax.broadcasted_iota(jnp.int32, (half, half), 0) <= lax.broadcasted_iota(jnp.int32, (half, half), 1)
    for n in range(N):

        def kblock(i, _):
            s = lax.rem(first + i, S)
            j = n * S + s
            key = ka_ref[s, n * RB : (n + 1) * RB, :]
            value = v1_ref[s, n * RB : (n + 1) * RB, :]
            kv = kv_ref[s, n * RB : (n + 1) * RB, :]

            def weights(k0, q0):
                qs = slice(q0, q0 + half)
                sc = dot(key[k0 : k0 + half], qa_ref[j, qs], NT)
                dp = dot(value[k0 : k0 + half], du_ref[j, qs], NT)
                e = jnp.exp2(sc)
                if k0 == q0:
                    e = jnp.where(tri, e, 0.0)
                return e.astype(bf16), (e * dp).astype(bf16)

            lo, hi = slice(0, half), slice(half, RB)
            e00, s00 = weights(0, 0)
            e01, s01 = weights(0, half)
            e11, s11 = weights(half, half)
            v_acc[lo] = dot(e00, du_ref[j, lo], NN) + dot(e01, du_ref[j, hi], NN)
            v_acc[hi] = dot(e11, du_ref[j, hi], NN)
            k_acc[lo] = dot(s00, qa_ref[j, lo], NN) + dot(s01, qa_ref[j, hi], NN)
            k_acc[hi] = dot(s11, qa_ref[j, hi], NN)
            dq_acc[j, lo] += dot(s00, kv[:half], TN)
            dq_acc[j, hi] += dot(s01, kv[:half], TN) + dot(s11, kv[half:], TN)

            def qstep(b, _):
                e = jnp.exp2(dot(key, qa_ref[b], NT))
                ds = (e * dot(value, du_ref[b], NT)).astype(bf16)
                v_acc[...] += dot(e.astype(bf16), du_ref[b], NN)
                k_acc[...] += dot(ds, qa_ref[b], NN)
                dq_acc[b] += dot(ds, kv, TN)
                return 0

            lax.fori_loop(j + 1, N * S, qstep, 0)
            whole = jnp.where(lanes < 64, k_acc[...] * math.log(2.0), v_acc[...])
            dkv_ref[s, n * RB : (n + 1) * RB, :] = whole.astype(bf16)
            done(n, s, i)
            return 0

        lax.fori_loop(0, S, kblock, 0)

        def pack(s, _):
            dq = dq_acc[n * S + s] * 0.125
            dq_ref[n, s] = jnp.where(lanes < 64, dq[:half], pltpu.roll(dq[half:], 64, 1)).astype(bf16)
            return 0

        lax.fori_loop(0, S, pack, 0)
        phase(n)


def hidden_kernel(chunks, n_ref, x_ref, dm_ref, g0, g1, g2, u0, u1, u2, m_ref, dg_ref, dp_ref):
    half = g0.shape[0]
    a = pl.ds(pl.multiple_of(n_ref[0] * half, half), half)
    part = half // 2
    b = pl.ds(pl.multiple_of((1 - n_ref[0]) * half + n_ref[1] * part, part), part)
    d = pl.ds(pl.multiple_of((1 - n_ref[0]) * half + (1 - n_ref[1]) * part, part), part)
    rows = x_ref.shape[0] // chunks
    for c in range(chunks):
        r = slice(c * rows, (c + 1) * rows)

        def product(y, w0, w1, w2):
            return dot(y[r, a], w0[...], NN) + dot(y[r, b], w1[...], NN) + dot(y[r, d], w2[...], NN)

        gate, up, dh = product(x_ref, g0, g1, g2), product(x_ref, u0, u1, u2), dm_ref[r].astype(f32)
        sig = 1.0 / (1.0 + jnp.exp(-gate))
        act = gate * sig
        m_ref[r] = (act * up).astype(bf16)
        dp_ref[r] = (dh * act).astype(bf16)
        dg_ref[r] = (dh * up * (sig + act * (1.0 - sig))).astype(bf16)


def hidden_units(n_idx, x, dm, mine, got, tile=256, chunks=3):
    R, D = x.shape
    half, H = 2 * got[0][0].shape[0], got[0][0].shape[1]
    steps = H // tile
    own = pl.BlockSpec((half, tile), lambda i, n: (0, n[0] * steps + i))
    oth = pl.BlockSpec((half // 2, tile), lambda i, n: (0, i))
    full = pl.BlockSpec((R, D), lambda i, n: (0, 0), pipeline_mode=pl.Buffered(1))
    out = pl.BlockSpec((R, tile), lambda i, n: (0, i))
    return pl.pallas_call(
        functools.partial(hidden_kernel, chunks),
        grid_spec=pltpu.PrefetchScalarGridSpec(
            num_scalar_prefetch=1,
            grid=(steps,),
            in_specs=[full, out] + [own, oth, oth] * 2,
            out_specs=[out] * 3,
        ),
        out_shape=[jax.ShapeDtypeStruct((R, H), bf16)] * 3,
        compiler_params=pltpu.CompilerParams(vmem_limit_bytes=56 << 20),
        cost_estimate=pl.CostEstimate(flops=4 * R * D * H, bytes_accessed=0, transcendentals=0),
        name="hidden",
    )(n_idx, x, dm, mine[0], *got[0], mine[1], *got[1])


def back_kernel(chunks, per, n_ref, dg, dp, g0, g1, g2, u0, u1, u2, o_ref):
    i = pl.program_id(0)
    rows = dg.shape[0] // chunks

    def go(g, u):
        for c in range(chunks):
            r = slice(c * rows, (c + 1) * rows)
            o_ref[r] = (dot(dg[r], g[...], NT) + dot(dp[r], u[...], NT)).astype(bf16)

    for which, (g, u) in enumerate(((g0, u0), (g1, u1), (g2, u2))):

        @pl.when(source_of(i, per, n_ref) == which)
        def _(g=g, u=u):
            go(g, u)


def source_of(i, per, n_ref):
    part = i % per // (per // 2)
    return jnp.where(i // per == n_ref[0], 0, jnp.where(part == n_ref[1], 1, 2))


def hidden_back(n_idx, dg, dp, mine, got, tile=256, chunks=3):
    R, H = dg.shape
    half = 2 * got[0][0].shape[0]
    per = half // tile

    def spec(which, count, column):
        def index(i, n):
            return jnp.where(source_of(i, per, n) == which, i % count, 0), column(n)

        return pl.BlockSpec((tile, H), index)

    specs = [spec(0, per, lambda n: n[0]), spec(1, per // 2, lambda n: 0), spec(2, per // 2, lambda n: 0)]
    full = pl.BlockSpec((R, H), lambda i, n: (0, 0), pipeline_mode=pl.Buffered(1))
    return pl.pallas_call(
        functools.partial(back_kernel, chunks, per),
        grid_spec=pltpu.PrefetchScalarGridSpec(
            num_scalar_prefetch=1,
            grid=(2 * per,),
            in_specs=[full, full] + specs * 2,
            out_specs=pl.BlockSpec((R, tile), lambda i, n: (0, i)),
        ),
        out_shape=jax.ShapeDtypeStruct((R, 2 * half), bf16),
        compiler_params=pltpu.CompilerParams(vmem_limit_bytes=56 << 20),
        cost_estimate=pl.CostEstimate(flops=8 * R * H * half, bytes_accessed=0, transcendentals=0),
        name="hidden_back",
    )(n_idx, dg, dp, mine[0], *got[0], mine[1], *got[1])


def by_rows(
    tokens,
    gain_attn,
    w_query,
    w_key,
    w_value,
    w_out,
    gain_ffn,
    w_gate,
    w_up,
    w_down,
    lengths,
    cotangent,
):
    f32 = jnp.float32
    bf16 = jnp.bfloat16
    tok_rows = tokens.shape[0]
    col_count = tokens.shape[1]
    all_rows = tok_rows * lax.axis_size("narrow") * lax.axis_size("seq")
    block_id = lax.axis_index(("narrow", "seq"))
    row_ids = block_id * tok_rows + jnp.arange(tok_rows, dtype=jnp.int32)
    seq_first = seq_starts(lengths, row_ids)
    lowest_key = jnp.min(seq_first)
    highest_key = block_id * tok_rows + tok_rows - 1
    full_in = lax.all_gather(tokens, "wide", axis=1, tiled=True)
    inputs = full_in.astype(f32)
    recip1 = lax.rsqrt(jnp.mean(inputs * inputs, axis=1, keepdims=True) + NORM_EPSILON)
    normed1 = (inputs * recip1 * gain_attn).astype(bf16)
    query_w, key_w, value_w, out_w = (
        lax.all_gather(w_query, ("narrow", "seq"), axis=0, tiled=True),
        lax.all_gather(w_key, ("narrow", "seq"), axis=0, tiled=True),
        lax.all_gather(w_value, ("narrow", "seq"), axis=0, tiled=True),
        lax.all_gather(w_out, ("narrow", "seq"), axis=0, tiled=True),
    )
    gate_w, up_w, down_w = (
        lax.all_gather(w_gate, "narrow", axis=0, tiled=True),
        lax.all_gather(w_up, "narrow", axis=0, tiled=True),
        lax.all_gather(w_down, "narrow", axis=0, tiled=True),
    )
    heads_kv = key_w.shape[1]
    head_dim = key_w.shape[2]
    group_size = query_w.shape[2] // head_dim
    kv_width = heads_kv * head_dim
    score_scale = 1.0 / math.sqrt(head_dim)
    cos_table, sin_table = rotation(row_ids - seq_first, head_dim)
    query_raw = jnp.einsum("td,dkc->tkc", normed1, query_w, preferred_element_type=f32)
    key_raw = jnp.einsum("td,dkc->tkc", normed1, key_w, preferred_element_type=f32)
    value_raw = jnp.einsum("td,dkc->tkc", normed1, value_w, preferred_element_type=f32)
    query_b = rotate(
        query_raw.reshape(tok_rows, heads_kv, group_size, head_dim), cos_table, sin_table
    ).astype(bf16)
    key_b = rotate(key_raw, cos_table, sin_table).astype(bf16)
    value_b = value_raw.astype(bf16)
    kv_local = jnp.concatenate(
        [key_b.reshape(tok_rows, kv_width), value_b.reshape(tok_rows, kv_width)], axis=1
    )

    def block_scores(kv_part, key_start):
        part_rows = kv_part.shape[0]
        key_part = kv_part[:, :kv_width].reshape(part_rows, heads_kv, head_dim)
        value_part = kv_part[:, kv_width:].reshape(part_rows, heads_kv, head_dim)
        raw_scores = (
            jnp.einsum("qkgh,pkh->kgqp", query_b, key_part, preferred_element_type=f32)
            * score_scale
        )
        key_rows = key_start + jnp.arange(part_rows, dtype=jnp.int32)
        causal_mask = (key_rows[None, :] >= seq_first[:, None]) & (
            key_rows[None, :] <= row_ids[:, None]
        )
        weights = jnp.where(causal_mask[None, None], jnp.exp(raw_scores), 0.0)
        return (weights, key_part, value_part)

    def forward_block(state_in, kv_part, key_start):
        summed, row_total = state_in
        weights, key_part, value_part = block_scores(kv_part, key_start)
        row_total = row_total + jnp.sum(weights, axis=3)
        summed = summed + jnp.einsum(
            "kgqp,pkh->qkgh", weights.astype(bf16), value_part, preferred_element_type=f32
        )
        return (summed, row_total)

    start_state = (
        jnp.zeros((tok_rows, heads_kv, group_size, head_dim), f32),
        jnp.zeros((heads_kv, group_size, tok_rows), f32),
    )
    summed, row_total = over_blocks(
        forward_block,
        start_state,
        lax.all_gather(kv_local, ("narrow", "seq"), axis=0, tiled=True),
        tok_rows,
        lowest_key,
        highest_key,
    )
    inv_total = 1.0 / jnp.transpose(row_total, (2, 0, 1))
    attn_out = summed * inv_total[..., None]
    attn_b = attn_out.astype(bf16).reshape(tok_rows, heads_kv, group_size * head_dim)
    branch_part = jnp.einsum("tkc,dkc->td", attn_b, out_w, preferred_element_type=f32)
    branch = lax.psum(branch_part, "wide")
    residual = inputs + branch
    recip2 = lax.rsqrt(jnp.mean(residual * residual, axis=1, keepdims=True) + NORM_EPSILON)
    normed2 = (residual * recip2 * gain_ffn).astype(bf16)
    gate_val = jnp.dot(normed2, gate_w, preferred_element_type=f32)
    up_val = jnp.dot(normed2, up_w, preferred_element_type=f32)
    sigmoid_gate = jax.nn.sigmoid(gate_val)
    hidden = (gate_val * sigmoid_gate * up_val).astype(bf16)
    down_part = jnp.einsum("tf,df->td", hidden, down_w, preferred_element_type=f32)
    down = lax.psum_scatter(
        down_part.astype(jnp.bfloat16), "wide", scatter_dimension=1, tiled=True
    ).astype(jnp.float32)
    wide_id = lax.axis_index("wide")
    local_resid = lax.dynamic_slice_in_dim(residual, wide_id * col_count, col_count, 1)
    output = (local_resid + down).astype(bf16)
    grad_full = lax.all_gather(cotangent, "wide", axis=1, tiled=True)
    grad_hidden = jnp.einsum("td,df->tf", grad_full, down_w, preferred_element_type=f32)
    silu_slope = sigmoid_gate * (1.0 + gate_val * (1.0 - sigmoid_gate))
    grad_gate_val = (grad_hidden * up_val * silu_slope).astype(bf16)
    grad_up_val = (grad_hidden * gate_val * sigmoid_gate).astype(bf16)
    dw_down = jnp.einsum("td,tf->df", grad_full, hidden, preferred_element_type=f32)
    dw_gate = jnp.einsum("td,tf->df", normed2, grad_gate_val, preferred_element_type=f32)
    dw_up = jnp.einsum("td,tf->df", normed2, grad_up_val, preferred_element_type=f32)
    dn2_part = jnp.einsum(
        "tf,df->td", grad_gate_val, gate_w, preferred_element_type=f32
    ) + jnp.einsum("tf,df->td", grad_up_val, up_w, preferred_element_type=f32)
    dn2 = lax.psum(dn2_part, "wide")
    dgain_ffn = jnp.sum(dn2 * residual * recip2, axis=0)
    scaled2 = dn2 * gain_ffn
    dresid = (
        grad_full.astype(f32)
        + recip2 * scaled2
        - residual
        * (recip2 * recip2 * recip2)
        * jnp.mean(scaled2 * residual, axis=1, keepdims=True)
    )
    dbranch = dresid.astype(bf16)
    dw_out = jnp.einsum("td,tkc->dkc", dbranch, attn_b, preferred_element_type=f32)
    grad_attn = jnp.einsum("td,dkc->tkc", dbranch, out_w, preferred_element_type=f32).reshape(
        tok_rows, heads_kv, group_size, head_dim
    )
    grad_summed = (grad_attn * inv_total[..., None]).astype(bf16)
    delta_rows = jnp.transpose(jnp.sum(grad_attn * attn_out, axis=3) * inv_total, (1, 2, 0))

    def backward_block(state_in, kv_part, key_start):
        dquery, dkv_all = state_in
        weights, key_part, value_part = block_scores(kv_part, key_start)
        part_rows = kv_part.shape[0]
        dprob = jnp.einsum("qkgh,pkh->kgqp", grad_summed, value_part, preferred_element_type=f32)
        dscore = (weights * (dprob - delta_rows[..., None])).astype(bf16)
        dquery = dquery + jnp.einsum("kgqp,pkh->qkgh", dscore, key_part, preferred_element_type=f32)
        dkey = (
            jnp.einsum("kgqp,qkgh->pkh", dscore, query_b, preferred_element_type=f32) * score_scale
        )
        dvalue = jnp.einsum(
            "kgqp,qkgh->pkh", weights.astype(bf16), grad_summed, preferred_element_type=f32
        )
        block_grad = jnp.concatenate(
            [dkey.reshape(part_rows, kv_width), dvalue.reshape(part_rows, kv_width)], axis=1
        )
        current = lax.dynamic_slice_in_dim(dkv_all, key_start, part_rows, 0)
        dkv_all = lax.dynamic_update_slice_in_dim(dkv_all, current + block_grad, key_start, 0)
        return (dquery, dkv_all)

    back_state = (
        jnp.zeros((tok_rows, heads_kv, group_size, head_dim), f32),
        jnp.zeros((all_rows, 2 * kv_width), f32),
    )
    dquery, dkv_all = over_blocks(
        backward_block,
        back_state,
        lax.all_gather(kv_local, ("narrow", "seq"), axis=0, tiled=True),
        tok_rows,
        lowest_key,
        highest_key,
    )
    dkv_own = lax.psum_scatter(
        dkv_all.astype(jnp.bfloat16), ("narrow", "seq"), scatter_dimension=0, tiled=True
    ).astype(jnp.float32)
    dquery_b = (
        unrotate(dquery * score_scale, cos_table, sin_table)
        .astype(bf16)
        .reshape(tok_rows, heads_kv, group_size * head_dim)
    )
    dkey_b = unrotate(
        dkv_own[:, :kv_width].reshape(tok_rows, heads_kv, head_dim), cos_table, sin_table
    ).astype(bf16)
    dvalue_b = dkv_own[:, kv_width:].reshape(tok_rows, heads_kv, head_dim).astype(bf16)
    dw_query = jnp.einsum("td,tkc->dkc", normed1, dquery_b, preferred_element_type=f32)
    dw_key = jnp.einsum("td,tkc->dkc", normed1, dkey_b, preferred_element_type=f32)
    dw_value = jnp.einsum("td,tkc->dkc", normed1, dvalue_b, preferred_element_type=f32)
    dn1_part = jnp.einsum("tkc,dkc->td", dquery_b, query_w, preferred_element_type=f32)
    dn1_part = dn1_part + jnp.einsum("tkc,dkc->td", dkey_b, key_w, preferred_element_type=f32)
    dn1_part = dn1_part + jnp.einsum("tkc,dkc->td", dvalue_b, value_w, preferred_element_type=f32)
    dn1 = lax.psum(dn1_part.astype(jnp.bfloat16), "wide").astype(jnp.float32)
    dgain_attn = jnp.sum(dn1 * inputs * recip1, axis=0)
    scaled1 = dn1 * gain_attn
    dinputs = (
        dresid
        + recip1 * scaled1
        - inputs * (recip1 * recip1 * recip1) * jnp.mean(scaled1 * inputs, axis=1, keepdims=True)
    )
    grad_input = lax.dynamic_slice_in_dim(dinputs, wide_id * col_count, col_count, 1).astype(bf16)
    summed_grads = (
        lax.psum_scatter(
            dgain_attn.astype(jnp.bfloat16), ("narrow", "seq"), scatter_dimension=0, tiled=True
        ).astype(jnp.float32),
        lax.psum_scatter(
            dw_query.astype(jnp.bfloat16), ("narrow", "seq"), scatter_dimension=0, tiled=True
        ).astype(jnp.float32),
        lax.psum_scatter(
            dw_key.astype(jnp.bfloat16), ("narrow", "seq"), scatter_dimension=0, tiled=True
        ).astype(jnp.float32),
        lax.psum_scatter(
            dw_value.astype(jnp.bfloat16), ("narrow", "seq"), scatter_dimension=0, tiled=True
        ).astype(jnp.float32),
        lax.psum_scatter(
            dw_out.astype(jnp.bfloat16), ("narrow", "seq"), scatter_dimension=0, tiled=True
        ).astype(jnp.float32),
        lax.psum_scatter(
            dgain_ffn.astype(jnp.bfloat16), ("narrow", "seq"), scatter_dimension=0, tiled=True
        ).astype(jnp.float32),
        lax.psum_scatter(
            dw_gate.astype(jnp.bfloat16), ("narrow", "seq"), scatter_dimension=0, tiled=True
        ).astype(jnp.float32),
        lax.psum_scatter(
            dw_up.astype(jnp.bfloat16), ("narrow", "seq"), scatter_dimension=0, tiled=True
        ).astype(jnp.float32),
        lax.psum_scatter(
            dw_down.astype(jnp.bfloat16), ("narrow", "seq"), scatter_dimension=0, tiled=True
        ).astype(jnp.float32),
    )
    return (
        output,
        grad_input,
        summed_grads[0],
        summed_grads[1],
        summed_grads[2],
        summed_grads[3],
        summed_grads[4],
        summed_grads[5],
        summed_grads[6],
        summed_grads[7],
        summed_grads[8],
    )


def by_plane(
    tokens,
    gain_attn,
    w_query,
    w_key,
    w_value,
    w_out,
    gain_ffn,
    w_gate,
    w_up,
    w_down,
    lengths,
    cotangent,
):
    N, W, S = (lax.axis_size(a) for a in ("narrow", "wide", "seq"))
    n, s = lax.axis_index("narrow"), lax.axis_index("seq")
    P8 = N * W
    RB, cols = tokens.shape
    R, D = N * RB, W * cols
    hd = w_key.shape[2]
    group = w_query.shape[2] // hd
    qw = group * hd
    rows, block = RB // W, D // (N * S)
    half_d, half_h = w_gate.shape[0], w_gate.shape[1] // N
    nseq = lengths.shape[0]
    chunk = RB // 2
    chunks = R // chunk
    fold = math.log2(math.e) / math.sqrt(hd)
    starts = jnp.cumsum(lengths) - lengths
    heads_shape, kv_shape, full_shape = (S, RB, N * hd), (S, R, 2 * hd), (R, D)
    slab_shape, own_shape = (N, S, block, half_h), (rows, D)

    def block_view(ref, chip, core):
        a, b = chip // (W // 2), lax.rem(chip, W // 2) * 2 + core
        return ref.at[pl.ds(a * RB, RB), pl.ds(b * cols, cols)]

    def row_view(ref, chip, core):
        return ref.at[chip * 2 + core]

    def to_seq():
        return Exchange(S, "seq", lambda src, j: src.at[j])

    def to_rows():
        return Exchange(N * S, "rows", lambda src, j: src.at[j])

    def to_narrow():
        return Exchange(N, "narrow", lambda src, j: src.at[j])

    def own_rows(at):
        return pl.ds(pl.multiple_of(at.n * RB + at.w * rows, rows), rows)

    def chunk_rows(c):
        k = c * chunk // RB
        return slice(c * chunk, (c + 1) * chunk), slice(c * chunk - k * RB, (c + 1) * chunk - k * RB), k

    def scale_of(x):
        return lax.rsqrt(jnp.mean(x * x, axis=1, keepdims=True) + NORM_EPSILON)

    w_mine = jnp.concatenate([w_query, w_key, w_value], axis=2).transpose(1, 0, 2)
    width = w_mine.shape[2]
    g_tok, g_w, g_wo = PlaneGather(block_view), HeadGather(S), HeadGather(S)

    def start_body(at, ins, outs, scratch):
        g_w.start(at, ins[1], outs[1])
        g_tok.start(at, ins[0], outs[0])
        g_w.relay()
        g_tok.relay()
        g_tok.relay2()
        g_tok.finish()
        g_w.finish()

    full_in, w_qkv = fused(
        1,
        "gather_start",
        55,
        [g_tok, g_w],
        start_body,
        [(tokens, HBM), (w_mine, HBM)],
        [(full_shape, bf16, HBM), ((N * S,) + w_mine.shape[1:], bf16, HBM)],
    )
    w_qkv = w_qkv.reshape(D, width)

    part_d = half_d // 2
    part_shape = (part_d, half_h)
    mine_w = [w_gate, w_up, w_down]
    n_idx = jnp.stack([n, lax.rem(s, 2)]).astype(jnp.int32)
    swaps = [Swap("narrow") for _ in range(4)]
    passes = [Swap("seq") for _ in range(4)]

    def for_partner(at, ref, start=0, size=part_d):
        rows_ = pl.ds(pl.multiple_of(lax.rem(at.s, 2) * part_d + start, size), size)
        return ref.at[rows_, pl.ds(pl.multiple_of((1 - at.n) * half_h, half_h), half_h)]

    row_ids = ((jnp.arange(N, dtype=jnp.int32) * S + s) * RB)[:, None] + jnp.arange(RB, dtype=jnp.int32)
    row_ids = row_ids.reshape(R)
    cos_table, sin_table = rotation(row_ids - seq_starts(lengths, row_ids), hd)
    cos_lanes = jnp.tile(cos_table, (1, 4))
    sin_lanes = jnp.tile(jnp.concatenate([-sin_table, sin_table], axis=1), (1, 2))

    e_q, e_kv, mv = to_seq(), Exchange(S, "seq", lambda src, j: src), Move()

    def qkv_body(at, ins, outs, scratch):
        x_ref, w_ref, gain_ref, cos_ref, sin_ref, *w_ins = ins
        q_out, kv_out, n1_out, *w_outs = outs
        n1, qs, kvs = scratch
        for sw, src, dst in zip(swaps[:2], w_ins, w_outs):
            sw.start(at, for_partner(at, src), dst)
        swaps[2].start(at, for_partner(at, w_ins[2], 0, part_d // 2), w_outs[2])
        lanes = lax.broadcasted_iota(jnp.int32, (1, 128), 1)
        for c in range(chunks):
            r, rb, k = chunk_rows(c)
            x = x_ref[r].astype(f32)
            normed = (x * scale_of(x) * gain_ref[...]).astype(bf16)
            n1[r] = normed
            qkv = dot(normed, w_ref[...], NN)
            cos, sin = cos_ref[r], sin_ref[r]
            for g in range(0, group, 2):
                y = qkv[:, g * hd : (g + 2) * hd]
                put_pair(qs, g, rb, k, (y * cos + half_swap(y) * sin) * fold)
            y = qkv[:, qw:]
            kvs[r] = jnp.where(lanes < hd, y * cos + half_swap(y) * sin, y).astype(bf16)
        e_kv.start(at, kvs, kv_out)
        e_q.start(at, qs, q_out)
        mv.start(at, n1, n1_out)
        e_kv.finish()
        e_q.finish()
        mv.finish()
        for sw in swaps[:3]:
            sw.finish()

    q_all, kv_all, normed1, *near_w = fused(
        2,
        "qkv_to_heads",
        60,
        [e_q, e_kv, mv] + swaps[:3],
        qkv_body,
        [
            (full_in, VMEM),
            (w_qkv, VMEM),
            (gain_attn[None], VMEM),
            (cos_lanes, VMEM),
            (sin_lanes, VMEM),
            (w_gate, HBM),
            (w_up, HBM),
            (w_down, HBM),
        ],
        [
            (heads_shape, bf16, HBM),
            (kv_shape, bf16, HBM),
            (full_shape, bf16, HBM),
            (part_shape, bf16, HBM),
            (part_shape, bf16, HBM),
            ((part_d // 2, half_h), bf16, HBM),
        ],
        [pltpu.VMEM(full_shape, bf16), pltpu.VMEM((group, RB, N * hd), bf16), pltpu.VMEM((R, 2 * hd), bf16)],
        40,
    )

    g_cot, st_o = PlaneGather(block_view), Stream(S)

    def forward_body(at, ins, outs, scratch):
        cot_in, w_in, wd_in, *attn_ins = ins
        grad_full, back, wo_out, near_out, res = outs
        heads, *work = scratch
        g_wo.start(at, w_in, wo_out)
        swaps[3].start(at, for_partner(at, wd_in, part_d // 2, part_d // 2), near_out)
        g_cot.start(at, cot_in, grad_full)

        def done(k, j):
            turn = lax.rem(j - at.s - 1 + 2 * S, S)
            if k == N - 1:
                st_o.send(at, heads.at[j], back.at[at.s], j)
                pl.when(turn == 1)(g_cot.relay)
                pl.when(turn == 2)(g_cot.relay2)
            else:
                pl.when(turn == 2)(g_wo.relay)

        attn_fwd_body(S, RB, N, nseq, at.s + 1, done, *attn_ins, heads, res, *work)
        st_o.finish(at, heads.at[0], back.at[at.s])
        g_cot.finish()
        g_wo.finish()
        swaps[3].finish()

    kv_scratch = pltpu.VMEM(kv_shape, bf16)
    grad_full, attn_back, w_o, near_last, attn_res = fused(
        8,
        "attn_fwd",
        48,
        [g_cot, st_o, g_wo, swaps[3]],
        forward_body,
        [
            (cotangent, HBM),
            (w_out.transpose(1, 0, 2), HBM),
            (w_down, HBM),
            (starts, SMEM),
            (q_all, VMEM),
            (kv_all, VMEM),
        ],
        [
            (full_shape, bf16, HBM),
            (heads_shape, bf16, HBM),
            ((N * S, block, qw), bf16, HBM),
            ((part_d // 2, half_h), bf16, HBM),
            ((N * S, RB, 2 * hd), f32, VMEM),
        ],
        [pltpu.VMEM(heads_shape, bf16), kv_scratch, kv_scratch, pltpu.VMEM((RB, 2 * hd), f32)],
        48,
    )

    w_o = w_o.reshape(D, qw)

    sc_a, g_n2, mv_x = PlaneScatter(own_shape, row_view), PlaneGather(row_view), Move()
    mvd = [Move() for _ in range(6)]

    def down_parts(at, wd, own_in, near0, near1, far_in):
        odd, m = lax.rem(at.s, 2), part_d // 2
        mine = own_in.at[:, pl.ds(pl.multiple_of(at.n * half_h, half_h), half_h)]

        def place(start, size):
            return wd.at[1 - at.n, pl.ds(pl.multiple_of(start, m), size)]

        parts = [(mine, wd.at[at.n]), (near0, place(odd * part_d, m)), (near1, place(odd * part_d + m, m))]
        return parts + [(far_in, place((1 - odd) * part_d, part_d))]

    def mid_body(at, ins, outs, scratch):
        heads, wo, x_in, gain_ref, dy_in, wd_in, *w_ins = ins
        attn_b, resid, n2_out, dm_out, *w_outs = outs
        part, xr, n2, dy, wd, dm = scratch
        m = part_d // 2
        passes[2].start(at, w_ins[2], w_outs[2].at[pl.ds(0, m)])
        passes[3].start(at, w_ins[3], w_outs[2].at[pl.ds(m, m)])
        for i in range(2):
            passes[i].start(at, w_ins[i], w_outs[i])
        parts = down_parts(at, wd, wd_in, w_ins[2], w_ins[3], w_outs[2])
        mvd[0].start(at, dy_in, dy)
        for i in range(3):
            mvd[1 + i].start(at, *parts[i])
        mv_x.start(at, x_in.at[own_rows(at)], xr)
        for k in range(N):
            for g in range(0, group, 2):
                pair = pair_up(heads[g], heads[g + 1], k).astype(bf16)
                attn_b[k * RB : (k + 1) * RB, g * hd : (g + 2) * hd] = pair
        for c in range(chunks):
            r = slice(c * chunk, (c + 1) * chunk)
            b = c * chunk // rows
            out = dot(attn_b[r], wo[...], NT).astype(bf16)
            part[b : b + chunk // rows] = out.reshape(chunk // rows, rows, D)
        sc_a.start(at, part)
        sc_a.mid()
        sc_a.mid2()
        passes[2].finish()
        passes[3].finish()
        mvd[4].start(at, *parts[3])
        mv_x.finish()
        h = xr[...].astype(f32) + sc_a.finish()
        resid[...] = h
        n2[...] = (h * scale_of(h) * gain_ref[...]).astype(bf16)
        g_n2.start(at, n2, n2_out)
        for mv_ in mvd[:5]:
            mv_.finish()
        quarter = half_h // 4

        def dm_tile(i, _):
            c = pl.ds(pl.multiple_of(i * quarter, quarter), quarter)
            dm[:, c] = dot(dy[...], wd.at[:, :, c][...].reshape(D, quarter), NN).astype(bf16)
            return 0

        lax.fori_loop(0, 4, dm_tile, 0)
        mvd[5].start(at, dm, dm_out)
        g_n2.relay()
        g_n2.relay2()
        g_n2.finish()
        mvd[5].finish()
        for ps in passes[:2]:
            ps.finish()

    attn_b, residual, normed2, grad_hidden, *far_w = fused(
        3,
        "attn_to_ffn",
        88,
        [sc_a, g_n2, mv_x] + passes + mvd,
        mid_body,
        [
            (attn_back, VMEM),
            (w_o, VMEM),
            (full_in, HBM),
            (gain_ffn[None], VMEM),
            (grad_full, HBM),
            (w_down, HBM),
        ]
        + [(x, HBM) for x in (*near_w, near_last)],
        [
            ((R, qw), bf16, VMEM),
            (own_shape, f32, VMEM),
            ((P8,) + own_shape, bf16, HBM),
            ((R, half_h), bf16, HBM),
        ]
        + [(part_shape, bf16, HBM)] * 3,
        [
            pltpu.VMEM((P8,) + own_shape, bf16),
            pltpu.VMEM(own_shape, bf16),
            pltpu.VMEM(own_shape, bf16),
            pltpu.VMEM(full_shape, bf16),
            pltpu.VMEM((N, half_d, half_h), bf16),
            pltpu.VMEM((R, half_h), bf16),
        ],
        60,
    )
    normed2 = normed2.reshape(full_shape)
    got_w = list(zip(near_w[:2], far_w[:2]))

    hidden, grad_gate_val, grad_up_val = hidden_units(n_idx, normed2, grad_hidden, mine_w, got_w)

    slab_block = (N, block, half_h)

    half_block = (1,) + slab_block[1:]

    def seq_sum():
        return SeqSum(slab_block, lambda src, j: src.at[:, j])

    def seq_sum_half(a):
        return SeqSum(half_block, lambda src, j: src.at[pl.ds(a, 1), j])

    sc_n, g_db = PlaneScatter(own_shape, row_view), PlaneGather(row_view)
    q_down, q_gate0 = seq_sum(), seq_sum_half(0)
    mvs, mvk, mvw = ([Move() for _ in range(i)] for i in (6, N * S, 2 * N * S))

    def tile_cols(a, j):
        return pl.ds(pl.multiple_of((a * S + j) * block, block), block)

    def ffn_body(at, ins, outs, scratch):
        dy_in, m_in, n2_in, dg_in, dp_in, resid, gain_ref, *w_ins = ins
        db_out, dresid, dgain, down_out, gate0_out, gate_out, up_out = outs
        dy, m, n2, dg, dp, down, gate, db = scratch
        for mv_, src, dst in zip(mvs, (m_in, dy_in, dg_in, dp_in), (m, dy, dg, dp)):
            mv_.start(at, src, dst)

        def side_tile(ref, t):
            r = pl.ds(pl.multiple_of((t // 2) * block, block), block)
            return ref.at[r, pl.ds(pl.multiple_of(lax.rem(t, 2) * half_h, half_h), half_h)]

        odd, per = lax.rem(at.s, 2), part_d // block
        for i, (own_w, near, far) in enumerate((w_ins[:3], w_ins[3:])):
            own_cols = pl.ds(pl.multiple_of(at.n * half_h, half_h), half_h)
            pieces = [(own_w.at[pl.ds(k * block, block), own_cols], at.n * S + k) for k in range(S)]
            for k in range(per):
                r = pl.ds(k * block, block)
                pieces.append((near.at[r], (1 - at.n) * S + odd * per + k))
                pieces.append((far.at[r], (1 - at.n) * S + (1 - odd) * per + k))
            for k, (src, t) in enumerate(pieces):
                dst = side_tile(n2, t) if i else gate.at[t // S, lax.rem(t, S)]
                mvw[i * N * S + k].start(at, src, dst)
        sc_n.begin(at)
        q_down.begin(at, down)
        q_gate0.begin(at, gate)
        mvs[0].finish()
        mvs[1].finish()

        def down_block(i):
            j = q_down.order(at)[i]
            for a in range(N):
                down[a, j] = dot(dy[:, tile_cols(a, j)], m[...], TN).astype(bf16)
            q_down.ready(at, i)

        down_block(0)
        down_block(1)
        for mv_ in mvs[2:4] + mvw:
            mv_.finish()
        mine = sc_n.bufs[0]

        def outgoing(i):
            return n2.at[pl.ds(half_d + (i % 2) * rows, rows)]

        def back_rows(i):
            r = pl.ds(pl.multiple_of(sc_n.chips(at)[i] * 2 * rows, 2 * rows), 2 * rows)

            def tile_(t, _):
                out = dot(dg[r], gate[t // S, lax.rem(t, S)], NT) + dot(dp[r], side_tile(n2, t)[...], NT)
                c = pl.ds(pl.multiple_of(t * block, block), block)
                low, high = out[:rows].astype(bf16), out[rows:].astype(bf16)
                first = at.core == 0
                mine[i, :, c] = jnp.where(first, low, high)
                outgoing(i)[:, c] = jnp.where(first, high, low)
                return 0

            lax.fori_loop(0, N * S, tile_, 0)
            sc_n.hand(at, i, outgoing(i))

        back_rows(0)
        back_rows(1)
        sc_n.near[0].wait_send()
        back_rows(2)
        sc_n.near[1].wait_send()
        back_rows(3)
        sc_n.mid()
        q_down.step(at, 0)
        sc_n.near[2].wait_send()
        sc_n.near[3].wait_send()
        mvs[4].start(at, n2_in, n2)
        down_block(2)
        sc_n.mid2()
        mvs[4].finish()
        for i in range(4):
            j = q_gate0.order(at)[i]
            gate[0, j] = dot(n2[:, tile_cols(0, j)], dg[...], TN).astype(bf16)
            q_gate0.ready(at, i)
        down_block(3)
        db[...] = dy[own_rows(at)]

        def other_tiles(j, _):
            for a in range(N):
                c = tile_cols(a, j)
                if a:
                    gate[a, j] = dot(n2[:, c], dg[...], TN).astype(bf16)
                side_tile(dy, a * S + j)[...] = dot(n2[:, c], dp[...], TN).astype(bf16)
            return 0

        lax.fori_loop(0, 2, other_tiles, 0)
        q_gate0.step(at, 0)
        lax.fori_loop(2, S, other_tiles, 0)
        mvs[5].start(at, gate, gate_out)
        for t, mv_ in enumerate(mvk):
            mv_.start(at, side_tile(dy, t), up_out.at[t // S, t % S])
        dn2 = sc_n.finish()
        h = resid[...]
        r2 = scale_of(h)
        dgain[...] = jnp.sum(dn2 * h * r2, axis=0, keepdims=True)
        scaled = dn2 * gain_ref[...]
        own = db[...].astype(f32)
        grad = own + r2 * scaled - h * (r2 * r2 * r2) * jnp.mean(scaled * h, axis=1, keepdims=True)
        dresid[...] = grad
        db[...] = grad.astype(bf16)
        g_db.start(at, db, db_out)
        q_down.step(at, 1)
        q_down.step3(at)
        q_gate0.step(at, 1)
        q_gate0.step3(at)
        g_db.relay()
        g_db.relay2()
        g_db.finish()
        down_out[...] = q_down.total(at).astype(bf16)
        gate0_out[...] = q_gate0.total(at).astype(bf16)
        for mv_ in mvs[5:] + mvk:
            mv_.finish()

    dbranch, dresid, dgain_ffn, down_own, gate_own0, dw_gate, dw_up = fused(
        4,
        "ffn_grads",
        110,
        [sc_n, g_db, q_down, q_gate0] + mvs + mvk + mvw,
        ffn_body,
        [
            (grad_full, HBM),
            (hidden, HBM),
            (normed2, HBM),
            (grad_gate_val, HBM),
            (grad_up_val, HBM),
            (residual, VMEM),
            (gain_ffn[None], VMEM),
            (w_gate, HBM),
            (got_w[0][0], HBM),
            (got_w[0][1], HBM),
            (w_up, HBM),
            (got_w[1][0], HBM),
            (got_w[1][1], HBM),
        ],
        [
            ((P8,) + own_shape, bf16, HBM),
            (own_shape, f32, VMEM),
            ((1, D), f32, VMEM),
            (slab_block, bf16, VMEM),
            (half_block, bf16, VMEM),
            (slab_shape, bf16, HBM),
            (slab_shape, bf16, HBM),
        ],
        [
            pltpu.VMEM(full_shape, bf16),
            pltpu.VMEM((R, half_h), bf16),
            pltpu.VMEM(full_shape, bf16),
            pltpu.VMEM((R, half_h), bf16),
            pltpu.VMEM((R, half_h), bf16),
            pltpu.VMEM(slab_shape, bf16),
            pltpu.VMEM(slab_shape, bf16),
            pltpu.VMEM(own_shape, bf16),
        ],
        60,
    )

    e_do, t_down = to_seq(), to_narrow()
    mvt = [Move() for _ in range(8)]
    tile = half_d // 4

    def grad_heads_body(at, ins, outs, scratch):
        db_in, w_ref, ab, down_in, m_in, wd_in, wd0_in, wd1_in, wd2_in, resid = ins
        do_out, dwo_out, y_out, down_out = outs
        db, dos, m, wd, y, dwo = scratch
        moves = [(db_in, db), (m_in, m)] + down_parts(at, wd, wd_in, wd0_in, wd1_in, wd2_in)
        for mv_, (src, dst) in zip(mvt, moves):
            mv_.start(at, src, dst)
        mvt[0].finish()
        for c in range(chunks):
            r, rb, k = chunk_rows(c)
            out = dot(db[r], w_ref[...], NN)
            for g in range(0, group, 2):
                put_pair(dos, g, rb, k, out[:, g * hd : (g + 2) * hd])
        e_do.start(at, dos, do_out)
        t_down.start(at, down_in, down_out)

        def wo_tile(p, _):
            c = pl.ds(pl.multiple_of(p * block, block), block)
            dwo[p] = dot(db[:, c], ab[...], TN).astype(bf16)
            return 0

        lax.fori_loop(0, N * S, wo_tile, 0)
        mvt[6].start(at, dwo, dwo_out)
        for mv_ in mvt[1:6]:
            mv_.finish()
        for a in range(N):

            def y_tile(i, _):
                c = pl.ds(pl.multiple_of(a * half_d + i * tile, tile), tile)
                w_tile = wd[a, pl.ds(pl.multiple_of(i * tile, tile), tile), :]
                y[:, c] = dot(m[...], w_tile, NT).astype(bf16)
                return 0

            lax.fori_loop(0, half_d // tile, y_tile, 0)
        o = own_rows(at)
        y[o] = (y[o].astype(f32) + resid[...]).astype(bf16)
        mvt[7].start(at, y, y_out)
        e_do.finish()
        t_down.finish()
        mvt[6].finish()
        mvt[7].finish()

    do_all, dw_o, down_part, traded_down = fused(
        5,
        "grad_to_heads",
        25,
        [e_do, t_down] + mvt,
        grad_heads_body,
        [
            (dbranch.reshape(full_shape), HBM),
            (w_o, VMEM),
            (attn_b, VMEM),
            (down_own, HBM),
            (hidden, HBM),
            (w_down, HBM),
            (near_w[2], HBM),
            (near_last, HBM),
            (far_w[2], HBM),
            (residual, VMEM),
        ],
        [
            (heads_shape, bf16, HBM),
            ((N * S, block, qw), bf16, HBM),
            (full_shape, bf16, HBM),
            ((N, block, half_h), bf16, HBM),
        ],
        [
            pltpu.VMEM(full_shape, bf16),
            pltpu.VMEM((group, RB, N * hd), bf16),
            pltpu.VMEM((R, half_h), bf16),
            pltpu.VMEM((N, half_d, half_h), bf16),
            pltpu.VMEM(full_shape, bf16),
            pltpu.VMEM((N * S, block, qw), bf16),
        ],
        56,
    )

    q_gate, t_up, sc_y = seq_sum_half(1), to_narrow(), PlaneScatter((RB, cols), block_view)
    st_kv, st_q = [Stream(S) for _ in range(N)], [Stream(S) for _ in range(N)]

    def backward_body(at, ins, outs, scratch):
        gate_in, up_in, y_in, *attn_ins = ins
        gate_out, up_out, out_ref, dq_all, dkv_all = outs
        dq, dkv, *work = scratch
        sc_y.start(at, y_in)
        t_up.start(at, up_in, up_out)
        q_gate.start(at, gate_in)

        def pieces(k):
            r = pl.ds(k * RB, RB)
            return (lambda j: dkv.at[j, r]), dkv_all.at[at.s, r]

        def done(k, j, turn):
            src, dst = pieces(k)
            st_kv[k].send(at, src(j), dst, j)
            if k == 0:

                @pl.when(turn == 0)
                def _():
                    sc_y.mid()
                    q_gate.step(at, 0)

                @pl.when(turn == 1)
                def _():
                    q_gate.step(at, 1)
                    q_gate.step3(at)

                pl.when(turn == 2)(sc_y.mid2)

        def phase(k):
            for j in range(S):
                st_q[k].send(at, dq.at[k, j], dq_all.at[at.s, k], j)

        attn_bwd_body(S, RB, N, nseq, at.s + 1, done, phase, *attn_ins, dq, dkv, *work)
        out_ref[...] = sc_y.finish().astype(bf16)
        gate_out[...] = q_gate.total(at).astype(bf16)
        for k in range(N):
            src, dst = pieces(k)
            st_kv[k].finish(at, src(0), dst)
            st_q[k].finish(at, dq.at[k, 0], dq_all.at[at.s, k])
        t_up.finish()

    q_scratch, acc_scratch = pltpu.VMEM((N * S, RB, 2 * hd), bf16), pltpu.VMEM((RB, 2 * hd), f32)
    gate_own1, traded_up, output, dq_all, dkv_all = fused(
        6,
        "attn_bwd",
        110,
        [q_gate, t_up, sc_y] + st_q + st_kv,
        backward_body,
        [
            (dw_gate, HBM),
            (dw_up, HBM),
            (down_part, HBM),
            (starts, SMEM),
            (q_all, VMEM),
            (kv_all, VMEM),
            (do_all, VMEM),
            (attn_res, VMEM),
        ],
        [
            (half_block, bf16, VMEM),
            (slab_shape, bf16, HBM),
            ((RB, cols), bf16, VMEM),
            ((S, N, chunk, 2 * hd), bf16, HBM),
            (kv_shape, bf16, HBM),
        ],
        [
            pltpu.VMEM((N, S, chunk, 2 * hd), bf16),
            kv_scratch,
            kv_scratch,
            kv_scratch,
            q_scratch,
            q_scratch,
            pltpu.VMEM((N * S, RB, 2 * hd), f32),
            acc_scratch,
            acc_scratch,
        ],
        60,
    )

    q_up, t_gate, e_wog, e_wq = seq_sum(), to_narrow(), to_rows(), to_rows()
    sc_1 = PlaneScatter(own_shape, row_view)
    e_in = Exchange(W, "wide", lambda src, j: src.at[:, pl.ds(pl.multiple_of(j * cols, cols), cols)])
    e_gain = Exchange(N * S * W, "all", lambda src, j: src.at[j // W])
    mvu = [Move() for _ in range(2)]

    def last_body(at, ins, outs, scratch):
        dq, dkv, gate_in0, gate_in1, down_in, dwo_in, n1_in, up_in, x_in, w_ref, cos_ref, sin_ref, dresid_ref, gain_ref, dgain_ref = ins
        gi_out, gains_out, got_wq, got_wo, gate_out, up_out, down_out = outs
        n1, dqkv, part, dwq, xr, gi, gains, gate_s, gate_r = scratch

        def widen(out, halves):
            for a in range(N):
                out[:, a * half_h : (a + 1) * half_h] = halves[a].astype(f32)

        q_up.start(at, up_in)
        mvu[0].start(at, n1_in, n1)
        mvu[1].start(at, x_in.at[own_rows(at)], xr)
        gate_s[0] = gate_in0[0]
        gate_s[1] = gate_in1[0]
        t_gate.start(at, gate_s, gate_r)
        lanes = lax.broadcasted_iota(jnp.int32, (1, 128), 1)
        for c in range(chunks):
            r, rb, k = chunk_rows(c)
            cos, sin = cos_ref[r], sin_ref[r]
            for g in range(0, group, 2):
                y = pair_up(dq[g, k], dq[g + 1, k], c % 2)
                dqkv[r, g * hd : (g + 2) * hd] = (y * cos - half_swap(y) * sin).astype(bf16)
            y = sum(dkv[i, r].astype(f32) for i in range(S))
            dqkv[r, qw:] = jnp.where(lanes < hd, y * cos - half_swap(y) * sin, y).astype(bf16)
            out = dot(dqkv[r], w_ref[...], NT).astype(bf16)
            b = c * chunk // rows
            part[b : b + chunk // rows] = out.reshape(chunk // rows, rows, D)
        sc_1.start(at, part)
        mvu[0].finish()

        def wq_tile(p, _):
            c = pl.ds(pl.multiple_of(p * block, block), block)
            dwq[p] = dot(n1[:, c], dqkv[...], TN).astype(bf16)
            return 0

        lax.fori_loop(0, N * S, wq_tile, 0)
        sc_1.mid()
        q_up.step(at, 0)
        sc_1.mid2()
        e_wq.start(at, dwq, got_wq)
        e_wog.start(at, dwo_in, got_wo)
        mvu[1].finish()
        x = xr[...].astype(f32)
        r1 = scale_of(x)
        dn1 = sc_1.finish()
        q_up.step(at, 1)
        q_up.step3(at)
        dgain = jnp.sum(dn1 * x * r1, axis=0, keepdims=True)
        dgain2 = dgain_ref[...]
        for p in range(N * S):
            for i in range(block // 128):
                c = slice(p * block + i * 128, p * block + (i + 1) * 128)
                gains[p, i : i + 1, :] = dgain[:, c]
                gains[p, block // 128 + i : block // 128 + i + 1, :] = dgain2[:, c]
        e_gain.start(at, gains, gains_out)
        scaled = dn1 * gain_ref[...]
        grad = dresid_ref[...] + r1 * scaled - x * (r1 * r1 * r1) * jnp.mean(scaled * x, axis=1, keepdims=True)
        gi[...] = grad.astype(bf16)
        e_in.start(at, gi, gi_out)
        widen(down_out, down_in)
        t_gate.finish()
        widen(gate_out, gate_r)
        widen(up_out, q_up.total(at))
        for p in (e_in, e_gain, e_wq, e_wog):
            p.finish()

    gains_shape = (N * S, 2 * block // 128, 128)
    grad_input, gains, got_wq, got_wo, gate_grad, up_grad, down_grad = fused(
        7,
        "last",
        160,
        [q_up, t_gate, e_wog, e_wq, sc_1, e_in, e_gain] + mvu,
        last_body,
        [
            (dq_all, VMEM),
            (dkv_all, VMEM),
            (gate_own0, VMEM),
            (gate_own1, VMEM),
            (traded_down, VMEM),
            (dw_o, HBM),
            (normed1, HBM),
            (traded_up, HBM),
            (full_in, HBM),
            (w_qkv, VMEM),
            (cos_lanes, VMEM),
            (sin_lanes, VMEM),
            (dresid, VMEM),
            (gain_attn[None], VMEM),
            (dgain_ffn, VMEM),
        ],
        [
            ((W, rows, cols), bf16, HBM),
            ((N * S * W,) + gains_shape[1:], f32, HBM),
            ((N * S, block, width), bf16, HBM),
            ((N * S, block, qw), bf16, HBM),
            ((block, N * half_h), f32, VMEM),
            ((block, N * half_h), f32, VMEM),
            ((block, N * half_h), f32, VMEM),
        ],
        [
            pltpu.VMEM(full_shape, bf16),
            pltpu.VMEM((R, width), bf16),
            pltpu.VMEM((P8,) + own_shape, bf16),
            pltpu.VMEM((N * S, block, width), bf16),
            pltpu.VMEM(own_shape, bf16),
            pltpu.VMEM(own_shape, bf16),
            pltpu.VMEM(gains_shape, f32),
            pltpu.VMEM(slab_block, bf16),
            pltpu.VMEM(slab_block, bf16),
        ],
        60,
    )

    def over_seq(got):
        return jnp.sum(got.reshape(N, S, *got.shape[1:]).astype(f32), axis=1)

    gains = jnp.sum(gains, axis=0).reshape(2, block)
    qkv_grads = over_seq(got_wq).transpose(1, 0, 2)
    return (
        output,
        grad_input.reshape(RB, cols),
        gains[0],
        qkv_grads[:, :, :qw],
        qkv_grads[:, :, qw : qw + hd],
        qkv_grads[:, :, qw + hd :],
        over_seq(got_wo).transpose(1, 0, 2),
        gains[1],
        gate_grad,
        up_grad,
        down_grad,
    )


def local(tokens, gain_attn, w_query, w_key, *others):
    plane = lax.axis_size("narrow") * lax.axis_size("wide")
    heads_kv = w_key.shape[1] * lax.axis_size("wide")
    group = w_query.shape[2] // w_key.shape[2]
    fits = lax.axis_size("narrow") == 2 and heads_kv == plane and group == lax.axis_size("seq")
    body = by_plane if fits and w_key.shape[2] == 64 else by_rows
    return body(tokens, gain_attn, w_query, w_key, *others)


def solution(mesh):
    return jax.shard_map(
        local,
        mesh=mesh,
        in_specs=(
            P(("narrow", "seq"), "wide"),
            P(),
            P(("narrow", "seq"), "wide", None),
            P(("narrow", "seq"), "wide", None),
            P(("narrow", "seq"), "wide", None),
            P(("narrow", "seq"), "wide", None),
            P(),
            P("narrow", "wide"),
            P("narrow", "wide"),
            P("narrow", "wide"),
            P(),
            P(("narrow", "seq"), "wide"),
        ),
        out_specs=(
            P(("narrow", "seq"), "wide"),
            P(("narrow", "seq"), "wide"),
            P(("narrow", "seq")),
            P(("narrow", "seq"), "wide", None),
            P(("narrow", "seq"), "wide", None),
            P(("narrow", "seq"), "wide", None),
            P(("narrow", "seq"), "wide", None),
            P(("narrow", "seq")),
            P(("narrow", "seq"), "wide"),
            P(("narrow", "seq"), "wide"),
            P(("narrow", "seq"), "wide"),
        ),
        check_vma=False,
    )
```
